32 devices in a mesh: fsdp: 4 (over y, x), tp: 8 (over z, core).
Axes of the slice: x: 2, y: 2, z: 4, core: 2. Of those that a mesh axis runs over, the one named last changes fastest.
Arguments:
- activations: float32 [8192, 2048], P(('fsdp', 'tp')), may hold values from -6 to 6
- gain_attn: float32 [2048], replicated, may hold values from 0.1 to 1.9
- w_query: bfloat16 [2048, 2048], P('fsdp', 'tp'), may hold values from -0.1875 to 0.1875
- w_key: bfloat16 [2048, 2048], P('fsdp', 'tp'), may hold values from -0.1875 to 0.1875
- w_value: bfloat16 [2048, 2048], P('fsdp', 'tp'), may hold values from -0.125 to 0.125
- w_out: bfloat16 [2048, 2048], P('tp', 'fsdp'), may hold values from -0.25 to 0.25
- gain_mlp: float32 [2048], replicated, may hold values from 0.1 to 1.9
- w_gate: bfloat16 [2048, 8192], P('fsdp', 'tp'), may hold values from -0.125 to 0.125
- w_up: bfloat16 [2048, 8192], P('fsdp', 'tp'), may hold values from -0.125 to 0.125
- w_down: bfloat16 [8192, 2048], P('tp', 'fsdp'), may hold values from -0.0625 to 0.0625
- cotangent: float32 [8192, 2048], P(('fsdp', 'tp')), may hold values from -6 to 6
Outputs:
- output: float32 [8192, 2048], P(('fsdp', 'tp'))
- input_grad: float32 [8192, 2048], P(('fsdp', 'tp'))
- grad_gain_attn: float32 [2048], replicated
- grad_query: float32 [2048, 2048], P('fsdp', 'tp')
- grad_key: float32 [2048, 2048], P('fsdp', 'tp')
- grad_value: float32 [2048, 2048], P('fsdp', 'tp')
- grad_out: float32 [2048, 2048], P('tp', 'fsdp')
- grad_gain_mlp: float32 [2048], replicated
- grad_gate: float32 [2048, 8192], P('fsdp', 'tp')
- grad_up: float32 [2048, 8192], P('fsdp', 'tp')
- grad_down: float32 [8192, 2048], P('tp', 'fsdp')
The draws below stay inside these ranges and needn't reach their ends.
All inputs are finite; a program needn't handle non-finite values.
Results may differ from the reference program's by a relative error of at most 0.019.
Values may be sent and summed in bfloat16 or wider, within the bound.
A program may use at most 320 MiB of HBM per device.

```python
import jax
import jax.numpy as jnp
from jax import lax

D = 2048
HEADS = 32
HEAD_DIM = 64
FF = 8192
SEQ_LEN = 2048
BLOCK = 512
TOKENS = 8192


def with_spikes(values, key, source, target, blocks, factor):
    owner, partner = [(jnp.arange(values.shape[position]) // (values.shape[position] // blocks)).reshape([-1 if axis == position else 1 for axis in range(values.ndim)]) for position in (source, target)]
    chosen = jax.random.permutation(key, blocks)[partner]
    strong = (owner == chosen) | (owner == (partner + blocks // 2) % blocks)
    return jnp.where(strong, factor * values, values)


def block_scale(own_key, extent, split, least, top_value):
    level, own = 1.0, jax.random.fold_in(own_key, 6)
    for position, shards_of in split:
        heights = jnp.exp(jax.random.uniform(jax.random.fold_in(own, position), (shards_of,), jnp.float32, least / len(split), top_value / len(split)))
        level = level * jnp.repeat(heights, extent[position] // shards_of).reshape([-1 if axis == position else 1 for axis in range(len(extent))])
    return level


def scatter_about(rng, extent, deviation, limit, cuts=(), kind=jnp.bfloat16):
    loudness = block_scale(rng, extent, cuts, -0.22, 0.18) if cuts else 1.0
    array = jax.random.normal(rng, extent, jnp.float32) * deviation * loudness
    return jnp.minimum(jnp.maximum(array, -limit), limit).astype(kind)


def gaussian_with(own_key, shape, deviation, bound, cuts, heavy, held_as=jnp.bfloat16):
    array = deviation * jax.random.normal(own_key, shape, jnp.float32)
    if cuts:
        array = array * block_scale(own_key, shape, cuts, -0.22, 0.18)
    return jnp.clip(with_spikes(array, jax.random.fold_in(own_key, 3), *heavy), -bound, bound).astype(held_as)


def setup_inputs(seed: int = 0) -> dict:
    splits = jax.random.split(jax.random.key(seed), 12)
    return {
        "activations": scatter_about(splits[0], (TOKENS, D), 1.0, 6.0, ((0, 32),), jnp.float32),
        "gain_attn": jnp.clip(1.0 + 0.18 * jax.random.normal(splits[1], (D,), jnp.float32), 0.1, 1.9),
        "w_query": scatter_about(splits[2], (D, D), (D // 2) ** -0.5, 0.1875, ((0, 4), (1, 8))),
        "w_key": scatter_about(splits[3], (D, D), (D // 2) ** -0.5, 0.1875, ((0, 4), (1, 8))),
        "w_value": scatter_about(splits[4], (D, D), D ** -0.5, 0.125, ((0, 4), (1, 8))),
        "w_out": scatter_about(splits[5], (D, D), (D // 4) ** -0.5, 0.25, ((0, 8), (1, 4))),
        "gain_mlp": jnp.clip(1.0 + 0.18 * jax.random.normal(splits[6], (D,), jnp.float32), 0.1, 1.9),
        "w_gate": scatter_about(splits[7], (D, FF), D ** -0.5, 0.125, ((0, 4), (1, 8))),
        "w_up": scatter_about(splits[8], (D, FF), D ** -0.5, 0.125, ((0, 4), (1, 8))),
        "w_down": scatter_about(splits[9], (FF, D), FF ** -0.5, 0.0625, ((0, 8), (1, 4))),
        "cotangent": gaussian_with(splits[10], (TOKENS, D), 1.0, 6.0, ((0, 32),), (0, 1, 32, 2.75), jnp.float32),
    }


@jax.custom_vjp
def low(v):
    return lax.optimization_barrier(v.astype(jnp.bfloat16)).astype(jnp.float32)

@jax.custom_vjp
def low_back(v):
    return v

def low_keep(v):
    return (low(v), None)

def low_pass(kept, grad):
    return (grad,)

def back_keep(v):
    return (v, None)

def back_low(kept, grad):
    return (low(grad),)
low.defvjp(low_keep, low_pass)
low_back.defvjp(back_keep, back_low)
rope_base = 130000.0
norm_eps = 1e-05
masked_score = -1e+30
highest = lax.Precision.HIGHEST

def matmul(left, right):
    return jnp.dot(left, right, precision=highest, preferred_element_type=jnp.float32)

def rms_norm(values, gain):
    return values * lax.rsqrt(lax.optimization_barrier(jnp.mean(values * values, axis=-1, keepdims=True)) + norm_eps) * gain

def rope_tables(count):
    positions = (jnp.arange(count, dtype=jnp.int32) % SEQ_LEN).astype(jnp.float32)
    column = jnp.arange(HEAD_DIM, dtype=jnp.int32) % (HEAD_DIM // 2)
    inverse = jnp.power(jnp.float32(rope_base), -2.0 * column.astype(jnp.float32) / HEAD_DIM)
    angle = positions[:, None] * inverse[None, :]
    return (jnp.cos(angle)[:, None, :], jnp.sin(angle)[:, None, :])

def rotate(values, cosine, sine):
    half = HEAD_DIM // 2
    turned = jnp.concatenate([-values[..., half:], values[..., :half]], axis=-1)
    return values * cosine + turned * sine

def split_heads(block):
    return block.reshape(block.shape[0], HEADS, HEAD_DIM)

def attention(query, keys, values):
    blocks = SEQ_LEN // BLOCK
    scale = HEAD_DIM ** (-0.5)

    def one_block(index):
        start = index * BLOCK
        rows = lax.dynamic_slice_in_dim(query, start, BLOCK, 0)
        scores = low_back(jnp.einsum('bhd,lhd->hbl', rows, keys, precision=highest) * scale)
        query_pos = start + jnp.arange(BLOCK, dtype=jnp.int32)
        key_pos = jnp.arange(SEQ_LEN, dtype=jnp.int32)
        scores = jnp.where(key_pos[None, None, :] <= query_pos[None, :, None], scores, masked_score)
        probs = low(jax.nn.softmax(scores, axis=-1))
        return jnp.einsum('hbl,lhd->bhd', probs, values, precision=highest)
    mixed = lax.map(jax.checkpoint(one_block), jnp.arange(blocks, dtype=jnp.int32))
    return mixed.reshape(SEQ_LEN, HEADS * HEAD_DIM)

def layer(activations, gain_attn, w_query, w_key, w_value, w_out, gain_mlp, w_gate, w_up, w_down):
    cosine, sine = rope_tables(SEQ_LEN)
    normed_attn = low(rms_norm(activations, gain_attn))
    query = low(rotate(split_heads(low_back(matmul(normed_attn, w_query))), cosine, sine))
    keys = low(rotate(split_heads(low_back(matmul(normed_attn, w_key))), cosine, sine))
    values = low(split_heads(low_back(matmul(normed_attn, w_value))))
    mixed = low(low_back(attention(query, keys, values)))
    hidden_state = activations + low_back(matmul(mixed, w_out))
    normed_mlp = low(rms_norm(hidden_state, gain_mlp))
    gate = low_back(matmul(normed_mlp, w_gate))
    up_value = low_back(matmul(normed_mlp, w_up))
    inner = low(jax.nn.silu(gate) * up_value)
    return hidden_state + low_back(matmul(inner, w_down))

def reference(activations, gain_attn, w_query, w_key, w_value, w_out, gain_mlp, w_gate, w_up, w_down, cotangent):
    params = (gain_attn.astype(jnp.float32), w_query.astype(jnp.float32), w_key.astype(jnp.float32), w_value.astype(jnp.float32), w_out.astype(jnp.float32), gain_mlp.astype(jnp.float32), w_gate.astype(jnp.float32), w_up.astype(jnp.float32), w_down.astype(jnp.float32))
    seq_inputs = activations.astype(jnp.float32).reshape(-1, SEQ_LEN, D)
    seq_grads = cotangent.astype(jnp.float32).reshape(-1, SEQ_LEN, D)

    def step(totals, pair):
        outputs, pull = jax.vjp(layer, pair[0], *params)
        grads = pull(pair[1])
        summed = tuple((total + grad for total, grad in zip(totals, grads[1:])))
        return (summed, (outputs, grads[0]))
    zeros = tuple((jnp.zeros(param.shape, jnp.float32) for param in params))
    totals, (outputs, input_grads) = lax.scan(step, zeros, (seq_inputs, seq_grads))
    return (outputs.reshape(TOKENS, D), input_grads.reshape(TOKENS, D), totals[0], totals[1], totals[2], totals[3], totals[4], totals[5], totals[6], totals[7], totals[8])
```

```python
import jax
import jax.numpy as jnp
from jax import lax
from jax.experimental import pallas as pl
from jax.experimental.pallas import tpu as pltpu
from jax.sharding import PartitionSpec as P

HEAD_DIM = 64
SEQ_LEN = 2048
rope_base = 130000.0
norm_eps = 1e-05
masked_score = -1e30

NT = (((1,), (1,)), ((), ()))
NN = (((1,), (0,)), ((), ()))


def dot(left, right, dims=NN):
    return lax.dot_general(left, right, dims, preferred_element_type=jnp.float32)


def only_head(block, head):
    lane = lax.broadcasted_iota(jnp.int32, block.shape, 1)
    return jnp.where(lane // HEAD_DIM == head, block, jnp.zeros_like(block))


def causal(tile):
    key = lax.broadcasted_iota(jnp.int32, tile.shape, 0)
    query = lax.broadcasted_iota(jnp.int32, tile.shape, 1)
    return jnp.where(key <= query, tile, masked_score)


def attend_kernel(place_ref, query_ref, keys_ref, values_t_ref, mixed_ref, total_ref, heads_ref, acc_ref, out_ref, top_ref, sum_ref):
    rows, width = query_ref.shape
    half = rows // 2
    heads = width // HEAD_DIM
    core = place_ref[0]
    start = place_ref[1] * rows
    first = start // SEQ_LEN * SEQ_LEN
    full = (start - first) // rows
    scaled = query_ref[...] * jnp.bfloat16(HEAD_DIM**-0.5)
    for head in range(heads):
        heads_ref[head] = only_head(scaled, head)
    acc_ref[...] = jnp.zeros_like(acc_ref)
    top_ref[...] = jnp.full_like(top_ref, masked_score)
    sum_ref[...] = jnp.zeros_like(sum_ref)

    def visit(offset, diagonal):
        key_block = keys_ref[pl.ds(offset, rows), :]
        for head in range(heads):
            feature = pl.ds(head * HEAD_DIM, HEAD_DIM)
            scores = dot(key_block, heads_ref[head], NT)
            if diagonal:
                scores = causal(scores)
            old = top_ref[pl.ds(head, 1), :]
            top = jnp.maximum(old, jnp.max(scores, axis=0, keepdims=True))
            shrink = jnp.exp(old - top)
            weights = jnp.exp(scores - top)
            top_ref[pl.ds(head, 1), :] = top
            sum_ref[pl.ds(head, 1), :] = sum_ref[pl.ds(head, 1), :] * shrink + jnp.sum(weights, axis=0, keepdims=True)
            value_t = values_t_ref[feature, pl.ds(offset, rows)]
            acc_ref[feature, :] = acc_ref[feature, :] * shrink + dot(value_t, weights.astype(jnp.bfloat16))

    def step(index, carry):
        visit(pl.multiple_of(first + index * rows, rows), False)
        return carry

    lax.fori_loop(0, full, step, 0)
    visit(pl.multiple_of(start, rows), True)
    for head in range(heads):
        feature = pl.ds(head * HEAD_DIM, HEAD_DIM)
        acc_ref[feature, :] = acc_ref[feature, :] / sum_ref[pl.ds(head, 1), :]
    out_ref[...] = acc_ref[...].T
    for side, part in enumerate((core, 1 - core)):
        mixed_ref[side] = out_ref[pl.ds(pl.multiple_of(part * half, half), half), :].astype(jnp.bfloat16)
    total_ref[...] = top_ref[...] + jnp.log(sum_ref[...])


def attend(place, qkv, values_t, rows):
    group_rows, width = qkv.shape[0], qkv.shape[1] // 3
    heads = width // HEAD_DIM
    return pl.pallas_call(
        attend_kernel,
        grid_spec=pltpu.PrefetchScalarGridSpec(
            num_scalar_prefetch=1,
            grid=(1,),
            in_specs=[
                pl.BlockSpec((rows, width), lambda i, s: (s[1], 0)),
                pl.BlockSpec((group_rows, width), lambda i, s: (0, 1)),
                pl.BlockSpec(values_t.shape, lambda i, s: (0, 0)),
            ],
            out_specs=[
                pl.BlockSpec((2, rows // 2, width), lambda i, s: (0, 0, 0)),
                pl.BlockSpec((heads, rows), lambda i, s: (0, 0)),
            ],
            scratch_shapes=[
                pltpu.VMEM((heads, rows, width), jnp.bfloat16),
                pltpu.VMEM((width, rows), jnp.float32),
                pltpu.VMEM((rows, width), jnp.float32),
                pltpu.VMEM((heads, rows), jnp.float32),
                pltpu.VMEM((heads, rows), jnp.float32),
            ],
        ),
        out_shape=[
            jax.ShapeDtypeStruct((2, rows // 2, width), jnp.bfloat16),
            jax.ShapeDtypeStruct((heads, rows), jnp.float32),
        ],
        cost_estimate=pl.CostEstimate(flops=4 * rows * SEQ_LEN * width, bytes_accessed=4 * rows * width + 4 * group_rows * width, transcendentals=rows * SEQ_LEN * heads // 2),
        name="attend",
    )(place, qkv, qkv, values_t)


def attend_back_kernel(place_ref, query_ref, mixed_in, grad_same, grad_other, total_ref, keys_ref, keys_t_ref, values_ref, dquery_in, dkey_in, dvalue_in, dquery_ref, dkey_ref, dvalue_ref, heads_ref, grads_ref, acc_ref, inner_ref, mixed_ref, grad_ref):
    rows, width = query_ref.shape
    half = rows // 2
    heads = width // HEAD_DIM
    core = place_ref[0]
    start = place_ref[1] * rows
    for side, part in enumerate((core, 1 - core)):
        span = pl.ds(pl.multiple_of(part * half, half), half)
        mixed_ref[span, :] = mixed_in[side]
        grad_ref[span, :] = (grad_same, grad_other)[side][...]
    first = start // SEQ_LEN * SEQ_LEN
    full = (start - first) // rows
    scaled = query_ref[...] * jnp.bfloat16(HEAD_DIM**-0.5)
    grad = grad_ref[...]
    product = grad.astype(jnp.float32) * mixed_ref[...].astype(jnp.float32)
    pick = (lax.broadcasted_iota(jnp.int32, inner_ref.shape[:1] + (width,), 1) // HEAD_DIM == lax.broadcasted_iota(jnp.int32, inner_ref.shape[:1] + (width,), 0)).astype(jnp.float32)
    inner_ref[...] = lax.dot_general(pick, product, NT, precision=lax.Precision.HIGHEST, preferred_element_type=jnp.float32)
    for head in range(heads):
        heads_ref[head] = only_head(scaled, head)
        grads_ref[head] = only_head(grad, head)
    acc_ref[...] = jnp.zeros_like(acc_ref)

    def visit(offset, diagonal):
        span = pl.ds(offset, rows)
        key_block = keys_ref[span, :]
        value_block = values_ref[span, :]
        dkey = dkey_in[span, :]
        dvalue = dvalue_in[span, :]
        for head in range(heads):
            feature = pl.ds(head * HEAD_DIM, HEAD_DIM)
            scores = dot(key_block, heads_ref[head], NT)
            if diagonal:
                scores = causal(scores)
            probs = jnp.exp(scores - total_ref[pl.ds(head, 1), :])
            dprobs = dot(value_block, grads_ref[head], NT)
            dscores = (probs * (dprobs - inner_ref[pl.ds(head, 1), :])).astype(jnp.bfloat16)
            dvalue = dvalue + dot(probs.astype(jnp.bfloat16), grads_ref[head])
            dkey = dkey + dot(dscores, heads_ref[head])
            acc_ref[feature, :] = acc_ref[feature, :] + dot(keys_t_ref[feature, span], dscores)
        dkey_ref[span, :] = dkey
        dvalue_ref[span, :] = dvalue

    def step(index, carry):
        visit(pl.multiple_of(first + index * rows, rows), False)
        return carry

    dkey_ref[...] = dkey_in[...]
    dvalue_ref[...] = dvalue_in[...]
    lax.fori_loop(0, full, step, 0)
    visit(pl.multiple_of(start, rows), True)
    dquery_ref[...] = acc_ref[...].T * HEAD_DIM**-0.5


def attend_back(place, qkv, mixed, grad_same, grad_other, total, keys_t, dquery, dkey, dvalue):
    _, half, width = mixed.shape
    rows = 2 * half
    group_rows = qkv.shape[0]
    heads = width // HEAD_DIM
    whole = lambda a: pl.BlockSpec(a.shape, lambda i, s: (0,) * a.ndim)
    return pl.pallas_call(
        attend_back_kernel,
        grid_spec=pltpu.PrefetchScalarGridSpec(
            num_scalar_prefetch=1,
            grid=(1,),
            in_specs=[
                pl.BlockSpec((rows, width), lambda i, s: (s[1], 0)),
                whole(mixed),
                whole(grad_same),
                whole(grad_other),
                whole(total),
                pl.BlockSpec((group_rows, width), lambda i, s: (0, 1)),
                whole(keys_t),
                pl.BlockSpec((group_rows, width), lambda i, s: (0, 2)),
                pl.BlockSpec(memory_space=pl.ANY),
                whole(dkey),
                whole(dvalue),
            ],
            out_specs=[
                pl.BlockSpec((rows, width), lambda i, s: (s[1], 0)),
                whole(dkey),
                whole(dvalue),
            ],
            scratch_shapes=[
                pltpu.VMEM((heads, rows, width), jnp.bfloat16),
                pltpu.VMEM((heads, rows, width), jnp.bfloat16),
                pltpu.VMEM((width, rows), jnp.float32),
                pltpu.VMEM((8, rows), jnp.float32),
                pltpu.VMEM((rows, width), jnp.bfloat16),
                pltpu.VMEM((rows, width), jnp.bfloat16),
            ],
        ),
        out_shape=[jax.ShapeDtypeStruct(a.shape, jnp.float32) for a in (dquery, dkey, dvalue)],
        input_output_aliases={9: 0, 10: 1, 11: 2},
        cost_estimate=pl.CostEstimate(flops=10 * rows * SEQ_LEN * width, bytes_accessed=8 * rows * width + 20 * group_rows * width, transcendentals=rows * SEQ_LEN * heads // 2),
        name="attend_back",
    )(place, qkv, mixed, grad_same, grad_other, total, qkv, keys_t, qkv, dquery, dkey, dvalue)


def turned(block, sign):
    half = HEAD_DIM // 2
    lane = lax.broadcasted_iota(jnp.int32, block.shape, 1)
    width = block.shape[1]
    up = pltpu.roll(block, width - half, 1)
    down = pltpu.roll(block, half, 1)
    return jnp.where(lane % HEAD_DIM < half, -sign * up, sign * down)


def project_kernel(place_ref, same_ref, other_ref, weight_ref, cosine_ref, sine_ref, out_in, out_ref, acc_ref):
    rows = same_ref.shape[0]
    core = place_ref[0]
    same = pl.ds(pl.multiple_of(core * rows, rows), rows)
    other = pl.ds(pl.multiple_of((1 - core) * rows, rows), rows)
    acc_ref[same, :] = dot(same_ref[...], weight_ref[...])
    acc_ref[other, :] = dot(other_ref[...], weight_ref[...])

    @pl.when(pl.program_id(0) < 2)
    def _():
        block = acc_ref[...]
        out_ref[...] = (block * cosine_ref[...] + turned(block, 1.0) * sine_ref[...]).astype(jnp.bfloat16)

    @pl.when(pl.program_id(0) == 2)
    def _():
        out_ref[...] = acc_ref[...].astype(jnp.bfloat16)


def project(place, same, other, weight, cosine, sine, out):
    rows, depth = same.shape
    pair = 2 * rows
    width = weight.shape[1] // 3
    cycle = SEQ_LEN // pair
    fixed = lambda shape: pl.BlockSpec(shape, lambda i, s: (0, 0))
    table = pl.BlockSpec((pair, width), lambda i, s: (s[1] % cycle, 0))
    return pl.pallas_call(
        project_kernel,
        grid_spec=pltpu.PrefetchScalarGridSpec(
            num_scalar_prefetch=1,
            grid=(3,),
            in_specs=[
                fixed(same.shape),
                fixed(other.shape),
                pl.BlockSpec((depth, width), lambda i, s: (0, i)),
                table,
                table,
                pl.BlockSpec(memory_space=pl.ANY),
            ],
            out_specs=pl.BlockSpec((pair, width), lambda i, s: (s[1], i)),
            scratch_shapes=[pltpu.VMEM((pair, width), jnp.float32)],
        ),
        out_shape=jax.ShapeDtypeStruct(out.shape, jnp.bfloat16),
        input_output_aliases={6: 0},
        cost_estimate=pl.CostEstimate(flops=12 * rows * depth * width, bytes_accessed=4 * rows * depth + 6 * depth * width, transcendentals=0),
        name="project",
    )(place, same, other, weight, cosine, sine, out)


def unrotate_kernel(order_ref, dquery_ref, dkey_ref, dvalue_ref, cosine_ref, sine_ref, out_ref):
    width = dquery_ref.shape[1]
    for place, ref in enumerate((dquery_ref, dkey_ref)):
        block = ref[...]
        out_ref[:, pl.ds(place * width, width)] = (block * cosine_ref[...] + turned(block * sine_ref[...], -1.0)).astype(jnp.bfloat16)
    out_ref[:, pl.ds(2 * width, width)] = dvalue_ref[...].astype(jnp.bfloat16)


def unrotate(order, dquery, dkey, dvalue, cosine, sine):
    group_rows, width = dquery.shape
    blocks = order.shape[0]
    rows = group_rows // blocks
    cycle = SEQ_LEN // rows
    spec = pl.BlockSpec((rows, width), lambda i, s: (s[i], 0))
    table = pl.BlockSpec((rows, width), lambda i, s: (s[i] % cycle, 0))
    return pl.pallas_call(
        unrotate_kernel,
        grid_spec=pltpu.PrefetchScalarGridSpec(
            num_scalar_prefetch=1,
            grid=(blocks,),
            in_specs=[spec, spec, spec, table, table],
            out_specs=pl.BlockSpec((rows, 3 * width), lambda i, s: (i, 0)),
        ),
        out_shape=jax.ShapeDtypeStruct((group_rows, 3 * width), jnp.bfloat16),
        cost_estimate=pl.CostEstimate(flops=20 * group_rows * width, bytes_accessed=18 * group_rows * width, transcendentals=0),
        name="unrotate",
    )(order, dquery, dkey, dvalue, cosine, sine)


def rms_norm(values, gain):
    return values * lax.rsqrt(jnp.mean(values * values, axis=-1, keepdims=True) + norm_eps) * gain


def rope_tables(width):
    half = HEAD_DIM // 2
    positions = jnp.arange(SEQ_LEN, dtype=jnp.int32).astype(jnp.float32)
    column = jnp.arange(width, dtype=jnp.int32) % half
    inverse = jnp.power(jnp.float32(rope_base), -2.0 * column.astype(jnp.float32) / HEAD_DIM)
    angle = positions[:, None] * inverse[None, :]
    return (jnp.cos(angle), jnp.sin(angle))


class Ring:
    def __init__(self, size):
        self.chips = size // 2
        self.order = [2 * p if 2 * p < self.chips else 2 * (self.chips - 1 - p) + 1 for p in range(self.chips)]
        place = [self.order.index(chip) for chip in range(self.chips)]
        follower = [self.order[(place[chip] + 1) % self.chips] for chip in range(self.chips)]
        self.forward = [(2 * chip + core, 2 * follower[chip] + core) for chip in range(self.chips) for core in range(2)]
        self.swap = [(device, device ^ 1) for device in range(size)]
        index = lax.axis_index("tp")
        self.chip, self.core = index // 2, index % 2
        table = [[self.order[(place[chip] - slot) % self.chips] for chip in range(self.chips)] for slot in range(self.chips)]
        self.sources = [jnp.array(row, jnp.int32)[self.chip] for row in table]

    def exchange(self, block):
        return lax.ppermute(block, "tp", self.swap)

    def gather(self, block):
        slots = []
        for slot in range(self.chips):
            following = lax.ppermute(block, "tp", self.forward) if slot < self.chips - 1 else None
            slots.append((block, self.exchange(block)))
            block = following
        return slots

    def scatter(self, parts):
        total = None
        for slot in list(range(1, self.chips)) + [0]:
            same, other = parts(slot)
            term = same.astype(jnp.float32) + self.exchange(other).astype(jnp.float32)
            if total is not None:
                term = term + lax.ppermute(total, "tp", self.forward).astype(jnp.float32)
            total = term.astype(jnp.bfloat16) if slot else term
        return total


def swap_sum(values, mesh):
    for axis in ("tp", "fsdp"):
        step = 1
        while step < mesh[axis]:
            values = values + lax.ppermute(values, axis, [(i, i ^ step) for i in range(mesh[axis])])
            step *= 2
    return values


def make_body(mesh):
    sizes = dict(mesh.shape)

    def body(activations, gain_attn, w_query, w_key, w_value, w_out, gain_mlp, w_gate, w_up, w_down, cotangent):
        ring = Ring(sizes["tp"])
        chips, core = ring.chips, ring.core
        rows = activations.shape[0]
        width = w_query.shape[1]
        pair = 2 * rows
        group_rows = chips * pair
        w_qkv = lax.all_gather(jnp.concatenate([w_query, w_key, w_value], axis=1), "fsdp", axis=0, tiled=True)
        full_out = lax.all_gather(w_out, "fsdp", axis=1, tiled=True)
        full_gate = lax.all_gather(w_gate, "fsdp", axis=0, tiled=True)
        full_up = lax.all_gather(w_up, "fsdp", axis=0, tiled=True)
        full_down = lax.all_gather(w_down, "fsdp", axis=1, tiled=True)
        cosine, sine = rope_tables(width)
        places = [jnp.stack([core, source]) for source in ring.sources]
        order = jnp.stack([2 * source + part for source in ring.sources for part in (core, 1 - core)])

        normed_attn = rms_norm(activations, gain_attn).astype(jnp.bfloat16)
        seen_attn = ring.gather(normed_attn)
        qkv = jnp.zeros((group_rows, 3 * width), jnp.bfloat16)
        for slot, (same, other) in enumerate(seen_attn):
            qkv = project(places[slot], same, other, w_qkv, cosine, sine, qkv)
        keys_t, values_t = qkv[:, width : 2 * width].T, qkv[:, 2 * width :].T

        seen_grad = ring.gather(cotangent.astype(jnp.bfloat16))

        kept = {}

        def attention_part(slot):
            kept[slot] = attend(places[slot], qkv, values_t, pair)
            mixed = kept[slot][0]
            return [dot(mixed[side], full_out).astype(jnp.bfloat16) for side in range(2)]

        attn_branch = ring.scatter(attention_part)
        hidden_state = activations + attn_branch
        normed_mlp = rms_norm(hidden_state, gain_mlp).astype(jnp.bfloat16)
        seen_mlp = ring.gather(normed_mlp)
        mlp = {}

        def mlp_part(slot):
            tokens = jnp.concatenate(seen_mlp[slot], axis=0)
            grads = jnp.concatenate(seen_grad[slot], axis=0)
            gate = dot(tokens, full_gate)
            up = dot(tokens, full_up)
            act, pull = jax.vjp(lambda g, u: jax.nn.silu(g) * u, gate, up)
            gate_grad, up_grad = pull(dot(grads, full_down, NT))
            gate_grad = gate_grad.astype(jnp.bfloat16)
            up_grad = up_grad.astype(jnp.bfloat16)
            mlp[slot] = (tokens, grads, act.astype(jnp.bfloat16), gate_grad, up_grad)
            back = (dot(gate_grad, full_gate, NT) + dot(up_grad, full_up, NT)).astype(jnp.bfloat16)
            return back[:rows], back[rows:]

        normed_mlp_grad = ring.scatter(mlp_part)

        def down_part(slot):
            part = dot(mlp[slot][2], full_down).astype(jnp.bfloat16)
            return part[:rows], part[rows:]

        output = hidden_state + ring.scatter(down_part)
        all_tokens, all_grads, inner, gate_grad, up_grad = [
            jnp.concatenate([mlp[slot][item] for slot in range(chips)], axis=0) for item in range(5)
        ]
        _, pull_norm_mlp = jax.vjp(rms_norm, hidden_state, gain_mlp)
        hidden_norm_grad, gain_mlp_part = pull_norm_mlp(normed_mlp_grad)
        hidden_grad = cotangent + hidden_norm_grad
        seen_branch = ring.gather(hidden_grad.astype(jnp.bfloat16))

        def over_fsdp(grad, dimension):
            return lax.psum_scatter(grad.astype(jnp.bfloat16), "fsdp", scatter_dimension=dimension, tiled=True).astype(jnp.float32)

        TN = (((0,), (0,)), ((), ()))
        grad_down = over_fsdp(dot(inner, all_grads, TN), 1)
        grad_gate = over_fsdp(dot(all_tokens, gate_grad, TN), 0)
        grad_up = over_fsdp(dot(all_tokens, up_grad, TN), 0)

        empty = jnp.zeros((group_rows, width), jnp.float32)
        dquery, dkey, dvalue = empty, empty, empty
        mixed_parts, branch_parts = [], []
        for slot in range(chips):
            mixed, totals = kept[slot]
            same, other = seen_branch[slot]
            grad_same = dot(same, full_out, NT).astype(jnp.bfloat16)
            grad_other = dot(other, full_out, NT).astype(jnp.bfloat16)
            mixed_parts.append(mixed.reshape(pair, width))
            branch_parts.extend((same, other))
            dquery, dkey, dvalue = attend_back(places[slot], qkv, mixed, grad_same, grad_other, totals, keys_t, dquery, dkey, dvalue)
        grad_out = over_fsdp(dot(jnp.concatenate(mixed_parts, axis=0), jnp.concatenate(branch_parts, axis=0), TN), 1)
        qkv_grad = unrotate(order, dquery, dkey, dvalue, cosine, sine)

        def qkv_part(slot):
            part = dot(qkv_grad[slot * pair : (slot + 1) * pair], w_qkv, NT).astype(jnp.bfloat16)
            return part[:rows], part[rows:]

        normed_attn_grad = ring.scatter(qkv_part)
        flat_attn = jnp.concatenate([half for slot in range(chips) for half in seen_attn[slot]], axis=0)
        grad_qkv = over_fsdp(dot(flat_attn, qkv_grad, TN), 0)
        _, pull_norm_attn = jax.vjp(rms_norm, activations, gain_attn)
        input_norm_grad, gain_attn_part = pull_norm_attn(normed_attn_grad)
        input_grad = hidden_grad + input_norm_grad
        gain_sums = swap_sum(jnp.stack([gain_attn_part, gain_mlp_part]), sizes)
        return (
            output,
            input_grad,
            gain_sums[0],
            grad_qkv[:, :width],
            grad_qkv[:, width : 2 * width],
            grad_qkv[:, 2 * width :],
            grad_out,
            gain_sums[1],
            grad_gate,
            grad_up,
            grad_down,
        )

    return body


def solution(mesh):
    tokens = P(("fsdp", "tp"), None)
    column = P("fsdp", "tp")
    row = P("tp", "fsdp")
    in_specs = (tokens, P(), column, column, column, row, P(), column, column, row, tokens)
    out_specs = (tokens, tokens, P(), column, column, column, row, P(), column, column, row)
    return jax.shard_map(make_body(mesh), mesh=mesh, in_specs=in_specs, out_specs=out_specs, check_vma=False)
```

```python
import jax
import jax.numpy as jnp
from jax import lax
from jax.experimental import pallas as pl
from jax.experimental.pallas import tpu as pltpu
from jax.sharding import PartitionSpec as P

HEAD_DIM = 64
SEQ_LEN = 2048
rope_base = 130000.0
norm_eps = 1e-05
masked_score = -1e30

NT = (((1,), (1,)), ((), ()))
NN = (((1,), (0,)), ((), ()))


def dot(left, right, dims=NN):
    return lax.dot_general(left, right, dims, preferred_element_type=jnp.float32)


def only_head(block, head):
    lane = lax.broadcasted_iota(jnp.int32, block.shape, 1)
    return jnp.where(lane // HEAD_DIM == head, block, jnp.zeros_like(block))


def causal(tile):
    key = lax.broadcasted_iota(jnp.int32, tile.shape, 0)
    query = lax.broadcasted_iota(jnp.int32, tile.shape, 1)
    return jnp.where(key <= query, tile, masked_score)


def attend_kernel(place_ref, query_ref, keys_ref, values_t_ref, mixed_ref, total_ref, heads_ref, acc_ref, out_ref, top_ref, sum_ref):
    rows, width = query_ref.shape
    half = rows // 2
    heads = width // HEAD_DIM
    core = place_ref[0]
    start = place_ref[1] * rows
    first = start // SEQ_LEN * SEQ_LEN
    full = (start - first) // rows
    scaled = query_ref[...] * jnp.bfloat16(HEAD_DIM**-0.5)
    for head in range(heads):
        heads_ref[head] = only_head(scaled, head)
    acc_ref[...] = jnp.zeros_like(acc_ref)
    top_ref[...] = jnp.full_like(top_ref, masked_score)
    sum_ref[...] = jnp.zeros_like(sum_ref)

    def visit(offset, diagonal):
        key_block = keys_ref[pl.ds(offset, rows), :]
        for head in range(heads):
            feature = pl.ds(head * HEAD_DIM, HEAD_DIM)
            scores = dot(key_block, heads_ref[head], NT)
            if diagonal:
                scores = causal(scores)
            old = top_ref[pl.ds(head, 1), :]
            top = jnp.maximum(old, jnp.max(scores, axis=0, keepdims=True))
            shrink = jnp.exp(old - top)
            weights = jnp.exp(scores - top)
            top_ref[pl.ds(head, 1), :] = top
            sum_ref[pl.ds(head, 1), :] = sum_ref[pl.ds(head, 1), :] * shrink + jnp.sum(weights, axis=0, keepdims=True)
            value_t = values_t_ref[feature, pl.ds(offset, rows)]
            acc_ref[feature, :] = acc_ref[feature, :] * shrink + dot(value_t, weights.astype(jnp.bfloat16))

    def step(index, carry):
        visit(pl.multiple_of(first + index * rows, rows), False)
        return carry

    lax.fori_loop(0, full, step, 0)
    visit(pl.multiple_of(start, rows), True)
    for head in range(heads):
        feature = pl.ds(head * HEAD_DIM, HEAD_DIM)
        acc_ref[feature, :] = acc_ref[feature, :] / sum_ref[pl.ds(head, 1), :]
    out_ref[...] = acc_ref[...].T
    for side, part in enumerate((core, 1 - core)):
        mixed_ref[side] = out_ref[pl.ds(pl.multiple_of(part * half, half), half), :].astype(jnp.bfloat16)
    total_ref[...] = top_ref[...] + jnp.log(sum_ref[...])


def attend(place, qkv, values_t, rows):
    group_rows, width = qkv.shape[0], qkv.shape[1] // 3
    heads = width // HEAD_DIM
    return pl.pallas_call(
        attend_kernel,
        grid_spec=pltpu.PrefetchScalarGridSpec(
            num_scalar_prefetch=1,
            grid=(1,),
            in_specs=[
                pl.BlockSpec((rows, width), lambda i, s: (s[1], 0)),
                pl.BlockSpec((group_rows, width), lambda i, s: (0, 1)),
                pl.BlockSpec(values_t.shape, lambda i, s: (0, 0)),
            ],
            out_specs=[
                pl.BlockSpec((2, rows // 2, width), lambda i, s: (0, 0, 0)),
                pl.BlockSpec((heads, rows), lambda i, s: (0, 0)),
            ],
            scratch_shapes=[
                pltpu.VMEM((heads, rows, width), jnp.bfloat16),
                pltpu.VMEM((width, rows), jnp.float32),
                pltpu.VMEM((rows, width), jnp.float32),
                pltpu.VMEM((heads, rows), jnp.float32),
                pltpu.VMEM((heads, rows), jnp.float32),
            ],
        ),
        out_shape=[
            jax.ShapeDtypeStruct((2, rows // 2, width), jnp.bfloat16),
            jax.ShapeDtypeStruct((heads, rows), jnp.float32),
        ],
        cost_estimate=pl.CostEstimate(flops=4 * rows * SEQ_LEN * width, bytes_accessed=4 * rows * width + 4 * group_rows * width, transcendentals=rows * SEQ_LEN * heads // 2),
        name="attend",
    )(place, qkv, qkv, values_t)


def attend_back_kernel(place_ref, query_ref, mixed_in, grad_same, grad_other, total_ref, keys_ref, keys_t_ref, values_ref, dquery_in, dkey_in, dvalue_in, dquery_ref, dkey_ref, dvalue_ref, heads_ref, grads_ref, acc_ref, inner_ref, mixed_ref, grad_ref):
    rows, width = query_ref.shape
    half = rows // 2
    heads = width // HEAD_DIM
    core = place_ref[0]
    start = place_ref[1] * rows
    for side, part in enumerate((core, 1 - core)):
        span = pl.ds(pl.multiple_of(part * half, half), half)
        mixed_ref[span, :] = mixed_in[side]
        grad_ref[span, :] = (grad_same, grad_other)[side][...]
    first = start // SEQ_LEN * SEQ_LEN
    full = (start - first) // rows
    scaled = query_ref[...] * jnp.bfloat16(HEAD_DIM**-0.5)
    grad = grad_ref[...]
    product = grad.astype(jnp.float32) * mixed_ref[...].astype(jnp.float32)
    pick = (lax.broadcasted_iota(jnp.int32, inner_ref.shape[:1] + (width,), 1) // HEAD_DIM == lax.broadcasted_iota(jnp.int32, inner_ref.shape[:1] + (width,), 0)).astype(jnp.float32)
    inner_ref[...] = lax.dot_general(pick, product, NT, precision=lax.Precision.HIGHEST, preferred_element_type=jnp.float32)
    for head in range(heads):
        heads_ref[head] = only_head(scaled, head)
        grads_ref[head] = only_head(grad, head)
    acc_ref[...] = jnp.zeros_like(acc_ref)

    def visit(offset, diagonal):
        span = pl.ds(offset, rows)
        key_block = keys_ref[span, :]
        value_block = values_ref[span, :]
        dkey = dkey_in[span, :]
        dvalue = dvalue_in[span, :]
        for head in range(heads):
            feature = pl.ds(head * HEAD_DIM, HEAD_DIM)
            scores = dot(key_block, heads_ref[head], NT)
            if diagonal:
                scores = causal(scores)
            probs = jnp.exp(scores - total_ref[pl.ds(head, 1), :])
            dprobs = dot(value_block, grads_ref[head], NT)
            dscores = (probs * (dprobs - inner_ref[pl.ds(head, 1), :])).astype(jnp.bfloat16)
            dvalue = dvalue + dot(probs.astype(jnp.bfloat16), grads_ref[head])
            dkey = dkey + dot(dscores, heads_ref[head])
            acc_ref[feature, :] = acc_ref[feature, :] + dot(keys_t_ref[feature, span], dscores)
        dkey_ref[span, :] = dkey
        dvalue_ref[span, :] = dvalue

    def step(index, carry):
        visit(pl.multiple_of(first + index * rows, rows), False)
        return carry

    dkey_ref[...] = dkey_in[...]
    dvalue_ref[...] = dvalue_in[...]
    lax.fori_loop(0, full, step, 0)
    visit(pl.multiple_of(start, rows), True)
    dquery_ref[...] = acc_ref[...].T * HEAD_DIM**-0.5


def attend_back(place, qkv, mixed, grad_same, grad_other, total, keys_t, dquery, dkey, dvalue):
    _, half, width = mixed.shape
    rows = 2 * half
    group_rows = qkv.shape[0]
    heads = width // HEAD_DIM
    whole = lambda a: pl.BlockSpec(a.shape, lambda i, s: (0,) * a.ndim)
    return pl.pallas_call(
        attend_back_kernel,
        grid_spec=pltpu.PrefetchScalarGridSpec(
            num_scalar_prefetch=1,
            grid=(1,),
            in_specs=[
                pl.BlockSpec((rows, width), lambda i, s: (s[1], 0)),
                whole(mixed),
                whole(grad_same),
                whole(grad_other),
                whole(total),
                pl.BlockSpec((group_rows, width), lambda i, s: (0, 1)),
                whole(keys_t),
                pl.BlockSpec((group_rows, width), lambda i, s: (0, 2)),
                pl.BlockSpec(memory_space=pl.ANY),
                whole(dkey),
                whole(dvalue),
            ],
            out_specs=[
                pl.BlockSpec((rows, width), lambda i, s: (s[1], 0)),
                whole(dkey),
                whole(dvalue),
            ],
            scratch_shapes=[
                pltpu.VMEM((heads, rows, width), jnp.bfloat16),
                pltpu.VMEM((heads, rows, width), jnp.bfloat16),
                pltpu.VMEM((width, rows), jnp.float32),
                pltpu.VMEM((8, rows), jnp.float32),
                pltpu.VMEM((rows, width), jnp.bfloat16),
                pltpu.VMEM((rows, width), jnp.bfloat16),
            ],
        ),
        out_shape=[jax.ShapeDtypeStruct(a.shape, jnp.float32) for a in (dquery, dkey, dvalue)],
        input_output_aliases={9: 0, 10: 1, 11: 2},
        cost_estimate=pl.CostEstimate(flops=10 * rows * SEQ_LEN * width, bytes_accessed=8 * rows * width + 20 * group_rows * width, transcendentals=rows * SEQ_LEN * heads // 2),
        name="attend_back",
    )(place, qkv, mixed, grad_same, grad_other, total, qkv, keys_t, qkv, dquery, dkey, dvalue)


def turned(block, sign):
    half = HEAD_DIM // 2
    lane = lax.broadcasted_iota(jnp.int32, block.shape, 1)
    width = block.shape[1]
    up = pltpu.roll(block, width - half, 1)
    down = pltpu.roll(block, half, 1)
    return jnp.where(lane % HEAD_DIM < half, -sign * up, sign * down)


def project_kernel(place_ref, same_ref, other_ref, weight_ref, cosine_ref, sine_ref, out_in, out_ref, acc_ref):
    rows = same_ref.shape[0]
    core = place_ref[0]
    same = pl.ds(pl.multiple_of(core * rows, rows), rows)
    other = pl.ds(pl.multiple_of((1 - core) * rows, rows), rows)
    acc_ref[same, :] = dot(same_ref[...], weight_ref[...])
    acc_ref[other, :] = dot(other_ref[...], weight_ref[...])

    @pl.when(pl.program_id(0) < 2)
    def _():
        block = acc_ref[...]
        out_ref[...] = (block * cosine_ref[...] + turned(block, 1.0) * sine_ref[...]).astype(jnp.bfloat16)

    @pl.when(pl.program_id(0) == 2)
    def _():
        out_ref[...] = acc_ref[...].astype(jnp.bfloat16)


def project(place, same, other, weight, cosine, sine, out):
    rows, depth = same.shape
    pair = 2 * rows
    width = weight.shape[1] // 3
    cycle = SEQ_LEN // pair
    fixed = lambda shape: pl.BlockSpec(shape, lambda i, s: (0, 0))
    table = pl.BlockSpec((pair, width), lambda i, s: (s[1] % cycle, 0))
    return pl.pallas_call(
        project_kernel,
        grid_spec=pltpu.PrefetchScalarGridSpec(
            num_scalar_prefetch=1,
            grid=(3,),
            in_specs=[
                fixed(same.shape),
                fixed(other.shape),
                pl.BlockSpec((depth, width), lambda i, s: (0, i)),
                table,
                table,
                pl.BlockSpec(memory_space=pl.ANY),
            ],
            out_specs=pl.BlockSpec((pair, width), lambda i, s: (s[1], i)),
            scratch_shapes=[pltpu.VMEM((pair, width), jnp.float32)],
        ),
        out_shape=jax.ShapeDtypeStruct(out.shape, jnp.bfloat16),
        input_output_aliases={6: 0},
        cost_estimate=pl.CostEstimate(flops=12 * rows * depth * width, bytes_accessed=4 * rows * depth + 6 * depth * width, transcendentals=0),
        name="project",
    )(place, same, other, weight, cosine, sine, out)


def unrotate_kernel(order_ref, dquery_ref, dkey_ref, dvalue_ref, cosine_ref, sine_ref, out_ref):
    width = dquery_ref.shape[1]
    for place, ref in enumerate((dquery_ref, dkey_ref)):
        block = ref[...]
        out_ref[:, pl.ds(place * width, width)] = (block * cosine_ref[...] + turned(block * sine_ref[...], -1.0)).astype(jnp.bfloat16)
    out_ref[:, pl.ds(2 * width, width)] = dvalue_ref[...].astype(jnp.bfloat16)


def unrotate(order, dquery, dkey, dvalue, cosine, sine):
    group_rows, width = dquery.shape
    blocks = order.shape[0]
    rows = group_rows // blocks
    cycle = SEQ_LEN // rows
    spec = pl.BlockSpec((rows, width), lambda i, s: (s[i], 0))
    table = pl.BlockSpec((rows, width), lambda i, s: (s[i] % cycle, 0))
    return pl.pallas_call(
        unrotate_kernel,
        grid_spec=pltpu.PrefetchScalarGridSpec(
            num_scalar_prefetch=1,
            grid=(blocks,),
            in_specs=[spec, spec, spec, table, table],
            out_specs=pl.BlockSpec((rows, 3 * width), lambda i, s: (i, 0)),
        ),
        out_shape=jax.ShapeDtypeStruct((group_rows, 3 * width), jnp.bfloat16),
        cost_estimate=pl.CostEstimate(flops=20 * group_rows * width, bytes_accessed=18 * group_rows * width, transcendentals=0),
        name="unrotate",
    )(order, dquery, dkey, dvalue, cosine, sine)


def chip_at(place, chips):
    return jnp.where(2 * place < chips, 2 * place, 2 * (chips - 1 - place) + 1)


def place_of(chip, chips):
    return jnp.where(chip % 2 == 0, chip // 2, chips - 1 - chip // 2)


def remote(source, target, send, receive, device):
    return pltpu.make_async_remote_copy(
        src_ref=source, dst_ref=target, send_sem=send, recv_sem=receive,
        device_id={"tp": device}, device_id_type=pl.DeviceIdType.MESH,
    )


def greet(devices):
    barrier = pltpu.get_barrier_semaphore()
    for device in devices:
        pl.semaphore_signal(barrier, inc=1, device_id={"tp": device}, device_id_type=pl.DeviceIdType.MESH)
    pl.semaphore_wait(barrier, len(devices))


def feed_kernel(
    chips,
    tokens_ref, grads_hbm, gate_hbm, up_hbm, down_hbm,
    back_ref, tokens_out, inner_out, gate_out, up_out,
    tokens_all, gate_w, up_w, down_w, grads, inner, gate_grad, up_grad, own, term, stage, from_core, from_ring, total,
    load_sem, grad_sem, keep_sem, store_sem, ring_send, ring_recv, core_send, core_recv, stage_send, stage_recv, total_send, total_recv,
):
    rows, depth = tokens_ref.shape
    pair = 2 * rows
    hidden = gate_w.shape[1]
    me = lax.axis_index("tp")
    chip, core = me // 2, me % 2
    place = place_of(chip, chips)
    following = 2 * chip_at((place + 1) % chips, chips) + core
    before = 2 * chip_at((place + chips - 1) % chips, chips) + core
    partner = 2 * chip + 1 - core

    loads = [pltpu.make_async_copy(a, b, load_sem.at[i]) for i, (a, b) in enumerate(((gate_hbm, gate_w), (up_hbm, up_w), (down_hbm, down_w)))]
    for load in loads:
        load.start()

    def source(slot):
        return chip_at((place + chips - slot) % chips, chips)

    def fetch(slot):
        start = pl.multiple_of(source(slot) * pair, pair)
        return pltpu.make_async_copy(grads_hbm.at[pl.ds(start, pair)], grads.at[slot % 2], grad_sem.at[slot % 2])

    def block(ref, index):
        return ref.at[pl.ds(pl.multiple_of(index * rows, rows), rows)]

    def to_ring(slot):
        index = 2 * source(slot) + core
        return remote(block(tokens_all, index), block(tokens_all, index), ring_send.at[slot], ring_recv.at[slot], following)

    def to_core(slot):
        index = 2 * source(slot) + core
        return remote(block(tokens_all, index), block(tokens_all, index), core_send.at[slot], core_recv.at[slot], partner)

    def keep(slot):
        start = pl.multiple_of(source(slot) * pair, pair)
        span = pl.ds(start, pair)
        return pltpu.make_async_copy(tokens_all.at[span], tokens_out.at[span], keep_sem.at[slot])

    def stores(slot):
        span = pl.ds(pl.multiple_of(source(slot) * pair, pair), pair)
        return [
            pltpu.make_async_copy(ref.at[slot % 2], out.at[span], store_sem.at[i, slot % 2])
            for i, (ref, out) in enumerate(((inner, inner_out), (gate_grad, gate_out), (up_grad, up_out)))
        ]

    def stage_copy(slot):
        return remote(stage.at[slot % 2], from_core.at[slot], stage_send.at[slot % 2], stage_recv.at[slot], partner)

    def total_copy(slot):
        return remote(total.at[slot - 1], from_ring.at[slot - 1], total_send.at[slot - 1], total_recv.at[slot - 1], following)

    fetch(0).start()
    tokens_all[pl.ds(pl.multiple_of(me * rows, rows), rows), :] = tokens_ref[...]
    greet((following, before, partner))

    def step(slot, carry):
        @pl.when(slot > 0)
        def _():
            to_ring(slot - 1).wait_recv()

        @pl.when(slot < chips - 1)
        def _():
            to_ring(slot).start()
            fetch(slot + 1).start()

        to_core(slot).start()

        @pl.when(slot == 0)
        def _():
            for load in loads:
                load.wait()

        @pl.when(slot > 1)
        def _():
            for store in stores(slot - 2):
                store.wait()

        to_core(slot).wait_recv()
        keep(slot).start()
        fetch(slot).wait()
        here = slot % 2
        span = pl.ds(pl.multiple_of(source(slot) * pair, pair), pair)

        def narrow(tile, carry):
            columns = pl.ds(pl.multiple_of(tile * 256, 256), 256)
            token = tokens_all[span, :]
            gate = dot(token, gate_w[:, columns])
            up = dot(token, up_w[:, columns])
            grad = dot(grads[here], down_w[columns, :], NT)
            squash = jax.nn.sigmoid(gate)
            act = gate * squash
            inner[here, :, columns] = (act * up).astype(jnp.bfloat16)
            up_grad[here, :, columns] = (grad * act).astype(jnp.bfloat16)
            gate_grad[here, :, columns] = (grad * up * squash * (1.0 + gate * (1.0 - squash))).astype(jnp.bfloat16)
            return carry

        lax.fori_loop(0, hidden // 256, narrow, 0)
        for store in stores(slot):
            store.start()

        @pl.when(slot > 1)
        def _():
            stage_copy(slot - 2).wait_send()

        def wide(tile, carry):
            columns = pl.ds(pl.multiple_of(tile * 256, 256), 256)
            part = dot(gate_grad[here], gate_w[columns, :], NT) + dot(up_grad[here], up_w[columns, :], NT)
            term[:, columns] = part.astype(jnp.bfloat16)
            return carry

        lax.fori_loop(0, depth // 256, wide, 0)
        stage[here] = term[pl.ds(pl.multiple_of((1 - core) * rows, rows), rows), :]
        stage_copy(slot).start()
        mine = pl.ds(pl.multiple_of(core * rows, rows), rows)

        @pl.when(slot == 0)
        def _():
            own[...] = term[mine, :].astype(jnp.float32)

        @pl.when(slot > 0)
        def _():
            stage_copy(slot).wait_recv()

        @pl.when(slot == 1)
        def _():
            total[slot - 1] = (term[mine, :].astype(jnp.float32) + from_core[slot].astype(jnp.float32)).astype(jnp.bfloat16)

        @pl.when(slot > 1)
        def _():
            total_copy(slot - 1).wait_recv()
            total[slot - 1] = (term[mine, :].astype(jnp.float32) + from_core[slot].astype(jnp.float32) + from_ring[slot - 2].astype(jnp.float32)).astype(jnp.bfloat16)

        @pl.when(slot > 0)
        def _():
            total_copy(slot).start()

        return carry

    lax.fori_loop(0, chips, step, 0)
    stage_copy(0).wait_recv()
    total_copy(chips - 1).wait_recv()
    back_ref[...] = own[...] + from_core[0].astype(jnp.float32) + from_ring[chips - 2].astype(jnp.float32)
    for slot in range(chips):
        to_core(slot).wait_send()
        keep(slot).wait()
        if slot < chips - 1:
            to_ring(slot).wait_send()
        if slot > 0:
            total_copy(slot).wait_send()
        if slot >= chips - 2:
            stage_copy(slot).wait_send()
            for store in stores(slot):
                store.wait()


def feed(chips, tokens, grads, gate_w, up_w, down_w):
    rows, depth = tokens.shape
    pair = 2 * rows
    group_rows = chips * pair
    hidden = gate_w.shape[1]
    low = jnp.bfloat16
    anywhere = pl.BlockSpec(memory_space=pl.ANY)
    vmem = pl.BlockSpec(memory_space=pltpu.VMEM)
    dma = pltpu.SemaphoreType.DMA
    return pl.pallas_call(
        lambda *refs: feed_kernel(chips, *refs),
        in_specs=[vmem] + [anywhere] * 4,
        out_specs=[vmem] + [anywhere] * 4,
        out_shape=[
            jax.ShapeDtypeStruct((rows, depth), jnp.float32),
            jax.ShapeDtypeStruct((group_rows, depth), low),
        ] + [jax.ShapeDtypeStruct((group_rows, hidden), low)] * 3,
        scratch_shapes=[
            pltpu.VMEM((group_rows, depth), low),
            pltpu.VMEM(gate_w.shape, low),
            pltpu.VMEM(up_w.shape, low),
            pltpu.VMEM(down_w.shape, low),
            pltpu.VMEM((2, pair, depth), low),
            pltpu.VMEM((2, pair, hidden), low),
            pltpu.VMEM((2, pair, hidden), low),
            pltpu.VMEM((2, pair, hidden), low),
            pltpu.VMEM((rows, depth), jnp.float32),
            pltpu.VMEM((pair, depth), low),
            pltpu.VMEM((2, rows, depth), low),
            pltpu.VMEM((chips, rows, depth), low),
            pltpu.VMEM((chips - 1, rows, depth), low),
            pltpu.VMEM((chips - 1, rows, depth), low),
            dma((3,)), dma((2,)), dma((chips,)), dma((3, 2)),
            dma((chips,)), dma((chips,)), dma((chips,)), dma((chips,)),
            dma((2,)), dma((chips,)), dma((chips - 1,)), dma((chips - 1,)),
        ],
        compiler_params=pltpu.CompilerParams(collective_id=3, has_side_effects=True, vmem_limit_bytes=63 << 20),
        cost_estimate=pl.CostEstimate(flops=12 * group_rows * depth * hidden, bytes_accessed=10 * group_rows * depth, transcendentals=group_rows * hidden),
        name="feed",
    )(tokens, grads, gate_w, up_w, down_w)


def rms_norm(values, gain):
    return values * lax.rsqrt(jnp.mean(values * values, axis=-1, keepdims=True) + norm_eps) * gain


def rope_tables(width):
    half = HEAD_DIM // 2
    positions = jnp.arange(SEQ_LEN, dtype=jnp.int32).astype(jnp.float32)
    column = jnp.arange(width, dtype=jnp.int32) % half
    inverse = jnp.power(jnp.float32(rope_base), -2.0 * column.astype(jnp.float32) / HEAD_DIM)
    angle = positions[:, None] * inverse[None, :]
    return (jnp.cos(angle), jnp.sin(angle))


class Ring:
    def __init__(self, size):
        self.chips = size // 2
        self.order = [2 * p if 2 * p < self.chips else 2 * (self.chips - 1 - p) + 1 for p in range(self.chips)]
        place = [self.order.index(chip) for chip in range(self.chips)]
        follower = [self.order[(place[chip] + 1) % self.chips] for chip in range(self.chips)]
        self.forward = [(2 * chip + core, 2 * follower[chip] + core) for chip in range(self.chips) for core in range(2)]
        self.swap = [(device, device ^ 1) for device in range(size)]
        index = lax.axis_index("tp")
        self.chip, self.core = index // 2, index % 2
        table = [[self.order[(place[chip] - slot) % self.chips] for chip in range(self.chips)] for slot in range(self.chips)]
        self.sources = [jnp.array(row, jnp.int32)[self.chip] for row in table]

    def exchange(self, block):
        return lax.ppermute(block, "tp", self.swap)

    def gather(self, block):
        slots = []
        for slot in range(self.chips):
            following = lax.ppermute(block, "tp", self.forward) if slot < self.chips - 1 else None
            slots.append((block, self.exchange(block)))
            block = following
        return slots

    def scatter(self, parts):
        total = None
        for slot in list(range(1, self.chips)) + [0]:
            same, other = parts(slot)
            term = same.astype(jnp.float32) + self.exchange(other).astype(jnp.float32)
            if total is not None:
                term = term + lax.ppermute(total, "tp", self.forward).astype(jnp.float32)
            total = term.astype(jnp.bfloat16) if slot else term
        return total


def swap_sum(values, mesh):
    for axis in ("tp", "fsdp"):
        step = 1
        while step < mesh[axis]:
            values = values + lax.ppermute(values, axis, [(i, i ^ step) for i in range(mesh[axis])])
            step *= 2
    return values


def make_body(mesh):
    sizes = dict(mesh.shape)

    def body(activations, gain_attn, w_query, w_key, w_value, w_out, gain_mlp, w_gate, w_up, w_down, cotangent):
        ring = Ring(sizes["tp"])
        chips, core = ring.chips, ring.core
        rows = activations.shape[0]
        width = w_query.shape[1]
        pair = 2 * rows
        group_rows = chips * pair
        w_qkv = lax.all_gather(jnp.concatenate([w_query, w_key, w_value], axis=1), "fsdp", axis=0, tiled=True)
        full_out = lax.all_gather(w_out, "fsdp", axis=1, tiled=True)
        full_gate = lax.all_gather(w_gate, "fsdp", axis=0, tiled=True)
        full_up = lax.all_gather(w_up, "fsdp", axis=0, tiled=True)
        full_down = lax.all_gather(w_down, "fsdp", axis=1, tiled=True)
        cosine, sine = rope_tables(width)
        starts = [source * pair for source in ring.sources]
        places = [jnp.stack([core, source]) for source in ring.sources]
        order = jnp.stack([2 * source + part for source in ring.sources for part in (core, 1 - core)])

        normed_attn = rms_norm(activations, gain_attn).astype(jnp.bfloat16)
        seen_attn = ring.gather(normed_attn)
        qkv = jnp.zeros((group_rows, 3 * width), jnp.bfloat16)
        for slot, (same, other) in enumerate(seen_attn):
            qkv = project(places[slot], same, other, w_qkv, cosine, sine, qkv)
        keys_t, values_t = qkv[:, width : 2 * width].T, qkv[:, 2 * width :].T

        seen_grad = ring.gather(cotangent.astype(jnp.bfloat16))

        kept = {}

        def attention_part(slot):
            kept[slot] = attend(places[slot], qkv, values_t, pair)
            mixed = kept[slot][0]
            return [dot(mixed[side], full_out).astype(jnp.bfloat16) for side in range(2)]

        attn_branch = ring.scatter(attention_part)
        hidden_state = activations + attn_branch
        normed_mlp = rms_norm(hidden_state, gain_mlp).astype(jnp.bfloat16)
        all_grads = jnp.zeros((group_rows, activations.shape[1]), jnp.bfloat16)
        for slot, (same, other) in enumerate(seen_grad):
            all_grads = lax.dynamic_update_slice_in_dim(all_grads, same, starts[slot] + core * rows, 0)
            all_grads = lax.dynamic_update_slice_in_dim(all_grads, other, starts[slot] + (1 - core) * rows, 0)
        normed_mlp_grad, all_tokens, inner, gate_grad, up_grad = feed(chips, normed_mlp, all_grads, full_gate, full_up, full_down)
        down = dot(inner, full_down).astype(jnp.bfloat16)

        def down_part(slot):
            return (
                lax.dynamic_slice_in_dim(down, starts[slot] + core * rows, rows, 0),
                lax.dynamic_slice_in_dim(down, starts[slot] + (1 - core) * rows, rows, 0),
            )

        output = hidden_state + ring.scatter(down_part)
        _, pull_norm_mlp = jax.vjp(rms_norm, hidden_state, gain_mlp)
        hidden_norm_grad, gain_mlp_part = pull_norm_mlp(normed_mlp_grad)
        hidden_grad = cotangent + hidden_norm_grad
        seen_branch = ring.gather(hidden_grad.astype(jnp.bfloat16))

        def over_fsdp(grad, dimension):
            return lax.psum_scatter(grad.astype(jnp.bfloat16), "fsdp", scatter_dimension=dimension, tiled=True).astype(jnp.float32)

        TN = (((0,), (0,)), ((), ()))
        grad_down = over_fsdp(dot(inner, all_grads, TN), 1)
        grad_gate = over_fsdp(dot(all_tokens, gate_grad, TN), 0)
        grad_up = over_fsdp(dot(all_tokens, up_grad, TN), 0)

        empty = jnp.zeros((group_rows, width), jnp.float32)
        dquery, dkey, dvalue = empty, empty, empty
        mixed_parts, branch_parts = [], []
        for slot in range(chips):
            mixed, totals = kept[slot]
            same, other = seen_branch[slot]
            grad_same = dot(same, full_out, NT).astype(jnp.bfloat16)
            grad_other = dot(other, full_out, NT).astype(jnp.bfloat16)
            mixed_parts.append(mixed.reshape(pair, width))
            branch_parts.extend((same, other))
            dquery, dkey, dvalue = attend_back(places[slot], qkv, mixed, grad_same, grad_other, totals, keys_t, dquery, dkey, dvalue)
        grad_out = over_fsdp(dot(jnp.concatenate(mixed_parts, axis=0), jnp.concatenate(branch_parts, axis=0), TN), 1)
        qkv_grad = unrotate(order, dquery, dkey, dvalue, cosine, sine)

        def qkv_part(slot):
            part = dot(qkv_grad[slot * pair : (slot + 1) * pair], w_qkv, NT).astype(jnp.bfloat16)
            return part[:rows], part[rows:]

        normed_attn_grad = ring.scatter(qkv_part)
        flat_attn = jnp.concatenate([half for slot in range(chips) for half in seen_attn[slot]], axis=0)
        grad_qkv = over_fsdp(dot(flat_attn, qkv_grad, TN), 0)
        _, pull_norm_attn = jax.vjp(rms_norm, activations, gain_attn)
        input_norm_grad, gain_attn_part = pull_norm_attn(normed_attn_grad)
        input_grad = hidden_grad + input_norm_grad
        gain_sums = swap_sum(jnp.stack([gain_attn_part, gain_mlp_part]), sizes)
        return (
            output,
            input_grad,
            gain_sums[0],
            grad_qkv[:, :width],
            grad_qkv[:, width : 2 * width],
            grad_qkv[:, 2 * width :],
            grad_out,
            gain_sums[1],
            grad_gate,
            grad_up,
            grad_down,
        )

    return body


def solution(mesh):
    tokens = P(("fsdp", "tp"), None)
    column = P("fsdp", "tp")
    row = P("tp", "fsdp")
    in_specs = (tokens, P(), column, column, column, row, P(), column, column, row, tokens)
    out_specs = (tokens, tokens, P(), column, column, column, row, P(), column, column, row)
    return jax.shard_map(make_body(mesh), mesh=mesh, in_specs=in_specs, out_specs=out_specs, check_vma=False)
```

```python
import jax
import jax.numpy as jnp
from jax import lax
from jax.experimental import pallas as pl
from jax.experimental.pallas import tpu as pltpu
from jax.sharding import PartitionSpec as P

HEAD_DIM = 64
SEQ_LEN = 2048
LANES = 128
rope_base = 130000.0
norm_eps = 1e-05
masked_score = -1e30

NT = (((1,), (1,)), ((), ()))
NN = (((1,), (0,)), ((), ()))
TN = (((0,), (0,)), ((), ()))
MESH = pl.DeviceIdType.MESH
DMA = pltpu.SemaphoreType.DMA
ANYWHERE = pl.BlockSpec(memory_space=pl.ANY)
VMEM = pl.BlockSpec(memory_space=pltpu.VMEM)
low = jnp.bfloat16


def dot(left, right, dims=NN):
    return lax.dot_general(left, right, dims, preferred_element_type=jnp.float32)


def span(index, size):
    return pl.ds(pl.multiple_of(index * size, size), size)


def remote(source, target, send, receive, device):
    return pltpu.make_async_remote_copy(
        src_ref=source, dst_ref=target, send_sem=send, recv_sem=receive,
        device_id=device, device_id_type=MESH,
    )


def hello(device):
    pl.semaphore_signal(pltpu.get_barrier_semaphore(), inc=1, device_id=device, device_id_type=MESH)


class Line:
    def __init__(self, chips):
        self.chips = chips
        self.me = lax.axis_index("tp")
        self.chip, self.core = self.me // 2, self.me % 2
        self.partner = 2 * self.chip + 1 - self.core
        self.has_left, self.has_right = self.chip > 0, self.chip < chips - 1

    def greet(self, more=()):
        hello({"tp": self.partner})

        @pl.when(self.has_left)
        def _():
            hello({"tp": self.me - 2})

        @pl.when(self.has_right)
        def _():
            hello({"tp": self.me + 2})

        for device in more:
            hello(device)
        count = 1 + len(more) + jnp.where(self.has_left, 1, 0) + jnp.where(self.has_right, 1, 0)
        pl.semaphore_wait(pltpu.get_barrier_semaphore(), count)

    def target(self, step):
        after = self.chips - 1 - self.chip
        most, least = jnp.maximum(self.chip, after), jnp.minimum(self.chip, after)
        sign = jnp.where(after >= self.chip, 1, -1)
        late = step - (most - least)
        side = jnp.where(late % 2 == 0, sign, -sign)
        return jnp.where(late < 0, self.chip + sign * (most - step), self.chip + side * (least - late // 2))


class Gather:
    scratch = staticmethod(lambda chips: [DMA((2 * chips,)), DMA((chips,)), DMA((chips,)), DMA((chips,)), DMA])

    def __init__(self, line, own, out, received, right, left, across, local):
        self.line, self.own, self.out = line, own, out
        self.received, self.right, self.left, self.across, self.local = received, right, left, across, local
        self.rows = own.shape[0]

    def block(self, index):
        return self.out.at[span(index, self.rows)]

    def copy(self, source, sems, chip, device, mine):
        index = 2 * chip + self.line.core
        return remote(source if mine else self.block(index), self.block(index), sems.at[chip], self.received.at[index], {"tp": device})

    def keep(self):
        return pltpu.make_async_copy(self.own, self.block(self.line.me), self.local)

    def start(self):
        line = self.line
        self.keep().start()

        @pl.when(line.has_right)
        def _():
            self.copy(self.own, self.right, line.chip, line.me + 2, True).start()

        @pl.when(line.has_left)
        def _():
            self.copy(self.own, self.left, line.chip, line.me - 2, True).start()

        self.copy(self.own, self.across, line.chip, line.partner, True).start()

    def arrive(self, index):
        remote(self.own, self.block(index), self.right.at[0], self.received.at[index], {"tp": self.line.partner}).wait_recv()

    def arrive_across(self, chip):
        self.arrive(2 * chip + 1 - self.line.core)

    def step(self, distance):
        line = self.line
        before, after = line.chip - distance, line.chip + distance

        @pl.when(before >= 0)
        def _():
            self.arrive(2 * before + line.core)

            @pl.when(line.has_right)
            def _():
                self.copy(None, self.right, before, line.me + 2, False).start()

            self.copy(None, self.across, before, line.partner, False).start()

        @pl.when(after < line.chips)
        def _():
            self.arrive(2 * after + line.core)

            @pl.when(line.has_left)
            def _():
                self.copy(None, self.left, after, line.me - 2, False).start()

            self.copy(None, self.across, after, line.partner, False).start()

    def finish(self, arrivals):
        line = self.line
        if arrivals:
            self.keep().wait()
        for chip in range(line.chips):
            if arrivals:
                self.arrive_across(chip)
            self.copy(self.own, self.across, chip, line.partner, True).wait_send()

            @pl.when(jnp.logical_and(line.has_right, chip <= line.chip))
            def _():
                self.copy(self.own, self.right, chip, line.me + 2, True).wait_send()

            @pl.when(jnp.logical_and(line.has_left, chip >= line.chip))
            def _():
                self.copy(self.own, self.left, chip, line.me - 2, True).wait_send()


class Scatter:
    @staticmethod
    def scratch(chips, rows, depth):
        shares = min(chips, 4)
        return [
            pltpu.VMEM((2, 2 * rows, depth), low),
            pltpu.VMEM((shares, rows, depth), low),
            pltpu.VMEM((chips + 1, rows, depth), low),
            pltpu.VMEM((2, rows, depth), low),
            DMA((2,)), DMA((shares,)), DMA((2,)), DMA((chips + 1,)),
        ]

    def __init__(self, line, out, term, shares, lines, total, share_send, share_recv, line_send, line_recv):
        self.line, self.out = line, out
        self.term, self.shares, self.lines, self.total = term, shares, lines, total
        self.share_send, self.share_recv, self.line_send, self.line_recv = share_send, share_recv, line_send, line_recv
        self.rows = out.shape[0]

    def share(self, step):
        slot = step % self.shares.shape[0]
        source = self.term.at[step % 2, span(1 - self.line.core, self.rows)]
        return remote(source, self.shares.at[slot], self.share_send.at[step % 2], self.share_recv.at[slot], {"tp": self.line.partner})

    def pass_on(self, step):
        line, target = self.line, self.line.target(step)
        onward = target > line.chip
        slot = jnp.where(onward, target, jnp.where(target == line.chip - 1, line.chips, target))
        device = jnp.where(onward, line.me + 2, line.me - 2)
        return remote(self.total.at[step % 2], self.lines.at[slot], self.line_send.at[step % 2], self.line_recv.at[slot], {"tp": device})

    def add(self, slot):
        remote(self.total.at[0], self.lines.at[slot], self.line_send.at[0], self.line_recv.at[slot], {"tp": self.line.partner}).wait_recv()
        self.out[...] += self.lines[slot].astype(jnp.float32)

    def free(self, step):
        @pl.when(step >= 2)
        def _():
            self.share(step - 2).wait_send()

    def step(self, step):
        line, target = self.line, self.line.target(step)
        self.share(step).wait_recv()
        mine = self.term[step % 2, span(line.core, self.rows), :].astype(jnp.float32)
        self.out[...] = mine + self.shares[step % self.shares.shape[0]].astype(jnp.float32)

        @pl.when(jnp.logical_and(target >= line.chip, line.has_left))
        def _():
            self.add(target)

        @pl.when(jnp.logical_and(target <= line.chip, line.has_right))
        def _():
            self.add(jnp.where(target == line.chip, line.chips, target))

        @pl.when(step < line.chips - 1)
        def _():
            @pl.when(step >= 2)
            def _():
                self.pass_on(step - 2).wait_send()

            self.total[step % 2] = self.out[...].astype(low)
            self.pass_on(step).start()

    def finish(self):
        chips = self.line.chips
        for step in range(max(0, chips - 3), chips - 1):
            self.pass_on(step).wait_send()
        for step in range(max(0, chips - 2), chips):
            self.share(step).wait_send()


def turned(block, sign):
    half = HEAD_DIM // 2
    lane = lax.broadcasted_iota(jnp.int32, block.shape, 1)
    width = block.shape[1]
    up = pltpu.roll(block, width - half, 1)
    down = pltpu.roll(block, half, 1)
    return jnp.where(lane % HEAD_DIM < half, -sign * up, sign * down)


def widened(table, width):
    return table if table.shape[1] == width else jnp.concatenate([table] * (width // table.shape[1]), axis=1)


def only_head(block, head):
    lane = lax.broadcasted_iota(jnp.int32, block.shape, 1)
    return jnp.where(lane // HEAD_DIM == head, block, jnp.zeros_like(block))


def causal(tile):
    key = lax.broadcasted_iota(jnp.int32, tile.shape, 0)
    query = lax.broadcasted_iota(jnp.int32, tile.shape, 1)
    return jnp.where(key <= query, tile, masked_score)


def over_keys(chunk, rows, visit):
    start = chunk * rows
    first = start // SEQ_LEN * SEQ_LEN

    def step(index, carry):
        visit(pl.multiple_of(first + index * rows, rows), False)
        return carry

    lax.fori_loop(0, (start - first) // rows, step, 0)
    visit(pl.multiple_of(start, rows), True)


def project_kernel(
    chips, shards,
    tokens, w_query, w_key, w_value, cosine, sine,
    tokens_out, weight, qkv, keys_t, values_t,
    chunks, chunk_sem, weight_send, weight_recv, weight_keep, *gather_sems,
):
    line = Line(chips)
    rows = tokens.shape[0]
    pair = 2 * rows
    depth, width = w_query.shape
    shard = lax.axis_index("fsdp")
    others = [(shard + ahead) % shards for ahead in range(1, shards)]
    gather = Gather(line, tokens, tokens_out, *gather_sems)
    parts = (w_query, w_key, w_value)

    def place(index, part):
        return weight.at[span(index, depth), pl.ds(part * width, width)]

    def give(ahead, part):
        return remote(parts[part], place(shard, part), weight_send.at[ahead, part], weight_recv.at[ahead, part], {"fsdp": others[ahead]})

    def keep(part):
        return pltpu.make_async_copy(parts[part], place(shard, part), weight_keep.at[part])

    line.greet([{"fsdp": other} for other in others])
    gather.start()
    for part in range(3):
        keep(part).start()
        for ahead in range(shards - 1):
            give(ahead, part).start()

    def project(chip):
        @pl.when(jnp.logical_and(chip >= 0, chip < chips))
        def _():
            gather.arrive_across(chip)
            load = pltpu.make_async_copy(tokens_out.at[span(chip, pair)], chunks, chunk_sem)
            load.start()
            load.wait()
            here = span(chip, pair)
            table = span(chip % (SEQ_LEN // pair), pair)
            for part in range(3):
                columns = pl.ds(part * width, width)
                block = dot(chunks[...], weight[:, columns])
                if part < 2:
                    block = block * widened(cosine[table, :], width) + turned(block, 1.0) * widened(sine[table, :], width)
                qkv[here, columns] = block.astype(low)
                if part:
                    (keys_t, values_t)[part - 1][:, here] = block.T.astype(low)

    def step(index, carry):
        @pl.when(jnp.logical_and(index >= 1, index < chips))
        def _():
            gather.step(index)

        @pl.when(index == 1)
        def _():
            gather.keep().wait()
            for part in range(3):
                keep(part).wait()
                for ahead in range(shards - 1):
                    give(ahead, part).wait_recv()

        def side(which, carry):
            distance = index - 1

            @pl.when(jnp.logical_and(distance >= 0, jnp.logical_or(which == 0, distance > 0)))
            def _():
                project(jnp.where(which == 0, line.chip - distance, line.chip + distance))

            return carry

        lax.fori_loop(0, 2, side, 0)
        return carry

    lax.fori_loop(0, chips + 1, step, 0)
    gather.finish(False)
    for part in range(3):
        for ahead in range(shards - 1):
            give(ahead, part).wait_send()


def project(chips, shards, tokens, w_query, w_key, w_value, cosine, sine):
    rows, depth = tokens.shape
    group_rows = 2 * chips * rows
    shard_rows, width = w_query.shape
    shape = jax.ShapeDtypeStruct
    return pl.pallas_call(
        lambda *refs: project_kernel(chips, shards, *refs),
        in_specs=[VMEM] * 6,
        out_specs=[ANYWHERE] + [VMEM] * 4,
        out_shape=[
            shape((group_rows, depth), low),
            shape((depth, 3 * width), low),
            shape((group_rows, 3 * width), low),
            shape((width, group_rows), low),
            shape((width, group_rows), low),
        ],
        scratch_shapes=[pltpu.VMEM((2 * rows, depth), low), DMA, DMA((shards - 1, 3)), DMA((shards - 1, 3)), DMA((3,))] + Gather.scratch(chips),
        compiler_params=pltpu.CompilerParams(collective_id=1, has_side_effects=True, vmem_limit_bytes=40 << 20),
        cost_estimate=pl.CostEstimate(flops=6 * group_rows * depth * width, bytes_accessed=4 * group_rows * depth, transcendentals=0),
        name="project",
    )(tokens, w_query, w_key, w_value, cosine, sine)


def attend_chunk(chunk, rows, qkv, values_t, heads_ref, acc, out, top_ref, sum_ref):
    width = acc.shape[0]
    heads = width // HEAD_DIM
    scaled = qkv[span(chunk, rows), pl.ds(0, width)] * low(HEAD_DIM**-0.5)
    for head in range(heads):
        heads_ref[head] = only_head(scaled, head)
    acc[...] = jnp.zeros_like(acc)
    top_ref[...] = jnp.full_like(top_ref, masked_score)
    sum_ref[...] = jnp.zeros_like(sum_ref)

    def visit(offset, diagonal):
        key_block = qkv[pl.ds(offset, rows), pl.ds(width, width)]
        for head in range(heads):
            feature = pl.ds(head * HEAD_DIM, HEAD_DIM)
            one = pl.ds(head, 1)
            scores = dot(key_block, heads_ref[head], NT)
            if diagonal:
                scores = causal(scores)
            old = top_ref[one, :]
            top = jnp.maximum(old, jnp.max(scores, axis=0, keepdims=True))
            shrink = jnp.exp(old - top)
            weights = jnp.exp(scores - top)
            top_ref[one, :] = top
            sum_ref[one, :] = sum_ref[one, :] * shrink + jnp.sum(weights, axis=0, keepdims=True)
            acc[feature, :] = acc[feature, :] * shrink + dot(values_t[feature, pl.ds(offset, rows)], weights.astype(low))

    over_keys(chunk, rows, visit)
    for head in range(heads):
        feature = pl.ds(head * HEAD_DIM, HEAD_DIM)
        acc[feature, :] = acc[feature, :] / sum_ref[pl.ds(head, 1), :]
    out[...] = acc[...].T.astype(low)


def attend_kernel(
    chips,
    qkv, values_t, w_out, grads,
    branch, mixed, totals, grads_out,
    heads_ref, acc, out, top_ref, sum_ref, *sems,
):
    line = Line(chips)
    rows, depth = branch.shape
    pair = 2 * rows
    scatter = Scatter(line, branch, *sems[:8])
    gather = Gather(line, grads, grads_out, *sems[8:])
    line.greet()
    gather.start()

    def step(index, carry):
        work = jnp.where(index == chips, chips - 1, index)

        @pl.when(jnp.logical_or(index < chips - 1, index == chips))
        def _():
            chunk = line.target(work)
            attend_chunk(chunk, pair, qkv, values_t, heads_ref, acc, out, top_ref, sum_ref)
            mixed[span(chunk, pair), :] = out[...]
            totals[:, span(chunk, pair)] = top_ref[...] + jnp.log(sum_ref[...])
            scatter.free(work)

            def tile(place, carry):
                columns = span(place, 512)
                scatter.term[work % 2, :, columns] = dot(out[...], w_out[:, columns]).astype(low)
                return carry

            lax.fori_loop(0, depth // 512, tile, 0)
            scatter.share(work).start()

        @pl.when(jnp.logical_and(index >= 1, index < chips))
        def _():
            gather.step(index)

        @pl.when(index >= 1)
        def _():
            scatter.step(index - 1)

        return carry

    lax.fori_loop(0, chips + 1, step, 0)
    scatter.finish()
    gather.finish(True)


def attend(chips, qkv, values_t, w_out, grads):
    rows, depth = grads.shape
    pair = 2 * rows
    group_rows = chips * pair
    width = w_out.shape[0]
    heads = width // HEAD_DIM
    shape = jax.ShapeDtypeStruct
    return pl.pallas_call(
        lambda *refs: attend_kernel(chips, *refs),
        in_specs=[VMEM] * 4,
        out_specs=[VMEM] * 3 + [ANYWHERE],
        out_shape=[
            shape((rows, depth), jnp.float32),
            shape((group_rows, width), low),
            shape((heads, group_rows), jnp.float32),
            shape((group_rows, depth), low),
        ],
        scratch_shapes=[
            pltpu.VMEM((heads, pair, width), low),
            pltpu.VMEM((width, pair), jnp.float32),
            pltpu.VMEM((pair, width), low),
            pltpu.VMEM((heads, pair), jnp.float32),
            pltpu.VMEM((heads, pair), jnp.float32),
        ] + Scatter.scratch(chips, rows, depth) + Gather.scratch(chips),
        compiler_params=pltpu.CompilerParams(collective_id=2, has_side_effects=True, vmem_limit_bytes=60 << 20),
        cost_estimate=pl.CostEstimate(flops=2 * group_rows * (SEQ_LEN + depth) * width, bytes_accessed=4 * group_rows * depth, transcendentals=group_rows * SEQ_LEN * heads // 2),
        name="attend",
    )(qkv, values_t, w_out, grads)


def back_chunk(chunk, rows, grad, qkv, keys_t, mixed, totals, dkey, dvalue, heads_ref, grads_ref, acc, inner_ref):
    width = acc.shape[0]
    heads = width // HEAD_DIM
    here = span(chunk, rows)
    scaled = qkv[here, pl.ds(0, width)] * low(HEAD_DIM**-0.5)
    product = grad.astype(jnp.float32) * mixed[here, :].astype(jnp.float32)
    shape = (inner_ref.shape[0], width)
    pick = (lax.broadcasted_iota(jnp.int32, shape, 1) // HEAD_DIM == lax.broadcasted_iota(jnp.int32, shape, 0)).astype(jnp.float32)
    inner_ref[...] = lax.dot_general(pick, product, NT, precision=lax.Precision.HIGHEST, preferred_element_type=jnp.float32)
    for head in range(heads):
        heads_ref[head] = only_head(scaled, head)
        grads_ref[head] = only_head(grad, head)
    acc[...] = jnp.zeros_like(acc)

    def visit(offset, diagonal):
        keys = pl.ds(offset, rows)
        key_block = qkv[keys, pl.ds(width, width)]
        value_block = qkv[keys, pl.ds(2 * width, width)]
        key_sum, value_sum = dkey[keys, :], dvalue[keys, :]
        for head in range(heads):
            feature = pl.ds(head * HEAD_DIM, HEAD_DIM)
            scores = dot(key_block, heads_ref[head], NT)
            if diagonal:
                scores = causal(scores)
            probs = jnp.exp(scores - totals[pl.ds(head, 1), here])
            dprobs = dot(value_block, grads_ref[head], NT)
            dscores = (probs * (dprobs - inner_ref[pl.ds(head, 1), :])).astype(low)
            value_sum = value_sum + dot(probs.astype(low), grads_ref[head])
            key_sum = key_sum + dot(dscores, heads_ref[head])
            acc[feature, :] = acc[feature, :] + dot(keys_t[feature, keys], dscores)
        dkey[keys, :] = key_sum
        dvalue[keys, :] = value_sum

    over_keys(chunk, rows, visit)


def back_kernel(
    chips,
    branch, inner, w_down, w_out, qkv, keys_t, mixed, totals, cosine, sine,
    down, branch_out, qkv_grad,
    down_w, inner_chunk, branch_chunk, dkey, dvalue, heads_ref, grads_ref, acc, inner_ref, load_sem, inner_sem, branch_sem, *sems,
):
    line = Line(chips)
    rows, depth = down.shape
    pair = 2 * rows
    width = w_out.shape[0]
    scatter = Scatter(line, down, *sems[:8])
    gather = Gather(line, branch, branch_out, *sems[8:])

    def load():
        return pltpu.make_async_copy(w_down, down_w, load_sem)

    def fetch(step):
        return pltpu.make_async_copy(inner.at[span(line.target(step), pair)], inner_chunk.at[step % 2], inner_sem.at[step % 2])

    load().start()
    fetch(0).start()
    line.greet()
    gather.start()
    dkey[...] = jnp.zeros_like(dkey)
    dvalue[...] = jnp.zeros_like(dvalue)

    def unrotated(block, chunk):
        table = span(chunk % (SEQ_LEN // pair), pair)
        return (block * widened(cosine[table, :], width) + turned(block * widened(sine[table, :], width), -1.0)).astype(low)

    def attention(chunk):
        gather.arrive_across(chunk)
        copy = pltpu.make_async_copy(branch_out.at[span(chunk, pair)], branch_chunk, branch_sem)
        copy.start()
        copy.wait()
        grad = dot(branch_chunk[...], w_out[...], NT).astype(low)
        back_chunk(chunk, pair, grad, qkv, keys_t, mixed, totals, dkey, dvalue, heads_ref, grads_ref, acc, inner_ref)
        qkv_grad[span(chunk, pair), pl.ds(0, width)] = unrotated(acc[...].T * HEAD_DIM**-0.5, chunk)

    def step(index, carry):
        @pl.when(index == 0)
        def _():
            load().wait()
            gather.keep().wait()

        @pl.when(index < chips)
        def _():
            @pl.when(index < chips - 1)
            def _():
                fetch(index + 1).start()

            fetch(index).wait()
            scatter.free(index)

            def tile(place, carry):
                columns = span(place, 256)
                scatter.term[index % 2, :, columns] = dot(inner_chunk[index % 2], down_w[:, columns]).astype(low)
                return carry

            lax.fori_loop(0, depth // 256, tile, 0)
            scatter.share(index).start()

        @pl.when(jnp.logical_and(index >= 1, index < chips))
        def _():
            gather.step(index)

        def side(which, carry):
            chunk = jnp.where(which == 0, line.chip - index, line.chip + index)
            there = jnp.logical_and(chunk >= 0, chunk < chips)

            @pl.when(jnp.logical_and(there, jnp.logical_or(which == 0, index > 0)))
            def _():
                attention(chunk)

            return carry

        lax.fori_loop(0, 2, side, 0)

        @pl.when(index >= 1)
        def _():
            scatter.step(index - 1)

        return carry

    lax.fori_loop(0, chips + 1, step, 0)

    def close(chunk, carry):
        here = span(chunk, pair)
        qkv_grad[here, pl.ds(width, width)] = unrotated(dkey[here, :], chunk)
        qkv_grad[here, pl.ds(2 * width, width)] = dvalue[here, :].astype(low)
        return carry

    lax.fori_loop(0, chips, close, 0)
    scatter.finish()
    gather.finish(False)


def back(chips, branch, inner, w_down, w_out, qkv, keys_t, mixed, totals, cosine, sine):
    rows, depth = branch.shape
    pair = 2 * rows
    group_rows = chips * pair
    width = w_out.shape[0]
    hidden = w_down.shape[0]
    heads = width // HEAD_DIM
    shape = jax.ShapeDtypeStruct
    return pl.pallas_call(
        lambda *refs: back_kernel(chips, *refs),
        in_specs=[VMEM, ANYWHERE, ANYWHERE] + [VMEM] * 7,
        out_specs=[VMEM, ANYWHERE, VMEM],
        out_shape=[
            shape((rows, depth), jnp.float32),
            shape((group_rows, depth), low),
            shape((group_rows, 3 * width), low),
        ],
        scratch_shapes=[
            pltpu.VMEM((hidden, depth), low),
            pltpu.VMEM((2, pair, hidden), low),
            pltpu.VMEM((pair, depth), low),
            pltpu.VMEM((group_rows, width), jnp.float32),
            pltpu.VMEM((group_rows, width), jnp.float32),
            pltpu.VMEM((heads, pair, width), low),
            pltpu.VMEM((heads, pair, width), low),
            pltpu.VMEM((width, pair), jnp.float32),
            pltpu.VMEM((8, pair), jnp.float32),
            DMA, DMA((2,)), DMA,
        ] + Scatter.scratch(chips, rows, depth) + Gather.scratch(chips),
        compiler_params=pltpu.CompilerParams(collective_id=4, has_side_effects=True, vmem_limit_bytes=63 << 20),
        cost_estimate=pl.CostEstimate(flops=2 * group_rows * (depth * hidden + depth * width + 5 * SEQ_LEN * width // 2), bytes_accessed=6 * group_rows * depth, transcendentals=group_rows * SEQ_LEN * heads // 2),
        name="back",
    )(branch, inner, w_down, w_out, qkv, keys_t, mixed, totals, cosine, sine)


def spread_kernel(chips, qkv_grad, weight, out, *sems):
    line = Line(chips)
    rows, depth = out.shape
    pair = 2 * rows
    scatter = Scatter(line, out, *sems)
    line.greet()

    def step(index, carry):
        @pl.when(index < chips)
        def _():
            here = span(line.target(index), pair)
            scatter.free(index)

            def tile(place, carry):
                columns = span(place, 512)
                scatter.term[index % 2, :, columns] = dot(qkv_grad[here, :], weight[columns, :], NT).astype(low)
                return carry

            lax.fori_loop(0, depth // 512, tile, 0)
            scatter.share(index).start()

        @pl.when(index >= 1)
        def _():
            scatter.step(index - 1)

        return carry

    lax.fori_loop(0, chips + 1, step, 0)
    scatter.finish()


def spread(chips, qkv_grad, weight):
    group_rows = qkv_grad.shape[0]
    rows = group_rows // (2 * chips)
    depth = weight.shape[0]
    return pl.pallas_call(
        lambda *refs: spread_kernel(chips, *refs),
        in_specs=[VMEM] * 2,
        out_specs=VMEM,
        out_shape=jax.ShapeDtypeStruct((rows, depth), jnp.float32),
        scratch_shapes=Scatter.scratch(chips, rows, depth),
        compiler_params=pltpu.CompilerParams(collective_id=5, has_side_effects=True, vmem_limit_bytes=48 << 20),
        cost_estimate=pl.CostEstimate(flops=2 * group_rows * weight.size, bytes_accessed=4 * weight.size, transcendentals=0),
        name="spread",
    )(qkv_grad, weight)


def chip_at(place, chips):
    return jnp.where(2 * place < chips, 2 * place, 2 * (chips - 1 - place) + 1)


def place_of(chip, chips):
    return jnp.where(chip % 2 == 0, chip // 2, chips - 1 - chip // 2)


def feed_kernel(
    chips,
    tokens_ref, grads_hbm, gate_hbm, up_hbm, down_hbm,
    back_ref, tokens_out, inner_out, gate_out, up_out,
    tokens_all, gate_w, up_w, down_w, grads, inner, gate_grad, up_grad, own, term, stage, from_core, from_ring, total,
    load_sem, grad_sem, keep_sem, store_sem, ring_send, ring_recv, core_send, core_recv, stage_send, stage_recv, total_send, total_recv,
):
    rows, depth = tokens_ref.shape
    pair = 2 * rows
    hidden = gate_w.shape[1]
    me = lax.axis_index("tp")
    chip, core = me // 2, me % 2
    place = place_of(chip, chips)
    following = 2 * chip_at((place + 1) % chips, chips) + core
    before = 2 * chip_at((place + chips - 1) % chips, chips) + core
    partner = 2 * chip + 1 - core

    loads = [pltpu.make_async_copy(a, b, load_sem.at[i]) for i, (a, b) in enumerate(((gate_hbm, gate_w), (up_hbm, up_w), (down_hbm, down_w)))]
    for load in loads:
        load.start()

    def source(slot):
        return chip_at((place + chips - slot) % chips, chips)

    def fetch(slot):
        start = pl.multiple_of(source(slot) * pair, pair)
        return pltpu.make_async_copy(grads_hbm.at[pl.ds(start, pair)], grads.at[slot % 2], grad_sem.at[slot % 2])

    def block(ref, index):
        return ref.at[pl.ds(pl.multiple_of(index * rows, rows), rows)]

    def to_ring(slot):
        index = 2 * source(slot) + core
        return remote(block(tokens_all, index), block(tokens_all, index), ring_send.at[slot], ring_recv.at[slot], {"tp": following})

    def to_core(slot):
        index = 2 * source(slot) + core
        return remote(block(tokens_all, index), block(tokens_all, index), core_send.at[slot], core_recv.at[slot], {"tp": partner})

    def keep(slot):
        start = pl.multiple_of(source(slot) * pair, pair)
        span = pl.ds(start, pair)
        return pltpu.make_async_copy(tokens_all.at[span], tokens_out.at[span], keep_sem.at[slot])

    def stores(slot):
        span = pl.ds(pl.multiple_of(source(slot) * pair, pair), pair)
        return [
            pltpu.make_async_copy(ref.at[slot % 2], out.at[span], store_sem.at[i, slot % 2])
            for i, (ref, out) in enumerate(((inner, inner_out), (gate_grad, gate_out), (up_grad, up_out)))
        ]

    def stage_copy(slot):
        return remote(stage.at[slot % 2], from_core.at[slot], stage_send.at[slot % 2], stage_recv.at[slot], {"tp": partner})

    def total_copy(slot):
        return remote(total.at[slot - 1], from_ring.at[slot - 1], total_send.at[slot - 1], total_recv.at[slot - 1], {"tp": following})

    fetch(0).start()
    tokens_all[pl.ds(pl.multiple_of(me * rows, rows), rows), :] = tokens_ref[...]
    for device in (following, before, partner):
        hello({"tp": device})
    pl.semaphore_wait(pltpu.get_barrier_semaphore(), 3)

    def step(slot, carry):
        @pl.when(slot > 0)
        def _():
            to_ring(slot - 1).wait_recv()

        @pl.when(slot < chips - 1)
        def _():
            to_ring(slot).start()
            fetch(slot + 1).start()

        to_core(slot).start()

        @pl.when(slot == 0)
        def _():
            for load in loads:
                load.wait()

        @pl.when(slot > 1)
        def _():
            for store in stores(slot - 2):
                store.wait()

        to_core(slot).wait_recv()
        keep(slot).start()
        fetch(slot).wait()
        here = slot % 2
        span = pl.ds(pl.multiple_of(source(slot) * pair, pair), pair)

        def narrow(tile, carry):
            columns = pl.ds(pl.multiple_of(tile * 256, 256), 256)
            token = tokens_all[span, :]
            gate = dot(token, gate_w[:, columns])
            up = dot(token, up_w[:, columns])
            grad = dot(grads[here], down_w[columns, :], NT)
            squash = jax.nn.sigmoid(gate)
            act = gate * squash
            inner[here, :, columns] = (act * up).astype(jnp.bfloat16)
            up_grad[here, :, columns] = (grad * act).astype(jnp.bfloat16)
            gate_grad[here, :, columns] = (grad * up * squash * (1.0 + gate * (1.0 - squash))).astype(jnp.bfloat16)
            return carry

        lax.fori_loop(0, hidden // 256, narrow, 0)
        for store in stores(slot):
            store.start()

        @pl.when(slot > 1)
        def _():
            stage_copy(slot - 2).wait_send()

        def wide(tile, carry):
            columns = pl.ds(pl.multiple_of(tile * 256, 256), 256)
            part = dot(gate_grad[here], gate_w[columns, :], NT) + dot(up_grad[here], up_w[columns, :], NT)
            term[:, columns] = part.astype(jnp.bfloat16)
            return carry

        lax.fori_loop(0, depth // 256, wide, 0)
        stage[here] = term[pl.ds(pl.multiple_of((1 - core) * rows, rows), rows), :]
        stage_copy(slot).start()
        mine = pl.ds(pl.multiple_of(core * rows, rows), rows)

        @pl.when(slot == 0)
        def _():
            own[...] = term[mine, :].astype(jnp.float32)

        @pl.when(slot > 0)
        def _():
            stage_copy(slot).wait_recv()

        @pl.when(slot == 1)
        def _():
            total[slot - 1] = (term[mine, :].astype(jnp.float32) + from_core[slot].astype(jnp.float32)).astype(jnp.bfloat16)

        @pl.when(slot > 1)
        def _():
            total_copy(slot - 1).wait_recv()
            total[slot - 1] = (term[mine, :].astype(jnp.float32) + from_core[slot].astype(jnp.float32) + from_ring[slot - 2].astype(jnp.float32)).astype(jnp.bfloat16)

        @pl.when(slot > 0)
        def _():
            total_copy(slot).start()

        return carry

    lax.fori_loop(0, chips, step, 0)
    stage_copy(0).wait_recv()
    total_copy(chips - 1).wait_recv()
    back_ref[...] = own[...] + from_core[0].astype(jnp.float32) + from_ring[chips - 2].astype(jnp.float32)
    for slot in range(chips):
        to_core(slot).wait_send()
        keep(slot).wait()
        if slot < chips - 1:
            to_ring(slot).wait_send()
        if slot > 0:
            total_copy(slot).wait_send()
        if slot >= chips - 2:
            stage_copy(slot).wait_send()
            for store in stores(slot):
                store.wait()


def feed(chips, tokens, grads, gate_w, up_w, down_w):
    rows, depth = tokens.shape
    pair = 2 * rows
    group_rows = chips * pair
    hidden = gate_w.shape[1]
    return pl.pallas_call(
        lambda *refs: feed_kernel(chips, *refs),
        in_specs=[VMEM] + [ANYWHERE] * 4,
        out_specs=[VMEM] + [ANYWHERE] * 4,
        out_shape=[
            jax.ShapeDtypeStruct((rows, depth), jnp.float32),
            jax.ShapeDtypeStruct((group_rows, depth), low),
        ] + [jax.ShapeDtypeStruct((group_rows, hidden), low)] * 3,
        scratch_shapes=[
            pltpu.VMEM((group_rows, depth), low),
            pltpu.VMEM(gate_w.shape, low),
            pltpu.VMEM(up_w.shape, low),
            pltpu.VMEM(down_w.shape, low),
            pltpu.VMEM((2, pair, depth), low),
            pltpu.VMEM((2, pair, hidden), low),
            pltpu.VMEM((2, pair, hidden), low),
            pltpu.VMEM((2, pair, hidden), low),
            pltpu.VMEM((rows, depth), jnp.float32),
            pltpu.VMEM((pair, depth), low),
            pltpu.VMEM((2, rows, depth), low),
            pltpu.VMEM((chips, rows, depth), low),
            pltpu.VMEM((chips - 1, rows, depth), low),
            pltpu.VMEM((chips - 1, rows, depth), low),
            DMA((3,)), DMA((2,)), DMA((chips,)), DMA((3, 2)),
            DMA((chips,)), DMA((chips,)), DMA((chips,)), DMA((chips,)),
            DMA((2,)), DMA((chips,)), DMA((chips - 1,)), DMA((chips - 1,)),
        ],
        compiler_params=pltpu.CompilerParams(collective_id=3, has_side_effects=True, vmem_limit_bytes=63 << 20),
        cost_estimate=pl.CostEstimate(flops=12 * group_rows * depth * hidden, bytes_accessed=10 * group_rows * depth, transcendentals=group_rows * hidden),
        name="feed",
    )(tokens, grads, gate_w, up_w, down_w)


def rms_norm(values, gain):
    return values * lax.rsqrt(jnp.mean(values * values, axis=-1, keepdims=True) + norm_eps) * gain


def rope_tables(width):
    half = HEAD_DIM // 2
    positions = jnp.arange(SEQ_LEN, dtype=jnp.int32).astype(jnp.float32)
    column = jnp.arange(width, dtype=jnp.int32) % half
    inverse = jnp.power(jnp.float32(rope_base), -2.0 * column.astype(jnp.float32) / HEAD_DIM)
    angle = positions[:, None] * inverse[None, :]
    return (jnp.cos(angle), jnp.sin(angle))


def swap_sum(values, mesh):
    for axis in ("tp", "fsdp"):
        step = 1
        while step < mesh[axis]:
            values = values + lax.ppermute(values, axis, [(i, i ^ step) for i in range(mesh[axis])])
            step *= 2
    return values


def make_body(mesh):
    sizes = dict(mesh.shape)
    chips, shards = sizes["tp"] // 2, sizes["fsdp"]

    def body(activations, gain_attn, w_query, w_key, w_value, w_out, gain_mlp, w_gate, w_up, w_down, cotangent):
        width = w_query.shape[1]
        full_out = lax.all_gather(w_out, "fsdp", axis=1, tiled=True)
        full_gate = lax.all_gather(w_gate, "fsdp", axis=0, tiled=True)
        full_up = lax.all_gather(w_up, "fsdp", axis=0, tiled=True)
        full_down = lax.all_gather(w_down, "fsdp", axis=1, tiled=True)
        cosine, sine = rope_tables(LANES)

        normed_attn = rms_norm(activations, gain_attn).astype(low)
        seen_attn, w_qkv, qkv, keys_t, values_t = project(chips, shards, normed_attn, w_query, w_key, w_value, cosine, sine)
        attn_branch, mixed, totals, seen_grad = attend(chips, qkv, values_t, full_out, cotangent.astype(low))
        hidden_state = activations + attn_branch
        normed_mlp = rms_norm(hidden_state, gain_mlp).astype(low)
        normed_mlp_grad, seen_mlp, inner, gate_grad, up_grad = feed(chips, normed_mlp, seen_grad, full_gate, full_up, full_down)
        _, pull_norm_mlp = jax.vjp(rms_norm, hidden_state, gain_mlp)
        hidden_norm_grad, gain_mlp_part = pull_norm_mlp(normed_mlp_grad)
        hidden_grad = cotangent + hidden_norm_grad

        def over_fsdp(grad, dimension):
            return lax.psum_scatter(grad, "fsdp", scatter_dimension=dimension, tiled=True)

        branch_grad, grad_down, grad_gate, grad_up = lax.optimization_barrier(
            (
                hidden_grad.astype(low),
                dot(inner, seen_grad, TN).astype(low),
                dot(seen_mlp, gate_grad, TN).astype(low),
                dot(seen_mlp, up_grad, TN).astype(low),
            )
        )
        grad_down, grad_gate, grad_up = over_fsdp(grad_down, 1), over_fsdp(grad_gate, 0), over_fsdp(grad_up, 0)
        down, seen_branch, qkv_grad = back(
            chips, branch_grad, inner, full_down, full_out, qkv, keys_t, mixed, totals, cosine, sine
        )
        output = hidden_state + down
        qkv_grad, grad_out, grad_qkv, grad_down, grad_gate, grad_up = lax.optimization_barrier(
            (
                qkv_grad,
                dot(mixed, seen_branch, TN).astype(low),
                dot(seen_attn, qkv_grad, TN).astype(low),
                grad_down,
                grad_gate,
                grad_up,
            )
        )
        grad_out, grad_qkv = over_fsdp(grad_out, 1), over_fsdp(grad_qkv, 0)
        normed_attn_grad = spread(chips, qkv_grad, w_qkv)
        _, pull_norm_attn = jax.vjp(rms_norm, activations, gain_attn)
        input_norm_grad, gain_attn_part = pull_norm_attn(normed_attn_grad)
        input_grad = hidden_grad + input_norm_grad
        gain_sums = swap_sum(jnp.stack([gain_attn_part, gain_mlp_part]), sizes)
        grad_query, grad_key, grad_value = [grad_qkv[:, part * width : (part + 1) * width] for part in range(3)]
        weights = [
            grad.astype(jnp.float32)
            for grad in (grad_query, grad_key, grad_value, grad_out, grad_gate, grad_up, grad_down)
        ]
        return (output, input_grad, gain_sums[0], *weights[:4], gain_sums[1], *weights[4:])

    return body


def solution(mesh):
    tokens = P(("fsdp", "tp"), None)
    column = P("fsdp", "tp")
    row = P("tp", "fsdp")
    in_specs = (tokens, P(), column, column, column, row, P(), column, column, row, tokens)
    out_specs = (tokens, tokens, P(), column, column, column, row, P(), column, column, row)
    return jax.shard_map(make_body(mesh), mesh=mesh, in_specs=in_specs, out_specs=out_specs, check_vma=False)
```

```python
import jax
import jax.numpy as jnp
from jax import lax
from jax.experimental import pallas as pl
from jax.experimental.pallas import tpu as pltpu
from jax.sharding import PartitionSpec as P

HEAD_DIM = 64
SEQ_LEN = 2048
LANES = 128
rope_base = 130000.0
norm_eps = 1e-05
masked_score = -1e30

NT = (((1,), (1,)), ((), ()))
NN = (((1,), (0,)), ((), ()))
TN = (((0,), (0,)), ((), ()))
MESH = pl.DeviceIdType.MESH
DMA = pltpu.SemaphoreType.DMA
ANYWHERE = pl.BlockSpec(memory_space=pl.ANY)
VMEM = pl.BlockSpec(memory_space=pltpu.VMEM)
low = jnp.bfloat16


def dot(left, right, dims=NN):
    return lax.dot_general(left, right, dims, preferred_element_type=jnp.float32)


def span(index, size):
    return pl.ds(pl.multiple_of(index * size, size), size)


def remote(source, target, send, receive, device):
    return pltpu.make_async_remote_copy(
        src_ref=source, dst_ref=target, send_sem=send, recv_sem=receive,
        device_id=device, device_id_type=MESH,
    )


def hello(device):
    pl.semaphore_signal(pltpu.get_barrier_semaphore(), inc=1, device_id=device, device_id_type=MESH)


class Line:
    def __init__(self, chips):
        self.chips = chips
        self.me = lax.axis_index("tp")
        self.chip, self.core = self.me // 2, self.me % 2
        self.partner = 2 * self.chip + 1 - self.core
        self.has_left, self.has_right = self.chip > 0, self.chip < chips - 1

    def greet(self, more=()):
        hello({"tp": self.partner})

        @pl.when(self.has_left)
        def _():
            hello({"tp": self.me - 2})

        @pl.when(self.has_right)
        def _():
            hello({"tp": self.me + 2})

        for device in more:
            hello(device)
        count = 1 + len(more) + jnp.where(self.has_left, 1, 0) + jnp.where(self.has_right, 1, 0)
        pl.semaphore_wait(pltpu.get_barrier_semaphore(), count)

    def target(self, step):
        after = self.chips - 1 - self.chip
        most, least = jnp.maximum(self.chip, after), jnp.minimum(self.chip, after)
        sign = jnp.where(after >= self.chip, 1, -1)
        late = step - (most - least)
        side = jnp.where(late % 2 == 0, sign, -sign)
        return jnp.where(late < 0, self.chip + sign * (most - step), self.chip + side * (least - late // 2))


    def fed(self, target):
        after, before = jnp.logical_and(target >= self.chip, self.has_left), jnp.logical_and(target <= self.chip, self.has_right)
        return jnp.logical_or(after, before)


class Gather:
    scratch = staticmethod(lambda chips: [DMA((2 * chips,)), DMA((chips,)), DMA((chips,)), DMA((chips,)), DMA])

    def __init__(self, line, own, out, received, right, left, across, local):
        self.line, self.own, self.out = line, own, out
        self.received, self.right, self.left, self.across, self.local = received, right, left, across, local
        self.rows = own.shape[0]

    def block(self, index):
        return self.out.at[span(index, self.rows)]

    def copy(self, source, sems, chip, device, mine):
        index = 2 * chip + self.line.core
        return remote(source if mine else self.block(index), self.block(index), sems.at[chip], self.received.at[index], {"tp": device})

    def keep(self):
        return pltpu.make_async_copy(self.own, self.block(self.line.me), self.local)

    def start(self):
        line = self.line
        self.keep().start()

        @pl.when(line.has_right)
        def _():
            self.copy(self.own, self.right, line.chip, line.me + 2, True).start()

        @pl.when(line.has_left)
        def _():
            self.copy(self.own, self.left, line.chip, line.me - 2, True).start()

        self.copy(self.own, self.across, line.chip, line.partner, True).start()

    def arrive(self, index):
        remote(self.own, self.block(index), self.right.at[0], self.received.at[index], {"tp": self.line.partner}).wait_recv()

    def arrive_across(self, chip):
        self.arrive(2 * chip + 1 - self.line.core)

    def step(self, distance):
        line = self.line
        before, after = line.chip - distance, line.chip + distance

        @pl.when(before >= 0)
        def _():
            self.arrive(2 * before + line.core)

            @pl.when(line.has_right)
            def _():
                self.copy(None, self.right, before, line.me + 2, False).start()

            self.copy(None, self.across, before, line.partner, False).start()

        @pl.when(after < line.chips)
        def _():
            self.arrive(2 * after + line.core)

            @pl.when(line.has_left)
            def _():
                self.copy(None, self.left, after, line.me - 2, False).start()

            self.copy(None, self.across, after, line.partner, False).start()

    def finish(self, arrivals):
        line = self.line
        if arrivals:
            self.keep().wait()
        for chip in range(line.chips):
            if arrivals:
                self.arrive_across(chip)
            self.copy(self.own, self.across, chip, line.partner, True).wait_send()

            @pl.when(jnp.logical_and(line.has_right, chip <= line.chip))
            def _():
                self.copy(self.own, self.right, chip, line.me + 2, True).wait_send()

            @pl.when(jnp.logical_and(line.has_left, chip >= line.chip))
            def _():
                self.copy(self.own, self.left, chip, line.me - 2, True).wait_send()


class Scatter:
    @staticmethod
    def scratch(chips, rows, depth):
        shares = min(chips, 4)
        return [
            pltpu.VMEM((2, 2 * rows, depth), low),
            pltpu.VMEM((shares, rows, depth), low),
            pltpu.VMEM((chips + 1, rows, depth), low),
            pltpu.VMEM((2, rows, depth), low),
            DMA((2,)), DMA((shares,)), DMA((2,)), DMA((chips + 1,)),
        ]

    def __init__(self, line, out, term, shares, lines, total, share_send, share_recv, line_send, line_recv):
        self.line, self.out = line, out
        self.term, self.shares, self.lines, self.total = term, shares, lines, total
        self.share_send, self.share_recv, self.line_send, self.line_recv = share_send, share_recv, line_send, line_recv
        self.rows = out.shape[0]

    def share(self, step):
        slot = step % self.shares.shape[0]
        source = self.term.at[step % 2, span(1 - self.line.core, self.rows)]
        return remote(source, self.shares.at[slot], self.share_send.at[step % 2], self.share_recv.at[slot], {"tp": self.line.partner})

    def pass_on(self, step):
        line, target = self.line, self.line.target(step)
        onward = target > line.chip
        slot = jnp.where(onward, target, jnp.where(target == line.chip - 1, line.chips, target))
        device = jnp.where(onward, line.me + 2, line.me - 2)
        return remote(self.total.at[step % 2], self.lines.at[slot], self.line_send.at[step % 2], self.line_recv.at[slot], {"tp": device})

    def add(self, slot):
        remote(self.total.at[0], self.lines.at[slot], self.line_send.at[0], self.line_recv.at[slot], {"tp": self.line.partner}).wait_recv()
        self.out[...] += self.lines[slot].astype(jnp.float32)

    def free(self, step):
        @pl.when(step >= 2)
        def _():
            self.share(step - 2).wait_send()

    def step(self, step):
        line, target = self.line, self.line.target(step)
        self.share(step).wait_recv()
        mine = self.term[step % 2, span(line.core, self.rows), :].astype(jnp.float32)
        self.out[...] = mine + self.shares[step % self.shares.shape[0]].astype(jnp.float32)

        @pl.when(jnp.logical_and(target >= line.chip, line.has_left))
        def _():
            self.add(target)

        @pl.when(jnp.logical_and(target <= line.chip, line.has_right))
        def _():
            self.add(jnp.where(target == line.chip, line.chips, target))

        @pl.when(step < line.chips - 1)
        def _():
            @pl.when(step >= 2)
            def _():
                self.pass_on(step - 2).wait_send()

            self.total[step % 2] = self.out[...].astype(low)
            self.pass_on(step).start()

    def finish(self):
        chips = self.line.chips
        for step in range(max(0, chips - 3), chips - 1):
            self.pass_on(step).wait_send()
        for step in range(max(0, chips - 2), chips):
            self.share(step).wait_send()


NORM_ROWS = 64


def normed(value, gain):
    return value * lax.rsqrt(jnp.mean(value * value, axis=-1, keepdims=True) + norm_eps) * gain


def norm_back(value, gain, grad):
    scale = lax.rsqrt(jnp.mean(value * value, axis=-1, keepdims=True) + norm_eps)
    unit = value * scale
    scaled = grad * gain
    return scale * (scaled - unit * jnp.mean(scaled * unit, axis=-1, keepdims=True)), jnp.sum(grad * unit, axis=0, keepdims=True)


def by_rows(rows, work):
    def step(index, carry):
        work(span(index, NORM_ROWS))
        return carry

    lax.fori_loop(0, rows // NORM_ROWS, step, 0)


def turned(block, sign):
    half = HEAD_DIM // 2
    lane = lax.broadcasted_iota(jnp.int32, block.shape, 1)
    width = block.shape[1]
    up = pltpu.roll(block, width - half, 1)
    down = pltpu.roll(block, half, 1)
    return jnp.where(lane % HEAD_DIM < half, -sign * up, sign * down)


def widened(table, width):
    return table if table.shape[1] == width else jnp.concatenate([table] * (width // table.shape[1]), axis=1)


def only_head(block, head):
    lane = lax.broadcasted_iota(jnp.int32, block.shape, 1)
    return jnp.where(lane // HEAD_DIM == head, block, jnp.zeros_like(block))


def causal(tile):
    key = lax.broadcasted_iota(jnp.int32, tile.shape, 0)
    query = lax.broadcasted_iota(jnp.int32, tile.shape, 1)
    return jnp.where(key <= query, tile, masked_score)


def over_keys(chunk, rows, visit):
    start = chunk * rows
    first = start // SEQ_LEN * SEQ_LEN

    def step(index, carry):
        visit(pl.multiple_of(first + index * rows, rows), False)
        return carry

    lax.fori_loop(0, (start - first) // rows, step, 0)
    visit(pl.multiple_of(start, rows), True)


def project_kernel(
    chips, shards,
    activations, gain, w_query, w_key, w_value, cosine_t, sine_t,
    tokens_out, weight, qkv, keys_t, values_t, cosine, sine,
    tokens, chunks, chunk_sem, weight_send, weight_recv, weight_keep, *gather_sems,
):
    line = Line(chips)
    rows = tokens.shape[0]
    pair = 2 * rows
    depth, width = w_query.shape
    shard = lax.axis_index("fsdp")
    others = [(shard + ahead) % shards for ahead in range(1, shards)]
    gather = Gather(line, tokens, tokens_out, *gather_sems)
    parts = (w_query, w_key, w_value)

    def place(part):
        return weight.at[span(shard, depth), pl.ds(part * width, width)]

    def give(ahead, part):
        return remote(parts[part], place(part), weight_send.at[ahead, part], weight_recv.at[ahead, part], {"fsdp": others[ahead]})

    def keep(part):
        return pltpu.make_async_copy(parts[part], place(part), weight_keep.at[part])

    def norm(here):
        tokens[here, :] = normed(activations[here, :], gain[...]).astype(low)

    by_rows(rows, norm)
    line.greet([{"fsdp": other} for other in others])
    gather.start()
    for part in range(3):
        keep(part).start()
        for ahead in range(shards - 1):
            give(ahead, part).start()
    for table, table_t in ((cosine, cosine_t), (sine, sine_t)):
        turn = table_t[...].T
        table[...] = jnp.concatenate([turn] * (LANES // turn.shape[1]), axis=1)

    def project(chip):
        @pl.when(jnp.logical_and(chip >= 0, chip < chips))
        def _():
            gather.arrive_across(chip)
            load = pltpu.make_async_copy(tokens_out.at[span(chip, pair)], chunks, chunk_sem)
            load.start()
            load.wait()
            here = span(chip, pair)
            table = span(chip % (SEQ_LEN // pair), pair)
            for part in range(3):
                columns = pl.ds(part * width, width)
                block = dot(chunks[...], weight[:, columns])
                if part < 2:
                    block = block * widened(cosine[table, :], width) + turned(block, 1.0) * widened(sine[table, :], width)
                qkv[here, columns] = block.astype(low)
                if part:
                    (keys_t, values_t)[part - 1][:, here] = block.T.astype(low)

    def step(index, carry):
        @pl.when(jnp.logical_and(index >= 1, index < chips))
        def _():
            gather.step(index)

        @pl.when(index == 1)
        def _():
            gather.keep().wait()
            for part in range(3):
                keep(part).wait()
                for ahead in range(shards - 1):
                    give(ahead, part).wait_recv()

        def side(which, carry):
            distance = index - 1

            @pl.when(jnp.logical_and(distance >= 0, jnp.logical_or(which == 0, distance > 0)))
            def _():
                project(jnp.where(which == 0, line.chip - distance, line.chip + distance))

            return carry

        lax.fori_loop(0, 2, side, 0)
        return carry

    lax.fori_loop(0, chips + 1, step, 0)
    gather.finish(False)
    for part in range(3):
        for ahead in range(shards - 1):
            give(ahead, part).wait_send()


def project(chips, shards, activations, gain, w_query, w_key, w_value, cosine_t, sine_t):
    rows, depth = activations.shape
    group_rows = 2 * chips * rows
    width = w_query.shape[1]
    shape = jax.ShapeDtypeStruct
    return pl.pallas_call(
        lambda *refs: project_kernel(chips, shards, *refs),
        in_specs=[VMEM] * 7,
        out_specs=[ANYWHERE] + [VMEM] * 6,
        out_shape=[
            shape((group_rows, depth), low),
            shape((depth, 3 * width), low),
            shape((group_rows, 3 * width), low),
            shape((width, group_rows), low),
            shape((width, group_rows), low),
            shape((SEQ_LEN, LANES), jnp.float32),
            shape((SEQ_LEN, LANES), jnp.float32),
        ],
        scratch_shapes=[
            pltpu.VMEM((rows, depth), low),
            pltpu.VMEM((2 * rows, depth), low),
            DMA, DMA((shards - 1, 3)), DMA((shards - 1, 3)), DMA((3,)),
        ] + Gather.scratch(chips),
        compiler_params=pltpu.CompilerParams(collective_id=1, has_side_effects=True, vmem_limit_bytes=63 << 20),
        cost_estimate=pl.CostEstimate(flops=6 * group_rows * depth * width, bytes_accessed=4 * group_rows * depth, transcendentals=0),
        name="project",
    )(activations, gain, w_query, w_key, w_value, cosine_t, sine_t)


def attend_chunk(chunk, rows, qkv, values_t, heads_ref, acc, out, top_ref, sum_ref):
    width = acc.shape[0]
    heads = width // HEAD_DIM
    scaled = qkv[span(chunk, rows), pl.ds(0, width)] * low(HEAD_DIM**-0.5)
    for head in range(heads):
        heads_ref[head] = only_head(scaled, head)
    acc[...] = jnp.zeros_like(acc)
    top_ref[...] = jnp.full_like(top_ref, masked_score)
    sum_ref[...] = jnp.zeros_like(sum_ref)

    def visit(offset, diagonal):
        key_block = qkv[pl.ds(offset, rows), pl.ds(width, width)]
        for head in range(heads):
            feature = pl.ds(head * HEAD_DIM, HEAD_DIM)
            one = pl.ds(head, 1)
            scores = dot(key_block, heads_ref[head], NT)
            if diagonal:
                scores = causal(scores)
            old = top_ref[one, :]
            top = jnp.maximum(old, jnp.max(scores, axis=0, keepdims=True))
            shrink = jnp.exp(old - top)
            weights = jnp.exp(scores - top)
            top_ref[one, :] = top
            sum_ref[one, :] = sum_ref[one, :] * shrink + jnp.sum(weights, axis=0, keepdims=True)
            acc[feature, :] = acc[feature, :] * shrink + dot(values_t[feature, pl.ds(offset, rows)], weights.astype(low))

    over_keys(chunk, rows, visit)
    for head in range(heads):
        feature = pl.ds(head * HEAD_DIM, HEAD_DIM)
        acc[feature, :] = acc[feature, :] / sum_ref[pl.ds(head, 1), :]
    out[...] = acc[...].T.astype(low)


def attend_kernel(
    chips,
    qkv, values_t, w_out, activations, cotangent, gain,
    hidden, tokens, mixed, totals, grads_out,
    heads_ref, acc, out, top_ref, sum_ref, grads, *sems,
):
    line = Line(chips)
    rows, depth = hidden.shape
    pair = 2 * rows
    scatter = Scatter(line, hidden, *sems[:8])
    grads[...] = cotangent[...].astype(low)
    gather = Gather(line, grads, grads_out, *sems[8:])
    line.greet()
    gather.start()

    def step(index, carry):
        work = jnp.where(index == chips, chips - 1, index)

        @pl.when(jnp.logical_or(index < chips - 1, index == chips))
        def _():
            chunk = line.target(work)
            attend_chunk(chunk, pair, qkv, values_t, heads_ref, acc, out, top_ref, sum_ref)
            mixed[span(chunk, pair), :] = out[...]
            totals[:, span(chunk, pair)] = top_ref[...] + jnp.log(sum_ref[...])
            scatter.free(work)

            def tile(place, carry):
                columns = span(place, 512)
                scatter.term[work % 2, :, columns] = dot(out[...], w_out[:, columns]).astype(low)
                return carry

            lax.fori_loop(0, depth // 512, tile, 0)
            scatter.share(work).start()

        @pl.when(jnp.logical_and(index >= 1, index < chips))
        def _():
            gather.step(index)

        @pl.when(index >= 1)
        def _():
            scatter.step(index - 1)

        return carry

    lax.fori_loop(0, chips + 1, step, 0)

    def norm(here):
        state = activations[here, :] + hidden[here, :]
        hidden[here, :] = state
        tokens[here, :] = normed(state, gain[...]).astype(low)

    by_rows(rows, norm)
    scatter.finish()
    gather.finish(True)


def attend(chips, qkv, values_t, w_out, activations, cotangent, gain):
    rows, depth = activations.shape
    pair = 2 * rows
    group_rows = chips * pair
    width = w_out.shape[0]
    heads = width // HEAD_DIM
    shape = jax.ShapeDtypeStruct
    return pl.pallas_call(
        lambda *refs: attend_kernel(chips, *refs),
        in_specs=[VMEM] * 6,
        out_specs=[VMEM] * 4 + [ANYWHERE],
        out_shape=[
            shape((rows, depth), jnp.float32),
            shape((rows, depth), low),
            shape((group_rows, width), low),
            shape((heads, group_rows), jnp.float32),
            shape((group_rows, depth), low),
        ],
        scratch_shapes=[
            pltpu.VMEM((heads, pair, width), low),
            pltpu.VMEM((width, pair), jnp.float32),
            pltpu.VMEM((pair, width), low),
            pltpu.VMEM((heads, pair), jnp.float32),
            pltpu.VMEM((heads, pair), jnp.float32),
            pltpu.VMEM((rows, depth), low),
        ] + Scatter.scratch(chips, rows, depth) + Gather.scratch(chips),
        compiler_params=pltpu.CompilerParams(collective_id=2, has_side_effects=True, vmem_limit_bytes=63 << 20),
        cost_estimate=pl.CostEstimate(flops=2 * group_rows * (SEQ_LEN + depth) * width, bytes_accessed=4 * group_rows * depth, transcendentals=group_rows * SEQ_LEN * heads // 2),
        name="attend",
    )(qkv, values_t, w_out, activations, cotangent, gain)


def back_chunk(chunk, rows, grad, qkv, keys_t, mixed, totals, dkey, dvalue, heads_ref, grads_ref, acc, inner_ref):
    width = acc.shape[0]
    heads = width // HEAD_DIM
    here = span(chunk, rows)
    scaled = qkv[here, pl.ds(0, width)] * low(HEAD_DIM**-0.5)
    product = grad.astype(jnp.float32) * mixed[here, :].astype(jnp.float32)
    shape = (inner_ref.shape[0], width)
    pick = (lax.broadcasted_iota(jnp.int32, shape, 1) // HEAD_DIM == lax.broadcasted_iota(jnp.int32, shape, 0)).astype(jnp.float32)
    inner_ref[...] = lax.dot_general(pick, product, NT, precision=lax.Precision.HIGHEST, preferred_element_type=jnp.float32)
    for head in range(heads):
        heads_ref[head] = only_head(scaled, head)
        grads_ref[head] = only_head(grad, head)
    acc[...] = jnp.zeros_like(acc)

    def visit(offset, diagonal):
        keys = pl.ds(offset, rows)
        key_block = qkv[keys, pl.ds(width, width)]
        value_block = qkv[keys, pl.ds(2 * width, width)]
        key_sum, value_sum = dkey[keys, :], dvalue[keys, :]
        for head in range(heads):
            feature = pl.ds(head * HEAD_DIM, HEAD_DIM)
            scores = dot(key_block, heads_ref[head], NT)
            if diagonal:
                scores = causal(scores)
            probs = jnp.exp(scores - totals[pl.ds(head, 1), here])
            dprobs = dot(value_block, grads_ref[head], NT)
            dscores = (probs * (dprobs - inner_ref[pl.ds(head, 1), :])).astype(low)
            value_sum = value_sum + dot(probs.astype(low), grads_ref[head])
            key_sum = key_sum + dot(dscores, heads_ref[head])
            acc[feature, :] = acc[feature, :] + dot(keys_t[feature, keys], dscores)
        dkey[keys, :] = key_sum
        dvalue[keys, :] = value_sum

    over_keys(chunk, rows, visit)


def back_kernel(
    chips, shards,
    branch, inner, grads, w_down, w_out, qkv, keys_t, mixed, totals, cosine, sine,
    down, branch_out, qkv_grad, grad_down, grad_out,
    down_w, inner_chunk, grad_chunk, down_sum, down_tile, out_sum, out_stage, out_from, branch_chunk, dkey, dvalue, heads_ref, grads_ref, acc, inner_ref,
    load_sem, inner_sem, grad_sem, branch_sem, tile_sem, out_send, out_recv, *sems,
):
    line = Line(chips)
    rows, depth = down.shape
    pair = 2 * rows
    width = w_out.shape[0]
    scatter = Scatter(line, down, *sems[:8])
    gather = Gather(line, branch, branch_out, *sems[8:])

    def load():
        return pltpu.make_async_copy(w_down, down_w, load_sem)

    def fetch(step):
        return pltpu.make_async_copy(inner.at[span(line.target(step), pair)], inner_chunk.at[step % 2], inner_sem.at[step % 2])

    def fetch_grad(step):
        return pltpu.make_async_copy(grads.at[span(line.target(step), pair)], grad_chunk, grad_sem)

    shard = lax.axis_index("fsdp")
    columns_out = depth // shards
    others = [(shard + ahead) % shards for ahead in range(1, shards)]

    def give(turn):
        return remote(out_stage.at[turn], out_from.at[turn], out_send.at[turn], out_recv.at[turn], {"fsdp": others[turn]})

    def keep_tile(place):
        return pltpu.make_async_copy(down_tile, grad_down.at[span(place, 256)], tile_sem)

    load().start()
    fetch(0).start()
    line.greet([{"fsdp": other} for other in others])
    gather.start()
    out_sum[...] = jnp.zeros_like(out_sum)
    dkey[...] = jnp.zeros_like(dkey)
    dvalue[...] = jnp.zeros_like(dvalue)

    def unrotated(block, chunk):
        table = span(chunk % (SEQ_LEN // pair), pair)
        return (block * widened(cosine[table, :], width) + turned(block * widened(sine[table, :], width), -1.0)).astype(low)

    def attention(chunk):
        gather.arrive_across(chunk)
        copy = pltpu.make_async_copy(branch_out.at[span(chunk, pair)], branch_chunk, branch_sem)
        copy.start()
        copy.wait()
        out_sum[...] += dot(mixed[span(chunk, pair), :], branch_chunk[...], TN)
        grad = dot(branch_chunk[...], w_out[...], NT).astype(low)
        back_chunk(chunk, pair, grad, qkv, keys_t, mixed, totals, dkey, dvalue, heads_ref, grads_ref, acc, inner_ref)
        qkv_grad[span(chunk, pair), pl.ds(0, width)] = unrotated(acc[...].T * HEAD_DIM**-0.5, chunk)

    def close():
        def part(chunk, carry):
            here = span(chunk, pair)
            qkv_grad[here, pl.ds(width, width)] = unrotated(dkey[here, :], chunk)
            qkv_grad[here, pl.ds(2 * width, width)] = dvalue[here, :].astype(low)
            return carry

        lax.fori_loop(0, chips, part, 0)

    def step(index, carry):
        @pl.when(index == 0)
        def _():
            load().wait()
            gather.keep().wait()

        @pl.when(index < chips)
        def _():
            @pl.when(index < chips - 1)
            def _():
                fetch(index + 1).start()

            fetch(index).wait()
            scatter.free(index)

            def tile(place, carry):
                columns = span(place, 256)
                scatter.term[index % 2, :, columns] = dot(inner_chunk[index % 2], down_w[:, columns]).astype(low)
                return carry

            lax.fori_loop(0, depth // 256, tile, 0)
            scatter.share(index).start()

        @pl.when(jnp.logical_and(index >= 1, index < chips))
        def _():
            gather.step(index)

        @pl.when(index < chips)
        def _():
            fetch_grad(index).start()

        @pl.when(index == chips)
        def _():
            for turn in range(shards - 1):
                out_stage[turn] = out_sum[:, span(others[turn], columns_out)].astype(low)
                give(turn).start()
            close()

        def phase(which, carry):
            done = jnp.maximum(index - 1, 0)
            late = line.fed(line.target(done))
            turn = jnp.logical_or(jnp.logical_and(which == 0, jnp.logical_not(late)), jnp.logical_and(which == 3, late))

            @pl.when(jnp.logical_and(index >= 1, turn))
            def _():
                scatter.step(done)

            chunk = jnp.where(which == 1, line.chip - index, line.chip + index)
            there = jnp.logical_and(chunk >= 0, chunk < chips)
            turn = jnp.logical_or(which == 1, jnp.logical_and(which == 2, index > 0))

            @pl.when(jnp.logical_and(there, turn))
            def _():
                attention(chunk)

            return carry

        lax.fori_loop(0, 4, phase, 0)

        @pl.when(index < chips)
        def _():
            fetch_grad(index).wait()

            def tile(place, carry):
                here = span(place, 256)
                part = dot(inner_chunk[index % 2, :, here], grad_chunk[...], TN)

                @pl.when(index == 0)
                def _():
                    down_sum[here, :] = part

                @pl.when(index > 0)
                def _():
                    down_sum[here, :] += part

                @pl.when(index == chips - 1)
                def _():
                    @pl.when(place > 0)
                    def _():
                        keep_tile(place - 1).wait()

                    down_tile[...] = down_sum[here, :].astype(low)
                    keep_tile(place).start()

                return carry

            lax.fori_loop(0, down_sum.shape[0] // 256, tile, 0)

        return carry

    lax.fori_loop(0, chips + 1, step, 0)
    total = out_sum[:, span(shard, columns_out)]
    for turn in range(shards - 1):
        give(turn).wait_recv()
        total = total + out_from[turn].astype(jnp.float32)
    grad_out[...] = total
    for turn in range(shards - 1):
        give(turn).wait_send()
    keep_tile(down_sum.shape[0] // 256 - 1).wait()
    scatter.finish()
    gather.finish(False)


def back(chips, shards, branch, inner, grads, w_down, w_out, qkv, keys_t, mixed, totals, cosine, sine):
    rows, depth = branch.shape
    pair = 2 * rows
    group_rows = chips * pair
    width = w_out.shape[0]
    hidden = w_down.shape[0]
    heads = width // HEAD_DIM
    shape = jax.ShapeDtypeStruct
    return pl.pallas_call(
        lambda *refs: back_kernel(chips, shards, *refs),
        in_specs=[VMEM] + [ANYWHERE] * 3 + [VMEM] * 7,
        out_specs=[VMEM, ANYWHERE, VMEM, ANYWHERE, VMEM],
        out_shape=[
            shape((rows, depth), jnp.float32),
            shape((group_rows, depth), low),
            shape((group_rows, 3 * width), low),
            shape((hidden, depth), low),
            shape((width, depth // shards), jnp.float32),
        ],
        scratch_shapes=[
            pltpu.VMEM((hidden, depth), low),
            pltpu.VMEM((2, pair, hidden), low),
            pltpu.VMEM((pair, depth), low),
            pltpu.VMEM((hidden, depth), jnp.float32),
            pltpu.VMEM((256, depth), low),
            pltpu.VMEM((width, depth), jnp.float32),
            pltpu.VMEM((shards - 1, width, depth // shards), low),
            pltpu.VMEM((shards - 1, width, depth // shards), low),
            pltpu.VMEM((pair, depth), low),
            pltpu.VMEM((group_rows, width), jnp.float32),
            pltpu.VMEM((group_rows, width), jnp.float32),
            pltpu.VMEM((heads, pair, width), low),
            pltpu.VMEM((heads, pair, width), low),
            pltpu.VMEM((width, pair), jnp.float32),
            pltpu.VMEM((8, pair), jnp.float32),
            DMA, DMA((2,)), DMA, DMA, DMA, DMA((shards - 1,)), DMA((shards - 1,)),
        ] + Scatter.scratch(chips, rows, depth) + Gather.scratch(chips),
        compiler_params=pltpu.CompilerParams(collective_id=4, has_side_effects=True, vmem_limit_bytes=67043328),
        cost_estimate=pl.CostEstimate(flops=1 << 20, bytes_accessed=1 << 20, transcendentals=0),
        name="back",
    )(branch, inner, grads, w_down, w_out, qkv, keys_t, mixed, totals, cosine, sine)


def spread_kernel(
    chips, shards,
    qkv_grad, weight, activations, gain, gain_part, attn_tokens,
    input_part, grad_qkv, gain_sum,
    attn_cols, qkv_stage, qkv_from, gains, gains_tp, gains_fsdp,
    attn_sem, qkv_send, qkv_recv, tp_send, tp_recv, fsdp_send, fsdp_recv, *sems,
):
    line = Line(chips)
    size = 2 * chips
    rows, depth = input_part.shape
    pair = 2 * rows
    shard = lax.axis_index("fsdp")
    columns = depth // shards
    scatter = Scatter(line, input_part, *sems)

    def peer(turn):
        return (shard + 1 + turn) % shards

    def fetch(turn):
        return pltpu.make_async_copy(attn_tokens.at[:, span(peer(turn), columns)], attn_cols.at[turn % 2], attn_sem.at[turn % 2])

    def give(turn):
        return remote(qkv_stage.at[turn], qkv_from.at[turn], qkv_send.at[turn], qkv_recv.at[turn], {"fsdp": peer(turn)})

    def tell_tp(ahead):
        return remote(gains, gains_tp.at[line.me], tp_send.at[ahead - 1], tp_recv.at[line.me], {"tp": (line.me + ahead) % size})

    def tell_fsdp(ahead):
        return remote(gains, gains_fsdp.at[shard], fsdp_send.at[ahead - 1], fsdp_recv.at[shard], {"fsdp": (shard + ahead) % shards})

    fetch(0).start()
    for ahead in range(1, size):
        hello({"tp": (line.me + ahead) % size})
    for ahead in range(1, shards):
        hello({"fsdp": (shard + ahead) % shards})
    pl.semaphore_wait(pltpu.get_barrier_semaphore(), size - 1 + shards - 1)

    def weights(turn, carry):
        @pl.when(turn < shards - 1)
        def _():
            fetch(turn + 1).start()

        fetch(turn).wait()
        part = dot(attn_cols[turn % 2], qkv_grad[...], TN)

        @pl.when(turn < shards - 1)
        def _():
            qkv_stage[turn] = part.astype(low)
            give(turn).start()

        @pl.when(turn == shards - 1)
        def _():
            grad_qkv[...] = part

        return carry

    def step(index, carry):
        @pl.when(index < chips)
        def _():
            here = span(line.target(index), pair)
            scatter.free(index)

            def tile(place, carry):
                there = span(place, 512)
                scatter.term[index % 2, :, there] = dot(qkv_grad[here, :], weight[there, :], NT).astype(low)
                return carry

            lax.fori_loop(0, depth // 512, tile, 0)
            scatter.share(index).start()

        def phase(which, carry):
            done = jnp.maximum(index - 1, 0)
            late = line.fed(line.target(done))
            turn = jnp.logical_or(jnp.logical_and(which == 0, jnp.logical_not(late)), jnp.logical_and(which == 2, late))

            @pl.when(jnp.logical_and(index >= 1, turn))
            def _():
                scatter.step(done)

            @pl.when(jnp.logical_and(which == 1, index < 2))
            def _():
                lax.fori_loop(index, jnp.where(index == 0, 1, shards), weights, 0)

            return carry

        lax.fori_loop(0, 3, phase, 0)
        return carry

    lax.fori_loop(0, chips + 1, step, 0)
    for turn in range(shards - 1):
        give(turn).wait_recv()
        grad_qkv[...] += qkv_from[turn].astype(jnp.float32)
    gains[0:1, :] = jnp.zeros((1, depth), jnp.float32)
    gains[1:2, :] = gain_part[...]

    def norm(here):
        part, grad = norm_back(activations[here, :], gain[...], input_part[here, :])
        input_part[here, :] = part
        gains[0:1, :] += grad

    by_rows(rows, norm)

    gains_tp[line.me] = gains[...]
    for ahead in range(1, size):
        tell_tp(ahead).start()
    for ahead in range(1, size):
        source = (line.me + ahead) % size
        remote(gains, gains_tp.at[source], tp_send.at[0], tp_recv.at[source], {"tp": source}).wait_recv()
    total = gains_tp[0]
    for source in range(1, size):
        total = total + gains_tp[source]
    for ahead in range(1, size):
        tell_tp(ahead).wait_send()
    gains[...] = total
    gains_fsdp[shard] = total
    for ahead in range(1, shards):
        tell_fsdp(ahead).start()
    for ahead in range(1, shards):
        source = (shard + ahead) % shards
        remote(gains, gains_fsdp.at[source], fsdp_send.at[0], fsdp_recv.at[source], {"fsdp": source}).wait_recv()
    total = gains_fsdp[0]
    for source in range(1, shards):
        total = total + gains_fsdp[source]
    gain_sum[...] = total
    for ahead in range(1, shards):
        tell_fsdp(ahead).wait_send()
    for turn in range(shards - 1):
        give(turn).wait_send()
    scatter.finish()


def spread(chips, shards, qkv_grad, weight, activations, gain, gain_part, attn_tokens):
    group_rows = qkv_grad.shape[0]
    rows, depth = activations.shape
    width = qkv_grad.shape[1] // 3
    columns = depth // shards
    size = 2 * chips
    shape = jax.ShapeDtypeStruct
    return pl.pallas_call(
        lambda *refs: spread_kernel(chips, shards, *refs),
        in_specs=[VMEM] * 5 + [ANYWHERE],
        out_specs=[VMEM] * 3,
        out_shape=[
            shape((rows, depth), jnp.float32),
            shape((columns, 3 * width), jnp.float32),
            shape((2, depth), jnp.float32),
        ],
        scratch_shapes=[
            pltpu.VMEM((2, group_rows, columns), low),
            pltpu.VMEM((shards - 1, columns, 3 * width), low),
            pltpu.VMEM((shards - 1, columns, 3 * width), low),
            pltpu.VMEM((2, depth), jnp.float32),
            pltpu.VMEM((size, 2, depth), jnp.float32),
            pltpu.VMEM((shards, 2, depth), jnp.float32),
            DMA((2,)), DMA((shards - 1,)), DMA((shards - 1,)),
            DMA((size - 1,)), DMA((size,)), DMA((shards - 1,)), DMA((shards,)),
        ] + Scatter.scratch(chips, rows, depth),
        compiler_params=pltpu.CompilerParams(collective_id=5, has_side_effects=True, vmem_limit_bytes=63 << 20),
        cost_estimate=pl.CostEstimate(flops=1 << 20, bytes_accessed=1 << 20, transcendentals=0),
        name="spread",
    )(qkv_grad, weight, activations, gain, gain_part, attn_tokens)


def chip_at(place, chips):
    return jnp.where(2 * place < chips, 2 * place, 2 * (chips - 1 - place) + 1)


def place_of(chip, chips):
    return jnp.where(chip % 2 == 0, chip // 2, chips - 1 - chip // 2)


def feed_kernel(
    chips,
    hidden_state, cotangent, gain, tokens, grads_hbm, both_hbm, down_hbm,
    hidden_grad, branch, gain_part, inner_out, grad_both,
    tokens_all, gate_w, up_w, down_w, grads, inner, gate_grad, up_grad, term, from_core, from_ring, total, tile_gate, tile_up,
    load_sem, own_sem, grad_sem, store_sem, tile_sem,
    ring_send, ring_recv, core_send, core_recv, share_send, share_recv, total_send, total_recv,
):
    rows, depth = hidden_state.shape
    pair = 2 * rows
    width = gate_w.shape[1]
    me = lax.axis_index("tp")
    chip, core = me // 2, me % 2
    place = place_of(chip, chips)
    following = {"tp": 2 * chip_at((place + 1) % chips, chips) + core}
    before = {"tp": 2 * chip_at((place + chips - 1) % chips, chips) + core}
    partner = {"tp": 2 * chip + 1 - core}

    loads = [pltpu.make_async_copy(a, b, load_sem.at[i]) for i, (a, b) in enumerate(((both_hbm.at[:, pl.ds(0, width)], gate_w), (both_hbm.at[:, pl.ds(width, width)], up_w), (down_hbm, down_w)))]
    own = pltpu.make_async_copy(tokens, tokens_all.at[span(me, rows)], own_sem)

    def source(slot):
        return chip_at((place + chips - slot) % chips, chips)

    def fetch(slot):
        return pltpu.make_async_copy(grads_hbm.at[span(source(slot), pair)], grads.at[slot % 2], grad_sem.at[slot % 2])

    def block(slot):
        return tokens_all.at[span(2 * source(slot) + core, rows)]

    def to_ring(slot):
        return remote(block(slot), block(slot), ring_send.at[slot], ring_recv.at[slot], following)

    def to_core(slot):
        return remote(block(slot), block(slot), core_send.at[slot], core_recv.at[slot], partner)

    def store(slot):
        return pltpu.make_async_copy(inner.at[slot % 2], inner_out.at[span(source(slot), pair)], store_sem.at[slot % 2])

    def share(slot):
        place = jnp.where(slot == 0, 0, 1 + slot % 2)
        return remote(term.at[span(1 - core, rows)], from_core.at[place], share_send, share_recv.at[place], partner)

    def pass_on(slot):
        return remote(total.at[slot % 2], from_ring.at[slot - 1], total_send.at[slot % 2], total_recv.at[slot - 1], following)

    own.start()
    fetch(0).start()
    for load in loads:
        load.start()
    own.wait()
    for device in (following, before, partner):
        hello(device)
    pl.semaphore_wait(pltpu.get_barrier_semaphore(), 3)

    def step(slot, carry):
        here = slot % 2
        wide_rows = span(source(slot), pair)
        mine = span(core, rows)

        @pl.when(slot > 0)
        def _():
            to_ring(slot - 1).wait_recv()

        @pl.when(slot < chips - 1)
        def _():
            to_ring(slot).start()
            fetch(slot + 1).start()

        to_core(slot).start()

        @pl.when(slot == 0)
        def _():
            for load in loads:
                load.wait()

        @pl.when(slot > 1)
        def _():
            store(slot - 2).wait()

        to_core(slot).wait_recv()
        fetch(slot).wait()

        def narrow(tile, carry):
            columns = span(tile, 256)
            token = tokens_all[wide_rows, :]
            gate = dot(token, gate_w[:, columns])
            up = dot(token, up_w[:, columns])
            grad = dot(grads[here], down_w[columns, :], NT)
            squash = jax.nn.sigmoid(gate)
            act = gate * squash
            inner[here, :, columns] = (act * up).astype(low)
            up_grad[wide_rows, columns] = (grad * act).astype(low)
            gate_grad[wide_rows, columns] = (grad * up * squash * (1.0 + gate * (1.0 - squash))).astype(low)
            return carry

        lax.fori_loop(0, width // 256, narrow, 0)
        store(slot).start()

        @pl.when(slot > 0)
        def _():
            share(slot - 1).wait_send()

        def wide(tile, carry):
            columns = span(tile, 256)
            part = dot(gate_grad[wide_rows, :], gate_w[columns, :], NT) + dot(up_grad[wide_rows, :], up_w[columns, :], NT)
            term[:, columns] = part.astype(low)
            return carry

        lax.fori_loop(0, depth // 256, wide, 0)
        share(slot).start()

        @pl.when(slot == 0)
        def _():
            hidden_grad[...] = term[mine, :].astype(jnp.float32)

        @pl.when(slot > 0)
        def _():
            share(slot).wait_recv()

            @pl.when(slot > 2)
            def _():
                pass_on(slot - 2).wait_send()

            @pl.when(slot == 1)
            def _():
                total[here] = (term[mine, :].astype(jnp.float32) + from_core[1 + here].astype(jnp.float32)).astype(low)

            @pl.when(slot > 1)
            def _():
                pass_on(slot - 1).wait_recv()
                total[here] = (term[mine, :].astype(jnp.float32) + from_core[1 + here].astype(jnp.float32) + from_ring[slot - 2].astype(jnp.float32)).astype(low)

            pass_on(slot).start()

        return carry

    lax.fori_loop(0, chips, step, 0)

    def tiles(index):
        there = span(index, 256)
        return (
            pltpu.make_async_copy(tile_gate.at[index % 2], grad_both.at[there, pl.ds(0, width)], tile_sem.at[0, index % 2]),
            pltpu.make_async_copy(tile_up.at[index % 2], grad_both.at[there, pl.ds(width, width)], tile_sem.at[1, index % 2]),
        )

    def weights(index, carry):
        @pl.when(index > 1)
        def _():
            for copy in tiles(index - 2):
                copy.wait()

        token = tokens_all[:, span(index, 256)]
        tile_gate[index % 2] = dot(token, gate_grad[...], TN).astype(low)
        tile_up[index % 2] = dot(token, up_grad[...], TN).astype(low)
        for copy in tiles(index):
            copy.start()
        return carry

    lax.fori_loop(0, depth // 256, weights, 0)
    share(0).wait_recv()
    pass_on(chips - 1).wait_recv()
    gain_part[...] = jnp.zeros_like(gain_part)

    def norm(here):
        grad = hidden_grad[here, :] + from_core[0, here, :].astype(jnp.float32) + from_ring[chips - 2, here, :].astype(jnp.float32)
        part, gain_grad = norm_back(hidden_state[here, :], gain[...], grad)
        full = cotangent[here, :] + part
        hidden_grad[here, :] = full
        branch[here, :] = full.astype(low)
        gain_part[...] += gain_grad

    by_rows(rows, norm)
    share(chips - 1).wait_send()
    for slot in range(chips):
        to_core(slot).wait_send()
        if slot < chips - 1:
            to_ring(slot).wait_send()
        if slot >= max(1, chips - 2):
            pass_on(slot).wait_send()
        if slot >= chips - 2:
            store(slot).wait()
    for index in range(depth // 256 - 2, depth // 256):
        for copy in tiles(index):
            copy.wait()


def feed(chips, hidden_state, cotangent, gain, tokens, grads, both_w, down_w):
    rows, depth = tokens.shape
    pair = 2 * rows
    group_rows = chips * pair
    width = down_w.shape[0]
    shape = jax.ShapeDtypeStruct
    return pl.pallas_call(
        lambda *refs: feed_kernel(chips, *refs),
        in_specs=[VMEM] * 3 + [ANYWHERE] * 4,
        out_specs=[VMEM] * 3 + [ANYWHERE] * 2,
        out_shape=[
            shape((rows, depth), jnp.float32),
            shape((rows, depth), low),
            shape((1, depth), jnp.float32),
            shape((group_rows, width), low),
            shape((depth, 2 * width), low),
        ],
        scratch_shapes=[
            pltpu.VMEM((group_rows, depth), low),
            pltpu.VMEM((depth, width), low),
            pltpu.VMEM((depth, width), low),
            pltpu.VMEM(down_w.shape, low),
            pltpu.VMEM((2, pair, depth), low),
            pltpu.VMEM((2, pair, width), low),
            pltpu.VMEM((group_rows, width), low),
            pltpu.VMEM((group_rows, width), low),
            pltpu.VMEM((pair, depth), low),
            pltpu.VMEM((3, rows, depth), low),
            pltpu.VMEM((chips - 1, rows, depth), low),
            pltpu.VMEM((2, rows, depth), low),
            pltpu.VMEM((2, 256, width), low),
            pltpu.VMEM((2, 256, width), low),
            DMA((3,)), DMA, DMA((2,)), DMA((2,)), DMA((2, 2)),
            DMA((chips,)), DMA((chips,)), DMA((chips,)), DMA((chips,)),
            DMA, DMA((3,)), DMA((2,)), DMA((chips - 1,)),
        ],
        compiler_params=pltpu.CompilerParams(collective_id=3, has_side_effects=True, vmem_limit_bytes=63 << 20),
        cost_estimate=pl.CostEstimate(flops=16 * group_rows * depth * width, bytes_accessed=10 * group_rows * depth, transcendentals=group_rows * width),
        name="feed",
    )(hidden_state, cotangent, gain, tokens, grads, both_w, down_w)


def rope_tables():
    half = HEAD_DIM // 2
    positions = jnp.arange(SEQ_LEN, dtype=jnp.int32).astype(jnp.float32)
    column = jnp.arange(half, dtype=jnp.int32)
    inverse = jnp.power(jnp.float32(rope_base), -2.0 * column.astype(jnp.float32) / HEAD_DIM)
    angle = positions[None, :] * inverse[:, None]
    return (jnp.cos(angle), jnp.sin(angle))


def make_body(mesh):
    chips, shards = mesh.shape["tp"] // 2, mesh.shape["fsdp"]

    def body(activations, gain_attn, w_query, w_key, w_value, w_out, gain_mlp, w_gate, w_up, w_down, cotangent):
        width = w_query.shape[1]
        full_out = lax.all_gather(w_out, "fsdp", axis=1, tiled=True)
        full_both = lax.all_gather(jnp.concatenate([w_gate, w_up], axis=1), "fsdp", axis=0, tiled=True)
        full_down = lax.all_gather(w_down, "fsdp", axis=1, tiled=True)
        gain_attn, gain_mlp = gain_attn[None, :], gain_mlp[None, :]
        seen_attn, w_qkv, qkv, keys_t, values_t, cosine, sine = project(
            chips, shards, activations, gain_attn, w_query, w_key, w_value, *rope_tables()
        )
        hidden_state, normed_mlp, mixed, totals, seen_grad = attend(chips, qkv, values_t, full_out, activations, cotangent, gain_mlp)
        hidden_grad, branch_grad, gain_part, inner, grad_both = feed(
            chips, hidden_state, cotangent, gain_mlp, normed_mlp, seen_grad, full_both, full_down
        )

        def over_fsdp(grad, dimension):
            return lax.psum_scatter(grad, "fsdp", scatter_dimension=dimension, tiled=True)

        grad_both = over_fsdp(grad_both, 0)
        down, _, qkv_grad, grad_down, grad_out = back(
            chips, shards, branch_grad, inner, seen_grad, full_down, full_out, qkv, keys_t, mixed, totals, cosine, sine
        )
        output = hidden_state + down
        grad_down = over_fsdp(grad_down, 1)
        input_part, grad_qkv, gain_sums = spread(chips, shards, qkv_grad, w_qkv, activations, gain_attn, gain_part, seen_attn)
        input_grad = hidden_grad + input_part
        grad_query, grad_key, grad_value = [grad_qkv[:, part * width : (part + 1) * width] for part in range(3)]
        hidden = w_gate.shape[1]
        grad_gate, grad_up = grad_both[:, :hidden].astype(jnp.float32), grad_both[:, hidden:].astype(jnp.float32)
        grad_down, grad_gate, grad_up = lax.optimization_barrier((grad_down, grad_gate, grad_up))
        grad_down = grad_down.astype(jnp.float32)
        return (
            output, input_grad, gain_sums[0], grad_query, grad_key, grad_value, grad_out, gain_sums[1],
            grad_gate, grad_up, grad_down,
        )

    return body


def solution(mesh):
    tokens = P(("fsdp", "tp"), None)
    column = P("fsdp", "tp")
    row = P("tp", "fsdp")
    in_specs = (tokens, P(), column, column, column, row, P(), column, column, row, tokens)
    out_specs = (tokens, tokens, P(), column, column, column, row, P(), column, column, row)
    return jax.shard_map(make_body(mesh), mesh=mesh, in_specs=in_specs, out_specs=out_specs, check_vma=False)
```

```python
import jax
import jax.numpy as jnp
from jax import lax
from jax.experimental import pallas as pl
from jax.experimental.pallas import tpu as pltpu
from jax.sharding import PartitionSpec as P

HEAD_DIM = 64
SEQ_LEN = 2048
LANES = 128
rope_base = 130000.0
norm_eps = 1e-05
masked_score = -1e30

NT = (((1,), (1,)), ((), ()))
NN = (((1,), (0,)), ((), ()))
TN = (((0,), (0,)), ((), ()))
MESH = pl.DeviceIdType.MESH
DMA = pltpu.SemaphoreType.DMA
ANYWHERE = pl.BlockSpec(memory_space=pl.ANY)
VMEM = pl.BlockSpec(memory_space=pltpu.VMEM)
low = jnp.bfloat16


def dot(left, right, dims=NN):
    return lax.dot_general(left, right, dims, preferred_element_type=jnp.float32)


def span(index, size):
    return pl.ds(pl.multiple_of(index * size, size), size)


def remote(source, target, send, receive, device):
    return pltpu.make_async_remote_copy(
        src_ref=source, dst_ref=target, send_sem=send, recv_sem=receive,
        device_id=device, device_id_type=MESH,
    )


def hello(device):
    pl.semaphore_signal(pltpu.get_barrier_semaphore(), inc=1, device_id=device, device_id_type=MESH)


class Line:
    def __init__(self, chips):
        self.chips = chips
        self.me = lax.axis_index("tp")
        self.chip, self.core = self.me // 2, self.me % 2
        self.partner = 2 * self.chip + 1 - self.core
        self.has_left, self.has_right = self.chip > 0, self.chip < chips - 1

    def greet(self, more=()):
        hello({"tp": self.partner})

        @pl.when(self.has_left)
        def _():
            hello({"tp": self.me - 2})

        @pl.when(self.has_right)
        def _():
            hello({"tp": self.me + 2})

        for device in more:
            hello(device)
        count = 1 + len(more) + jnp.where(self.has_left, 1, 0) + jnp.where(self.has_right, 1, 0)
        pl.semaphore_wait(pltpu.get_barrier_semaphore(), count)

    def target(self, step):
        after = self.chips - 1 - self.chip
        most, least = jnp.maximum(self.chip, after), jnp.minimum(self.chip, after)
        sign = jnp.where(after >= self.chip, 1, -1)
        late = step - (most - least)
        side = jnp.where(late % 2 == 0, sign, -sign)
        return jnp.where(late < 0, self.chip + sign * (most - step), self.chip + side * (least - late // 2))


    def fed(self, target):
        after, before = jnp.logical_and(target >= self.chip, self.has_left), jnp.logical_and(target <= self.chip, self.has_right)
        return jnp.logical_or(after, before)


class Gather:
    scratch = staticmethod(lambda chips: [DMA((2 * chips,)), DMA((chips,)), DMA((chips,)), DMA((chips,)), DMA])

    def __init__(self, line, own, out, received, right, left, across, local):
        self.line, self.own, self.out = line, own, out
        self.received, self.right, self.left, self.across, self.local = received, right, left, across, local
        self.rows = own.shape[0]

    def block(self, index):
        return self.out.at[span(index, self.rows)]

    def copy(self, source, sems, chip, device, mine):
        index = 2 * chip + self.line.core
        return remote(source if mine else self.block(index), self.block(index), sems.at[chip], self.received.at[index], {"tp": device})

    def keep(self):
        return pltpu.make_async_copy(self.own, self.block(self.line.me), self.local)

    def start(self):
        line = self.line
        self.keep().start()

        @pl.when(line.has_right)
        def _():
            self.copy(self.own, self.right, line.chip, line.me + 2, True).start()

        @pl.when(line.has_left)
        def _():
            self.copy(self.own, self.left, line.chip, line.me - 2, True).start()

        self.copy(self.own, self.across, line.chip, line.partner, True).start()

    def arrive(self, index):
        remote(self.own, self.block(index), self.right.at[0], self.received.at[index], {"tp": self.line.partner}).wait_recv()

    def arrive_across(self, chip):
        self.arrive(2 * chip + 1 - self.line.core)

    def step(self, distance):
        line = self.line
        before, after = line.chip - distance, line.chip + distance

        @pl.when(before >= 0)
        def _():
            self.arrive(2 * before + line.core)

            @pl.when(line.has_right)
            def _():
                self.copy(None, self.right, before, line.me + 2, False).start()

            self.copy(None, self.across, before, line.partner, False).start()

        @pl.when(after < line.chips)
        def _():
            self.arrive(2 * after + line.core)

            @pl.when(line.has_left)
            def _():
                self.copy(None, self.left, after, line.me - 2, False).start()

            self.copy(None, self.across, after, line.partner, False).start()

    def finish(self, arrivals):
        line = self.line
        if arrivals:
            self.keep().wait()
        for chip in range(line.chips):
            if arrivals:
                self.arrive_across(chip)
            self.copy(self.own, self.across, chip, line.partner, True).wait_send()

            @pl.when(jnp.logical_and(line.has_right, chip <= line.chip))
            def _():
                self.copy(self.own, self.right, chip, line.me + 2, True).wait_send()

            @pl.when(jnp.logical_and(line.has_left, chip >= line.chip))
            def _():
                self.copy(self.own, self.left, chip, line.me - 2, True).wait_send()


class Scatter:
    @staticmethod
    def scratch(chips, rows, depth):
        shares = min(chips, 4)
        return [
            pltpu.VMEM((2, 2 * rows, depth), low),
            pltpu.VMEM((shares, rows, depth), low),
            pltpu.VMEM((chips + 1, rows, depth), low),
            pltpu.VMEM((2, rows, depth), low),
            DMA((2,)), DMA((shares,)), DMA((2,)), DMA((chips + 1,)),
        ]

    def __init__(self, line, out, term, shares, lines, total, share_send, share_recv, line_send, line_recv):
        self.line, self.out = line, out
        self.term, self.shares, self.lines, self.total = term, shares, lines, total
        self.share_send, self.share_recv, self.line_send, self.line_recv = share_send, share_recv, line_send, line_recv
        self.rows = out.shape[0]

    def share(self, step):
        slot = step % self.shares.shape[0]
        source = self.term.at[step % 2, span(1 - self.line.core, self.rows)]
        return remote(source, self.shares.at[slot], self.share_send.at[step % 2], self.share_recv.at[slot], {"tp": self.line.partner})

    def mine(self, step):
        return self.term[step % 2, span(self.line.core, self.rows), :]

    def pass_on(self, step):
        line, target = self.line, self.line.target(step)
        onward = target > line.chip
        slot = jnp.where(onward, target, jnp.where(target == line.chip - 1, line.chips, target))
        device = jnp.where(onward, line.me + 2, line.me - 2)
        return remote(self.total.at[step % 2], self.lines.at[slot], self.line_send.at[step % 2], self.line_recv.at[slot], {"tp": device})

    def add(self, slot):
        remote(self.total.at[0], self.lines.at[slot], self.line_send.at[0], self.line_recv.at[slot], {"tp": self.line.partner}).wait_recv()
        self.out[...] += self.lines[slot].astype(jnp.float32)

    def free(self, step):
        @pl.when(step >= 2)
        def _():
            self.share(step - 2).wait_send()

    def step(self, step):
        line, target = self.line, self.line.target(step)
        self.share(step).wait_recv()
        self.out[...] = self.mine(step).astype(jnp.float32) + self.shares[step % self.shares.shape[0]].astype(jnp.float32)

        @pl.when(jnp.logical_and(target >= line.chip, line.has_left))
        def _():
            self.add(target)

        @pl.when(jnp.logical_and(target <= line.chip, line.has_right))
        def _():
            self.add(jnp.where(target == line.chip, line.chips, target))

        @pl.when(step < line.chips - 1)
        def _():
            @pl.when(step >= 2)
            def _():
                self.pass_on(step - 2).wait_send()

            self.total[step % 2] = self.out[...].astype(low)
            self.pass_on(step).start()

    def finish(self):
        chips = self.line.chips
        for step in range(max(0, chips - 3), chips - 1):
            self.pass_on(step).wait_send()
        for step in range(max(0, chips - 2), chips):
            self.share(step).wait_send()


NORM_ROWS = 64


def normed(value, gain):
    return value * lax.rsqrt(jnp.mean(value * value, axis=-1, keepdims=True) + norm_eps) * gain


def norm_back(value, gain, grad):
    scale = lax.rsqrt(jnp.mean(value * value, axis=-1, keepdims=True) + norm_eps)
    unit = value * scale
    scaled = grad * gain
    return scale * (scaled - unit * jnp.mean(scaled * unit, axis=-1, keepdims=True)), jnp.sum(grad * unit, axis=0, keepdims=True)


def by_rows(rows, work):
    def step(index, carry):
        work(span(index, NORM_ROWS))
        return carry

    lax.fori_loop(0, rows // NORM_ROWS, step, 0)


class HeldScatter(Scatter):
    @staticmethod
    def scratch(chips, rows, depth):
        return [pltpu.VMEM((2, rows, depth), low)] + Scatter.scratch(chips, rows, depth)[1:] + [DMA((2,))]

    def __init__(self, line, out, held, *refs):
        super().__init__(line, out, *refs[:-1])
        self.held, self.load_sem = held, refs[-1]

    def load(self, step):
        source = self.held.at[span(2 * self.line.target(step) + self.line.core, self.rows)]
        return pltpu.make_async_copy(source, self.term.at[step % 2], self.load_sem.at[step % 2])

    def share(self, step):
        slot = step % self.shares.shape[0]
        source = self.held.at[span(2 * self.line.target(step) + 1 - self.line.core, self.rows)]
        return remote(source, self.shares.at[slot], self.share_send.at[step % 2], self.share_recv.at[slot], {"tp": self.line.partner})

    def mine(self, step):
        self.load(step).wait()
        return self.term[step % 2]


class Loads:
    @staticmethod
    def scratch(*operands):
        return [pltpu.VMEM(a.shape, a.dtype) for a in operands] + [DMA((len(operands),))]

    def __init__(self, sources, refs):
        self.refs = refs[: len(sources)]
        self.copies = [pltpu.make_async_copy(source, ref, refs[-1].at[i]) for i, (source, ref) in enumerate(zip(sources, self.refs))]

    def start(self):
        for copy in self.copies:
            copy.start()

    def wait(self, *which):
        for i in which:
            self.copies[i].wait()


def turned(block, sign):
    half = HEAD_DIM // 2
    lane = lax.broadcasted_iota(jnp.int32, block.shape, 1)
    width = block.shape[1]
    up = pltpu.roll(block, width - half, 1)
    down = pltpu.roll(block, half, 1)
    return jnp.where(lane % HEAD_DIM < half, -sign * up, sign * down)


def widened(table, width):
    return table if table.shape[1] == width else jnp.concatenate([table] * (width // table.shape[1]), axis=1)


def only_head(block, head):
    lane = lax.broadcasted_iota(jnp.int32, block.shape, 1)
    return jnp.where(lane // HEAD_DIM == head, block, jnp.zeros_like(block))


def causal(tile):
    key = lax.broadcasted_iota(jnp.int32, tile.shape, 0)
    query = lax.broadcasted_iota(jnp.int32, tile.shape, 1)
    return jnp.where(key <= query, tile, masked_score)


def over_keys(chunk, rows, visit):
    start = chunk * rows
    first = start // SEQ_LEN * SEQ_LEN

    def step(index, carry):
        visit(pl.multiple_of(first + index * rows, rows), False)
        return carry

    lax.fori_loop(0, (start - first) // rows, step, 0)
    visit(pl.multiple_of(start, rows), True)


def project_kernel(
    chips, shards,
    activations, gain, w_query, w_key, w_value, cosine_t, sine_t, w_gate, w_up,
    tokens_out, weight_out, qkv_out, keys_out, values_out, cosine_out, sine_out, both_out,
    weight, qkv, keys_t, values_t, cosine, sine, both, tokens, chunks,
    chunk_sem, weight_send, weight_recv, weight_keep, table_sem, both_sem, store_sem, *gather_sems,
):
    line = Line(chips)
    rows = tokens.shape[0]
    pair = 2 * rows
    depth, width = w_query.shape
    shard = lax.axis_index("fsdp")
    others = [(shard + ahead) % shards for ahead in range(1, shards)]
    gather = Gather(line, tokens, tokens_out, *gather_sems)
    parts = (w_query, w_key, w_value)

    def place(part):
        return weight.at[span(shard, depth), pl.ds(part * width, width)]

    def give(ahead, part):
        return remote(parts[part], place(part), weight_send.at[ahead, part], weight_recv.at[ahead, part], {"fsdp": others[ahead]})

    def keep(part):
        return pltpu.make_async_copy(parts[part], place(part), weight_keep.at[part])

    hidden = w_gate.shape[1]
    joins = [
        pltpu.make_async_copy(source, both.at[:, pl.ds(side * hidden, hidden)], both_sem.at[side])
        for side, source in enumerate((w_gate, w_up))
    ]
    joined = pltpu.make_async_copy(both, both_out, both_sem.at[2])
    tables = [
        pltpu.make_async_copy(source, out, table_sem.at[i])
        for i, (source, out) in enumerate(((cosine, cosine_out), (sine, sine_out), (weight, weight_out)))
    ]

    def stores(chip):
        here = span(chip, pair)
        return [
            pltpu.make_async_copy(qkv.at[here], qkv_out.at[here], store_sem.at[0, chip]),
            pltpu.make_async_copy(keys_t.at[:, here], keys_out.at[:, here], store_sem.at[1, chip]),
            pltpu.make_async_copy(values_t.at[:, here], values_out.at[:, here], store_sem.at[2, chip]),
        ]

    def norm(here):
        tokens[here, :] = normed(activations[here, :], gain[...]).astype(low)

    by_rows(rows, norm)
    line.greet([{"fsdp": other} for other in others])
    gather.start()
    for part in range(3):
        keep(part).start()
        for ahead in range(shards - 1):
            give(ahead, part).start()
    for table, table_t in ((cosine, cosine_t), (sine, sine_t)):
        turn = table_t[...].T
        table[...] = jnp.concatenate([turn] * (LANES // turn.shape[1]), axis=1)
    for copy in joins + tables[:2]:
        copy.start()

    def project(chip):
        @pl.when(jnp.logical_and(chip >= 0, chip < chips))
        def _():
            gather.arrive_across(chip)
            load = pltpu.make_async_copy(tokens_out.at[span(chip, pair)], chunks, chunk_sem)
            load.start()
            load.wait()
            here = span(chip, pair)
            table = span(chip % (SEQ_LEN // pair), pair)
            for part in range(3):
                columns = pl.ds(part * width, width)
                block = dot(chunks[...], weight[:, columns])
                if part < 2:
                    block = block * widened(cosine[table, :], width) + turned(block, 1.0) * widened(sine[table, :], width)
                qkv[here, columns] = block.astype(low)
                if part:
                    (keys_t, values_t)[part - 1][:, here] = block.T.astype(low)
            for copy in stores(chip):
                copy.start()

    def step(index, carry):
        @pl.when(jnp.logical_and(index >= 1, index < chips))
        def _():
            gather.step(index)

        @pl.when(index == 1)
        def _():
            gather.keep().wait()
            for part in range(3):
                keep(part).wait()
                for ahead in range(shards - 1):
                    give(ahead, part).wait_recv()
            tables[2].start()
            for copy in joins:
                copy.wait()
            joined.start()

        def side(which, carry):
            distance = index - 1

            @pl.when(jnp.logical_and(distance >= 0, jnp.logical_or(which == 0, distance > 0)))
            def _():
                project(jnp.where(which == 0, line.chip - distance, line.chip + distance))

            return carry

        lax.fori_loop(0, 2, side, 0)
        return carry

    lax.fori_loop(0, chips + 1, step, 0)
    gather.finish(False)
    for part in range(3):
        for ahead in range(shards - 1):
            give(ahead, part).wait_send()
    joined.wait()
    for copy in tables:
        copy.wait()
    for chip in range(chips):
        for copy in stores(chip):
            copy.wait()


def project(chips, shards, activations, gain, w_query, w_key, w_value, cosine_t, sine_t, w_gate, w_up):
    rows, depth = activations.shape
    group_rows = 2 * chips * rows
    width = w_query.shape[1]
    shape = jax.ShapeDtypeStruct
    held = [
        shape((depth, 3 * width), low),
        shape((group_rows, 3 * width), low),
        shape((width, group_rows), low),
        shape((width, group_rows), low),
        shape((SEQ_LEN, LANES), jnp.float32),
        shape((SEQ_LEN, LANES), jnp.float32),
        shape((w_gate.shape[0], 2 * w_gate.shape[1]), low),
    ]
    return pl.pallas_call(
        lambda *refs: project_kernel(chips, shards, *refs),
        in_specs=[VMEM] * 7 + [ANYWHERE] * 2,
        out_specs=[ANYWHERE] * 8,
        out_shape=[shape((group_rows, depth), low)] + held,
        scratch_shapes=[pltpu.VMEM(a.shape, a.dtype) for a in held] + [
            pltpu.VMEM((rows, depth), low),
            pltpu.VMEM((2 * rows, depth), low),
            DMA, DMA((shards - 1, 3)), DMA((shards - 1, 3)), DMA((3,)), DMA((3,)), DMA((3,)), DMA((3, chips)),
        ] + Gather.scratch(chips),
        compiler_params=pltpu.CompilerParams(collective_id=1, has_side_effects=True, vmem_limit_bytes=63 << 20),
        cost_estimate=pl.CostEstimate(flops=6 * group_rows * depth * width, bytes_accessed=4 * group_rows * depth, transcendentals=0),
        name="project",
    )(activations, gain, w_query, w_key, w_value, cosine_t, sine_t, w_gate, w_up)


def attend_chunk(chunk, rows, qkv, values_t, heads_ref, acc, out, top_ref, sum_ref):
    width = acc.shape[0]
    heads = width // HEAD_DIM
    scaled = qkv[span(chunk, rows), pl.ds(0, width)] * low(HEAD_DIM**-0.5)
    for head in range(heads):
        heads_ref[head] = only_head(scaled, head)
    acc[...] = jnp.zeros_like(acc)
    top_ref[...] = jnp.full_like(top_ref, masked_score)
    sum_ref[...] = jnp.zeros_like(sum_ref)

    def visit(offset, diagonal):
        key_block = qkv[pl.ds(offset, rows), pl.ds(width, width)]
        for head in range(heads):
            feature = pl.ds(head * HEAD_DIM, HEAD_DIM)
            one = pl.ds(head, 1)
            scores = dot(key_block, heads_ref[head], NT)
            if diagonal:
                scores = causal(scores)
            old = top_ref[one, :]
            top = jnp.maximum(old, jnp.max(scores, axis=0, keepdims=True))
            shrink = jnp.exp(old - top)
            weights = jnp.exp(scores - top)
            top_ref[one, :] = top
            sum_ref[one, :] = sum_ref[one, :] * shrink + jnp.sum(weights, axis=0, keepdims=True)
            acc[feature, :] = acc[feature, :] * shrink + dot(values_t[feature, pl.ds(offset, rows)], weights.astype(low))

    over_keys(chunk, rows, visit)
    for head in range(heads):
        feature = pl.ds(head * HEAD_DIM, HEAD_DIM)
        acc[feature, :] = acc[feature, :] / sum_ref[pl.ds(head, 1), :]
    out[...] = acc[...].T.astype(low)


def attend_kernel(
    chips,
    cotangent, gain, *refs,
):
    sources, (hidden, tokens, mixed, totals, grads_out) = refs[:4], refs[4:9]
    loads = Loads(sources, refs[9:14])
    qkv, values_t, w_out, activations = loads.refs
    heads_ref, acc, out, top_ref, sum_ref, grads = refs[14:20]
    sems = refs[20:]
    loads.start()
    line = Line(chips)
    rows, depth = hidden.shape
    pair = 2 * rows
    scatter = Scatter(line, hidden, *sems[:8])
    grads[...] = cotangent[...].astype(low)
    gather = Gather(line, grads, grads_out, *sems[8:])
    line.greet()
    gather.start()
    loads.wait(0, 1, 2, 3)

    def step(index, carry):
        work = jnp.where(index == chips, chips - 1, index)

        @pl.when(jnp.logical_or(index < chips - 1, index == chips))
        def _():
            chunk = line.target(work)
            attend_chunk(chunk, pair, qkv, values_t, heads_ref, acc, out, top_ref, sum_ref)
            mixed[span(chunk, pair), :] = out[...]
            totals[:, span(chunk, pair)] = top_ref[...] + jnp.log(sum_ref[...])
            scatter.free(work)

            def tile(place, carry):
                columns = span(place, 512)
                scatter.term[work % 2, :, columns] = dot(out[...], w_out[:, columns]).astype(low)
                return carry

            lax.fori_loop(0, depth // 512, tile, 0)
            scatter.share(work).start()

        @pl.when(jnp.logical_and(index >= 1, index < chips))
        def _():
            gather.step(index)

        @pl.when(index >= 1)
        def _():
            scatter.step(index - 1)

        return carry

    lax.fori_loop(0, chips + 1, step, 0)

    def norm(here):
        state = activations[here, :] + hidden[here, :]
        hidden[here, :] = state
        tokens[here, :] = normed(state, gain[...]).astype(low)

    by_rows(rows, norm)
    scatter.finish()
    gather.finish(True)


def attend(chips, qkv, values_t, w_out, activations, cotangent, gain):
    rows, depth = activations.shape
    pair = 2 * rows
    group_rows = chips * pair
    width = w_out.shape[0]
    heads = width // HEAD_DIM
    shape = jax.ShapeDtypeStruct
    return pl.pallas_call(
        lambda *refs: attend_kernel(chips, *refs),
        in_specs=[VMEM] * 2 + [ANYWHERE] * 4,
        out_specs=[VMEM] * 4 + [ANYWHERE],
        out_shape=[
            shape((rows, depth), jnp.float32),
            shape((rows, depth), low),
            shape((group_rows, width), low),
            shape((heads, group_rows), jnp.float32),
            shape((group_rows, depth), low),
        ],
        scratch_shapes=Loads.scratch(qkv, values_t, w_out, activations) + [
            pltpu.VMEM((heads, pair, width), low),
            pltpu.VMEM((width, pair), jnp.float32),
            pltpu.VMEM((pair, width), low),
            pltpu.VMEM((heads, pair), jnp.float32),
            pltpu.VMEM((heads, pair), jnp.float32),
            pltpu.VMEM((rows, depth), low),
        ] + Scatter.scratch(chips, rows, depth) + Gather.scratch(chips),
        compiler_params=pltpu.CompilerParams(collective_id=2, has_side_effects=True, vmem_limit_bytes=63 << 20),
        cost_estimate=pl.CostEstimate(flops=2 * group_rows * (SEQ_LEN + depth) * width, bytes_accessed=4 * group_rows * depth, transcendentals=group_rows * SEQ_LEN * heads // 2),
        name="attend",
    )(cotangent, gain, qkv, values_t, w_out, activations)


def back_chunk(chunk, rows, grad, qkv, keys_t, mixed, totals, dkey, dvalue, heads_ref, grads_ref, acc, inner_ref):
    width = acc.shape[0]
    heads = width // HEAD_DIM
    here = span(chunk, rows)
    scaled = qkv[here, pl.ds(0, width)] * low(HEAD_DIM**-0.5)
    product = grad.astype(jnp.float32) * mixed[here, :].astype(jnp.float32)
    shape = (inner_ref.shape[0], width)
    pick = (lax.broadcasted_iota(jnp.int32, shape, 1) // HEAD_DIM == lax.broadcasted_iota(jnp.int32, shape, 0)).astype(jnp.float32)
    inner_ref[...] = lax.dot_general(pick, product, NT, precision=lax.Precision.HIGHEST, preferred_element_type=jnp.float32)
    for head in range(heads):
        heads_ref[head] = only_head(scaled, head)
        grads_ref[head] = only_head(grad, head)
    acc[...] = jnp.zeros_like(acc)

    def visit(offset, diagonal):
        keys = pl.ds(offset, rows)
        key_block = qkv[keys, pl.ds(width, width)]
        value_block = qkv[keys, pl.ds(2 * width, width)]
        key_sum, value_sum = dkey[keys, :], dvalue[keys, :]
        for head in range(heads):
            feature = pl.ds(head * HEAD_DIM, HEAD_DIM)
            scores = dot(key_block, heads_ref[head], NT)
            if diagonal:
                scores = causal(scores)
            probs = jnp.exp(scores - totals[pl.ds(head, 1), here])
            dprobs = dot(value_block, grads_ref[head], NT)
            dscores = (probs * (dprobs - inner_ref[pl.ds(head, 1), :])).astype(low)
            value_sum = value_sum + dot(probs.astype(low), grads_ref[head])
            key_sum = key_sum + dot(dscores, heads_ref[head])
            acc[feature, :] = acc[feature, :] + dot(keys_t[feature, keys], dscores)
        dkey[keys, :] = key_sum
        dvalue[keys, :] = value_sum

    over_keys(chunk, rows, visit)


def back_kernel(
    chips, shards,
    branch, terms, inner, grads, *refs,
):
    sources, (down, branch_out, qkv_grad, grad_down, grad_out) = refs[:7], refs[7:12]
    loads = Loads(sources, refs[12:20])
    w_out, qkv, keys_t, mixed, totals, cosine, sine = loads.refs
    inner_chunk, grad_chunk, down_sum, down_tile, out_sum, out_stage, out_from, branch_chunk, dkey, dvalue = refs[20:30]
    heads_ref, grads_ref, acc, inner_ref, inner_sem, grad_sem, branch_sem, tile_sem, out_send, out_recv = refs[30:40]
    sems = refs[40:]
    line = Line(chips)
    rows, depth = down.shape
    pair = 2 * rows
    width = w_out.shape[0]
    scatter = HeldScatter(line, down, terms, *sems[:9])
    gather = Gather(line, branch, branch_out, *sems[9:])

    def fetch(step):
        return pltpu.make_async_copy(inner.at[span(line.target(step), pair)], inner_chunk, inner_sem)

    def fetch_grad(step):
        return pltpu.make_async_copy(grads.at[span(line.target(step), pair)], grad_chunk, grad_sem)

    shard = lax.axis_index("fsdp")
    columns_out = depth // shards
    others = [(shard + ahead) % shards for ahead in range(1, shards)]

    def give(turn):
        return remote(out_stage.at[turn], out_from.at[turn], out_send.at[turn], out_recv.at[turn], {"fsdp": others[turn]})

    def keep_tile(place):
        return pltpu.make_async_copy(down_tile, grad_down.at[span(place, 256)], tile_sem)

    loads.start()
    line.greet([{"fsdp": other} for other in others])
    gather.start()
    out_sum[...] = jnp.zeros_like(out_sum)
    dkey[...] = jnp.zeros_like(dkey)
    dvalue[...] = jnp.zeros_like(dvalue)

    def unrotated(block, chunk):
        table = span(chunk % (SEQ_LEN // pair), pair)
        return (block * widened(cosine[table, :], width) + turned(block * widened(sine[table, :], width), -1.0)).astype(low)

    def attention(chunk):
        gather.arrive_across(chunk)
        copy = pltpu.make_async_copy(branch_out.at[span(chunk, pair)], branch_chunk, branch_sem)
        copy.start()
        copy.wait()
        out_sum[...] += dot(mixed[span(chunk, pair), :], branch_chunk[...], TN)
        grad = dot(branch_chunk[...], w_out[...], NT).astype(low)
        back_chunk(chunk, pair, grad, qkv, keys_t, mixed, totals, dkey, dvalue, heads_ref, grads_ref, acc, inner_ref)
        qkv_grad[span(chunk, pair), pl.ds(0, width)] = unrotated(acc[...].T * HEAD_DIM**-0.5, chunk)

    def close():
        def part(chunk, carry):
            here = span(chunk, pair)
            qkv_grad[here, pl.ds(width, width)] = unrotated(dkey[here, :], chunk)
            qkv_grad[here, pl.ds(2 * width, width)] = dvalue[here, :].astype(low)
            return carry

        lax.fori_loop(0, chips, part, 0)

    def step(index, carry):
        @pl.when(index == 0)
        def _():
            loads.wait(*range(7))
            gather.keep().wait()

        @pl.when(index < chips)
        def _():
            fetch(index).start()
            fetch_grad(index).start()
            scatter.free(index)
            scatter.load(index).start()
            scatter.share(index).start()

        @pl.when(jnp.logical_and(index >= 1, index < chips))
        def _():
            gather.step(index)

        @pl.when(index == chips)
        def _():
            for turn in range(shards - 1):
                out_stage[turn] = out_sum[:, span(others[turn], columns_out)].astype(low)
                give(turn).start()
            close()

        def phase(which, carry):
            done = jnp.maximum(index - 1, 0)
            late = line.fed(line.target(done))
            turn = jnp.logical_or(jnp.logical_and(which == 0, jnp.logical_not(late)), jnp.logical_and(which == 3, late))

            @pl.when(jnp.logical_and(index >= 1, turn))
            def _():
                scatter.step(done)

            chunk = jnp.where(which == 1, line.chip - index, line.chip + index)
            there = jnp.logical_and(chunk >= 0, chunk < chips)
            turn = jnp.logical_or(which == 1, jnp.logical_and(which == 2, index > 0))

            @pl.when(jnp.logical_and(there, turn))
            def _():
                attention(chunk)

            return carry

        lax.fori_loop(0, 4, phase, 0)

        @pl.when(index < chips)
        def _():
            fetch(index).wait()
            fetch_grad(index).wait()

            def tile(place, carry):
                here = span(place, 256)
                part = dot(inner_chunk[:, here], grad_chunk[...], TN)

                @pl.when(index == 0)
                def _():
                    down_sum[here, :] = part

                @pl.when(index > 0)
                def _():
                    down_sum[here, :] += part

                @pl.when(index == chips - 1)
                def _():
                    @pl.when(place > 0)
                    def _():
                        keep_tile(place - 1).wait()

                    down_tile[...] = down_sum[here, :].astype(low)
                    keep_tile(place).start()

                return carry

            lax.fori_loop(0, down_sum.shape[0] // 256, tile, 0)

        return carry

    lax.fori_loop(0, chips + 1, step, 0)
    total = out_sum[:, span(shard, columns_out)]
    for turn in range(shards - 1):
        give(turn).wait_recv()
        total = total + out_from[turn].astype(jnp.float32)
    grad_out[...] = total
    for turn in range(shards - 1):
        give(turn).wait_send()
    keep_tile(down_sum.shape[0] // 256 - 1).wait()
    scatter.finish()
    gather.finish(False)


def back(chips, shards, branch, terms, inner, grads, w_out, qkv, keys_t, mixed, totals, cosine, sine):
    rows, depth = branch.shape
    pair = 2 * rows
    group_rows = chips * pair
    width = w_out.shape[0]
    hidden = inner.shape[1]
    heads = width // HEAD_DIM
    shape = jax.ShapeDtypeStruct
    held = (w_out, qkv, keys_t, mixed, totals, cosine, sine)
    return pl.pallas_call(
        lambda *refs: back_kernel(chips, shards, *refs),
        in_specs=[VMEM] + [ANYWHERE] * 10,
        out_specs=[VMEM, ANYWHERE, VMEM, ANYWHERE, VMEM],
        out_shape=[
            shape((rows, depth), jnp.float32),
            shape((group_rows, depth), low),
            shape((group_rows, 3 * width), low),
            shape((hidden, depth), low),
            shape((width, depth // shards), jnp.float32),
        ],
        scratch_shapes=Loads.scratch(*held) + [
            pltpu.VMEM((pair, hidden), low),
            pltpu.VMEM((pair, depth), low),
            pltpu.VMEM((hidden, depth), jnp.float32),
            pltpu.VMEM((256, depth), low),
            pltpu.VMEM((width, depth), jnp.float32),
            pltpu.VMEM((shards - 1, width, depth // shards), low),
            pltpu.VMEM((shards - 1, width, depth // shards), low),
            pltpu.VMEM((pair, depth), low),
            pltpu.VMEM((group_rows, width), jnp.float32),
            pltpu.VMEM((group_rows, width), jnp.float32),
            pltpu.VMEM((heads, pair, width), low),
            pltpu.VMEM((heads, pair, width), low),
            pltpu.VMEM((width, pair), jnp.float32),
            pltpu.VMEM((8, pair), jnp.float32),
            DMA, DMA, DMA, DMA, DMA((shards - 1,)), DMA((shards - 1,)),
        ] + HeldScatter.scratch(chips, rows, depth) + Gather.scratch(chips),
        compiler_params=pltpu.CompilerParams(collective_id=4, has_side_effects=True, vmem_limit_bytes=67043328),
        cost_estimate=pl.CostEstimate(flops=1 << 20, bytes_accessed=1 << 20, transcendentals=0),
        name="back",
    )(branch, terms, inner, grads, *held)


def spread_kernel(
    chips, shards,
    qkv_grad, weight, activations, gain, gain_part, attn_tokens,
    input_part, grad_qkv, gain_sum,
    attn_cols, qkv_stage, qkv_from, gains, gains_tp, gains_fsdp,
    attn_sem, qkv_send, qkv_recv, tp_send, tp_recv, fsdp_send, fsdp_recv, *sems,
):
    line = Line(chips)
    size = 2 * chips
    rows, depth = input_part.shape
    pair = 2 * rows
    shard = lax.axis_index("fsdp")
    columns = depth // shards
    scatter = Scatter(line, input_part, *sems)

    def peer(turn):
        return (shard + 1 + turn) % shards

    def fetch(turn):
        return pltpu.make_async_copy(attn_tokens.at[:, span(peer(turn), columns)], attn_cols.at[turn % 2], attn_sem.at[turn % 2])

    def give(turn):
        return remote(qkv_stage.at[turn], qkv_from.at[turn], qkv_send.at[turn], qkv_recv.at[turn], {"fsdp": peer(turn)})

    def tell_tp(ahead):
        return remote(gains, gains_tp.at[line.me], tp_send.at[ahead - 1], tp_recv.at[line.me], {"tp": (line.me + ahead) % size})

    def tell_fsdp(ahead):
        return remote(gains, gains_fsdp.at[shard], fsdp_send.at[ahead - 1], fsdp_recv.at[shard], {"fsdp": (shard + ahead) % shards})

    fetch(0).start()
    for ahead in range(1, size):
        hello({"tp": (line.me + ahead) % size})
    for ahead in range(1, shards):
        hello({"fsdp": (shard + ahead) % shards})
    pl.semaphore_wait(pltpu.get_barrier_semaphore(), size - 1 + shards - 1)

    def weights(turn, carry):
        @pl.when(turn < shards - 1)
        def _():
            fetch(turn + 1).start()

        fetch(turn).wait()
        part = dot(attn_cols[turn % 2], qkv_grad[...], TN)

        @pl.when(turn < shards - 1)
        def _():
            qkv_stage[turn] = part.astype(low)
            give(turn).start()

        @pl.when(turn == shards - 1)
        def _():
            grad_qkv[...] = part

        return carry

    def step(index, carry):
        @pl.when(index < chips)
        def _():
            here = span(line.target(index), pair)
            scatter.free(index)

            def tile(place, carry):
                there = span(place, 512)
                scatter.term[index % 2, :, there] = dot(qkv_grad[here, :], weight[there, :], NT).astype(low)
                return carry

            lax.fori_loop(0, depth // 512, tile, 0)
            scatter.share(index).start()

        def phase(which, carry):
            done = jnp.maximum(index - 1, 0)
            late = line.fed(line.target(done))
            turn = jnp.logical_or(jnp.logical_and(which == 0, jnp.logical_not(late)), jnp.logical_and(which == 2, late))

            @pl.when(jnp.logical_and(index >= 1, turn))
            def _():
                scatter.step(done)

            @pl.when(jnp.logical_and(which == 1, index < 2))
            def _():
                lax.fori_loop(index, jnp.where(index == 0, 1, shards), weights, 0)

            return carry

        lax.fori_loop(0, 3, phase, 0)
        return carry

    lax.fori_loop(0, chips + 1, step, 0)
    for turn in range(shards - 1):
        give(turn).wait_recv()
        grad_qkv[...] += qkv_from[turn].astype(jnp.float32)
    gains[0:1, :] = jnp.zeros((1, depth), jnp.float32)
    gains[1:2, :] = gain_part[...]

    def norm(here):
        part, grad = norm_back(activations[here, :], gain[...], input_part[here, :])
        input_part[here, :] = part
        gains[0:1, :] += grad

    by_rows(rows, norm)

    gains_tp[line.me] = gains[...]
    for ahead in range(1, size):
        tell_tp(ahead).start()
    for ahead in range(1, size):
        source = (line.me + ahead) % size
        remote(gains, gains_tp.at[source], tp_send.at[0], tp_recv.at[source], {"tp": source}).wait_recv()
    total = gains_tp[0]
    for source in range(1, size):
        total = total + gains_tp[source]
    for ahead in range(1, size):
        tell_tp(ahead).wait_send()
    gains[...] = total
    gains_fsdp[shard] = total
    for ahead in range(1, shards):
        tell_fsdp(ahead).start()
    for ahead in range(1, shards):
        source = (shard + ahead) % shards
        remote(gains, gains_fsdp.at[source], fsdp_send.at[0], fsdp_recv.at[source], {"fsdp": source}).wait_recv()
    total = gains_fsdp[0]
    for source in range(1, shards):
        total = total + gains_fsdp[source]
    gain_sum[...] = total
    for ahead in range(1, shards):
        tell_fsdp(ahead).wait_send()
    for turn in range(shards - 1):
        give(turn).wait_send()
    scatter.finish()


def spread(chips, shards, qkv_grad, weight, activations, gain, gain_part, attn_tokens):
    group_rows = qkv_grad.shape[0]
    rows, depth = activations.shape
    width = qkv_grad.shape[1] // 3
    columns = depth // shards
    size = 2 * chips
    shape = jax.ShapeDtypeStruct
    return pl.pallas_call(
        lambda *refs: spread_kernel(chips, shards, *refs),
        in_specs=[VMEM] * 5 + [ANYWHERE],
        out_specs=[VMEM] * 3,
        out_shape=[
            shape((rows, depth), jnp.float32),
            shape((columns, 3 * width), jnp.float32),
            shape((2, depth), jnp.float32),
        ],
        scratch_shapes=[
            pltpu.VMEM((2, group_rows, columns), low),
            pltpu.VMEM((shards - 1, columns, 3 * width), low),
            pltpu.VMEM((shards - 1, columns, 3 * width), low),
            pltpu.VMEM((2, depth), jnp.float32),
            pltpu.VMEM((size, 2, depth), jnp.float32),
            pltpu.VMEM((shards, 2, depth), jnp.float32),
            DMA((2,)), DMA((shards - 1,)), DMA((shards - 1,)),
            DMA((size - 1,)), DMA((size,)), DMA((shards - 1,)), DMA((shards,)),
        ] + Scatter.scratch(chips, rows, depth),
        compiler_params=pltpu.CompilerParams(collective_id=5, has_side_effects=True, vmem_limit_bytes=63 << 20),
        cost_estimate=pl.CostEstimate(flops=1 << 20, bytes_accessed=1 << 20, transcendentals=0),
        name="spread",
    )(qkv_grad, weight, activations, gain, gain_part, attn_tokens)


def chip_at(place, chips):
    return jnp.where(2 * place < chips, 2 * place, 2 * (chips - 1 - place) + 1)


def place_of(chip, chips):
    return jnp.where(chip % 2 == 0, chip // 2, chips - 1 - chip // 2)


def feed_kernel(
    chips,
    gain, hidden_hbm, cotangent_hbm, tokens, grads_hbm, both_hbm, down_hbm,
    hidden_grad, branch, gain_part, inner_out, grad_both, down_out,
    hidden_state, cotangent, state_sem, down_tile, down_sem, tokens_all, gate_w, up_w, down_w, grads, inner, gate_grad, up_grad, term, from_core, from_ring, total, tile_gate, tile_up,
    load_sem, own_sem, grad_sem, store_sem, tile_sem,
    ring_send, ring_recv, core_send, core_recv, share_send, share_recv, total_send, total_recv,
):
    rows, depth = hidden_grad.shape
    pair = 2 * rows
    width = gate_w.shape[1]
    me = lax.axis_index("tp")
    chip, core = me // 2, me % 2
    place = place_of(chip, chips)
    following = {"tp": 2 * chip_at((place + 1) % chips, chips) + core}
    before = {"tp": 2 * chip_at((place + chips - 1) % chips, chips) + core}
    partner = {"tp": 2 * chip + 1 - core}

    loads = [pltpu.make_async_copy(a, b, load_sem.at[i]) for i, (a, b) in enumerate(((both_hbm.at[:, pl.ds(0, width)], gate_w), (both_hbm.at[:, pl.ds(width, width)], up_w), (down_hbm, down_w)))]
    own = pltpu.make_async_copy(tokens, tokens_all.at[span(me, rows)], own_sem)
    states = Loads((hidden_hbm, cotangent_hbm), (hidden_state, cotangent, state_sem))

    def source(slot):
        return chip_at((place + chips - slot) % chips, chips)

    def fetch(slot):
        return pltpu.make_async_copy(grads_hbm.at[span(source(slot), pair)], grads.at[slot % 2], grad_sem.at[slot % 2])

    def block(slot):
        return tokens_all.at[span(2 * source(slot) + core, rows)]

    def to_ring(slot):
        return remote(block(slot), block(slot), ring_send.at[slot], ring_recv.at[slot], following)

    def to_core(slot):
        return remote(block(slot), block(slot), core_send.at[slot], core_recv.at[slot], partner)

    def store(slot):
        return pltpu.make_async_copy(inner.at[slot], inner_out.at[span(source(slot), pair)], store_sem.at[slot])

    def keep_down(slot, tile):
        there = down_out.at[span(source(slot), pair), span(tile, 256)]
        return pltpu.make_async_copy(down_tile.at[tile % 2], there, down_sem.at[tile % 2])

    def down_term(slot, carry):
        def tile(index, carry):
            @pl.when(index > 1)
            def _():
                keep_down(slot, index - 2).wait()

            down_tile[index % 2] = dot(inner[slot], down_w[:, span(index, 256)]).astype(low)
            keep_down(slot, index).start()
            return carry

        lax.fori_loop(0, depth // 256, tile, 0)
        for index in range(depth // 256 - 2, depth // 256):
            keep_down(slot, index).wait()
        return carry

    def share(slot):
        place = jnp.where(slot == 0, 0, 1 + slot % 2)
        return remote(term.at[span(1 - core, rows)], from_core.at[place], share_send, share_recv.at[place], partner)

    def pass_on(slot):
        return remote(total.at[slot % 2], from_ring.at[slot - 1], total_send.at[slot % 2], total_recv.at[slot - 1], following)

    own.start()
    fetch(0).start()
    for load in loads:
        load.start()
    own.wait()
    for device in (following, before, partner):
        hello(device)
    pl.semaphore_wait(pltpu.get_barrier_semaphore(), 3)

    def step(slot, carry):
        here = slot % 2
        wide_rows = span(source(slot), pair)
        mine = span(core, rows)

        @pl.when(slot > 0)
        def _():
            to_ring(slot - 1).wait_recv()

        @pl.when(slot < chips - 1)
        def _():
            to_ring(slot).start()
            fetch(slot + 1).start()

        to_core(slot).start()

        @pl.when(slot == 0)
        def _():
            for load in loads:
                load.wait()

        @pl.when(slot == 1)
        def _():
            states.start()

        to_core(slot).wait_recv()
        fetch(slot).wait()

        def narrow(tile, carry):
            columns = span(tile, 256)
            token = tokens_all[wide_rows, :]
            gate = dot(token, gate_w[:, columns])
            up = dot(token, up_w[:, columns])
            grad = dot(grads[here], down_w[columns, :], NT)
            squash = jax.nn.sigmoid(gate)
            act = gate * squash
            inner[slot, :, columns] = (act * up).astype(low)
            up_grad[wide_rows, columns] = (grad * act).astype(low)
            gate_grad[wide_rows, columns] = (grad * up * squash * (1.0 + gate * (1.0 - squash))).astype(low)
            return carry

        lax.fori_loop(0, width // 256, narrow, 0)
        store(slot).start()

        @pl.when(slot > 0)
        def _():
            share(slot - 1).wait_send()

        def wide(tile, carry):
            columns = span(tile, 256)
            part = dot(gate_grad[wide_rows, :], gate_w[columns, :], NT) + dot(up_grad[wide_rows, :], up_w[columns, :], NT)
            term[:, columns] = part.astype(low)
            return carry

        lax.fori_loop(0, depth // 256, wide, 0)
        share(slot).start()

        @pl.when(slot == 0)
        def _():
            hidden_grad[...] = term[mine, :].astype(jnp.float32)

        middle = jnp.logical_and(slot >= 2, slot < chips - 1)
        lax.fori_loop(jnp.where(slot == 2, 0, slot), jnp.where(middle, slot + 1, 0), down_term, 0)

        @pl.when(slot > 0)
        def _():
            share(slot).wait_recv()

            @pl.when(slot > 2)
            def _():
                pass_on(slot - 2).wait_send()

            @pl.when(slot == 1)
            def _():
                total[here] = (term[mine, :].astype(jnp.float32) + from_core[1 + here].astype(jnp.float32)).astype(low)

            @pl.when(slot > 1)
            def _():
                pass_on(slot - 1).wait_recv()
                total[here] = (term[mine, :].astype(jnp.float32) + from_core[1 + here].astype(jnp.float32) + from_ring[slot - 2].astype(jnp.float32)).astype(low)

            pass_on(slot).start()

        return carry

    lax.fori_loop(0, chips, step, 0)

    def tiles(index):
        there = span(index, 256)
        return (
            pltpu.make_async_copy(tile_gate.at[index % 2], grad_both.at[there, pl.ds(0, width)], tile_sem.at[0, index % 2]),
            pltpu.make_async_copy(tile_up.at[index % 2], grad_both.at[there, pl.ds(width, width)], tile_sem.at[1, index % 2]),
        )

    def weights(index, carry):
        @pl.when(index > 1)
        def _():
            for copy in tiles(index - 2):
                copy.wait()

        token = tokens_all[:, span(index, 256)]
        tile_gate[index % 2] = dot(token, gate_grad[...], TN).astype(low)
        tile_up[index % 2] = dot(token, up_grad[...], TN).astype(low)
        for copy in tiles(index):
            copy.start()
        return carry

    lax.fori_loop(0 if chips < 4 else chips - 1, chips, down_term, 0)
    lax.fori_loop(0, depth // 256, weights, 0)
    states.wait(0, 1)
    share(0).wait_recv()
    pass_on(chips - 1).wait_recv()
    gain_part[...] = jnp.zeros_like(gain_part)

    def norm(here):
        grad = hidden_grad[here, :] + from_core[0, here, :].astype(jnp.float32) + from_ring[chips - 2, here, :].astype(jnp.float32)
        part, gain_grad = norm_back(hidden_state[here, :], gain[...], grad)
        full = cotangent[here, :] + part
        hidden_grad[here, :] = full
        branch[here, :] = full.astype(low)
        gain_part[...] += gain_grad

    by_rows(rows, norm)
    share(chips - 1).wait_send()
    for slot in range(chips):
        to_core(slot).wait_send()
        if slot < chips - 1:
            to_ring(slot).wait_send()
        if slot >= max(1, chips - 2):
            pass_on(slot).wait_send()
        store(slot).wait()
    for index in range(depth // 256 - 2, depth // 256):
        for copy in tiles(index):
            copy.wait()


def feed(chips, hidden_state, cotangent, gain, tokens, grads, both_w, down_w):
    rows, depth = tokens.shape
    pair = 2 * rows
    group_rows = chips * pair
    width = down_w.shape[0]
    shape = jax.ShapeDtypeStruct
    return pl.pallas_call(
        lambda *refs: feed_kernel(chips, *refs),
        in_specs=[VMEM] + [ANYWHERE] * 6,
        out_specs=[VMEM] * 3 + [ANYWHERE] * 3,
        out_shape=[
            shape((rows, depth), jnp.float32),
            shape((rows, depth), low),
            shape((1, depth), jnp.float32),
            shape((group_rows, width), low),
            shape((depth, 2 * width), low),
            shape((group_rows, depth), low),
        ],
        scratch_shapes=Loads.scratch(hidden_state, cotangent) + [
            pltpu.VMEM((2, pair, 256), low),
            DMA((2,)),
            pltpu.VMEM((group_rows, depth), low),
            pltpu.VMEM((depth, width), low),
            pltpu.VMEM((depth, width), low),
            pltpu.VMEM(down_w.shape, low),
            pltpu.VMEM((2, pair, depth), low),
            pltpu.VMEM((chips, pair, width), low),
            pltpu.VMEM((group_rows, width), low),
            pltpu.VMEM((group_rows, width), low),
            pltpu.VMEM((pair, depth), low),
            pltpu.VMEM((3, rows, depth), low),
            pltpu.VMEM((chips - 1, rows, depth), low),
            pltpu.VMEM((2, rows, depth), low),
            pltpu.VMEM((2, 256, width), low),
            pltpu.VMEM((2, 256, width), low),
            DMA((3,)), DMA, DMA((2,)), DMA((chips,)), DMA((2, 2)),
            DMA((chips,)), DMA((chips,)), DMA((chips,)), DMA((chips,)),
            DMA, DMA((3,)), DMA((2,)), DMA((chips - 1,)),
        ],
        compiler_params=pltpu.CompilerParams(collective_id=3, has_side_effects=True, vmem_limit_bytes=67043328),
        cost_estimate=pl.CostEstimate(flops=16 * group_rows * depth * width, bytes_accessed=10 * group_rows * depth, transcendentals=group_rows * width),
        name="feed",
    )(gain, hidden_state, cotangent, tokens, grads, both_w, down_w)


def finish_kernel(hidden, down, hidden_grad, input_part, both, grad_down, grad_qkv, grad_out, output, input_grad, query, key, value, out, gate, up, down_out):
    output[...] = hidden[...] + down[...]
    input_grad[...] = hidden_grad[...] + input_part[...]
    width = query.shape[1]
    for part, ref in enumerate((query, key, value)):
        ref[...] = grad_qkv[:, pl.ds(part * width, width)]
    out[...] = grad_out[...]
    wide = gate.shape[1]
    gate[...] = both[:, pl.ds(0, wide)].astype(jnp.float32)
    up[...] = both[:, pl.ds(wide, wide)].astype(jnp.float32)
    down_out[...] = grad_down[...].astype(jnp.float32)


def finish(*operands):
    steps = 8
    hidden, _, _, _, both, grad_down, grad_qkv, grad_out = operands
    shape = lambda a, parts: jax.ShapeDtypeStruct((a.shape[0], a.shape[1] // parts), jnp.float32)
    results = [shape(hidden, 1)] * 2 + [shape(grad_qkv, 3)] * 3 + [shape(grad_out, 1)] + [shape(both, 2)] * 2 + [shape(grad_down, 1)]
    spec = lambda a: pl.BlockSpec((a.shape[0] // steps, a.shape[1]), lambda i: (i, 0))
    return pl.pallas_call(
        finish_kernel,
        grid=(steps,),
        in_specs=[spec(a) for a in operands],
        out_specs=[spec(a) for a in results],
        out_shape=results,
        name="finish",
    )(*operands)


def rope_tables():
    half = HEAD_DIM // 2
    positions = jnp.arange(SEQ_LEN, dtype=jnp.int32).astype(jnp.float32)
    column = jnp.arange(half, dtype=jnp.int32)
    inverse = jnp.power(jnp.float32(rope_base), -2.0 * column.astype(jnp.float32) / HEAD_DIM)
    angle = positions[None, :] * inverse[:, None]
    return (jnp.cos(angle), jnp.sin(angle))


def make_body(mesh):
    chips, shards = mesh.shape["tp"] // 2, mesh.shape["fsdp"]

    def body(activations, gain_attn, w_query, w_key, w_value, w_out, gain_mlp, w_gate, w_up, w_down, cotangent):
        width = w_query.shape[1]
        full_out = lax.all_gather(w_out, "fsdp", axis=1, tiled=True)
        full_down = lax.all_gather(w_down, "fsdp", axis=1, tiled=True)
        gain_attn, gain_mlp = gain_attn[None, :], gain_mlp[None, :]
        seen_attn, w_qkv, qkv, keys_t, values_t, cosine, sine, both = project(
            chips, shards, activations, gain_attn, w_query, w_key, w_value, *rope_tables(), w_gate, w_up
        )
        full_both = lax.all_gather(both, "fsdp", axis=0, tiled=True)
        hidden_state, normed_mlp, mixed, totals, seen_grad = attend(chips, qkv, values_t, full_out, activations, cotangent, gain_mlp)
        hidden_grad, branch_grad, gain_part, inner, grad_both, terms = feed(
            chips, hidden_state, cotangent, gain_mlp, normed_mlp, seen_grad, full_both, full_down
        )

        def over_fsdp(grad, dimension):
            return lax.psum_scatter(grad, "fsdp", scatter_dimension=dimension, tiled=True)

        grad_both = over_fsdp(grad_both, 0)
        down, _, qkv_grad, grad_down, grad_out = back(
            chips, shards, branch_grad, terms, inner, seen_grad, full_out, qkv, keys_t, mixed, totals, cosine, sine
        )
        grad_down = over_fsdp(grad_down, 1)
        qkv_grad, grad_both = lax.optimization_barrier((qkv_grad, grad_both))
        input_part, grad_qkv, gain_sums = spread(chips, shards, qkv_grad, w_qkv, activations, gain_attn, gain_part, seen_attn)
        output, input_grad, grad_query, grad_key, grad_value, grad_out, grad_gate, grad_up, grad_down = finish(
            hidden_state, down, hidden_grad, input_part, grad_both, grad_down, grad_qkv, grad_out
        )
        return (
            output, input_grad, gain_sums[0], grad_query, grad_key, grad_value, grad_out, gain_sums[1],
            grad_gate, grad_up, grad_down,
        )

    return body


def solution(mesh):
    tokens = P(("fsdp", "tp"), None)
    column = P("fsdp", "tp")
    row = P("tp", "fsdp")
    in_specs = (tokens, P(), column, column, column, row, P(), column, column, row, tokens)
    out_specs = (tokens, tokens, P(), column, column, column, row, P(), column, column, row)
    return jax.shard_map(make_body(mesh), mesh=mesh, in_specs=in_specs, out_specs=out_specs, check_vma=False)
```

```python
import jax
import jax.numpy as jnp
from jax import lax
from jax.experimental import pallas as pl
from jax.experimental.pallas import tpu as pltpu
from jax.sharding import PartitionSpec as P

HEAD_DIM = 64
SEQ_LEN = 2048
LANES = 128
rope_base = 130000.0
norm_eps = 1e-05
masked_score = -1e30

NT = (((1,), (1,)), ((), ()))
NN = (((1,), (0,)), ((), ()))
TN = (((0,), (0,)), ((), ()))
MESH = pl.DeviceIdType.MESH
DMA = pltpu.SemaphoreType.DMA
ANYWHERE = pl.BlockSpec(memory_space=pl.ANY)
VMEM = pl.BlockSpec(memory_space=pltpu.VMEM)
low = jnp.bfloat16


def dot(left, right, dims=NN):
    return lax.dot_general(left, right, dims, preferred_element_type=jnp.float32)


def span(index, size):
    return pl.ds(pl.multiple_of(index * size, size), size)


def remote(source, target, send, receive, device):
    return pltpu.make_async_remote_copy(
        src_ref=source, dst_ref=target, send_sem=send, recv_sem=receive,
        device_id=device, device_id_type=MESH,
    )


def hello(device):
    pl.semaphore_signal(pltpu.get_barrier_semaphore(), inc=1, device_id=device, device_id_type=MESH)


class Line:
    def __init__(self, chips):
        self.chips = chips
        self.me = lax.axis_index("tp")
        self.chip, self.core = self.me // 2, self.me % 2
        self.partner = 2 * self.chip + 1 - self.core
        self.has_left, self.has_right = self.chip > 0, self.chip < chips - 1

    def greet(self, more=()):
        hello({"tp": self.partner})

        @pl.when(self.has_left)
        def _():
            hello({"tp": self.me - 2})

        @pl.when(self.has_right)
        def _():
            hello({"tp": self.me + 2})

        for device in more:
            hello(device)
        count = 1 + len(more) + jnp.where(self.has_left, 1, 0) + jnp.where(self.has_right, 1, 0)
        pl.semaphore_wait(pltpu.get_barrier_semaphore(), count)

    def target(self, step):
        after = self.chips - 1 - self.chip
        most, least = jnp.maximum(self.chip, after), jnp.minimum(self.chip, after)
        sign = jnp.where(after >= self.chip, 1, -1)
        late = step - (most - least)
        side = jnp.where(late % 2 == 0, sign, -sign)
        return jnp.where(late < 0, self.chip + sign * (most - step), self.chip + side * (least - late // 2))


    def fed(self, target):
        after, before = jnp.logical_and(target >= self.chip, self.has_left), jnp.logical_and(target <= self.chip, self.has_right)
        return jnp.logical_or(after, before)


class Gather:
    scratch = staticmethod(lambda chips: [DMA((2 * chips,)), DMA((chips,)), DMA((chips,)), DMA((chips,)), DMA])

    def __init__(self, line, own, out, received, right, left, across, local):
        self.line, self.own, self.out = line, own, out
        self.received, self.right, self.left, self.across, self.local = received, right, left, across, local
        self.rows = own.shape[0]

    def block(self, index):
        return self.out.at[span(index, self.rows)]

    def copy(self, source, sems, chip, device, mine):
        index = 2 * chip + self.line.core
        return remote(source if mine else self.block(index), self.block(index), sems.at[chip], self.received.at[index], {"tp": device})

    def keep(self):
        return pltpu.make_async_copy(self.own, self.block(self.line.me), self.local)

    def start(self):
        line = self.line
        self.keep().start()

        @pl.when(line.has_right)
        def _():
            self.copy(self.own, self.right, line.chip, line.me + 2, True).start()

        @pl.when(line.has_left)
        def _():
            self.copy(self.own, self.left, line.chip, line.me - 2, True).start()

        self.copy(self.own, self.across, line.chip, line.partner, True).start()

    def arrive(self, index):
        remote(self.own, self.block(index), self.right.at[0], self.received.at[index], {"tp": self.line.partner}).wait_recv()

    def arrive_across(self, chip):
        self.arrive(2 * chip + 1 - self.line.core)

    def step(self, distance):
        line = self.line
        before, after = line.chip - distance, line.chip + distance

        @pl.when(before >= 0)
        def _():
            self.arrive(2 * before + line.core)

            @pl.when(line.has_right)
            def _():
                self.copy(None, self.right, before, line.me + 2, False).start()

            self.copy(None, self.across, before, line.partner, False).start()

        @pl.when(after < line.chips)
        def _():
            self.arrive(2 * after + line.core)

            @pl.when(line.has_left)
            def _():
                self.copy(None, self.left, after, line.me - 2, False).start()

            self.copy(None, self.across, after, line.partner, False).start()

    def finish(self, arrivals):
        line = self.line
        if arrivals:
            self.keep().wait()
        for chip in range(line.chips):
            if arrivals:
                self.arrive_across(chip)
            self.copy(self.own, self.across, chip, line.partner, True).wait_send()

            @pl.when(jnp.logical_and(line.has_right, chip <= line.chip))
            def _():
                self.copy(self.own, self.right, chip, line.me + 2, True).wait_send()

            @pl.when(jnp.logical_and(line.has_left, chip >= line.chip))
            def _():
                self.copy(self.own, self.left, chip, line.me - 2, True).wait_send()


class Scatter:
    @staticmethod
    def scratch(chips, rows, depth):
        shares = min(chips, 4)
        return [
            pltpu.VMEM((2, 2 * rows, depth), low),
            pltpu.VMEM((shares, rows, depth), low),
            pltpu.VMEM((chips + 1, rows, depth), low),
            pltpu.VMEM((2, rows, depth), low),
            DMA((2,)), DMA((shares,)), DMA((2,)), DMA((chips + 1,)),
        ]

    def __init__(self, line, out, term, shares, lines, total, share_send, share_recv, line_send, line_recv):
        self.line, self.out = line, out
        self.term, self.shares, self.lines, self.total = term, shares, lines, total
        self.share_send, self.share_recv, self.line_send, self.line_recv = share_send, share_recv, line_send, line_recv
        self.rows = out.shape[0]

    def share(self, step):
        slot = step % self.shares.shape[0]
        source = self.term.at[step % 2, span(1 - self.line.core, self.rows)]
        return remote(source, self.shares.at[slot], self.share_send.at[step % 2], self.share_recv.at[slot], {"tp": self.line.partner})

    def mine(self, step):
        return self.term[step % 2, span(self.line.core, self.rows), :]

    def pass_on(self, step):
        line, target = self.line, self.line.target(step)
        onward = target > line.chip
        slot = jnp.where(onward, target, jnp.where(target == line.chip - 1, line.chips, target))
        device = jnp.where(onward, line.me + 2, line.me - 2)
        return remote(self.total.at[step % 2], self.lines.at[slot], self.line_send.at[step % 2], self.line_recv.at[slot], {"tp": device})

    def add(self, slot):
        remote(self.total.at[0], self.lines.at[slot], self.line_send.at[0], self.line_recv.at[slot], {"tp": self.line.partner}).wait_recv()
        self.out[...] += self.lines[slot].astype(jnp.float32)

    def free(self, step):
        @pl.when(step >= 2)
        def _():
            self.share(step - 2).wait_send()

    def step(self, step):
        line, target = self.line, self.line.target(step)
        self.share(step).wait_recv()
        self.out[...] = self.mine(step).astype(jnp.float32) + self.shares[step % self.shares.shape[0]].astype(jnp.float32)

        @pl.when(jnp.logical_and(target >= line.chip, line.has_left))
        def _():
            self.add(target)

        @pl.when(jnp.logical_and(target <= line.chip, line.has_right))
        def _():
            self.add(jnp.where(target == line.chip, line.chips, target))

        @pl.when(step < line.chips - 1)
        def _():
            @pl.when(step >= 2)
            def _():
                self.pass_on(step - 2).wait_send()

            self.total[step % 2] = self.out[...].astype(low)
            self.pass_on(step).start()

    def finish(self):
        chips = self.line.chips
        for step in range(max(0, chips - 3), chips - 1):
            self.pass_on(step).wait_send()
        for step in range(max(0, chips - 2), chips):
            self.share(step).wait_send()


NORM_ROWS = 64


def normed(value, gain):
    return value * lax.rsqrt(jnp.mean(value * value, axis=-1, keepdims=True) + norm_eps) * gain


def norm_back(value, gain, grad):
    scale = lax.rsqrt(jnp.mean(value * value, axis=-1, keepdims=True) + norm_eps)
    unit = value * scale
    scaled = grad * gain
    return scale * (scaled - unit * jnp.mean(scaled * unit, axis=-1, keepdims=True)), jnp.sum(grad * unit, axis=0, keepdims=True)


def by_rows(rows, work):
    def step(index, carry):
        work(span(index, NORM_ROWS))
        return carry

    lax.fori_loop(0, rows // NORM_ROWS, step, 0)


class Grid:
    def __init__(self, shards):
        self.shards, self.across = shards, shards // 2
        self.me = lax.axis_index("fsdp")
        self.row, self.column = self.me // self.across, self.me % self.across
        self.others = [(self.me + ahead) % shards for ahead in range(1, shards)]
        self.mates = [self.row * self.across + (self.column + ahead) % self.across for ahead in range(1, self.across)]
        self.twin = (1 - self.row) * self.across + self.column
        self.near = self.mates + [self.twin]

    def is_near(self, shard):
        return jnp.logical_or(shard // self.across == self.row, shard % self.across == self.column)


class NearShards:
    scratch = staticmethod(lambda shards: [DMA((shards // 2,)), DMA((shards // 2,))])

    def __init__(self, grid, own, whole, at, send, receive):
        place = at(whole, grid.me, None)
        self.copies = [remote(own, place, send.at[i], receive.at[i], {"fsdp": peer}) for i, peer in enumerate(grid.near)]

    def start(self):
        for copy in self.copies:
            copy.start()

    def arrive(self):
        for copy in self.copies:
            copy.wait_recv()

    def finish(self):
        for copy in self.copies:
            copy.wait_send()


class FarShards:
    scratch = staticmethod(lambda shards: [DMA((2, shards // 2 - 1)), DMA((2, shards // 2 - 1))])

    def __init__(self, grid, near, whole, at, send, receive):
        self.copies = []
        for i, mate in enumerate(grid.mates):
            self.copies.append(remote(at(near, mate, 0), at(whole, mate, 0), send.at[0, i], receive.at[0, i], {"fsdp": grid.twin}))
            self.copies.append(remote(at(near, grid.twin, 1), at(whole, grid.twin, 1), send.at[1, i], receive.at[1, i], {"fsdp": mate}))

    def start(self):
        for copy in self.copies:
            copy.start()

    def finish(self):
        for copy in self.copies:
            copy.wait_recv()
            copy.wait_send()


def row_shard(depth):
    def at(ref, shard, half):
        if half is None:
            return ref.at[span(shard, depth)]
        return ref.at[span(2 * shard + half, depth // 2)]

    return at


def column_shard(rows, width):
    def at(ref, shard, half):
        if half is None:
            return ref.at[:, span(shard, width)]
        return ref.at[pl.ds(half * (rows // 2), rows // 2), span(shard, width)]

    return at


class HeldScatter(Scatter):
    @staticmethod
    def scratch(chips, rows, depth):
        return [pltpu.VMEM((2, rows, depth), low)] + Scatter.scratch(chips, rows, depth)[1:] + [DMA((2,))]

    def __init__(self, line, out, held, *refs):
        super().__init__(line, out, *refs[:-1])
        self.held, self.load_sem = held, refs[-1]

    def load(self, step):
        source = self.held.at[span(2 * self.line.target(step) + self.line.core, self.rows)]
        return pltpu.make_async_copy(source, self.term.at[step % 2], self.load_sem.at[step % 2])

    def share(self, step):
        slot = step % self.shares.shape[0]
        source = self.held.at[span(2 * self.line.target(step) + 1 - self.line.core, self.rows)]
        return remote(source, self.shares.at[slot], self.share_send.at[step % 2], self.share_recv.at[slot], {"tp": self.line.partner})

    def mine(self, step):
        self.load(step).wait()
        return self.term[step % 2]


class Loads:
    @staticmethod
    def scratch(*operands):
        return [pltpu.VMEM(a.shape, a.dtype) for a in operands] + [DMA((len(operands),))]

    def __init__(self, sources, refs):
        self.refs = refs[: len(sources)]
        self.copies = [pltpu.make_async_copy(source, ref, refs[-1].at[i]) for i, (source, ref) in enumerate(zip(sources, self.refs))]

    def start(self):
        for copy in self.copies:
            copy.start()

    def wait(self, *which):
        for i in which:
            self.copies[i].wait()


def turned(block, sign):
    half = HEAD_DIM // 2
    lane = lax.broadcasted_iota(jnp.int32, block.shape, 1)
    width = block.shape[1]
    up = pltpu.roll(block, width - half, 1)
    down = pltpu.roll(block, half, 1)
    return jnp.where(lane % HEAD_DIM < half, -sign * up, sign * down)


def widened(table, width):
    return table if table.shape[1] == width else jnp.concatenate([table] * (width // table.shape[1]), axis=1)


def only_head(block, head):
    lane = lax.broadcasted_iota(jnp.int32, block.shape, 1)
    return jnp.where(lane // HEAD_DIM == head, block, jnp.zeros_like(block))


def causal(tile):
    key = lax.broadcasted_iota(jnp.int32, tile.shape, 0)
    query = lax.broadcasted_iota(jnp.int32, tile.shape, 1)
    return jnp.where(key <= query, tile, masked_score)


def over_keys(chunk, rows, visit):
    start = chunk * rows
    first = start // SEQ_LEN * SEQ_LEN

    def step(index, carry):
        visit(pl.multiple_of(first + index * rows, rows), False)
        return carry

    lax.fori_loop(0, (start - first) // rows, step, 0)
    visit(pl.multiple_of(start, rows), True)


def project_kernel(
    chips, shards,
    activations, gain, w_query, w_key, w_value, w_out, cosine_t, sine_t, w_down,
    tokens_out, weight_out, full_out, qkv_out, keys_out, values_out, cosine_out, sine_out, down_near,
    weight, out_w, qkv, keys_t, values_t, cosine, sine, tokens, chunks,
    chunk_sem, weight_send, weight_recv, weight_keep, table_sem, store_sem, near_send, near_recv, *gather_sems,
):
    line = Line(chips)
    rows = tokens.shape[0]
    pair = 2 * rows
    depth, width = w_query.shape
    grid = Grid(shards)
    shard, others = grid.me, grid.others
    gather = Gather(line, tokens, tokens_out, *gather_sems)
    down = NearShards(grid, w_down, down_near, column_shard(*w_down.shape), near_send, near_recv)
    parts = (w_query, w_key, w_value, w_out)

    def place(part):
        if part == 3:
            return out_w.at[:, span(shard, depth)]
        return weight.at[span(shard, depth), pl.ds(part * width, width)]

    def give(ahead, part):
        return remote(parts[part], place(part), weight_send.at[ahead, part], weight_recv.at[ahead, part], {"fsdp": others[ahead]})

    def keep(part):
        return pltpu.make_async_copy(parts[part], place(part), weight_keep.at[part])

    tables = [
        pltpu.make_async_copy(source, out, table_sem.at[i])
        for i, (source, out) in enumerate(((cosine, cosine_out), (sine, sine_out), (weight, weight_out), (out_w, full_out)))
    ]

    def stores(chip):
        here = span(chip, pair)
        return [
            pltpu.make_async_copy(qkv.at[here], qkv_out.at[here], store_sem.at[0, chip]),
            pltpu.make_async_copy(keys_t.at[:, here], keys_out.at[:, here], store_sem.at[1, chip]),
            pltpu.make_async_copy(values_t.at[:, here], values_out.at[:, here], store_sem.at[2, chip]),
        ]

    def norm(here):
        tokens[here, :] = normed(activations[here, :], gain[...]).astype(low)

    by_rows(rows, norm)
    line.greet([{"fsdp": other} for other in others])
    gather.start()
    for part in range(4):
        keep(part).start()
        for ahead in range(shards - 1):
            give(ahead, part).start()
    for table, table_t in ((cosine, cosine_t), (sine, sine_t)):
        turn = table_t[...].T
        table[...] = jnp.concatenate([turn] * (LANES // turn.shape[1]), axis=1)
    for copy in tables[:2]:
        copy.start()

    def project(chip):
        @pl.when(jnp.logical_and(chip >= 0, chip < chips))
        def _():
            gather.arrive_across(chip)
            load = pltpu.make_async_copy(tokens_out.at[span(chip, pair)], chunks, chunk_sem)
            load.start()
            load.wait()
            here = span(chip, pair)
            table = span(chip % (SEQ_LEN // pair), pair)
            for part in range(3):
                columns = pl.ds(part * width, width)
                block = dot(chunks[...], weight[:, columns])
                if part < 2:
                    block = block * widened(cosine[table, :], width) + turned(block, 1.0) * widened(sine[table, :], width)
                qkv[here, columns] = block.astype(low)
                if part:
                    (keys_t, values_t)[part - 1][:, here] = block.T.astype(low)
            for copy in stores(chip):
                copy.start()

    def step(index, carry):
        @pl.when(jnp.logical_and(index >= 1, index < chips))
        def _():
            gather.step(index)

        @pl.when(index == 2)
        def _():
            gather.keep().wait()
            for part in range(4):
                keep(part).wait()
                for ahead in range(shards - 1):
                    give(ahead, part).wait_recv()
            for copy in tables[2:]:
                copy.start()
            down.start()

        def side(which, carry):
            distance = index - 1
            chip = jnp.where(which == 0, line.chip - distance, jnp.where(which == 1, line.chip + distance, line.chip))

            @pl.when(jnp.logical_and(index >= 2, jnp.logical_or(which < 2, index == 2)))
            def _():
                project(chip)

            return carry

        lax.fori_loop(0, 3, side, 0)
        return carry

    lax.fori_loop(0, chips + 1, step, 0)
    gather.finish(False)
    for part in range(4):
        for ahead in range(shards - 1):
            give(ahead, part).wait_send()
    for copy in tables:
        copy.wait()
    for chip in range(chips):
        for copy in stores(chip):
            copy.wait()
    down.arrive()
    down.finish()


def project(chips, shards, activations, gain, w_query, w_key, w_value, w_out, cosine_t, sine_t, w_down):
    rows, depth = activations.shape
    group_rows = 2 * chips * rows
    width = w_query.shape[1]
    shape = jax.ShapeDtypeStruct
    held = [
        shape((depth, 3 * width), low),
        shape((width, depth), low),
        shape((group_rows, 3 * width), low),
        shape((width, group_rows), low),
        shape((width, group_rows), low),
        shape((SEQ_LEN, LANES), jnp.float32),
        shape((SEQ_LEN, LANES), jnp.float32),
    ]
    return pl.pallas_call(
        lambda *refs: project_kernel(chips, shards, *refs),
        in_specs=[VMEM] * 8 + [ANYWHERE],
        out_specs=[ANYWHERE] * 9,
        out_shape=[shape((group_rows, depth), low)] + held + [shape((w_down.shape[0], depth), low)],
        scratch_shapes=[pltpu.VMEM(a.shape, a.dtype) for a in held] + [
            pltpu.VMEM((rows, depth), low),
            pltpu.VMEM((2 * rows, depth), low),
            DMA, DMA((shards - 1, 4)), DMA((shards - 1, 4)), DMA((4,)), DMA((4,)), DMA((3, chips)),
        ] + NearShards.scratch(shards) + Gather.scratch(chips),
        compiler_params=pltpu.CompilerParams(collective_id=1, has_side_effects=True, vmem_limit_bytes=63 << 20),
        cost_estimate=pl.CostEstimate(flops=6 * group_rows * depth * width, bytes_accessed=4 * group_rows * depth, transcendentals=0),
        name="project",
    )(activations, gain, w_query, w_key, w_value, w_out, cosine_t, sine_t, w_down)


def attend_chunk(chunk, rows, qkv, values_t, heads_ref, acc, out, top_ref, sum_ref):
    width = acc.shape[0]
    heads = width // HEAD_DIM
    scaled = qkv[span(chunk, rows), pl.ds(0, width)] * low(HEAD_DIM**-0.5)
    for head in range(heads):
        heads_ref[head] = only_head(scaled, head)
    acc[...] = jnp.zeros_like(acc)
    top_ref[...] = jnp.full_like(top_ref, masked_score)
    sum_ref[...] = jnp.zeros_like(sum_ref)

    def visit(offset, diagonal):
        key_block = qkv[pl.ds(offset, rows), pl.ds(width, width)]
        for head in range(heads):
            feature = pl.ds(head * HEAD_DIM, HEAD_DIM)
            one = pl.ds(head, 1)
            scores = dot(key_block, heads_ref[head], NT)
            if diagonal:
                scores = causal(scores)
            old = top_ref[one, :]
            top = jnp.maximum(old, jnp.max(scores, axis=0, keepdims=True))
            shrink = jnp.exp(old - top)
            weights = jnp.exp(scores - top)
            top_ref[one, :] = top
            sum_ref[one, :] = sum_ref[one, :] * shrink + jnp.sum(weights, axis=0, keepdims=True)
            acc[feature, :] = acc[feature, :] * shrink + dot(values_t[feature, pl.ds(offset, rows)], weights.astype(low))

    over_keys(chunk, rows, visit)
    for head in range(heads):
        feature = pl.ds(head * HEAD_DIM, HEAD_DIM)
        acc[feature, :] = acc[feature, :] / sum_ref[pl.ds(head, 1), :]
    out[...] = acc[...].T.astype(low)


def attend_kernel(
    chips, shards,
    cotangent, gain, *refs,
):
    sources, (w_gate, w_up, down_near) = refs[:4], refs[4:7]
    hidden, tokens, mixed, totals, grads_out, gate_all, up_all, down_far = refs[7:15]
    loads = Loads(sources, refs[15:20])
    qkv, values_t, w_out, activations = loads.refs
    heads_ref, acc, out, top_ref, sum_ref, grads = refs[20:26]
    grid = Grid(shards)
    rows_of = row_shard(w_gate.shape[0])
    down = FarShards(grid, down_near, down_far, column_shard(down_near.shape[0], down_near.shape[1] // shards), *refs[26:28])
    gate_near, gate_far = NearShards(grid, w_gate, gate_all, rows_of, *refs[28:30]), FarShards(grid, gate_all, gate_all, rows_of, *refs[30:32])
    up_near, up_far = NearShards(grid, w_up, up_all, rows_of, *refs[32:34]), FarShards(grid, up_all, up_all, rows_of, *refs[34:36])
    sems = refs[36:]
    loads.start()
    line = Line(chips)
    rows, depth = hidden.shape
    pair = 2 * rows
    scatter = Scatter(line, hidden, *sems[:8])
    grads[...] = cotangent[...].astype(low)
    gather = Gather(line, grads, grads_out, *sems[8:])
    line.greet([{"fsdp": peer} for peer in grid.near])
    gather.start()
    gate_near.start()
    down.start()
    loads.wait(0, 1, 2, 3)

    def step(index, carry):
        work = jnp.where(index == chips, chips - 1, index)

        @pl.when(jnp.logical_or(index < chips - 1, index == chips))
        def _():
            chunk = line.target(work)
            attend_chunk(chunk, pair, qkv, values_t, heads_ref, acc, out, top_ref, sum_ref)
            mixed[span(chunk, pair), :] = out[...]
            totals[:, span(chunk, pair)] = top_ref[...] + jnp.log(sum_ref[...])
            scatter.free(work)

            def tile(place, carry):
                columns = span(place, 512)
                scatter.term[work % 2, :, columns] = dot(out[...], w_out[:, columns]).astype(low)
                return carry

            lax.fori_loop(0, depth // 512, tile, 0)
            scatter.share(work).start()

        @pl.when(jnp.logical_and(index >= 1, index < chips))
        def _():
            gather.step(index)

        @pl.when(index == 1)
        def _():
            up_near.start()

        @pl.when(index == min(2, chips))
        def _():
            gate_near.arrive()
            gate_far.start()

        @pl.when(index == min(3, chips))
        def _():
            up_near.arrive()
            up_far.start()

        @pl.when(index >= 1)
        def _():
            scatter.step(index - 1)

        return carry

    lax.fori_loop(0, chips + 1, step, 0)

    def norm(here):
        state = activations[here, :] + hidden[here, :]
        hidden[here, :] = state
        tokens[here, :] = normed(state, gain[...]).astype(low)

    by_rows(rows, norm)
    scatter.finish()
    gather.finish(True)
    for near in (gate_near, up_near):
        near.finish()
    for far in (down, gate_far, up_far):
        far.finish()


def attend(chips, shards, qkv, values_t, w_out, activations, cotangent, gain, w_gate, w_up, down_near):
    rows, depth = activations.shape
    pair = 2 * rows
    group_rows = chips * pair
    width = w_out.shape[0]
    heads = width // HEAD_DIM
    shape = jax.ShapeDtypeStruct
    return pl.pallas_call(
        lambda *refs: attend_kernel(chips, shards, *refs),
        in_specs=[VMEM] * 2 + [ANYWHERE] * 7,
        out_specs=[VMEM] * 4 + [ANYWHERE] * 4,
        out_shape=[
            shape((rows, depth), jnp.float32),
            shape((rows, depth), low),
            shape((group_rows, width), low),
            shape((heads, group_rows), jnp.float32),
            shape((group_rows, depth), low),
            shape((depth, w_gate.shape[1]), low),
            shape((depth, w_gate.shape[1]), low),
            shape(down_near.shape, low),
        ],
        scratch_shapes=Loads.scratch(qkv, values_t, w_out, activations) + [
            pltpu.VMEM((heads, pair, width), low),
            pltpu.VMEM((width, pair), jnp.float32),
            pltpu.VMEM((pair, width), low),
            pltpu.VMEM((heads, pair), jnp.float32),
            pltpu.VMEM((heads, pair), jnp.float32),
            pltpu.VMEM((rows, depth), low),
        ] + FarShards.scratch(shards) + (NearShards.scratch(shards) + FarShards.scratch(shards)) * 2 + Scatter.scratch(chips, rows, depth) + Gather.scratch(chips),
        compiler_params=pltpu.CompilerParams(collective_id=2, has_side_effects=True, vmem_limit_bytes=63 << 20),
        cost_estimate=pl.CostEstimate(flops=2 * group_rows * (SEQ_LEN + depth) * width, bytes_accessed=4 * group_rows * depth, transcendentals=group_rows * SEQ_LEN * heads // 2),
        name="attend",
    )(cotangent, gain, qkv, values_t, w_out, activations, w_gate, w_up, down_near)


def back_chunk(chunk, rows, grad, qkv, keys_t, mixed, totals, dkey, dvalue, heads_ref, grads_ref, acc, inner_ref):
    width = acc.shape[0]
    heads = width // HEAD_DIM
    here = span(chunk, rows)
    scaled = qkv[here, pl.ds(0, width)] * low(HEAD_DIM**-0.5)
    product = grad.astype(jnp.float32) * mixed[here, :].astype(jnp.float32)
    shape = (inner_ref.shape[0], width)
    pick = (lax.broadcasted_iota(jnp.int32, shape, 1) // HEAD_DIM == lax.broadcasted_iota(jnp.int32, shape, 0)).astype(jnp.float32)
    inner_ref[...] = lax.dot_general(pick, product, NT, precision=lax.Precision.HIGHEST, preferred_element_type=jnp.float32)
    for head in range(heads):
        heads_ref[head] = only_head(scaled, head)
        grads_ref[head] = only_head(grad, head)
    acc[...] = jnp.zeros_like(acc)

    def visit(offset, diagonal):
        keys = pl.ds(offset, rows)
        key_block = qkv[keys, pl.ds(width, width)]
        value_block = qkv[keys, pl.ds(2 * width, width)]
        key_sum, value_sum = dkey[keys, :], dvalue[keys, :]
        for head in range(heads):
            feature = pl.ds(head * HEAD_DIM, HEAD_DIM)
            scores = dot(key_block, heads_ref[head], NT)
            if diagonal:
                scores = causal(scores)
            probs = jnp.exp(scores - totals[pl.ds(head, 1), here])
            dprobs = dot(value_block, grads_ref[head], NT)
            dscores = (probs * (dprobs - inner_ref[pl.ds(head, 1), :])).astype(low)
            value_sum = value_sum + dot(probs.astype(low), grads_ref[head])
            key_sum = key_sum + dot(dscores, heads_ref[head])
            acc[feature, :] = acc[feature, :] + dot(keys_t[feature, keys], dscores)
        dkey[keys, :] = key_sum
        dvalue[keys, :] = value_sum

    over_keys(chunk, rows, visit)


def back_kernel(
    chips, shards,
    branch, terms, inner, grads, grad_both, *refs,
):
    sources, (down, branch_out, qkv_grad, grad_down, grad_out, both_from) = refs[:7], refs[7:13]
    loads = Loads(sources, refs[13:21])
    w_out, qkv, keys_t, mixed, totals, cosine, sine = loads.refs
    inner_chunk, grad_chunk, down_sum, down_tile, out_sum, out_stage, out_from, branch_chunk, dkey, dvalue = refs[21:31]
    heads_ref, grads_ref, acc, inner_ref, inner_sem, grad_sem, branch_sem, tile_sem, out_send, out_recv, both_send, both_recv = refs[31:43]
    sems = refs[43:]
    line = Line(chips)
    rows, depth = down.shape
    pair = 2 * rows
    width = w_out.shape[0]
    scatter = HeldScatter(line, down, terms, *sems[:9])
    gather = Gather(line, branch, branch_out, *sems[9:])

    def fetch(step):
        return pltpu.make_async_copy(inner.at[span(line.target(step), pair)], inner_chunk, inner_sem)

    def fetch_grad(step):
        return pltpu.make_async_copy(grads.at[span(line.target(step), pair)], grad_chunk, grad_sem)

    shard = lax.axis_index("fsdp")
    columns_out = depth // shards
    others = [(shard + ahead) % shards for ahead in range(1, shards)]

    def give(turn):
        return remote(out_stage.at[turn], out_from.at[turn], out_send.at[turn], out_recv.at[turn], {"fsdp": others[turn]})

    def hand(turn):
        source = grad_both.at[span(others[turn], grad_both.shape[0] // shards)]
        return remote(source, both_from.at[turn], both_send.at[turn], both_recv.at[turn], {"fsdp": others[turn]})

    def keep_tile(place):
        return pltpu.make_async_copy(down_tile, grad_down.at[span(place, 256)], tile_sem)

    loads.start()
    line.greet([{"fsdp": other} for other in others])
    gather.start()
    for turn in range(shards - 1):
        hand(turn).start()
    out_sum[...] = jnp.zeros_like(out_sum)
    dkey[...] = jnp.zeros_like(dkey)
    dvalue[...] = jnp.zeros_like(dvalue)

    def unrotated(block, chunk):
        table = span(chunk % (SEQ_LEN // pair), pair)
        return (block * widened(cosine[table, :], width) + turned(block * widened(sine[table, :], width), -1.0)).astype(low)

    def attention(chunk):
        gather.arrive_across(chunk)
        copy = pltpu.make_async_copy(branch_out.at[span(chunk, pair)], branch_chunk, branch_sem)
        copy.start()
        copy.wait()
        out_sum[...] += dot(mixed[span(chunk, pair), :], branch_chunk[...], TN)
        grad = dot(branch_chunk[...], w_out[...], NT).astype(low)
        back_chunk(chunk, pair, grad, qkv, keys_t, mixed, totals, dkey, dvalue, heads_ref, grads_ref, acc, inner_ref)
        qkv_grad[span(chunk, pair), pl.ds(0, width)] = unrotated(acc[...].T * HEAD_DIM**-0.5, chunk)

    def close():
        def part(chunk, carry):
            here = span(chunk, pair)
            qkv_grad[here, pl.ds(width, width)] = unrotated(dkey[here, :], chunk)
            qkv_grad[here, pl.ds(2 * width, width)] = dvalue[here, :].astype(low)
            return carry

        lax.fori_loop(0, chips, part, 0)

    def step(index, carry):
        @pl.when(index == 0)
        def _():
            loads.wait(*range(7))
            gather.keep().wait()

        @pl.when(index < chips)
        def _():
            fetch(index).start()
            fetch_grad(index).start()
            scatter.free(index)
            scatter.load(index).start()
            scatter.share(index).start()

        @pl.when(jnp.logical_and(index >= 1, index < chips))
        def _():
            gather.step(index)

        @pl.when(index == chips)
        def _():
            for turn in range(shards - 1):
                out_stage[turn] = out_sum[:, span(others[turn], columns_out)].astype(low)
                give(turn).start()
            close()

        def phase(which, carry):
            done = jnp.maximum(index - 1, 0)
            late = line.fed(line.target(done))
            turn = jnp.logical_or(jnp.logical_and(which == 0, jnp.logical_not(late)), jnp.logical_and(which == 3, late))

            @pl.when(jnp.logical_and(index >= 1, turn))
            def _():
                scatter.step(done)

            chunk = jnp.where(which == 1, line.chip - index, line.chip + index)
            there = jnp.logical_and(chunk >= 0, chunk < chips)
            turn = jnp.logical_or(which == 1, jnp.logical_and(which == 2, index > 0))

            @pl.when(jnp.logical_and(there, turn))
            def _():
                attention(chunk)

            return carry

        lax.fori_loop(0, 4, phase, 0)

        @pl.when(index < chips)
        def _():
            fetch(index).wait()
            fetch_grad(index).wait()

            def tile(place, carry):
                here = span(place, 256)
                part = dot(inner_chunk[:, here], grad_chunk[...], TN)

                @pl.when(index == 0)
                def _():
                    down_sum[here, :] = part

                @pl.when(index > 0)
                def _():
                    down_sum[here, :] += part

                @pl.when(index == chips - 1)
                def _():
                    @pl.when(place > 0)
                    def _():
                        keep_tile(place - 1).wait()

                    down_tile[...] = down_sum[here, :].astype(low)
                    keep_tile(place).start()

                return carry

            lax.fori_loop(0, down_sum.shape[0] // 256, tile, 0)

        return carry

    lax.fori_loop(0, chips + 1, step, 0)
    total = out_sum[:, span(shard, columns_out)]
    for turn in range(shards - 1):
        give(turn).wait_recv()
        total = total + out_from[turn].astype(jnp.float32)
    grad_out[...] = total
    for turn in range(shards - 1):
        give(turn).wait_send()
    keep_tile(down_sum.shape[0] // 256 - 1).wait()
    for turn in range(shards - 1):
        hand(turn).wait_recv()
        hand(turn).wait_send()
    scatter.finish()
    gather.finish(False)


def back(chips, shards, branch, terms, inner, grads, grad_both, w_out, qkv, keys_t, mixed, totals, cosine, sine):
    rows, depth = branch.shape
    pair = 2 * rows
    group_rows = chips * pair
    width = w_out.shape[0]
    hidden = inner.shape[1]
    heads = width // HEAD_DIM
    shape = jax.ShapeDtypeStruct
    held = (w_out, qkv, keys_t, mixed, totals, cosine, sine)
    return pl.pallas_call(
        lambda *refs: back_kernel(chips, shards, *refs),
        in_specs=[VMEM] + [ANYWHERE] * 11,
        out_specs=[VMEM, ANYWHERE, VMEM, ANYWHERE, VMEM, ANYWHERE],
        out_shape=[
            shape((rows, depth), jnp.float32),
            shape((group_rows, depth), low),
            shape((group_rows, 3 * width), low),
            shape((hidden, depth), low),
            shape((width, depth // shards), jnp.float32),
            shape((shards - 1, depth // shards, grad_both.shape[1]), low),
        ],
        scratch_shapes=Loads.scratch(*held) + [
            pltpu.VMEM((pair, hidden), low),
            pltpu.VMEM((pair, depth), low),
            pltpu.VMEM((hidden, depth), jnp.float32),
            pltpu.VMEM((256, depth), low),
            pltpu.VMEM((width, depth), jnp.float32),
            pltpu.VMEM((shards - 1, width, depth // shards), low),
            pltpu.VMEM((shards - 1, width, depth // shards), low),
            pltpu.VMEM((pair, depth), low),
            pltpu.VMEM((group_rows, width), jnp.float32),
            pltpu.VMEM((group_rows, width), jnp.float32),
            pltpu.VMEM((heads, pair, width), low),
            pltpu.VMEM((heads, pair, width), low),
            pltpu.VMEM((width, pair), jnp.float32),
            pltpu.VMEM((8, pair), jnp.float32),
            DMA, DMA, DMA, DMA, DMA((shards - 1,)), DMA((shards - 1,)), DMA((shards - 1,)), DMA((shards - 1,)),
        ] + HeldScatter.scratch(chips, rows, depth) + Gather.scratch(chips),
        compiler_params=pltpu.CompilerParams(collective_id=4, has_side_effects=True, vmem_limit_bytes=67043328),
        cost_estimate=pl.CostEstimate(flops=1 << 20, bytes_accessed=1 << 20, transcendentals=0),
        name="back",
    )(branch, terms, inner, grads, grad_both, *held)


def spread_kernel(
    chips, shards,
    qkv_grad, weight, activations, gain, gain_part, attn_tokens, grad_down,
    input_part, grad_qkv, gain_sum, down_from,
    attn_cols, qkv_stage, qkv_from, gains, gains_tp, gains_fsdp,
    attn_sem, qkv_send, qkv_recv, down_send, down_recv, tp_send, tp_recv, fsdp_send, fsdp_recv, *sems,
):
    line = Line(chips)
    size = 2 * chips
    rows, depth = input_part.shape
    pair = 2 * rows
    shard = lax.axis_index("fsdp")
    columns = depth // shards
    scatter = Scatter(line, input_part, *sems)

    def peer(turn):
        return (shard + 1 + turn) % shards

    def fetch(turn):
        return pltpu.make_async_copy(attn_tokens.at[:, span(peer(turn), columns)], attn_cols.at[turn % 2], attn_sem.at[turn % 2])

    def give(turn):
        return remote(qkv_stage.at[turn], qkv_from.at[turn], qkv_send.at[turn], qkv_recv.at[turn], {"fsdp": peer(turn)})

    def hand(turn):
        source = grad_down.at[:, span(peer(turn), columns)]
        return remote(source, down_from.at[turn], down_send.at[turn], down_recv.at[turn], {"fsdp": peer(turn)})

    def tell_tp(ahead):
        return remote(gains, gains_tp.at[line.me], tp_send.at[ahead - 1], tp_recv.at[line.me], {"tp": (line.me + ahead) % size})

    def tell_fsdp(ahead):
        return remote(gains, gains_fsdp.at[shard], fsdp_send.at[ahead - 1], fsdp_recv.at[shard], {"fsdp": (shard + ahead) % shards})

    fetch(0).start()
    for ahead in range(1, size):
        hello({"tp": (line.me + ahead) % size})
    for ahead in range(1, shards):
        hello({"fsdp": (shard + ahead) % shards})
    pl.semaphore_wait(pltpu.get_barrier_semaphore(), size - 1 + shards - 1)
    for turn in range(shards - 1):
        hand(turn).start()

    def weights(turn, carry):
        @pl.when(turn < shards - 1)
        def _():
            fetch(turn + 1).start()

        fetch(turn).wait()
        part = dot(attn_cols[turn % 2], qkv_grad[...], TN)

        @pl.when(turn < shards - 1)
        def _():
            qkv_stage[turn] = part.astype(low)
            give(turn).start()

        @pl.when(turn == shards - 1)
        def _():
            grad_qkv[...] = part

        return carry

    def step(index, carry):
        @pl.when(index < chips)
        def _():
            here = span(line.target(index), pair)
            scatter.free(index)

            def tile(place, carry):
                there = span(place, 512)
                scatter.term[index % 2, :, there] = dot(qkv_grad[here, :], weight[there, :], NT).astype(low)
                return carry

            lax.fori_loop(0, depth // 512, tile, 0)
            scatter.share(index).start()

        def phase(which, carry):
            done = jnp.maximum(index - 1, 0)
            late = line.fed(line.target(done))
            turn = jnp.logical_or(jnp.logical_and(which == 0, jnp.logical_not(late)), jnp.logical_and(which == 2, late))

            @pl.when(jnp.logical_and(index >= 1, turn))
            def _():
                scatter.step(done)

            @pl.when(jnp.logical_and(which == 1, index < 2))
            def _():
                lax.fori_loop(index, jnp.where(index == 0, 1, shards), weights, 0)

            return carry

        lax.fori_loop(0, 3, phase, 0)
        return carry

    lax.fori_loop(0, chips + 1, step, 0)
    gains[0:1, :] = jnp.zeros((1, depth), jnp.float32)
    gains[1:2, :] = gain_part[...]

    def norm(here):
        part, grad = norm_back(activations[here, :], gain[...], input_part[here, :])
        input_part[here, :] = part
        gains[0:1, :] += grad

    by_rows(rows, norm)

    gains_tp[line.me] = gains[...]
    for ahead in range(1, size):
        tell_tp(ahead).start()
    for ahead in range(1, size):
        source = (line.me + ahead) % size
        remote(gains, gains_tp.at[source], tp_send.at[0], tp_recv.at[source], {"tp": source}).wait_recv()
    total = gains_tp[0]
    for source in range(1, size):
        total = total + gains_tp[source]
    for ahead in range(1, size):
        tell_tp(ahead).wait_send()
    gains[...] = total
    gains_fsdp[shard] = total
    for ahead in range(1, shards):
        tell_fsdp(ahead).start()
    for ahead in range(1, shards):
        source = (shard + ahead) % shards
        remote(gains, gains_fsdp.at[source], fsdp_send.at[0], fsdp_recv.at[source], {"fsdp": source}).wait_recv()
    total = gains_fsdp[0]
    for source in range(1, shards):
        total = total + gains_fsdp[source]
    gain_sum[...] = total
    for ahead in range(1, shards):
        tell_fsdp(ahead).wait_send()
    for turn in range(shards - 1):
        give(turn).wait_recv()
        grad_qkv[...] += qkv_from[turn].astype(jnp.float32)
    for turn in range(shards - 1):
        give(turn).wait_send()
        hand(turn).wait_recv()
        hand(turn).wait_send()
    scatter.finish()


def spread(chips, shards, qkv_grad, weight, activations, gain, gain_part, attn_tokens, grad_down):
    group_rows = qkv_grad.shape[0]
    rows, depth = activations.shape
    width = qkv_grad.shape[1] // 3
    columns = depth // shards
    size = 2 * chips
    shape = jax.ShapeDtypeStruct
    return pl.pallas_call(
        lambda *refs: spread_kernel(chips, shards, *refs),
        in_specs=[VMEM] * 5 + [ANYWHERE] * 2,
        out_specs=[VMEM] * 3 + [ANYWHERE],
        out_shape=[
            shape((rows, depth), jnp.float32),
            shape((columns, 3 * width), jnp.float32),
            shape((2, depth), jnp.float32),
            shape((shards - 1, grad_down.shape[0], columns), low),
        ],
        scratch_shapes=[
            pltpu.VMEM((2, group_rows, columns), low),
            pltpu.VMEM((shards - 1, columns, 3 * width), low),
            pltpu.VMEM((shards - 1, columns, 3 * width), low),
            pltpu.VMEM((2, depth), jnp.float32),
            pltpu.VMEM((size, 2, depth), jnp.float32),
            pltpu.VMEM((shards, 2, depth), jnp.float32),
            DMA((2,)), DMA((shards - 1,)), DMA((shards - 1,)), DMA((shards - 1,)), DMA((shards - 1,)),
            DMA((size - 1,)), DMA((size,)), DMA((shards - 1,)), DMA((shards,)),
        ] + Scatter.scratch(chips, rows, depth),
        compiler_params=pltpu.CompilerParams(collective_id=5, has_side_effects=True, vmem_limit_bytes=63 << 20),
        cost_estimate=pl.CostEstimate(flops=1 << 20, bytes_accessed=1 << 20, transcendentals=0),
        name="spread",
    )(qkv_grad, weight, activations, gain, gain_part, attn_tokens, grad_down)


def chip_at(place, chips):
    return jnp.where(2 * place < chips, 2 * place, 2 * (chips - 1 - place) + 1)


def place_of(chip, chips):
    return jnp.where(chip % 2 == 0, chip // 2, chips - 1 - chip // 2)


def feed_kernel(
    chips, shards,
    gain, hidden_hbm, cotangent_hbm, tokens, grads_hbm, w_gate, w_up, w_down, gate_all, up_all, down_near, down_far,
    hidden_grad, branch, gain_part, inner_out, grad_both, down_out,
    hidden_state, cotangent, state_sem, down_tile, down_sem, tokens_all, gate_w, up_w, down_w, grads, inner, gate_grad, up_grad, term, from_core, from_ring, total, tile_gate, tile_up,
    load_sem, own_sem, grad_sem, store_sem, tile_sem,
    ring_send, ring_recv, core_send, core_recv, share_send, share_recv, total_send, total_recv,
):
    rows, depth = hidden_grad.shape
    pair = 2 * rows
    width = gate_w.shape[1]
    me = lax.axis_index("tp")
    chip, core = me // 2, me % 2
    place = place_of(chip, chips)
    following = {"tp": 2 * chip_at((place + 1) % chips, chips) + core}
    before = {"tp": 2 * chip_at((place + chips - 1) % chips, chips) + core}
    partner = {"tp": 2 * chip + 1 - core}

    grid = Grid(shards)
    rows_of, columns_of = row_shard(w_gate.shape[0]), column_shard(*w_down.shape)

    def load(array, source, shard, whole):
        at = columns_of if array == 2 else rows_of
        target = at((gate_w, up_w, down_w)[array], shard, None)
        return pltpu.make_async_copy(at(source, shard, None) if whole else source, target, load_sem.at[array, shard])

    def load_weights():
        for shard in range(shards):
            own, near = grid.me == shard, grid.is_near(shard)

            @pl.when(own)
            def _():
                for array, source in enumerate((w_gate, w_up, w_down)):
                    load(array, source, shard, False).start()

            @pl.when(jnp.logical_not(own))
            def _():
                for array, source in enumerate((gate_all, up_all)):
                    load(array, source, shard, True).start()

            @pl.when(jnp.logical_and(near, jnp.logical_not(own)))
            def _():
                load(2, down_near, shard, True).start()

            @pl.when(jnp.logical_not(near))
            def _():
                load(2, down_far, shard, True).start()

    own = pltpu.make_async_copy(tokens, tokens_all.at[span(me, rows)], own_sem)
    states = Loads((hidden_hbm, cotangent_hbm), (hidden_state, cotangent, state_sem))

    def source(slot):
        return chip_at((place + chips - slot) % chips, chips)

    def fetch(slot):
        return pltpu.make_async_copy(grads_hbm.at[span(source(slot), pair)], grads.at[slot % 2], grad_sem.at[slot % 2])

    def block(slot):
        return tokens_all.at[span(2 * source(slot) + core, rows)]

    def to_ring(slot):
        return remote(block(slot), block(slot), ring_send.at[slot], ring_recv.at[slot], following)

    def to_core(slot):
        return remote(block(slot), block(slot), core_send.at[slot], core_recv.at[slot], partner)

    def store(slot):
        return pltpu.make_async_copy(inner.at[slot], inner_out.at[span(source(slot), pair)], store_sem.at[slot])

    def keep_down(slot, tile):
        there = down_out.at[span(source(slot), pair), span(tile, 256)]
        return pltpu.make_async_copy(down_tile.at[tile % 2], there, down_sem.at[tile % 2])

    def down_term(slot, carry):
        def tile(index, carry):
            @pl.when(index > 1)
            def _():
                keep_down(slot, index - 2).wait()

            down_tile[index % 2] = dot(inner[slot], down_w[:, span(index, 256)]).astype(low)
            keep_down(slot, index).start()
            return carry

        lax.fori_loop(0, depth // 256, tile, 0)
        for index in range(depth // 256 - 2, depth // 256):
            keep_down(slot, index).wait()
        return carry

    def share(slot):
        place = jnp.where(slot == 0, 0, 1 + slot % 2)
        return remote(term.at[span(1 - core, rows)], from_core.at[place], share_send, share_recv.at[place], partner)

    def pass_on(slot):
        return remote(total.at[slot % 2], from_ring.at[slot - 1], total_send.at[slot % 2], total_recv.at[slot - 1], following)

    own.start()
    fetch(0).start()
    load_weights()
    own.wait()
    for device in (following, before, partner):
        hello(device)
    pl.semaphore_wait(pltpu.get_barrier_semaphore(), 3)

    def step(slot, carry):
        here = slot % 2
        wide_rows = span(source(slot), pair)
        mine = span(core, rows)

        @pl.when(slot > 0)
        def _():
            to_ring(slot - 1).wait_recv()

        @pl.when(slot < chips - 1)
        def _():
            to_ring(slot).start()
            fetch(slot + 1).start()

        to_core(slot).start()

        @pl.when(slot == 0)
        def _():
            for shard in range(shards):
                for array, source in enumerate((gate_all, up_all, down_near)):
                    load(array, source, shard, True).wait()

        @pl.when(slot == 1)
        def _():
            states.start()

        to_core(slot).wait_recv()
        fetch(slot).wait()

        def narrow(tile, carry):
            columns = span(tile, 256)
            token = tokens_all[wide_rows, :]
            gate = dot(token, gate_w[:, columns])
            up = dot(token, up_w[:, columns])
            grad = dot(grads[here], down_w[columns, :], NT)
            squash = jax.nn.sigmoid(gate)
            act = gate * squash
            inner[slot, :, columns] = (act * up).astype(low)
            up_grad[wide_rows, columns] = (grad * act).astype(low)
            gate_grad[wide_rows, columns] = (grad * up * squash * (1.0 + gate * (1.0 - squash))).astype(low)
            return carry

        lax.fori_loop(0, width // 256, narrow, 0)
        store(slot).start()

        @pl.when(slot > 0)
        def _():
            share(slot - 1).wait_send()

        def wide(tile, carry):
            columns = span(tile, 256)
            part = dot(gate_grad[wide_rows, :], gate_w[columns, :], NT) + dot(up_grad[wide_rows, :], up_w[columns, :], NT)
            term[:, columns] = part.astype(low)
            return carry

        lax.fori_loop(0, depth // 256, wide, 0)
        share(slot).start()

        @pl.when(slot == 0)
        def _():
            hidden_grad[...] = term[mine, :].astype(jnp.float32)

        middle = jnp.logical_and(slot >= 2, slot < chips - 1)
        lax.fori_loop(jnp.where(slot == 2, 0, slot), jnp.where(middle, slot + 1, 0), down_term, 0)

        @pl.when(slot > 0)
        def _():
            share(slot).wait_recv()

            @pl.when(slot > 2)
            def _():
                pass_on(slot - 2).wait_send()

            @pl.when(slot == 1)
            def _():
                total[here] = (term[mine, :].astype(jnp.float32) + from_core[1 + here].astype(jnp.float32)).astype(low)

            @pl.when(slot > 1)
            def _():
                pass_on(slot - 1).wait_recv()
                total[here] = (term[mine, :].astype(jnp.float32) + from_core[1 + here].astype(jnp.float32) + from_ring[slot - 2].astype(jnp.float32)).astype(low)

            pass_on(slot).start()

        return carry

    lax.fori_loop(0, chips, step, 0)

    def tiles(index):
        there = span(index, 256)
        return (
            pltpu.make_async_copy(tile_gate.at[index % 2], grad_both.at[there, pl.ds(0, width)], tile_sem.at[0, index % 2]),
            pltpu.make_async_copy(tile_up.at[index % 2], grad_both.at[there, pl.ds(width, width)], tile_sem.at[1, index % 2]),
        )

    def weights(index, carry):
        @pl.when(index > 1)
        def _():
            for copy in tiles(index - 2):
                copy.wait()

        token = tokens_all[:, span(index, 256)]
        tile_gate[index % 2] = dot(token, gate_grad[...], TN).astype(low)
        tile_up[index % 2] = dot(token, up_grad[...], TN).astype(low)
        for copy in tiles(index):
            copy.start()
        return carry

    lax.fori_loop(0 if chips < 4 else chips - 1, chips, down_term, 0)
    lax.fori_loop(0, depth // 256, weights, 0)
    states.wait(0, 1)
    share(0).wait_recv()
    pass_on(chips - 1).wait_recv()
    gain_part[...] = jnp.zeros_like(gain_part)

    def norm(here):
        grad = hidden_grad[here, :] + from_core[0, here, :].astype(jnp.float32) + from_ring[chips - 2, here, :].astype(jnp.float32)
        part, gain_grad = norm_back(hidden_state[here, :], gain[...], grad)
        full = cotangent[here, :] + part
        hidden_grad[here, :] = full
        branch[here, :] = full.astype(low)
        gain_part[...] += gain_grad

    by_rows(rows, norm)
    share(chips - 1).wait_send()
    for slot in range(chips):
        to_core(slot).wait_send()
        if slot < chips - 1:
            to_ring(slot).wait_send()
        if slot >= max(1, chips - 2):
            pass_on(slot).wait_send()
        store(slot).wait()
    for index in range(depth // 256 - 2, depth // 256):
        for copy in tiles(index):
            copy.wait()


def feed(chips, shards, hidden_state, cotangent, gain, tokens, grads, w_gate, w_up, w_down, gate_all, up_all, down_near, down_far):
    rows, depth = tokens.shape
    pair = 2 * rows
    group_rows = chips * pair
    width = w_down.shape[0]
    shape = jax.ShapeDtypeStruct
    return pl.pallas_call(
        lambda *refs: feed_kernel(chips, shards, *refs),
        in_specs=[VMEM] + [ANYWHERE] * 11,
        out_specs=[VMEM] * 3 + [ANYWHERE] * 3,
        out_shape=[
            shape((rows, depth), jnp.float32),
            shape((rows, depth), low),
            shape((1, depth), jnp.float32),
            shape((group_rows, width), low),
            shape((depth, 2 * width), low),
            shape((group_rows, depth), low),
        ],
        scratch_shapes=Loads.scratch(hidden_state, cotangent) + [
            pltpu.VMEM((2, pair, 256), low),
            DMA((2,)),
            pltpu.VMEM((group_rows, depth), low),
            pltpu.VMEM((depth, width), low),
            pltpu.VMEM((depth, width), low),
            pltpu.VMEM((width, depth), low),
            pltpu.VMEM((2, pair, depth), low),
            pltpu.VMEM((chips, pair, width), low),
            pltpu.VMEM((group_rows, width), low),
            pltpu.VMEM((group_rows, width), low),
            pltpu.VMEM((pair, depth), low),
            pltpu.VMEM((3, rows, depth), low),
            pltpu.VMEM((chips - 1, rows, depth), low),
            pltpu.VMEM((2, rows, depth), low),
            pltpu.VMEM((2, 256, width), low),
            pltpu.VMEM((2, 256, width), low),
            DMA((3, shards)), DMA, DMA((2,)), DMA((chips,)), DMA((2, 2)),
            DMA((chips,)), DMA((chips,)), DMA((chips,)), DMA((chips,)),
            DMA, DMA((3,)), DMA((2,)), DMA((chips - 1,)),
        ],
        compiler_params=pltpu.CompilerParams(collective_id=3, has_side_effects=True, vmem_limit_bytes=67043328),
        cost_estimate=pl.CostEstimate(flops=16 * group_rows * depth * width, bytes_accessed=10 * group_rows * depth, transcendentals=group_rows * width),
        name="feed",
    )(gain, hidden_state, cotangent, tokens, grads, w_gate, w_up, w_down, gate_all, up_all, down_near, down_far)


def finish_kernel(
    shard_ref, hidden, down, hidden_grad, input_part, both, both_from, grad_down, down_from, grad_qkv, grad_out,
    output, input_grad, query, key, value, out, gate, up, down_out,
):
    output[...] = hidden[...] + down[...]
    input_grad[...] = hidden_grad[...] + input_part[...]
    width = query.shape[1]
    for part, ref in enumerate((query, key, value)):
        ref[...] = grad_qkv[:, pl.ds(part * width, width)]
    out[...] = grad_out[...]
    wide = gate.shape[1]
    for side, ref in enumerate((gate, up)):
        columns = pl.ds(side * wide, wide)
        total = both[:, columns].astype(jnp.float32)
        for turn in range(both_from.shape[0]):
            total = total + both_from[turn, :, columns].astype(jnp.float32)
        ref[...] = total
    total = grad_down[...].astype(jnp.float32)
    for turn in range(down_from.shape[0]):
        total = total + down_from[turn].astype(jnp.float32)
    down_out[...] = total


def finish(shard, hidden, down, hidden_grad, input_part, both, both_from, grad_down, down_from, grad_qkv, grad_out):
    steps = 8
    shape = jax.ShapeDtypeStruct
    columns = down_from.shape[2]
    results = [shape(hidden.shape, jnp.float32)] * 2
    results += [shape((columns, grad_qkv.shape[1] // 3), jnp.float32)] * 3 + [shape(grad_out.shape, jnp.float32)]
    results += [shape((columns, both.shape[1] // 2), jnp.float32)] * 2 + [shape((grad_down.shape[0], columns), jnp.float32)]
    spec = lambda a: pl.BlockSpec((a.shape[0] // steps, a.shape[1]), lambda i, s: (i, 0))
    spec3 = lambda a: pl.BlockSpec((a.shape[0], a.shape[1] // steps, a.shape[2]), lambda i, s: (0, i, 0))
    return pl.pallas_call(
        finish_kernel,
        grid_spec=pltpu.PrefetchScalarGridSpec(
            num_scalar_prefetch=1,
            grid=(steps,),
            in_specs=[
                spec(hidden), spec(down), spec(hidden_grad), spec(input_part),
                pl.BlockSpec((columns // steps, both.shape[1]), lambda i, s: (s[0] * steps + i, 0)),
                spec3(both_from),
                pl.BlockSpec((grad_down.shape[0] // steps, columns), lambda i, s: (i, s[0])),
                spec3(down_from), spec(grad_qkv), spec(grad_out),
            ],
            out_specs=[spec(a) for a in results],
        ),
        out_shape=results,
        name="finish",
    )(shard.reshape(1), hidden, down, hidden_grad, input_part, both, both_from, grad_down, down_from, grad_qkv, grad_out)


def rope_tables():
    half = HEAD_DIM // 2
    positions = jnp.arange(SEQ_LEN, dtype=jnp.int32).astype(jnp.float32)
    column = jnp.arange(half, dtype=jnp.int32)
    inverse = jnp.power(jnp.float32(rope_base), -2.0 * column.astype(jnp.float32) / HEAD_DIM)
    angle = positions[None, :] * inverse[:, None]
    return (jnp.cos(angle), jnp.sin(angle))


def make_body(mesh):
    chips, shards = mesh.shape["tp"] // 2, mesh.shape["fsdp"]

    def body(activations, gain_attn, w_query, w_key, w_value, w_out, gain_mlp, w_gate, w_up, w_down, cotangent):
        gain_attn, gain_mlp = gain_attn[None, :], gain_mlp[None, :]
        seen_attn, w_qkv, full_out, qkv, keys_t, values_t, cosine, sine, down_near = project(
            chips, shards, activations, gain_attn, w_query, w_key, w_value, w_out, *rope_tables(), w_down
        )
        hidden_state, normed_mlp, mixed, totals, seen_grad, gate_all, up_all, down_far = attend(
            chips, shards, qkv, values_t, full_out, activations, cotangent, gain_mlp, w_gate, w_up, down_near
        )
        hidden_grad, branch_grad, gain_part, inner, grad_both, terms = feed(
            chips, shards, hidden_state, cotangent, gain_mlp, normed_mlp, seen_grad,
            w_gate, w_up, w_down, gate_all, up_all, down_near, down_far,
        )
        down, _, qkv_grad, grad_down, grad_out, both_from = back(
            chips, shards, branch_grad, terms, inner, seen_grad, grad_both, full_out, qkv, keys_t, mixed, totals, cosine, sine
        )
        input_part, grad_qkv, gain_sums, down_from = spread(
            chips, shards, qkv_grad, w_qkv, activations, gain_attn, gain_part, seen_attn, grad_down
        )
        output, input_grad, grad_query, grad_key, grad_value, grad_out, grad_gate, grad_up, grad_down = finish(
            lax.axis_index("fsdp"), hidden_state, down, hidden_grad, input_part,
            grad_both, both_from, grad_down, down_from, grad_qkv, grad_out,
        )
        return (
            output, input_grad, gain_sums[0], grad_query, grad_key, grad_value, grad_out, gain_sums[1],
            grad_gate, grad_up, grad_down,
        )

    return body


def solution(mesh):
    tokens = P(("fsdp", "tp"), None)
    column = P("fsdp", "tp")
    row = P("tp", "fsdp")
    in_specs = (tokens, P(), column, column, column, row, P(), column, column, row, tokens)
    out_specs = (tokens, tokens, P(), column, column, column, row, P(), column, column, row)
    return jax.shard_map(make_body(mesh), mesh=mesh, in_specs=in_specs, out_specs=out_specs, check_vma=False)
```

```python
import jax
import jax.numpy as jnp
from jax import lax
from jax.experimental import pallas as pl
from jax.experimental.pallas import tpu as pltpu
from jax.sharding import PartitionSpec as P

HEAD_DIM = 64
SEQ_LEN = 2048
LANES = 128
rope_base = 130000.0
norm_eps = 1e-05
masked_score = -1e30

NT = (((1,), (1,)), ((), ()))
NN = (((1,), (0,)), ((), ()))
TN = (((0,), (0,)), ((), ()))
MESH = pl.DeviceIdType.MESH
DMA = pltpu.SemaphoreType.DMA
ANYWHERE = pl.BlockSpec(memory_space=pl.ANY)
VMEM = pl.BlockSpec(memory_space=pltpu.VMEM)
low = jnp.bfloat16


def dot(left, right, dims=NN):
    return lax.dot_general(left, right, dims, preferred_element_type=jnp.float32)


def span(index, size):
    return pl.ds(pl.multiple_of(index * size, size), size)


def remote(source, target, send, receive, device):
    return pltpu.make_async_remote_copy(
        src_ref=source, dst_ref=target, send_sem=send, recv_sem=receive,
        device_id=device, device_id_type=MESH,
    )


def hello(device):
    pl.semaphore_signal(pltpu.get_barrier_semaphore(), inc=1, device_id=device, device_id_type=MESH)


class Line:
    def __init__(self, chips):
        self.chips = chips
        self.me = lax.axis_index("tp")
        self.chip, self.core = self.me // 2, self.me % 2
        self.partner = 2 * self.chip + 1 - self.core
        self.has_left, self.has_right = self.chip > 0, self.chip < chips - 1

    def greet(self, more=()):
        hello({"tp": self.partner})

        @pl.when(self.has_left)
        def _():
            hello({"tp": self.me - 2})

        @pl.when(self.has_right)
        def _():
            hello({"tp": self.me + 2})

        for device in more:
            hello(device)
        count = 1 + len(more) + jnp.where(self.has_left, 1, 0) + jnp.where(self.has_right, 1, 0)
        pl.semaphore_wait(pltpu.get_barrier_semaphore(), count)

    def target(self, step):
        after = self.chips - 1 - self.chip
        most, least = jnp.maximum(self.chip, after), jnp.minimum(self.chip, after)
        sign = jnp.where(after >= self.chip, 1, -1)
        late = step - (most - least)
        side = jnp.where(late % 2 == 0, sign, -sign)
        return jnp.where(late < 0, self.chip + sign * (most - step), self.chip + side * (least - late // 2))


    def fed(self, target):
        after, before = jnp.logical_and(target >= self.chip, self.has_left), jnp.logical_and(target <= self.chip, self.has_right)
        return jnp.logical_or(after, before)


class Gather:
    scratch = staticmethod(lambda chips: [DMA((2 * chips,)), DMA((chips,)), DMA((chips,)), DMA((chips,)), DMA])

    def __init__(self, line, own, out, received, right, left, across, local):
        self.line, self.own, self.out = line, own, out
        self.received, self.right, self.left, self.across, self.local = received, right, left, across, local
        self.rows = own.shape[0]

    def block(self, index):
        return self.out.at[span(index, self.rows)]

    def copy(self, source, sems, chip, device, mine):
        index = 2 * chip + self.line.core
        return remote(source if mine else self.block(index), self.block(index), sems.at[chip], self.received.at[index], {"tp": device})

    def keep(self):
        return pltpu.make_async_copy(self.own, self.block(self.line.me), self.local)

    def start(self):
        line = self.line
        self.keep().start()

        @pl.when(line.has_right)
        def _():
            self.copy(self.own, self.right, line.chip, line.me + 2, True).start()

        @pl.when(line.has_left)
        def _():
            self.copy(self.own, self.left, line.chip, line.me - 2, True).start()

        self.copy(self.own, self.across, line.chip, line.partner, True).start()

    def arrive(self, index):
        remote(self.own, self.block(index), self.right.at[0], self.received.at[index], {"tp": self.line.partner}).wait_recv()

    def arrive_across(self, chip):
        self.arrive(2 * chip + 1 - self.line.core)

    def step(self, distance):
        line = self.line
        before, after = line.chip - distance, line.chip + distance

        @pl.when(before >= 0)
        def _():
            self.arrive(2 * before + line.core)

            @pl.when(line.has_right)
            def _():
                self.copy(None, self.right, before, line.me + 2, False).start()

            self.copy(None, self.across, before, line.partner, False).start()

        @pl.when(after < line.chips)
        def _():
            self.arrive(2 * after + line.core)

            @pl.when(line.has_left)
            def _():
                self.copy(None, self.left, after, line.me - 2, False).start()

            self.copy(None, self.across, after, line.partner, False).start()

    def finish(self, arrivals):
        line = self.line
        if arrivals:
            self.keep().wait()
        for chip in range(line.chips):
            if arrivals:
                self.arrive_across(chip)
            self.copy(self.own, self.across, chip, line.partner, True).wait_send()

            @pl.when(jnp.logical_and(line.has_right, chip <= line.chip))
            def _():
                self.copy(self.own, self.right, chip, line.me + 2, True).wait_send()

            @pl.when(jnp.logical_and(line.has_left, chip >= line.chip))
            def _():
                self.copy(self.own, self.left, chip, line.me - 2, True).wait_send()


class Scatter:
    @staticmethod
    def scratch(chips, rows, depth):
        shares = min(chips, 4)
        return [
            pltpu.VMEM((2, 2 * rows, depth), low),
            pltpu.VMEM((shares, rows, depth), low),
            pltpu.VMEM((chips + 1, rows, depth), low),
            pltpu.VMEM((2, rows, depth), low),
            DMA((2,)), DMA((shares,)), DMA((2,)), DMA((chips + 1,)),
        ]

    def __init__(self, line, out, term, shares, lines, total, share_send, share_recv, line_send, line_recv):
        self.line, self.out = line, out
        self.term, self.shares, self.lines, self.total = term, shares, lines, total
        self.share_send, self.share_recv, self.line_send, self.line_recv = share_send, share_recv, line_send, line_recv
        self.rows = out.shape[0]

    def share(self, step):
        slot = step % self.shares.shape[0]
        source = self.term.at[step % 2, span(1 - self.line.core, self.rows)]
        return remote(source, self.shares.at[slot], self.share_send.at[step % 2], self.share_recv.at[slot], {"tp": self.line.partner})

    def mine(self, step):
        return self.term[step % 2, span(self.line.core, self.rows), :]

    def pass_on(self, step):
        line, target = self.line, self.line.target(step)
        onward = target > line.chip
        slot = jnp.where(onward, target, jnp.where(target == line.chip - 1, line.chips, target))
        device = jnp.where(onward, line.me + 2, line.me - 2)
        return remote(self.total.at[step % 2], self.lines.at[slot], self.line_send.at[step % 2], self.line_recv.at[slot], {"tp": device})

    def add(self, slot):
        remote(self.total.at[0], self.lines.at[slot], self.line_send.at[0], self.line_recv.at[slot], {"tp": self.line.partner}).wait_recv()
        self.out[...] += self.lines[slot].astype(jnp.float32)

    def free(self, step):
        @pl.when(step >= 2)
        def _():
            self.share(step - 2).wait_send()

    def step(self, step):
        line, target = self.line, self.line.target(step)
        self.share(step).wait_recv()
        self.out[...] = self.mine(step).astype(jnp.float32) + self.shares[step % self.shares.shape[0]].astype(jnp.float32)

        @pl.when(jnp.logical_and(target >= line.chip, line.has_left))
        def _():
            self.add(target)

        @pl.when(jnp.logical_and(target <= line.chip, line.has_right))
        def _():
            self.add(jnp.where(target == line.chip, line.chips, target))

        @pl.when(step < line.chips - 1)
        def _():
            @pl.when(step >= 2)
            def _():
                self.pass_on(step - 2).wait_send()

            self.total[step % 2] = self.out[...].astype(low)
            self.pass_on(step).start()

    def finish(self):
        chips = self.line.chips
        for step in range(max(0, chips - 3), chips - 1):
            self.pass_on(step).wait_send()
        for step in range(max(0, chips - 2), chips):
            self.share(step).wait_send()


NORM_ROWS = 64


def normed(value, gain):
    return value * lax.rsqrt(jnp.mean(value * value, axis=-1, keepdims=True) + norm_eps) * gain


def norm_back(value, gain, grad):
    scale = lax.rsqrt(jnp.mean(value * value, axis=-1, keepdims=True) + norm_eps)
    unit = value * scale
    scaled = grad * gain
    return scale * (scaled - unit * jnp.mean(scaled * unit, axis=-1, keepdims=True)), jnp.sum(grad * unit, axis=0, keepdims=True)


def by_rows(rows, work):
    def step(index, carry):
        work(span(index, NORM_ROWS))
        return carry

    lax.fori_loop(0, rows // NORM_ROWS, step, 0)


class Grid:
    def __init__(self, shards):
        self.shards, self.across = shards, shards // 2
        self.me = lax.axis_index("fsdp")
        self.row, self.column = self.me // self.across, self.me % self.across
        self.others = [(self.me + ahead) % shards for ahead in range(1, shards)]
        self.mates = [self.row * self.across + (self.column + ahead) % self.across for ahead in range(1, self.across)]
        self.twin = (1 - self.row) * self.across + self.column
        self.near = self.mates + [self.twin]

    def is_near(self, shard):
        return jnp.logical_or(shard // self.across == self.row, shard % self.across == self.column)


class NearShards:
    scratch = staticmethod(lambda shards: [DMA((shards // 2,)), DMA((shards // 2,))])

    def __init__(self, grid, own, whole, at, send, receive):
        place = at(whole, grid.me, None)
        self.copies = [remote(own, place, send.at[i], receive.at[i], {"fsdp": peer}) for i, peer in enumerate(grid.near)]

    def start(self):
        for copy in self.copies:
            copy.start()

    def arrive(self):
        for copy in self.copies:
            copy.wait_recv()

    def finish(self):
        for copy in self.copies:
            copy.wait_send()


class FarShards:
    scratch = staticmethod(lambda shards: [DMA((2, shards // 2 - 1)), DMA((2, shards // 2 - 1))])

    def __init__(self, grid, near, whole, at, send, receive):
        self.copies = []
        for i, mate in enumerate(grid.mates):
            self.copies.append(remote(at(near, mate, 0), at(whole, mate, 0), send.at[0, i], receive.at[0, i], {"fsdp": grid.twin}))
            self.copies.append(remote(at(near, grid.twin, 1), at(whole, grid.twin, 1), send.at[1, i], receive.at[1, i], {"fsdp": mate}))

    def start(self):
        for copy in self.copies:
            copy.start()

    def finish(self):
        for copy in self.copies:
            copy.wait_recv()
            copy.wait_send()


class NearSums:
    @staticmethod
    def scratch(shards, rows, columns):
        across = shards // 2
        return [
            pltpu.VMEM((2, across - 1, rows // 2, columns), low),
            pltpu.VMEM((across, rows // 2, columns), low),
            DMA((2, across - 1)), DMA((2, across - 1)), DMA((across, 2)), DMA((across, 2)), DMA((across,)),
        ]

    def __init__(self, grid, part, out, at, relay, base, relay_send, relay_recv, near_send, near_recv, load_sem):
        self.relay, self.base = relay, base
        last = grid.across - 1
        half = base.shape[1]

        def near(source, slot, which, peer):
            target = out.at[slot, pl.ds(which * half, half)]
            return remote(source, target, near_send.at[slot, which], near_recv.at[slot, which], {"fsdp": peer})

        self.by_twin, self.by_mate, self.plain, self.joined, self.loads = [], [], [], [], []
        for i, mate in enumerate(grid.mates):
            far = (1 - grid.row) * grid.across + mate % grid.across
            self.by_twin.append(remote(at(part, far, 0), relay.at[0, i], relay_send.at[0, i], relay_recv.at[0, i], {"fsdp": grid.twin}))
            self.by_mate.append(remote(at(part, far, 1), relay.at[1, i], relay_send.at[1, i], relay_recv.at[1, i], {"fsdp": mate}))
            self.plain.append(near(at(part, mate, 1), i, 1, mate))
            self.joined.append(near(relay.at[0, i], i, 0, mate))
            self.loads.append(pltpu.make_async_copy(at(part, mate, 0), base.at[i], load_sem.at[i]))
        self.plain.append(near(at(part, grid.twin, 0), last, 0, grid.twin))
        self.joined.append(near(relay.at[1, 0], last, 1, grid.twin))
        self.loads.append(pltpu.make_async_copy(at(part, grid.twin, 1), base.at[last], load_sem.at[last]))

    def start(self):
        for copy in self.by_twin + self.by_mate + self.loads:
            copy.start()

    def start_plain(self):
        for copy in self.plain:
            copy.start()

    def join(self):
        for copy in self.by_twin + self.by_mate:
            copy.wait_recv()
        for copy in self.loads:
            copy.wait()
        last = self.base.shape[0] - 1
        for i in range(last):
            self.relay[0, i] = (self.base[i].astype(jnp.float32) + self.relay[0, i].astype(jnp.float32)).astype(low)
        total = self.base[last].astype(jnp.float32)
        for i in range(last):
            total = total + self.relay[1, i].astype(jnp.float32)
        self.relay[1, 0] = total.astype(low)
        for copy in self.joined:
            copy.start()

    def finish(self):
        for copy in self.by_twin + self.by_mate:
            copy.wait_send()
        for copy in self.plain + self.joined:
            copy.wait_recv()
            copy.wait_send()


def row_shard(depth):
    def at(ref, shard, half):
        if half is None:
            return ref.at[span(shard, depth)]
        return ref.at[span(2 * shard + half, depth // 2)]

    return at


def column_shard(rows, width):
    def at(ref, shard, half):
        if half is None:
            return ref.at[:, span(shard, width)]
        return ref.at[pl.ds(half * (rows // 2), rows // 2), span(shard, width)]

    return at


class HeldScatter(Scatter):
    @staticmethod
    def scratch(chips, rows, depth):
        return [
            pltpu.VMEM((2, rows, depth), low),
            pltpu.VMEM((chips, rows, depth), low),
            pltpu.VMEM((chips + 1, rows, depth), low),
            pltpu.VMEM((2, rows, depth), low),
            DMA((2,)), DMA((chips,)), DMA((2,)), DMA((chips + 1,)), DMA((2,)),
        ]

    def __init__(self, line, out, held, *refs):
        super().__init__(line, out, *refs[:-1])
        self.held, self.load_sem = held, refs[-1]

    def load(self, step):
        source = self.held.at[span(2 * self.line.target(step) + self.line.core, self.rows)]
        return pltpu.make_async_copy(source, self.term.at[step % 2], self.load_sem.at[step % 2])

    def share(self, step):
        slot = step % self.shares.shape[0]
        source = self.held.at[span(2 * self.line.target(step) + 1 - self.line.core, self.rows)]
        return remote(source, self.shares.at[slot], self.share_send.at[step % 2], self.share_recv.at[slot], {"tp": self.line.partner})

    def mine(self, step):
        self.load(step).wait()

        @pl.when(step < self.line.chips - 1)
        def _():
            self.load(step + 1).start()

        return self.term[step % 2]


class Loads:
    @staticmethod
    def scratch(*operands):
        return [pltpu.VMEM(a.shape, a.dtype) for a in operands] + [DMA((len(operands),))]

    def __init__(self, sources, refs):
        self.refs = refs[: len(sources)]
        self.copies = [pltpu.make_async_copy(source, ref, refs[-1].at[i]) for i, (source, ref) in enumerate(zip(sources, self.refs))]

    def start(self):
        for copy in self.copies:
            copy.start()

    def wait(self, *which):
        for i in which:
            self.copies[i].wait()


def turned(block, sign):
    half = HEAD_DIM // 2
    lane = lax.broadcasted_iota(jnp.int32, block.shape, 1)
    width = block.shape[1]
    up = pltpu.roll(block, width - half, 1)
    down = pltpu.roll(block, half, 1)
    return jnp.where(lane % HEAD_DIM < half, -sign * up, sign * down)


def widened(table, width):
    return table if table.shape[1] == width else jnp.concatenate([table] * (width // table.shape[1]), axis=1)


def only_head(block, head):
    lane = lax.broadcasted_iota(jnp.int32, block.shape, 1)
    return jnp.where(lane // HEAD_DIM == head, block, jnp.zeros_like(block))


def causal(tile):
    key = lax.broadcasted_iota(jnp.int32, tile.shape, 0)
    query = lax.broadcasted_iota(jnp.int32, tile.shape, 1)
    return jnp.where(key <= query, tile, masked_score)


def over_keys(chunk, rows, visit):
    start = chunk * rows
    first = start // SEQ_LEN * SEQ_LEN

    def step(index, carry):
        visit(pl.multiple_of(first + index * rows, rows), False)
        return carry

    lax.fori_loop(0, (start - first) // rows, step, 0)
    visit(pl.multiple_of(start, rows), True)


def project_kernel(
    chips, shards,
    activations, gain, w_query, w_key, w_value, w_out, cosine_t, sine_t, w_down,
    tokens_out, weight_out, full_out, qkv_out, keys_out, values_out, cosine_out, sine_out, down_near,
    weight, out_w, qkv, keys_t, values_t, cosine, sine, tokens, chunks,
    chunk_sem, weight_send, weight_recv, weight_keep, table_sem, store_sem, near_send, near_recv, *gather_sems,
):
    line = Line(chips)
    rows = tokens.shape[0]
    pair = 2 * rows
    depth, width = w_query.shape
    grid = Grid(shards)
    shard, others = grid.me, grid.others
    gather = Gather(line, tokens, tokens_out, *gather_sems)
    down = NearShards(grid, w_down, down_near, column_shard(*w_down.shape), near_send, near_recv)
    parts = (w_query, w_key, w_value, w_out)

    def place(part):
        if part == 3:
            return out_w.at[:, span(shard, depth)]
        return weight.at[span(shard, depth), pl.ds(part * width, width)]

    def give(ahead, part):
        return remote(parts[part], place(part), weight_send.at[ahead, part], weight_recv.at[ahead, part], {"fsdp": others[ahead]})

    def keep(part):
        return pltpu.make_async_copy(parts[part], place(part), weight_keep.at[part])

    tables = [
        pltpu.make_async_copy(source, out, table_sem.at[i])
        for i, (source, out) in enumerate(((cosine, cosine_out), (sine, sine_out), (weight, weight_out), (out_w, full_out)))
    ]

    def stores(chip):
        here = span(chip, pair)
        return [
            pltpu.make_async_copy(qkv.at[here], qkv_out.at[here], store_sem.at[0, chip]),
            pltpu.make_async_copy(keys_t.at[:, here], keys_out.at[:, here], store_sem.at[1, chip]),
            pltpu.make_async_copy(values_t.at[:, here], values_out.at[:, here], store_sem.at[2, chip]),
        ]

    def norm(here):
        tokens[here, :] = normed(activations[here, :], gain[...]).astype(low)

    by_rows(rows, norm)
    line.greet([{"fsdp": other} for other in others])
    gather.start()
    for part in range(4):
        keep(part).start()
        for ahead in range(shards - 1):
            give(ahead, part).start()
    for table, table_t in ((cosine, cosine_t), (sine, sine_t)):
        turn = table_t[...].T
        table[...] = jnp.concatenate([turn] * (LANES // turn.shape[1]), axis=1)
    for copy in tables[:2]:
        copy.start()

    def project(chip):
        @pl.when(jnp.logical_and(chip >= 0, chip < chips))
        def _():
            gather.arrive_across(chip)
            load = pltpu.make_async_copy(tokens_out.at[span(chip, pair)], chunks, chunk_sem)
            load.start()
            load.wait()
            here = span(chip, pair)
            table = span(chip % (SEQ_LEN // pair), pair)
            for part in range(3):
                columns = pl.ds(part * width, width)
                block = dot(chunks[...], weight[:, columns])
                if part < 2:
                    block = block * widened(cosine[table, :], width) + turned(block, 1.0) * widened(sine[table, :], width)
                qkv[here, columns] = block.astype(low)
                if part:
                    (keys_t, values_t)[part - 1][:, here] = block.T.astype(low)
            for copy in stores(chip):
                copy.start()

    def step(index, carry):
        @pl.when(jnp.logical_and(index >= 1, index < chips))
        def _():
            gather.step(index)

        @pl.when(index == 2)
        def _():
            gather.keep().wait()
            for part in range(4):
                keep(part).wait()
                for ahead in range(shards - 1):
                    give(ahead, part).wait_recv()
            for copy in tables[2:]:
                copy.start()
            down.start()

        def side(which, carry):
            distance = index - 1
            chip = jnp.where(which == 0, line.chip - distance, jnp.where(which == 1, line.chip + distance, line.chip))

            @pl.when(jnp.logical_and(index >= 2, jnp.logical_or(which < 2, index == 2)))
            def _():
                project(chip)

            return carry

        lax.fori_loop(0, 3, side, 0)
        return carry

    lax.fori_loop(0, chips + 1, step, 0)
    gather.finish(False)
    for part in range(4):
        for ahead in range(shards - 1):
            give(ahead, part).wait_send()
    for copy in tables:
        copy.wait()
    for chip in range(chips):
        for copy in stores(chip):
            copy.wait()
    down.arrive()
    down.finish()


def project(chips, shards, activations, gain, w_query, w_key, w_value, w_out, cosine_t, sine_t, w_down):
    rows, depth = activations.shape
    group_rows = 2 * chips * rows
    width = w_query.shape[1]
    shape = jax.ShapeDtypeStruct
    held = [
        shape((depth, 3 * width), low),
        shape((width, depth), low),
        shape((group_rows, 3 * width), low),
        shape((width, group_rows), low),
        shape((width, group_rows), low),
        shape((SEQ_LEN, LANES), jnp.float32),
        shape((SEQ_LEN, LANES), jnp.float32),
    ]
    return pl.pallas_call(
        lambda *refs: project_kernel(chips, shards, *refs),
        in_specs=[VMEM] * 8 + [ANYWHERE],
        out_specs=[ANYWHERE] * 9,
        out_shape=[shape((group_rows, depth), low)] + held + [shape((w_down.shape[0], depth), low)],
        scratch_shapes=[pltpu.VMEM(a.shape, a.dtype) for a in held] + [
            pltpu.VMEM((rows, depth), low),
            pltpu.VMEM((2 * rows, depth), low),
            DMA, DMA((shards - 1, 4)), DMA((shards - 1, 4)), DMA((4,)), DMA((4,)), DMA((3, chips)),
        ] + NearShards.scratch(shards) + Gather.scratch(chips),
        compiler_params=pltpu.CompilerParams(collective_id=1, has_side_effects=True, vmem_limit_bytes=63 << 20),
        cost_estimate=pl.CostEstimate(flops=6 * group_rows * depth * width, bytes_accessed=4 * group_rows * depth, transcendentals=0),
        name="project",
    )(activations, gain, w_query, w_key, w_value, w_out, cosine_t, sine_t, w_down)


def attend_chunk(chunk, rows, qkv, values_t, heads_ref, acc, out, top_ref, sum_ref):
    width = acc.shape[0]
    heads = width // HEAD_DIM
    scaled = qkv[span(chunk, rows), pl.ds(0, width)] * low(HEAD_DIM**-0.5)
    for head in range(heads):
        heads_ref[head] = only_head(scaled, head)
    acc[...] = jnp.zeros_like(acc)
    top_ref[...] = jnp.full_like(top_ref, masked_score)
    sum_ref[...] = jnp.zeros_like(sum_ref)

    def visit(offset, diagonal):
        key_block = qkv[pl.ds(offset, rows), pl.ds(width, width)]
        for head in range(heads):
            feature = pl.ds(head * HEAD_DIM, HEAD_DIM)
            one = pl.ds(head, 1)
            scores = dot(key_block, heads_ref[head], NT)
            if diagonal:
                scores = causal(scores)
            old = top_ref[one, :]
            top = jnp.maximum(old, jnp.max(scores, axis=0, keepdims=True))
            shrink = jnp.exp(old - top)
            weights = jnp.exp(scores - top)
            top_ref[one, :] = top
            sum_ref[one, :] = sum_ref[one, :] * shrink + jnp.sum(weights, axis=0, keepdims=True)
            acc[feature, :] = acc[feature, :] * shrink + dot(values_t[feature, pl.ds(offset, rows)], weights.astype(low))

    over_keys(chunk, rows, visit)
    for head in range(heads):
        feature = pl.ds(head * HEAD_DIM, HEAD_DIM)
        acc[feature, :] = acc[feature, :] / sum_ref[pl.ds(head, 1), :]
    out[...] = acc[...].T.astype(low)


def attend_kernel(
    chips, shards,
    cotangent, gain, *refs,
):
    sources, (w_gate, w_up, down_near) = refs[:4], refs[4:7]
    hidden, tokens, mixed, totals, grads_out, gate_all, up_all, down_far = refs[7:15]
    loads = Loads(sources, refs[15:20])
    qkv, values_t, w_out, activations = loads.refs
    heads_ref, acc, out, top_ref, sum_ref, grads = refs[20:26]
    grid = Grid(shards)
    rows_of = row_shard(w_gate.shape[0])
    down = FarShards(grid, down_near, down_far, column_shard(down_near.shape[0], down_near.shape[1] // shards), *refs[26:28])
    gate_near, gate_far = NearShards(grid, w_gate, gate_all, rows_of, *refs[28:30]), FarShards(grid, gate_all, gate_all, rows_of, *refs[30:32])
    up_near, up_far = NearShards(grid, w_up, up_all, rows_of, *refs[32:34]), FarShards(grid, up_all, up_all, rows_of, *refs[34:36])
    sems = refs[36:]
    loads.start()
    line = Line(chips)
    rows, depth = hidden.shape
    pair = 2 * rows
    scatter = Scatter(line, hidden, *sems[:8])
    grads[...] = cotangent[...].astype(low)
    gather = Gather(line, grads, grads_out, *sems[8:])
    line.greet([{"fsdp": peer} for peer in grid.near])
    gather.start()
    gate_near.start()
    down.start()
    loads.wait(0, 1, 2, 3)

    def step(index, carry):
        work = jnp.where(index == chips, chips - 1, index)

        @pl.when(jnp.logical_or(index < chips - 1, index == chips))
        def _():
            chunk = line.target(work)
            attend_chunk(chunk, pair, qkv, values_t, heads_ref, acc, out, top_ref, sum_ref)
            mixed[span(chunk, pair), :] = out[...]
            totals[:, span(chunk, pair)] = top_ref[...] + jnp.log(sum_ref[...])
            scatter.free(work)

            def tile(place, carry):
                columns = span(place, 512)
                scatter.term[work % 2, :, columns] = dot(out[...], w_out[:, columns]).astype(low)
                return carry

            lax.fori_loop(0, depth // 512, tile, 0)
            scatter.share(work).start()

        @pl.when(jnp.logical_and(index >= 1, index < chips))
        def _():
            gather.step(index)

        @pl.when(index == 1)
        def _():
            up_near.start()

        @pl.when(index == min(2, chips))
        def _():
            gate_near.arrive()
            gate_far.start()

        @pl.when(index == min(3, chips))
        def _():
            up_near.arrive()
            up_far.start()

        @pl.when(index >= 1)
        def _():
            scatter.step(index - 1)

        return carry

    lax.fori_loop(0, chips + 1, step, 0)

    def norm(here):
        state = activations[here, :] + hidden[here, :]
        hidden[here, :] = state
        tokens[here, :] = normed(state, gain[...]).astype(low)

    by_rows(rows, norm)
    scatter.finish()
    gather.finish(True)
    for near in (gate_near, up_near):
        near.finish()
    for far in (down, gate_far, up_far):
        far.finish()


def attend(chips, shards, qkv, values_t, w_out, activations, cotangent, gain, w_gate, w_up, down_near):
    rows, depth = activations.shape
    pair = 2 * rows
    group_rows = chips * pair
    width = w_out.shape[0]
    heads = width // HEAD_DIM
    shape = jax.ShapeDtypeStruct
    return pl.pallas_call(
        lambda *refs: attend_kernel(chips, shards, *refs),
        in_specs=[VMEM] * 2 + [ANYWHERE] * 7,
        out_specs=[VMEM] * 4 + [ANYWHERE] * 4,
        out_shape=[
            shape((rows, depth), jnp.float32),
            shape((rows, depth), low),
            shape((group_rows, width), low),
            shape((heads, group_rows), jnp.float32),
            shape((group_rows, depth), low),
            shape((depth, w_gate.shape[1]), low),
            shape((depth, w_gate.shape[1]), low),
            shape(down_near.shape, low),
        ],
        scratch_shapes=Loads.scratch(qkv, values_t, w_out, activations) + [
            pltpu.VMEM((heads, pair, width), low),
            pltpu.VMEM((width, pair), jnp.float32),
            pltpu.VMEM((pair, width), low),
            pltpu.VMEM((heads, pair), jnp.float32),
            pltpu.VMEM((heads, pair), jnp.float32),
            pltpu.VMEM((rows, depth), low),
        ] + FarShards.scratch(shards) + (NearShards.scratch(shards) + FarShards.scratch(shards)) * 2 + Scatter.scratch(chips, rows, depth) + Gather.scratch(chips),
        compiler_params=pltpu.CompilerParams(collective_id=2, has_side_effects=True, vmem_limit_bytes=63 << 20),
        cost_estimate=pl.CostEstimate(flops=2 * group_rows * (SEQ_LEN + depth) * width, bytes_accessed=4 * group_rows * depth, transcendentals=group_rows * SEQ_LEN * heads // 2),
        name="attend",
    )(cotangent, gain, qkv, values_t, w_out, activations, w_gate, w_up, down_near)


def back_chunk(chunk, rows, grad, qkv, keys_t, mixed, totals, dkey, dvalue, heads_ref, grads_ref, acc, inner_ref):
    width = acc.shape[0]
    heads = width // HEAD_DIM
    here = span(chunk, rows)
    scaled = qkv[here, pl.ds(0, width)] * low(HEAD_DIM**-0.5)
    product = grad.astype(jnp.float32) * mixed[here, :].astype(jnp.float32)
    shape = (inner_ref.shape[0], width)
    pick = (lax.broadcasted_iota(jnp.int32, shape, 1) // HEAD_DIM == lax.broadcasted_iota(jnp.int32, shape, 0)).astype(jnp.float32)
    inner_ref[...] = lax.dot_general(pick, product, NT, precision=lax.Precision.HIGHEST, preferred_element_type=jnp.float32)
    for head in range(heads):
        heads_ref[head] = only_head(scaled, head)
        grads_ref[head] = only_head(grad, head)
    acc[...] = jnp.zeros_like(acc)

    def visit(offset, diagonal):
        keys = pl.ds(offset, rows)
        key_block = qkv[keys, pl.ds(width, width)]
        value_block = qkv[keys, pl.ds(2 * width, width)]
        key_sum, value_sum = dkey[keys, :], dvalue[keys, :]
        for head in range(heads):
            feature = pl.ds(head * HEAD_DIM, HEAD_DIM)
            scores = dot(key_block, heads_ref[head], NT)
            if diagonal:
                scores = causal(scores)
            probs = jnp.exp(scores - totals[pl.ds(head, 1), here])
            dprobs = dot(value_block, grads_ref[head], NT)
            dscores = (probs * (dprobs - inner_ref[pl.ds(head, 1), :])).astype(low)
            value_sum = value_sum + dot(probs.astype(low), grads_ref[head])
            key_sum = key_sum + dot(dscores, heads_ref[head])
            acc[feature, :] = acc[feature, :] + dot(keys_t[feature, keys], dscores)
        dkey[keys, :] = key_sum
        dvalue[keys, :] = value_sum

    over_keys(chunk, rows, visit)


def back_kernel(
    chips, shards,
    branch, terms, inner, grads, grad_both, *refs,
):
    sources, (down, branch_out, qkv_grad, grad_down, grad_out, both_from) = refs[:7], refs[7:13]
    loads = Loads(sources, refs[13:21])
    w_out, qkv, keys_t, mixed, totals, cosine, sine = loads.refs
    inner_chunk, grad_chunk, down_sum, down_tile, out_sum, out_stage, out_from, branch_chunk, dkey, dvalue = refs[21:31]
    heads_ref, grads_ref, acc, inner_ref, inner_sem, grad_sem, branch_sem, tile_sem, out_send, out_recv = refs[31:41]
    sums = refs[41:48]
    sems = refs[48:]
    line = Line(chips)
    rows, depth = down.shape
    pair = 2 * rows
    width = w_out.shape[0]
    scatter = HeldScatter(line, down, terms, *sems[:9])
    gather = Gather(line, branch, branch_out, *sems[9:])

    def fetch(step):
        return pltpu.make_async_copy(inner.at[span(line.target(step), pair)], inner_chunk, inner_sem)

    def fetch_grad(step):
        return pltpu.make_async_copy(grads.at[span(line.target(step), pair)], grad_chunk, grad_sem)

    grid = Grid(shards)
    shard, others = grid.me, grid.others
    columns_out = depth // shards
    both = NearSums(grid, grad_both, both_from, row_shard(columns_out), *sums)

    def give(turn):
        return remote(out_stage.at[turn], out_from.at[turn], out_send.at[turn], out_recv.at[turn], {"fsdp": others[turn]})

    def keep_tile(place):
        return pltpu.make_async_copy(down_tile, grad_down.at[span(place, 256)], tile_sem)

    loads.start()
    fetch(0).start()
    fetch_grad(0).start()
    scatter.load(0).start()
    line.greet([{"fsdp": other} for other in others])
    gather.start()
    both.start()
    out_sum[...] = jnp.zeros_like(out_sum)
    dkey[...] = jnp.zeros_like(dkey)
    dvalue[...] = jnp.zeros_like(dvalue)

    def unrotated(block, chunk):
        table = span(chunk % (SEQ_LEN // pair), pair)
        return (block * widened(cosine[table, :], width) + turned(block * widened(sine[table, :], width), -1.0)).astype(low)

    def attention(chunk):
        gather.arrive_across(chunk)
        copy = pltpu.make_async_copy(branch_out.at[span(chunk, pair)], branch_chunk, branch_sem)
        copy.start()
        copy.wait()
        out_sum[...] += dot(mixed[span(chunk, pair), :], branch_chunk[...], TN)
        grad = dot(branch_chunk[...], w_out[...], NT).astype(low)
        back_chunk(chunk, pair, grad, qkv, keys_t, mixed, totals, dkey, dvalue, heads_ref, grads_ref, acc, inner_ref)
        qkv_grad[span(chunk, pair), pl.ds(0, width)] = unrotated(acc[...].T * HEAD_DIM**-0.5, chunk)

    def close():
        def part(chunk, carry):
            here = span(chunk, pair)
            qkv_grad[here, pl.ds(width, width)] = unrotated(dkey[here, :], chunk)
            qkv_grad[here, pl.ds(2 * width, width)] = dvalue[here, :].astype(low)
            return carry

        lax.fori_loop(0, chips, part, 0)

    def step(index, carry):
        @pl.when(index == 0)
        def _():
            loads.wait(*range(7))
            gather.keep().wait()

        @pl.when(index < chips)
        def _():
            scatter.free(index)
            scatter.share(index).start()

        @pl.when(index == chips)
        def _():
            for turn in range(shards - 1):
                out_stage[turn] = out_sum[:, span(others[turn], columns_out)].astype(low)
                give(turn).start()
            close()

        def due(done, carry):
            target = line.target(done)
            distance = jnp.where(target > line.chip, target - line.chip, line.chip - target)

            @pl.when(distance == chips - index)
            def _():
                scatter.step(done)

            return carry

        lax.fori_loop(0, chips, due, 0)

        @pl.when(jnp.logical_and(index >= 1, index < chips))
        def _():
            gather.step(index)

        @pl.when(index == 1)
        def _():
            both.start_plain()

        @pl.when(index == 2)
        def _():
            both.join()

        @pl.when(index < chips)
        def _():
            attention(line.target(chips - 1 - index))

        def weights(turn, carry):
            fetch(turn).wait()
            fetch_grad(turn).wait()

            def tile(place, carry):
                here = span(place, 256)
                part = dot(inner_chunk[:, here], grad_chunk[...], TN)

                @pl.when(turn == 0)
                def _():
                    down_sum[here, :] = part

                @pl.when(turn > 0)
                def _():
                    down_sum[here, :] += part

                @pl.when(turn == chips - 1)
                def _():
                    @pl.when(place > 0)
                    def _():
                        keep_tile(place - 1).wait()

                    down_tile[...] = down_sum[here, :].astype(low)
                    keep_tile(place).start()

                return carry

            lax.fori_loop(0, down_sum.shape[0] // 256, tile, 0)

            @pl.when(turn < chips - 1)
            def _():
                fetch(turn + 1).start()
                fetch_grad(turn + 1).start()

            return carry

        lax.fori_loop(jnp.where(index == 0, 0, index + 1), jnp.minimum(index + 2, chips), weights, 0)
        return carry

    lax.fori_loop(0, chips + 1, step, 0)
    total = out_sum[:, span(shard, columns_out)]
    for turn in range(shards - 1):
        give(turn).wait_recv()
        total = total + out_from[turn].astype(jnp.float32)
    grad_out[...] = total
    for turn in range(shards - 1):
        give(turn).wait_send()
    keep_tile(down_sum.shape[0] // 256 - 1).wait()
    both.finish()
    scatter.finish()
    gather.finish(False)


def back(chips, shards, branch, terms, inner, grads, grad_both, w_out, qkv, keys_t, mixed, totals, cosine, sine):
    rows, depth = branch.shape
    pair = 2 * rows
    group_rows = chips * pair
    width = w_out.shape[0]
    hidden = inner.shape[1]
    heads = width // HEAD_DIM
    shape = jax.ShapeDtypeStruct
    held = (w_out, qkv, keys_t, mixed, totals, cosine, sine)
    return pl.pallas_call(
        lambda *refs: back_kernel(chips, shards, *refs),
        in_specs=[VMEM] + [ANYWHERE] * 11,
        out_specs=[VMEM, ANYWHERE, VMEM, ANYWHERE, VMEM, ANYWHERE],
        out_shape=[
            shape((rows, depth), jnp.float32),
            shape((group_rows, depth), low),
            shape((group_rows, 3 * width), low),
            shape((hidden, depth), low),
            shape((width, depth // shards), jnp.float32),
            shape((shards // 2, depth // shards, grad_both.shape[1]), low),
        ],
        scratch_shapes=Loads.scratch(*held) + [
            pltpu.VMEM((pair, hidden), low),
            pltpu.VMEM((pair, depth), low),
            pltpu.VMEM((hidden, depth), jnp.float32),
            pltpu.VMEM((256, depth), low),
            pltpu.VMEM((width, depth), jnp.float32),
            pltpu.VMEM((shards - 1, width, depth // shards), low),
            pltpu.VMEM((shards - 1, width, depth // shards), low),
            pltpu.VMEM((pair, depth), low),
            pltpu.VMEM((group_rows, width), jnp.float32),
            pltpu.VMEM((group_rows, width), jnp.float32),
            pltpu.VMEM((heads, pair, width), low),
            pltpu.VMEM((heads, pair, width), low),
            pltpu.VMEM((width, pair), jnp.float32),
            pltpu.VMEM((8, pair), jnp.float32),
            DMA, DMA, DMA, DMA, DMA((shards - 1,)), DMA((shards - 1,)),
        ] + NearSums.scratch(shards, depth // shards, grad_both.shape[1]) + HeldScatter.scratch(chips, rows, depth) + Gather.scratch(chips),
        compiler_params=pltpu.CompilerParams(collective_id=4, has_side_effects=True, vmem_limit_bytes=67043328),
        cost_estimate=pl.CostEstimate(flops=1 << 20, bytes_accessed=1 << 20, transcendentals=0),
        name="back",
    )(branch, terms, inner, grads, grad_both, *held)


def spread_kernel(
    chips, shards,
    gain, gain_part, qkv_hbm, weight_hbm, activations_hbm, attn_tokens, grad_down,
    input_part, grad_qkv, gain_sum, down_from,
    qkv_grad, weight, activations, held_sem,
    attn_cols, qkv_stage, qkv_from, gains, gains_tp, gains_fsdp,
    attn_sem, qkv_send, qkv_recv, tp_send, tp_recv, fsdp_send, fsdp_recv, *sems,
):
    line = Line(chips)
    size = 2 * chips
    rows, depth = input_part.shape
    pair = 2 * rows
    grid = Grid(shards)
    shard = grid.me
    columns = depth // shards
    loads = Loads((qkv_hbm, weight_hbm, activations_hbm), (qkv_grad, weight, activations, held_sem))
    down = NearSums(grid, grad_down, down_from, column_shard(grad_down.shape[0], columns), *sems[:7])
    scatter = Scatter(line, input_part, *sems[7:])

    def peer(turn):
        return (shard + 1 + turn) % shards

    def fetch(turn):
        return pltpu.make_async_copy(attn_tokens.at[:, span(peer(turn), columns)], attn_cols.at[turn % 2], attn_sem.at[turn % 2])

    def give(turn):
        return remote(qkv_stage.at[turn], qkv_from.at[turn], qkv_send.at[turn], qkv_recv.at[turn], {"fsdp": peer(turn)})

    def tell_tp(ahead):
        return remote(gains, gains_tp.at[line.me], tp_send.at[ahead - 1], tp_recv.at[line.me], {"tp": (line.me + ahead) % size})

    def tell_fsdp(ahead):
        return remote(gains, gains_fsdp.at[shard], fsdp_send.at[ahead - 1], fsdp_recv.at[shard], {"fsdp": (shard + ahead) % shards})

    loads.start()
    fetch(0).start()
    for ahead in range(1, size):
        hello({"tp": (line.me + ahead) % size})
    for ahead in range(1, shards):
        hello({"fsdp": (shard + ahead) % shards})
    pl.semaphore_wait(pltpu.get_barrier_semaphore(), size - 1 + shards - 1)
    down.start()
    loads.wait(0, 1)

    def weights(turn, carry):
        @pl.when(turn < shards - 1)
        def _():
            fetch(turn + 1).start()

        fetch(turn).wait()
        part = dot(attn_cols[turn % 2], qkv_grad[...], TN)

        @pl.when(turn < shards - 1)
        def _():
            qkv_stage[turn] = part.astype(low)
            give(turn).start()

        @pl.when(turn == shards - 1)
        def _():
            grad_qkv[...] = part

        return carry

    def step(index, carry):
        @pl.when(index < chips)
        def _():
            here = span(line.target(index), pair)
            scatter.free(index)

            def tile(place, carry):
                there = span(place, 512)
                scatter.term[index % 2, :, there] = dot(qkv_grad[here, :], weight[there, :], NT).astype(low)
                return carry

            lax.fori_loop(0, depth // 512, tile, 0)
            scatter.share(index).start()

        @pl.when(index == 1)
        def _():
            down.start_plain()

        @pl.when(index == 2)
        def _():
            down.join()

        def phase(which, carry):
            done = jnp.maximum(index - 1, 0)
            late = line.fed(line.target(done))
            turn = jnp.logical_or(jnp.logical_and(which == 0, jnp.logical_not(late)), jnp.logical_and(which == 2, late))

            @pl.when(jnp.logical_and(index >= 1, turn))
            def _():
                scatter.step(done)

            @pl.when(jnp.logical_and(which == 1, index < 2))
            def _():
                lax.fori_loop(index, jnp.where(index == 0, 1, shards), weights, 0)

            return carry

        lax.fori_loop(0, 3, phase, 0)
        return carry

    lax.fori_loop(0, chips + 1, step, 0)
    gains[0:1, :] = jnp.zeros((1, depth), jnp.float32)
    gains[1:2, :] = gain_part[...]

    def norm(here):
        part, grad = norm_back(activations[here, :], gain[...], input_part[here, :])
        input_part[here, :] = part
        gains[0:1, :] += grad

    loads.wait(2)
    by_rows(rows, norm)

    gains_tp[line.me] = gains[...]
    for ahead in range(1, size):
        tell_tp(ahead).start()
    for turn in range(shards - 1):
        give(turn).wait_recv()
        grad_qkv[...] += qkv_from[turn].astype(jnp.float32)
    for ahead in range(1, size):
        source = (line.me + ahead) % size
        remote(gains, gains_tp.at[source], tp_send.at[0], tp_recv.at[source], {"tp": source}).wait_recv()
    total = gains_tp[0]
    for source in range(1, size):
        total = total + gains_tp[source]
    for ahead in range(1, size):
        tell_tp(ahead).wait_send()
    gains[...] = total
    gains_fsdp[shard] = total
    for ahead in range(1, shards):
        tell_fsdp(ahead).start()
    for ahead in range(1, shards):
        source = (shard + ahead) % shards
        remote(gains, gains_fsdp.at[source], fsdp_send.at[0], fsdp_recv.at[source], {"fsdp": source}).wait_recv()
    total = gains_fsdp[0]
    for source in range(1, shards):
        total = total + gains_fsdp[source]
    gain_sum[...] = total
    for ahead in range(1, shards):
        tell_fsdp(ahead).wait_send()
    for turn in range(shards - 1):
        give(turn).wait_send()
    down.finish()
    scatter.finish()


def spread(chips, shards, qkv_grad, weight, activations, gain, gain_part, attn_tokens, grad_down):
    group_rows = qkv_grad.shape[0]
    rows, depth = activations.shape
    width = qkv_grad.shape[1] // 3
    columns = depth // shards
    size = 2 * chips
    shape = jax.ShapeDtypeStruct
    return pl.pallas_call(
        lambda *refs: spread_kernel(chips, shards, *refs),
        in_specs=[VMEM] * 2 + [ANYWHERE] * 5,
        out_specs=[VMEM] * 3 + [ANYWHERE],
        out_shape=[
            shape((rows, depth), jnp.float32),
            shape((columns, 3 * width), jnp.float32),
            shape((2, depth), jnp.float32),
            shape((shards // 2, grad_down.shape[0], columns), low),
        ],
        scratch_shapes=Loads.scratch(qkv_grad, weight, activations) + [
            pltpu.VMEM((2, group_rows, columns), low),
            pltpu.VMEM((shards - 1, columns, 3 * width), low),
            pltpu.VMEM((shards - 1, columns, 3 * width), low),
            pltpu.VMEM((2, depth), jnp.float32),
            pltpu.VMEM((size, 2, depth), jnp.float32),
            pltpu.VMEM((shards, 2, depth), jnp.float32),
            DMA((2,)), DMA((shards - 1,)), DMA((shards - 1,)),
            DMA((size - 1,)), DMA((size,)), DMA((shards - 1,)), DMA((shards,)),
        ] + NearSums.scratch(shards, grad_down.shape[0], columns) + Scatter.scratch(chips, rows, depth),
        compiler_params=pltpu.CompilerParams(collective_id=5, has_side_effects=True, vmem_limit_bytes=63 << 20),
        cost_estimate=pl.CostEstimate(flops=1 << 20, bytes_accessed=1 << 20, transcendentals=0),
        name="spread",
    )(gain, gain_part, qkv_grad, weight, activations, attn_tokens, grad_down)


def chip_at(place, chips):
    return jnp.where(2 * place < chips, 2 * place, 2 * (chips - 1 - place) + 1)


def place_of(chip, chips):
    return jnp.where(chip % 2 == 0, chip // 2, chips - 1 - chip // 2)


def feed_kernel(
    chips, shards,
    gain, hidden_hbm, cotangent_hbm, tokens, grads_hbm, w_gate, w_up, w_down, gate_all, up_all, down_near, down_far,
    hidden_grad, branch, gain_part, inner_out, grad_both, down_out,
    hidden_state, cotangent, state_sem, down_tile, down_sem, tokens_all, gate_w, up_w, down_w, grads, inner, gate_grad, up_grad, term, from_core, from_ring, total, tile_gate, tile_up,
    load_sem, own_sem, grad_sem, store_sem, tile_sem,
    ring_send, ring_recv, core_send, core_recv, share_send, share_recv, total_send, total_recv,
):
    rows, depth = hidden_grad.shape
    pair = 2 * rows
    width = gate_w.shape[1]
    me = lax.axis_index("tp")
    chip, core = me // 2, me % 2
    place = place_of(chip, chips)
    following = {"tp": 2 * chip_at((place + 1) % chips, chips) + core}
    before = {"tp": 2 * chip_at((place + chips - 1) % chips, chips) + core}
    partner = {"tp": 2 * chip + 1 - core}

    grid = Grid(shards)
    rows_of, columns_of = row_shard(w_gate.shape[0]), column_shard(*w_down.shape)

    def load(array, source, shard, whole):
        at = columns_of if array == 2 else rows_of
        target = at((gate_w, up_w, down_w)[array], shard, None)
        return pltpu.make_async_copy(at(source, shard, None) if whole else source, target, load_sem.at[array, shard])

    def load_weights():
        for shard in range(shards):
            own, near = grid.me == shard, grid.is_near(shard)

            @pl.when(own)
            def _():
                for array, source in enumerate((w_gate, w_up, w_down)):
                    load(array, source, shard, False).start()

            @pl.when(jnp.logical_not(own))
            def _():
                for array, source in enumerate((gate_all, up_all)):
                    load(array, source, shard, True).start()

            @pl.when(jnp.logical_and(near, jnp.logical_not(own)))
            def _():
                load(2, down_near, shard, True).start()

            @pl.when(jnp.logical_not(near))
            def _():
                load(2, down_far, shard, True).start()

    own = pltpu.make_async_copy(tokens, tokens_all.at[span(me, rows)], own_sem)
    states = Loads((hidden_hbm, cotangent_hbm), (hidden_state, cotangent, state_sem))

    def source(slot):
        return chip_at((place + chips - slot) % chips, chips)

    def fetch(slot):
        return pltpu.make_async_copy(grads_hbm.at[span(source(slot), pair)], grads.at[slot % 2], grad_sem.at[slot % 2])

    def block(slot):
        return tokens_all.at[span(2 * source(slot) + core, rows)]

    def to_ring(slot):
        return remote(block(slot), block(slot), ring_send.at[slot], ring_recv.at[slot], following)

    def to_core(slot):
        return remote(block(slot), block(slot), core_send.at[slot], core_recv.at[slot], partner)

    def store(slot):
        return pltpu.make_async_copy(inner.at[slot], inner_out.at[span(source(slot), pair)], store_sem.at[slot])

    def keep_down(slot, tile):
        there = down_out.at[span(source(slot), pair), span(tile, 256)]
        return pltpu.make_async_copy(down_tile.at[tile % 2], there, down_sem.at[tile % 2])

    def down_term(slot, carry):
        def tile(index, carry):
            @pl.when(index > 1)
            def _():
                keep_down(slot, index - 2).wait()

            down_tile[index % 2] = dot(inner[slot], down_w[:, span(index, 256)]).astype(low)
            keep_down(slot, index).start()
            return carry

        lax.fori_loop(0, depth // 256, tile, 0)
        for index in range(depth // 256 - 2, depth // 256):
            keep_down(slot, index).wait()
        return carry

    def share(slot):
        place = jnp.where(slot == 0, 0, 1 + slot % 2)
        return remote(term.at[span(1 - core, rows)], from_core.at[place], share_send, share_recv.at[place], partner)

    def pass_on(slot):
        return remote(total.at[slot % 2], from_ring.at[slot - 1], total_send.at[slot % 2], total_recv.at[slot - 1], following)

    own.start()
    fetch(0).start()
    load_weights()
    own.wait()
    for device in (following, before, partner):
        hello(device)
    pl.semaphore_wait(pltpu.get_barrier_semaphore(), 3)

    def step(slot, carry):
        here = slot % 2
        wide_rows = span(source(slot), pair)
        mine = span(core, rows)

        @pl.when(slot > 0)
        def _():
            to_ring(slot - 1).wait_recv()

        @pl.when(slot < chips - 1)
        def _():
            to_ring(slot).start()
            fetch(slot + 1).start()

        to_core(slot).start()

        @pl.when(slot == 0)
        def _():
            for shard in range(shards):
                for array, source in enumerate((gate_all, up_all, down_near)):
                    load(array, source, shard, True).wait()

        @pl.when(slot == 1)
        def _():
            states.start()

        to_core(slot).wait_recv()
        fetch(slot).wait()

        def narrow(tile, carry):
            columns = span(tile, 256)
            token = tokens_all[wide_rows, :]
            gate = dot(token, gate_w[:, columns])
            up = dot(token, up_w[:, columns])
            grad = dot(grads[here], down_w[columns, :], NT)
            squash = jax.nn.sigmoid(gate)
            act = gate * squash
            inner[slot, :, columns] = (act * up).astype(low)
            up_grad[wide_rows, columns] = (grad * act).astype(low)
            gate_grad[wide_rows, columns] = (grad * up * squash * (1.0 + gate * (1.0 - squash))).astype(low)
            return carry

        lax.fori_loop(0, width // 256, narrow, 0)
        store(slot).start()

        @pl.when(slot > 0)
        def _():
            share(slot - 1).wait_send()

        def wide(tile, carry):
            columns = span(tile, 256)
            part = dot(gate_grad[wide_rows, :], gate_w[columns, :], NT) + dot(up_grad[wide_rows, :], up_w[columns, :], NT)
            term[:, columns] = part.astype(low)
            return carry

        lax.fori_loop(0, depth // 256, wide, 0)
        share(slot).start()

        @pl.when(slot == 0)
        def _():
            hidden_grad[...] = term[mine, :].astype(jnp.float32)

        middle = jnp.logical_and(slot >= 2, slot < chips - 1)
        lax.fori_loop(jnp.where(slot == 2, 0, slot), jnp.where(middle, slot + 1, 0), down_term, 0)

        @pl.when(slot > 0)
        def _():
            share(slot).wait_recv()

            @pl.when(slot > 2)
            def _():
                pass_on(slot - 2).wait_send()

            @pl.when(slot == 1)
            def _():
                total[here] = (term[mine, :].astype(jnp.float32) + from_core[1 + here].astype(jnp.float32)).astype(low)

            @pl.when(slot > 1)
            def _():
                pass_on(slot - 1).wait_recv()
                total[here] = (term[mine, :].astype(jnp.float32) + from_core[1 + here].astype(jnp.float32) + from_ring[slot - 2].astype(jnp.float32)).astype(low)

            pass_on(slot).start()

        return carry

    lax.fori_loop(0, chips, step, 0)

    def tiles(index):
        there = span(index, 256)
        return (
            pltpu.make_async_copy(tile_gate.at[index % 2], grad_both.at[there, pl.ds(0, width)], tile_sem.at[0, index % 2]),
            pltpu.make_async_copy(tile_up.at[index % 2], grad_both.at[there, pl.ds(width, width)], tile_sem.at[1, index % 2]),
        )

    def weights(index, carry):
        @pl.when(index > 1)
        def _():
            for copy in tiles(index - 2):
                copy.wait()

        token = tokens_all[:, span(index, 256)]
        tile_gate[index % 2] = dot(token, gate_grad[...], TN).astype(low)
        tile_up[index % 2] = dot(token, up_grad[...], TN).astype(low)
        for copy in tiles(index):
            copy.start()
        return carry

    lax.fori_loop(0 if chips < 4 else chips - 1, chips, down_term, 0)
    lax.fori_loop(0, depth // 256, weights, 0)
    states.wait(0, 1)
    share(0).wait_recv()
    pass_on(chips - 1).wait_recv()
    gain_part[...] = jnp.zeros_like(gain_part)

    def norm(here):
        grad = hidden_grad[here, :] + from_core[0, here, :].astype(jnp.float32) + from_ring[chips - 2, here, :].astype(jnp.float32)
        part, gain_grad = norm_back(hidden_state[here, :], gain[...], grad)
        full = cotangent[here, :] + part
        hidden_grad[here, :] = full
        branch[here, :] = full.astype(low)
        gain_part[...] += gain_grad

    by_rows(rows, norm)
    share(chips - 1).wait_send()
    for slot in range(chips):
        to_core(slot).wait_send()
        if slot < chips - 1:
            to_ring(slot).wait_send()
        if slot >= max(1, chips - 2):
            pass_on(slot).wait_send()
        store(slot).wait()
    for index in range(depth // 256 - 2, depth // 256):
        for copy in tiles(index):
            copy.wait()


def feed(chips, shards, hidden_state, cotangent, gain, tokens, grads, w_gate, w_up, w_down, gate_all, up_all, down_near, down_far):
    rows, depth = tokens.shape
    pair = 2 * rows
    group_rows = chips * pair
    width = w_down.shape[0]
    shape = jax.ShapeDtypeStruct
    return pl.pallas_call(
        lambda *refs: feed_kernel(chips, shards, *refs),
        in_specs=[VMEM] + [ANYWHERE] * 11,
        out_specs=[VMEM] * 3 + [ANYWHERE] * 3,
        out_shape=[
            shape((rows, depth), jnp.float32),
            shape((rows, depth), low),
            shape((1, depth), jnp.float32),
            shape((group_rows, width), low),
            shape((depth, 2 * width), low),
            shape((group_rows, depth), low),
        ],
        scratch_shapes=Loads.scratch(hidden_state, cotangent) + [
            pltpu.VMEM((2, pair, 256), low),
            DMA((2,)),
            pltpu.VMEM((group_rows, depth), low),
            pltpu.VMEM((depth, width), low),
            pltpu.VMEM((depth, width), low),
            pltpu.VMEM((width, depth), low),
            pltpu.VMEM((2, pair, depth), low),
            pltpu.VMEM((chips, pair, width), low),
            pltpu.VMEM((group_rows, width), low),
            pltpu.VMEM((group_rows, width), low),
            pltpu.VMEM((pair, depth), low),
            pltpu.VMEM((3, rows, depth), low),
            pltpu.VMEM((chips - 1, rows, depth), low),
            pltpu.VMEM((2, rows, depth), low),
            pltpu.VMEM((2, 256, width), low),
            pltpu.VMEM((2, 256, width), low),
            DMA((3, shards)), DMA, DMA((2,)), DMA((chips,)), DMA((2, 2)),
            DMA((chips,)), DMA((chips,)), DMA((chips,)), DMA((chips,)),
            DMA, DMA((3,)), DMA((2,)), DMA((chips - 1,)),
        ],
        compiler_params=pltpu.CompilerParams(collective_id=3, has_side_effects=True, vmem_limit_bytes=67043328),
        cost_estimate=pl.CostEstimate(flops=16 * group_rows * depth * width, bytes_accessed=10 * group_rows * depth, transcendentals=group_rows * width),
        name="feed",
    )(gain, hidden_state, cotangent, tokens, grads, w_gate, w_up, w_down, gate_all, up_all, down_near, down_far)


def finish_kernel(
    shard_ref, hidden, down, hidden_grad, input_part, both, both_from, grad_down, down_from, grad_qkv, grad_out,
    output, input_grad, query, key, value, out, gate, up, down_out,
):
    output[...] = hidden[...] + down[...]
    input_grad[...] = hidden_grad[...] + input_part[...]
    width = query.shape[1]
    for part, ref in enumerate((query, key, value)):
        ref[...] = grad_qkv[:, pl.ds(part * width, width)]
    out[...] = grad_out[...]
    wide = gate.shape[1]
    for side, ref in enumerate((gate, up)):
        columns = pl.ds(side * wide, wide)
        total = both[:, columns].astype(jnp.float32)
        for turn in range(both_from.shape[0]):
            total = total + both_from[turn, :, columns].astype(jnp.float32)
        ref[...] = total
    total = grad_down[...].astype(jnp.float32)
    for turn in range(down_from.shape[0]):
        total = total + down_from[turn].astype(jnp.float32)
    down_out[...] = total


def finish(shard, hidden, down, hidden_grad, input_part, both, both_from, grad_down, down_from, grad_qkv, grad_out):
    steps = 8
    shape = jax.ShapeDtypeStruct
    columns = down_from.shape[2]
    results = [shape(hidden.shape, jnp.float32)] * 2
    results += [shape((columns, grad_qkv.shape[1] // 3), jnp.float32)] * 3 + [shape(grad_out.shape, jnp.float32)]
    results += [shape((columns, both.shape[1] // 2), jnp.float32)] * 2 + [shape((grad_down.shape[0], columns), jnp.float32)]
    spec = lambda a: pl.BlockSpec((a.shape[0] // steps, a.shape[1]), lambda i, s: (i, 0))
    spec3 = lambda a: pl.BlockSpec((a.shape[0], a.shape[1] // steps, a.shape[2]), lambda i, s: (0, i, 0))
    return pl.pallas_call(
        finish_kernel,
        grid_spec=pltpu.PrefetchScalarGridSpec(
            num_scalar_prefetch=1,
            grid=(steps,),
            in_specs=[
                spec(hidden), spec(down), spec(hidden_grad), spec(input_part),
                pl.BlockSpec((columns // steps, both.shape[1]), lambda i, s: (s[0] * steps + i, 0)),
                spec3(both_from),
                pl.BlockSpec((grad_down.shape[0] // steps, columns), lambda i, s: (i, s[0])),
                spec3(down_from), spec(grad_qkv), spec(grad_out),
            ],
            out_specs=[spec(a) for a in results],
        ),
        out_shape=results,
        name="finish",
    )(shard.reshape(1), hidden, down, hidden_grad, input_part, both, both_from, grad_down, down_from, grad_qkv, grad_out)


def rope_tables():
    half = HEAD_DIM // 2
    positions = jnp.arange(SEQ_LEN, dtype=jnp.int32).astype(jnp.float32)
    column = jnp.arange(half, dtype=jnp.int32)
    inverse = jnp.power(jnp.float32(rope_base), -2.0 * column.astype(jnp.float32) / HEAD_DIM)
    angle = positions[None, :] * inverse[:, None]
    return (jnp.cos(angle), jnp.sin(angle))


def make_body(mesh):
    chips, shards = mesh.shape["tp"] // 2, mesh.shape["fsdp"]

    def body(activations, gain_attn, w_query, w_key, w_value, w_out, gain_mlp, w_gate, w_up, w_down, cotangent):
        gain_attn, gain_mlp = gain_attn[None, :], gain_mlp[None, :]
        seen_attn, w_qkv, full_out, qkv, keys_t, values_t, cosine, sine, down_near = project(
            chips, shards, activations, gain_attn, w_query, w_key, w_value, w_out, *rope_tables(), w_down
        )
        hidden_state, normed_mlp, mixed, totals, seen_grad, gate_all, up_all, down_far = attend(
            chips, shards, qkv, values_t, full_out, activations, cotangent, gain_mlp, w_gate, w_up, down_near
        )
        hidden_grad, branch_grad, gain_part, inner, grad_both, terms = feed(
            chips, shards, hidden_state, cotangent, gain_mlp, normed_mlp, seen_grad,
            w_gate, w_up, w_down, gate_all, up_all, down_near, down_far,
        )
        down, _, qkv_grad, grad_down, grad_out, both_from = back(
            chips, shards, branch_grad, terms, inner, seen_grad, grad_both, full_out, qkv, keys_t, mixed, totals, cosine, sine
        )
        input_part, grad_qkv, gain_sums, down_from = spread(
            chips, shards, qkv_grad, w_qkv, activations, gain_attn, gain_part, seen_attn, grad_down
        )
        output, input_grad, grad_query, grad_key, grad_value, grad_out, grad_gate, grad_up, grad_down = finish(
            lax.axis_index("fsdp"), hidden_state, down, hidden_grad, input_part,
            grad_both, both_from, grad_down, down_from, grad_qkv, grad_out,
        )
        return (
            output, input_grad, gain_sums[0], grad_query, grad_key, grad_value, grad_out, gain_sums[1],
            grad_gate, grad_up, grad_down,
        )

    return body


def solution(mesh):
    tokens = P(("fsdp", "tp"), None)
    column = P("fsdp", "tp")
    row = P("tp", "fsdp")
    in_specs = (tokens, P(), column, column, column, row, P(), column, column, row, tokens)
    out_specs = (tokens, tokens, P(), column, column, column, row, P(), column, column, row)
    return jax.shard_map(make_body(mesh), mesh=mesh, in_specs=in_specs, out_specs=out_specs, check_vma=False)
```

```python
import jax
import jax.numpy as jnp
from jax import lax
from jax.experimental import pallas as pl
from jax.experimental.pallas import tpu as pltpu
from jax.sharding import PartitionSpec as P

HEAD_DIM = 64
SEQ_LEN = 2048
LANES = 128
rope_base = 130000.0
norm_eps = 1e-05
masked_score = -1e30

NT = (((1,), (1,)), ((), ()))
NN = (((1,), (0,)), ((), ()))
TN = (((0,), (0,)), ((), ()))
MESH = pl.DeviceIdType.MESH
DMA = pltpu.SemaphoreType.DMA
ANYWHERE = pl.BlockSpec(memory_space=pl.ANY)
VMEM = pl.BlockSpec(memory_space=pltpu.VMEM)
low = jnp.bfloat16


def dot(left, right, dims=NN):
    return lax.dot_general(left, right, dims, preferred_element_type=jnp.float32)


def span(index, size):
    return pl.ds(pl.multiple_of(index * size, size), size)


def remote(source, target, send, receive, device):
    return pltpu.make_async_remote_copy(
        src_ref=source, dst_ref=target, send_sem=send, recv_sem=receive,
        device_id=device, device_id_type=MESH,
    )


def hello(device):
    pl.semaphore_signal(pltpu.get_barrier_semaphore(), inc=1, device_id=device, device_id_type=MESH)


class Line:
    def __init__(self, chips):
        self.chips = chips
        self.me = lax.axis_index("tp")
        self.chip, self.core = self.me // 2, self.me % 2
        self.partner = 2 * self.chip + 1 - self.core
        self.has_left, self.has_right = self.chip > 0, self.chip < chips - 1

    def hello(self, more=()):
        hello({"tp": self.partner})

        @pl.when(self.has_left)
        def _():
            hello({"tp": self.me - 2})

        @pl.when(self.has_right)
        def _():
            hello({"tp": self.me + 2})

        for device in more:
            hello(device)

    def ready(self, more=()):
        count = 1 + len(more) + jnp.where(self.has_left, 1, 0) + jnp.where(self.has_right, 1, 0)
        pl.semaphore_wait(pltpu.get_barrier_semaphore(), count)

    def target(self, step):
        after = self.chips - 1 - self.chip
        most, least = jnp.maximum(self.chip, after), jnp.minimum(self.chip, after)
        sign = jnp.where(after >= self.chip, 1, -1)
        late = step - (most - least)
        side = jnp.where(late % 2 == 0, sign, -sign)
        return jnp.where(late < 0, self.chip + sign * (most - step), self.chip + side * (least - late // 2))


    def fed(self, target):
        after, before = jnp.logical_and(target >= self.chip, self.has_left), jnp.logical_and(target <= self.chip, self.has_right)
        return jnp.logical_or(after, before)


class Gather:
    @staticmethod
    def scratch(chips, parts=1):
        return [DMA((2 * chips, parts)), DMA((chips, parts)), DMA((chips, parts)), DMA((chips, parts)), DMA]

    def __init__(self, line, own, out, received, right, left, across, local, parts=1):
        self.line, self.out = line, out
        self.received, self.right, self.left, self.across, self.local = received, right, left, across, local
        self.parts = parts
        self.rows = out.shape[0] // (2 * line.chips * parts)
        self.held = own is None
        self.own = out.at[span(line.me, self.rows * parts)] if self.held else own

    def block(self, index, part):
        return self.out.at[span(index * self.parts + part, self.rows)]

    def mine(self, part):
        return self.own.at[pl.ds(part * self.rows, self.rows)]

    def copy(self, sems, chip, part, device, mine):
        index = 2 * chip + self.line.core
        source = self.mine(part) if mine else self.block(index, part)
        return remote(source, self.block(index, part), sems.at[chip, part], self.received.at[index, part], {"tp": device})

    def keep(self):
        return pltpu.make_async_copy(self.own, self.out.at[span(self.line.me, self.rows * self.parts)], self.local)

    def start(self):
        line = self.line
        if not self.held:
            self.keep().start()
        for part in range(self.parts):
            @pl.when(line.has_right)
            def _():
                self.copy(self.right, line.chip, part, line.me + 2, True).start()

            @pl.when(line.has_left)
            def _():
                self.copy(self.left, line.chip, part, line.me - 2, True).start()

            self.copy(self.across, line.chip, part, line.partner, True).start()

    def arrive(self, index, part):
        remote(self.mine(part), self.block(index, part), self.right.at[0, part], self.received.at[index, part], {"tp": self.line.partner}).wait_recv()

    def arrive_across(self, chip):
        for part in range(self.parts):
            self.arrive(2 * chip + 1 - self.line.core, part)

    def step(self, distance):
        line = self.line
        before, after = line.chip - distance, line.chip + distance
        for part in range(self.parts):
            @pl.when(before >= 0)
            def _():
                self.arrive(2 * before + line.core, part)

                @pl.when(line.has_right)
                def _():
                    self.copy(self.right, before, part, line.me + 2, False).start()

                self.copy(self.across, before, part, line.partner, False).start()

            @pl.when(after < line.chips)
            def _():
                self.arrive(2 * after + line.core, part)

                @pl.when(line.has_left)
                def _():
                    self.copy(self.left, after, part, line.me - 2, False).start()

                self.copy(self.across, after, part, line.partner, False).start()

    def finish(self, arrivals):
        line = self.line
        if arrivals:
            self.keep().wait()
        for chip in range(line.chips):
            if arrivals:
                self.arrive_across(chip)
            for part in range(self.parts):
                self.copy(self.across, chip, part, line.partner, True).wait_send()

                @pl.when(jnp.logical_and(line.has_right, chip <= line.chip))
                def _():
                    self.copy(self.right, chip, part, line.me + 2, True).wait_send()

                @pl.when(jnp.logical_and(line.has_left, chip >= line.chip))
                def _():
                    self.copy(self.left, chip, part, line.me - 2, True).wait_send()


class Scatter:
    @staticmethod
    def scratch(chips, rows, depth):
        shares = min(chips, 4)
        return [
            pltpu.VMEM((2, 2 * rows, depth), low),
            pltpu.VMEM((shares, rows, depth), low),
            pltpu.VMEM((chips + 1, rows, depth), low),
            pltpu.VMEM((2, rows, depth), low),
            DMA((2,)), DMA((shares,)), DMA((2,)), DMA((chips + 1,)),
        ]

    def __init__(self, line, out, term, shares, lines, total, share_send, share_recv, line_send, line_recv):
        self.line, self.out = line, out
        self.term, self.shares, self.lines, self.total = term, shares, lines, total
        self.share_send, self.share_recv, self.line_send, self.line_recv = share_send, share_recv, line_send, line_recv
        self.rows = out.shape[0]

    def share(self, step):
        slot = step % self.shares.shape[0]
        source = self.term.at[step % 2, span(1 - self.line.core, self.rows)]
        return remote(source, self.shares.at[slot], self.share_send.at[step % 2], self.share_recv.at[slot], {"tp": self.line.partner})

    def mine(self, step):
        return self.term[step % 2, span(self.line.core, self.rows), :]

    def pass_on(self, step):
        line, target = self.line, self.line.target(step)
        onward = target > line.chip
        slot = jnp.where(onward, target, jnp.where(target == line.chip - 1, line.chips, target))
        device = jnp.where(onward, line.me + 2, line.me - 2)
        return remote(self.total.at[step % 2], self.lines.at[slot], self.line_send.at[step % 2], self.line_recv.at[slot], {"tp": device})

    def add(self, slot):
        remote(self.total.at[0], self.lines.at[slot], self.line_send.at[0], self.line_recv.at[slot], {"tp": self.line.partner}).wait_recv()
        self.out[...] += self.lines[slot].astype(jnp.float32)

    def free(self, step):
        @pl.when(step >= 2)
        def _():
            self.share(step - 2).wait_send()

    def step(self, step):
        line, target = self.line, self.line.target(step)
        self.share(step).wait_recv()
        self.out[...] = self.mine(step).astype(jnp.float32) + self.shares[step % self.shares.shape[0]].astype(jnp.float32)

        @pl.when(jnp.logical_and(target >= line.chip, line.has_left))
        def _():
            self.add(target)

        @pl.when(jnp.logical_and(target <= line.chip, line.has_right))
        def _():
            self.add(jnp.where(target == line.chip, line.chips, target))

        @pl.when(step < line.chips - 1)
        def _():
            @pl.when(step >= 2)
            def _():
                self.pass_on(step - 2).wait_send()

            self.total[step % 2] = self.out[...].astype(low)
            self.pass_on(step).start()

    def finish(self):
        chips = self.line.chips
        for step in range(max(0, chips - 3), chips - 1):
            self.pass_on(step).wait_send()
        for step in range(max(0, chips - 2), chips):
            self.share(step).wait_send()


NORM_ROWS = 64


def normed(value, gain):
    return value * lax.rsqrt(jnp.mean(value * value, axis=-1, keepdims=True) + norm_eps) * gain


def norm_back(value, gain, grad):
    scale = lax.rsqrt(jnp.mean(value * value, axis=-1, keepdims=True) + norm_eps)
    unit = value * scale
    scaled = grad * gain
    return scale * (scaled - unit * jnp.mean(scaled * unit, axis=-1, keepdims=True)), jnp.sum(grad * unit, axis=0, keepdims=True)


def by_rows(rows, work):
    def step(index, carry):
        work(span(index, NORM_ROWS))
        return carry

    lax.fori_loop(0, rows // NORM_ROWS, step, 0)


class Grid:
    def __init__(self, shards):
        self.shards, self.across = shards, shards // 2
        self.me = lax.axis_index("fsdp")
        self.row, self.column = self.me // self.across, self.me % self.across
        self.others = [(self.me + ahead) % shards for ahead in range(1, shards)]
        self.mates = [self.row * self.across + (self.column + ahead) % self.across for ahead in range(1, self.across)]
        self.twin = (1 - self.row) * self.across + self.column
        self.near = self.mates + [self.twin]

    def is_near(self, shard):
        return jnp.logical_or(shard // self.across == self.row, shard % self.across == self.column)


class NearShards:
    scratch = staticmethod(lambda shards: [DMA((shards // 2,)), DMA((shards // 2,))])

    def __init__(self, grid, own, whole, at, send, receive):
        place = at(whole, grid.me, None)
        self.copies = [remote(own, place, send.at[i], receive.at[i], {"fsdp": peer}) for i, peer in enumerate(grid.near)]

    def start(self):
        for copy in self.copies:
            copy.start()

    def arrive(self):
        for copy in self.copies:
            copy.wait_recv()

    def finish(self):
        for copy in self.copies:
            copy.wait_send()


class FarShards:
    scratch = staticmethod(lambda shards: [DMA((2, shards // 2 - 1)), DMA((2, shards // 2 - 1))])

    def __init__(self, grid, near, whole, at, send, receive):
        self.copies = []
        for i, mate in enumerate(grid.mates):
            self.copies.append(remote(at(near, mate, 0), at(whole, mate, 0), send.at[0, i], receive.at[0, i], {"fsdp": grid.twin}))
            self.copies.append(remote(at(near, grid.twin, 1), at(whole, grid.twin, 1), send.at[1, i], receive.at[1, i], {"fsdp": mate}))

    def start(self):
        for copy in self.copies:
            copy.start()

    def finish(self):
        for copy in self.copies:
            copy.wait_recv()
            copy.wait_send()


class NearSums:
    @staticmethod
    def scratch(shards, rows, columns):
        across = shards // 2
        return [
            pltpu.VMEM((2, across - 1, rows // 2, columns), low),
            pltpu.VMEM((across, rows // 2, columns), low),
            DMA((2, across - 1)), DMA((2, across - 1)), DMA((across, 2)), DMA((across, 2)), DMA((across,)),
        ]

    def __init__(self, grid, part, out, at, relay, base, relay_send, relay_recv, near_send, near_recv, load_sem):
        self.relay, self.base = relay, base
        last = grid.across - 1
        half = base.shape[1]

        def near(source, slot, which, peer):
            target = out.at[slot, pl.ds(which * half, half)]
            return remote(source, target, near_send.at[slot, which], near_recv.at[slot, which], {"fsdp": peer})

        self.by_twin, self.by_mate, self.plain, self.joined, self.loads = [], [], [], [], []
        for i, mate in enumerate(grid.mates):
            far = (1 - grid.row) * grid.across + mate % grid.across
            self.by_twin.append(remote(at(part, far, 0), relay.at[0, i], relay_send.at[0, i], relay_recv.at[0, i], {"fsdp": grid.twin}))
            self.by_mate.append(remote(at(part, far, 1), relay.at[1, i], relay_send.at[1, i], relay_recv.at[1, i], {"fsdp": mate}))
            self.plain.append(near(at(part, mate, 1), i, 1, mate))
            self.joined.append(near(relay.at[0, i], i, 0, mate))
            self.loads.append(pltpu.make_async_copy(at(part, mate, 0), base.at[i], load_sem.at[i]))
        self.plain.append(near(at(part, grid.twin, 0), last, 0, grid.twin))
        self.joined.append(near(relay.at[1, 0], last, 1, grid.twin))
        self.loads.append(pltpu.make_async_copy(at(part, grid.twin, 1), base.at[last], load_sem.at[last]))

    def start(self):
        for copy in self.by_twin + self.by_mate + self.loads:
            copy.start()

    def start_plain(self):
        for copy in self.plain:
            copy.start()

    def join(self):
        for copy in self.by_twin + self.by_mate:
            copy.wait_recv()
        for copy in self.loads:
            copy.wait()
        last = self.base.shape[0] - 1
        for i in range(last):
            self.relay[0, i] = (self.base[i].astype(jnp.float32) + self.relay[0, i].astype(jnp.float32)).astype(low)
        total = self.base[last].astype(jnp.float32)
        for i in range(last):
            total = total + self.relay[1, i].astype(jnp.float32)
        self.relay[1, 0] = total.astype(low)
        for copy in self.joined:
            copy.start()

    def finish(self):
        for copy in self.by_twin + self.by_mate:
            copy.wait_send()
        for copy in self.plain + self.joined:
            copy.wait_recv()
            copy.wait_send()


def row_shard(depth):
    def at(ref, shard, half):
        if half is None:
            return ref.at[span(shard, depth)]
        return ref.at[span(2 * shard + half, depth // 2)]

    return at


def column_shard(rows, width):
    def at(ref, shard, half):
        if half is None:
            return ref.at[:, span(shard, width)]
        return ref.at[pl.ds(half * (rows // 2), rows // 2), span(shard, width)]

    return at


class HeldScatter(Scatter):
    @staticmethod
    def scratch(chips, rows, depth):
        return [
            pltpu.VMEM((2, rows, depth), low),
            pltpu.VMEM((chips, rows, depth), low),
            pltpu.VMEM((chips + 1, rows, depth), low),
            pltpu.VMEM((2, rows, depth), low),
            DMA((2,)), DMA((chips,)), DMA((2,)), DMA((chips + 1,)), DMA((2,)),
        ]

    def __init__(self, line, out, held, *refs):
        super().__init__(line, out, *refs[:-1])
        self.held, self.load_sem = held, refs[-1]

    def load(self, step):
        source = self.held.at[span(2 * self.line.target(step) + self.line.core, self.rows)]
        return pltpu.make_async_copy(source, self.term.at[step % 2], self.load_sem.at[step % 2])

    def share(self, step):
        slot = step % self.shares.shape[0]
        source = self.held.at[span(2 * self.line.target(step) + 1 - self.line.core, self.rows)]
        return remote(source, self.shares.at[slot], self.share_send.at[step % 2], self.share_recv.at[slot], {"tp": self.line.partner})

    def mine(self, step):
        self.load(step).wait()

        @pl.when(step < self.line.chips - 1)
        def _():
            self.load(step + 1).start()

        return self.term[step % 2]


class Loads:
    @staticmethod
    def scratch(*operands):
        return [pltpu.VMEM(a.shape, a.dtype) for a in operands] + [DMA((len(operands),))]

    def __init__(self, sources, refs):
        self.refs = refs[: len(sources)]
        self.copies = [pltpu.make_async_copy(source, ref, refs[-1].at[i]) for i, (source, ref) in enumerate(zip(sources, self.refs))]

    def start(self):
        for copy in self.copies:
            copy.start()

    def wait(self, *which):
        for i in which:
            self.copies[i].wait()


def turned(block, sign):
    half = HEAD_DIM // 2
    lane = lax.broadcasted_iota(jnp.int32, block.shape, 1)
    width = block.shape[1]
    up = pltpu.roll(block, width - half, 1)
    down = pltpu.roll(block, half, 1)
    return jnp.where(lane % HEAD_DIM < half, -sign * up, sign * down)


def widened(table, width):
    return table if table.shape[1] == width else jnp.concatenate([table] * (width // table.shape[1]), axis=1)


def only_head(block, head):
    lane = lax.broadcasted_iota(jnp.int32, block.shape, 1)
    return jnp.where(lane // HEAD_DIM == head, block, jnp.zeros_like(block))


def causal(tile):
    key = lax.broadcasted_iota(jnp.int32, tile.shape, 0)
    query = lax.broadcasted_iota(jnp.int32, tile.shape, 1)
    return jnp.where(key <= query, tile, masked_score)


def over_keys(chunk, rows, visit):
    start = chunk * rows
    first = start // SEQ_LEN * SEQ_LEN

    def step(index, carry):
        visit(pl.multiple_of(first + index * rows, rows), False)
        return carry

    lax.fori_loop(0, (start - first) // rows, step, 0)
    visit(pl.multiple_of(start, rows), True)


def project_kernel(
    chips, shards,
    gain, cosine_t, sine_t, activations_hbm, w_query, w_key, w_value, w_out, w_down,
    tokens_out, weight_out, full_out, qkv_out, keys_out, values_out, cosine_out, sine_out, down_near,
    weight, out_w, qkv, keys_t, values_t, cosine, sine, tokens, activations,
    load_sem, weight_send, weight_recv, weight_keep, table_sem, store_sem, near_send, near_recv, *gather_sems,
):
    line = Line(chips)
    rows = activations.shape[0]
    depth, width = w_query.shape
    grid = Grid(shards)
    shard, others = grid.me, grid.others
    gather = Gather(line, None, tokens, *gather_sems, parts=2)
    down = NearShards(grid, w_down, down_near, column_shard(*w_down.shape), near_send, near_recv)
    parts = (w_query, w_key, w_value, w_out)

    def place(part):
        if part == 3:
            return out_w.at[:, span(shard, depth)]
        return weight.at[span(shard, depth), pl.ds(part * width, width)]

    def give(ahead, part):
        return remote(parts[part], place(part), weight_send.at[ahead, part], weight_recv.at[ahead, part], {"fsdp": others[ahead]})

    def keep(part):
        return pltpu.make_async_copy(parts[part], place(part), weight_keep.at[part])

    tables = [
        pltpu.make_async_copy(source, out, table_sem.at[i])
        for i, (source, out) in enumerate(((cosine, cosine_out), (sine, sine_out), (weight, weight_out), (out_w, full_out)))
    ]

    def stores(index):
        here = span(index, rows)
        return [
            pltpu.make_async_copy(qkv.at[here], qkv_out.at[here], store_sem.at[0, index]),
            pltpu.make_async_copy(keys_t.at[:, here], keys_out.at[:, here], store_sem.at[1, index]),
            pltpu.make_async_copy(values_t.at[:, here], values_out.at[:, here], store_sem.at[2, index]),
            pltpu.make_async_copy(tokens.at[here], tokens_out.at[here], store_sem.at[3, index]),
        ]

    def norm(index, carry):
        there = span(line.me * (rows // NORM_ROWS) + index, NORM_ROWS)
        tokens[there, :] = normed(activations[span(index, NORM_ROWS), :], gain[...]).astype(low)
        return carry

    load = pltpu.make_async_copy(activations_hbm, activations, load_sem)
    load.start()
    line.hello([{"fsdp": other} for other in others])
    load.wait()
    lax.fori_loop(0, rows // NORM_ROWS, norm, 0)
    line.ready(others)
    gather.start()
    for part in range(4):
        keep(part).start()
        for ahead in range(shards - 1):
            give(ahead, part).start()
    for table, table_t in ((cosine, cosine_t), (sine, sine_t)):
        turn = table_t[...].T
        table[...] = jnp.concatenate([turn] * (LANES // turn.shape[1]), axis=1)
    for copy in tables[:2]:
        copy.start()

    def project(index):
        here = span(index, rows)
        table = span(index % (SEQ_LEN // rows), rows)
        for part in range(3):
            columns = pl.ds(part * width, width)
            block = dot(tokens[here, :], weight[:, columns])
            if part < 2:
                block = block * widened(cosine[table, :], width) + turned(block, 1.0) * widened(sine[table, :], width)
            qkv[here, columns] = block.astype(low)
            if part:
                (keys_t, values_t)[part - 1][:, here] = block.T.astype(low)
        for copy in stores(index):
            copy.start()

    def step(index, carry):
        @pl.when(jnp.logical_and(index >= 1, index < chips))
        def _():
            gather.step(index)

        @pl.when(index == 2)
        def _():
            for part in range(4):
                keep(part).wait()
                for ahead in range(shards - 1):
                    give(ahead, part).wait_recv()
            for copy in tables[2:]:
                copy.start()
            down.start()

        def side(turn, carry):
            distance, which, across = index - 1, turn % 3, turn // 3
            chip = jnp.where(which == 0, line.chip - distance, jnp.where(which == 1, line.chip + distance, line.chip))
            there = jnp.logical_and(chip >= 0, chip < chips)

            @pl.when(jnp.logical_and(there, jnp.logical_and(index >= 2, jnp.logical_or(which < 2, index == 2))))
            def _():
                @pl.when(across == 1)
                def _():
                    gather.arrive_across(chip)

                project(2 * chip + jnp.where(across == 1, 1 - line.core, line.core))

            return carry

        lax.fori_loop(0, 6, side, 0)
        return carry

    lax.fori_loop(0, chips + 1, step, 0)
    gather.finish(False)
    for part in range(4):
        for ahead in range(shards - 1):
            give(ahead, part).wait_send()
    for copy in tables:
        copy.wait()
    for index in range(2 * chips):
        for copy in stores(index):
            copy.wait()
    down.arrive()
    down.finish()


def project(chips, shards, activations, gain, w_query, w_key, w_value, w_out, cosine_t, sine_t, w_down):
    rows, depth = activations.shape
    group_rows = 2 * chips * rows
    width = w_query.shape[1]
    shape = jax.ShapeDtypeStruct
    held = [
        shape((depth, 3 * width), low),
        shape((width, depth), low),
        shape((group_rows, 3 * width), low),
        shape((width, group_rows), low),
        shape((width, group_rows), low),
        shape((SEQ_LEN, LANES), jnp.float32),
        shape((SEQ_LEN, LANES), jnp.float32),
    ]
    return pl.pallas_call(
        lambda *refs: project_kernel(chips, shards, *refs),
        in_specs=[VMEM] * 3 + [ANYWHERE] * 6,
        out_specs=[ANYWHERE] * 9,
        out_shape=[shape((group_rows, depth), low)] + held + [shape((w_down.shape[0], depth), low)],
        scratch_shapes=[pltpu.VMEM(a.shape, a.dtype) for a in held] + [
            pltpu.VMEM((group_rows, depth), low),
            pltpu.VMEM((rows, depth), jnp.float32),
            DMA, DMA((shards - 1, 4)), DMA((shards - 1, 4)), DMA((4,)), DMA((4,)), DMA((4, 2 * chips)),
        ] + NearShards.scratch(shards) + Gather.scratch(chips, 2),
        compiler_params=pltpu.CompilerParams(collective_id=1, has_side_effects=True, vmem_limit_bytes=63 << 20),
        cost_estimate=pl.CostEstimate(flops=6 * group_rows * depth * width, bytes_accessed=4 * group_rows * depth, transcendentals=0),
        name="project",
    )(gain, cosine_t, sine_t, activations, w_query, w_key, w_value, w_out, w_down)


def attend_chunk(chunk, rows, qkv, values_t, heads_ref, acc, out, top_ref, sum_ref):
    width = acc.shape[0]
    heads = width // HEAD_DIM
    scaled = qkv[span(chunk, rows), pl.ds(0, width)] * low(HEAD_DIM**-0.5)
    for head in range(heads):
        heads_ref[head] = only_head(scaled, head)
    acc[...] = jnp.zeros_like(acc)
    top_ref[...] = jnp.full_like(top_ref, masked_score)
    sum_ref[...] = jnp.zeros_like(sum_ref)

    def visit(offset, diagonal):
        key_block = qkv[pl.ds(offset, rows), pl.ds(width, width)]
        for head in range(heads):
            feature = pl.ds(head * HEAD_DIM, HEAD_DIM)
            one = pl.ds(head, 1)
            scores = dot(key_block, heads_ref[head], NT)
            if diagonal:
                scores = causal(scores)
            old = top_ref[one, :]
            top = jnp.maximum(old, jnp.max(scores, axis=0, keepdims=True))
            shrink = jnp.exp(old - top)
            weights = jnp.exp(scores - top)
            top_ref[one, :] = top
            sum_ref[one, :] = sum_ref[one, :] * shrink + jnp.sum(weights, axis=0, keepdims=True)
            acc[feature, :] = acc[feature, :] * shrink + dot(values_t[feature, pl.ds(offset, rows)], weights.astype(low))

    over_keys(chunk, rows, visit)
    for head in range(heads):
        feature = pl.ds(head * HEAD_DIM, HEAD_DIM)
        acc[feature, :] = acc[feature, :] / sum_ref[pl.ds(head, 1), :]
    out[...] = acc[...].T.astype(low)


def attend_kernel(
    chips, shards,
    gain, *refs,
):
    sources, (w_gate, w_up, down_near) = refs[:5], refs[5:8]
    hidden, tokens, mixed, totals, grads_out, gate_all, up_all, down_far = refs[8:16]
    loads = Loads(sources, refs[16:22])
    cotangent, qkv, values_t, w_out, activations = loads.refs
    heads_ref, acc, out, top_ref, sum_ref, grads = refs[22:28]
    loads.start()
    line = Line(chips)
    grid = Grid(shards)
    rows_of = row_shard(w_gate.shape[0])
    line.hello([{"fsdp": peer} for peer in grid.near])
    down = FarShards(grid, down_near, down_far, column_shard(down_near.shape[0], down_near.shape[1] // shards), *refs[28:30])
    gate_near, gate_far = NearShards(grid, w_gate, gate_all, rows_of, *refs[30:32]), FarShards(grid, gate_all, gate_all, rows_of, *refs[32:34])
    up_near, up_far = NearShards(grid, w_up, up_all, rows_of, *refs[34:36]), FarShards(grid, up_all, up_all, rows_of, *refs[36:38])
    sems = refs[38:]
    rows, depth = hidden.shape
    pair = 2 * rows
    scatter = Scatter(line, hidden, *sems[:8])
    loads.wait(0)
    grads[...] = cotangent[...].astype(low)
    gather = Gather(line, grads, grads_out, *sems[8:])
    line.ready(grid.near)
    gather.start()
    gate_near.start()
    down.start()
    loads.wait(1, 2, 3, 4)

    def step(index, carry):
        work = jnp.where(index == chips, chips - 1, index)

        @pl.when(jnp.logical_or(index < chips - 1, index == chips))
        def _():
            chunk = line.target(work)
            attend_chunk(chunk, pair, qkv, values_t, heads_ref, acc, out, top_ref, sum_ref)
            mixed[span(chunk, pair), :] = out[...]
            totals[:, span(chunk, pair)] = top_ref[...] + jnp.log(sum_ref[...])
            scatter.free(work)

            def tile(place, carry):
                columns = span(place, 512)
                scatter.term[work % 2, :, columns] = dot(out[...], w_out[:, columns]).astype(low)
                return carry

            lax.fori_loop(0, depth // 512, tile, 0)
            scatter.share(work).start()

        @pl.when(jnp.logical_and(index >= 1, index < chips))
        def _():
            gather.step(index)

        @pl.when(index == 1)
        def _():
            up_near.start()

        @pl.when(index == min(2, chips))
        def _():
            gate_near.arrive()
            gate_far.start()

        @pl.when(index == min(3, chips))
        def _():
            up_near.arrive()
            up_far.start()

        @pl.when(index >= 1)
        def _():
            scatter.step(index - 1)

        return carry

    lax.fori_loop(0, chips + 1, step, 0)

    def norm(here):
        state = activations[here, :] + hidden[here, :]
        hidden[here, :] = state
        tokens[here, :] = normed(state, gain[...]).astype(low)

    by_rows(rows, norm)
    scatter.finish()
    gather.finish(True)
    for near in (gate_near, up_near):
        near.finish()
    for far in (down, gate_far, up_far):
        far.finish()


def attend(chips, shards, qkv, values_t, w_out, activations, cotangent, gain, w_gate, w_up, down_near):
    rows, depth = activations.shape
    pair = 2 * rows
    group_rows = chips * pair
    width = w_out.shape[0]
    heads = width // HEAD_DIM
    shape = jax.ShapeDtypeStruct
    return pl.pallas_call(
        lambda *refs: attend_kernel(chips, shards, *refs),
        in_specs=[VMEM] + [ANYWHERE] * 8,
        out_specs=[VMEM] * 4 + [ANYWHERE] * 4,
        out_shape=[
            shape((rows, depth), jnp.float32),
            shape((rows, depth), low),
            shape((group_rows, width), low),
            shape((heads, group_rows), jnp.float32),
            shape((group_rows, depth), low),
            shape((depth, w_gate.shape[1]), low),
            shape((depth, w_gate.shape[1]), low),
            shape(down_near.shape, low),
        ],
        scratch_shapes=Loads.scratch(cotangent, qkv, values_t, w_out, activations) + [
            pltpu.VMEM((heads, pair, width), low),
            pltpu.VMEM((width, pair), jnp.float32),
            pltpu.VMEM((pair, width), low),
            pltpu.VMEM((heads, pair), jnp.float32),
            pltpu.VMEM((heads, pair), jnp.float32),
            pltpu.VMEM((rows, depth), low),
        ] + FarShards.scratch(shards) + (NearShards.scratch(shards) + FarShards.scratch(shards)) * 2 + Scatter.scratch(chips, rows, depth) + Gather.scratch(chips),
        compiler_params=pltpu.CompilerParams(collective_id=2, has_side_effects=True, vmem_limit_bytes=63 << 20),
        cost_estimate=pl.CostEstimate(flops=2 * group_rows * (SEQ_LEN + depth) * width, bytes_accessed=4 * group_rows * depth, transcendentals=group_rows * SEQ_LEN * heads // 2),
        name="attend",
    )(gain, cotangent, qkv, values_t, w_out, activations, w_gate, w_up, down_near)


def back_chunk(chunk, rows, grad, qkv, keys_t, mixed, totals, dkey, dvalue, heads_ref, grads_ref, acc, inner_ref):
    width = acc.shape[0]
    heads = width // HEAD_DIM
    here = span(chunk, rows)
    scaled = qkv[here, pl.ds(0, width)] * low(HEAD_DIM**-0.5)
    product = grad.astype(jnp.float32) * mixed[here, :].astype(jnp.float32)
    shape = (inner_ref.shape[0], width)
    pick = (lax.broadcasted_iota(jnp.int32, shape, 1) // HEAD_DIM == lax.broadcasted_iota(jnp.int32, shape, 0)).astype(jnp.float32)
    inner_ref[...] = lax.dot_general(pick, product, NT, precision=lax.Precision.HIGHEST, preferred_element_type=jnp.float32)
    for head in range(heads):
        heads_ref[head] = only_head(scaled, head)
        grads_ref[head] = only_head(grad, head)
    acc[...] = jnp.zeros_like(acc)

    def visit(offset, diagonal):
        keys = pl.ds(offset, rows)
        key_block = qkv[keys, pl.ds(width, width)]
        value_block = qkv[keys, pl.ds(2 * width, width)]
        key_sum, value_sum = dkey[keys, :], dvalue[keys, :]
        for head in range(heads):
            feature = pl.ds(head * HEAD_DIM, HEAD_DIM)
            scores = dot(key_block, heads_ref[head], NT)
            if diagonal:
                scores = causal(scores)
            probs = jnp.exp(scores - totals[pl.ds(head, 1), here])
            dprobs = dot(value_block, grads_ref[head], NT)
            dscores = (probs * (dprobs - inner_ref[pl.ds(head, 1), :])).astype(low)
            value_sum = value_sum + dot(probs.astype(low), grads_ref[head])
            key_sum = key_sum + dot(dscores, heads_ref[head])
            acc[feature, :] = acc[feature, :] + dot(keys_t[feature, keys], dscores)
        dkey[keys, :] = key_sum
        dvalue[keys, :] = value_sum

    over_keys(chunk, rows, visit)


def back_kernel(
    chips, shards,
    branch, terms, inner, grads, grad_both, *refs,
):
    sources, (down, branch_out, qkv_grad, grad_down, grad_out, both_from) = refs[:7], refs[7:13]
    loads = Loads(sources, refs[13:21])
    w_out, qkv, keys_t, mixed, totals, cosine, sine = loads.refs
    inner_chunk, grad_chunk, down_sum, down_tile, out_sum, out_stage, out_from, branch_chunk, dkey, dvalue = refs[21:31]
    heads_ref, grads_ref, acc, inner_ref, inner_sem, grad_sem, branch_sem, tile_sem, out_send, out_recv = refs[31:41]
    sums = refs[41:48]
    sems = refs[48:]
    line = Line(chips)
    rows, depth = down.shape
    pair = 2 * rows
    width = w_out.shape[0]
    scatter = HeldScatter(line, down, terms, *sems[:9])
    gather = Gather(line, branch, branch_out, *sems[9:])

    def fetch(step):
        return pltpu.make_async_copy(inner.at[span(line.target(step), pair)], inner_chunk, inner_sem)

    def fetch_grad(step):
        return pltpu.make_async_copy(grads.at[span(line.target(step), pair)], grad_chunk, grad_sem)

    grid = Grid(shards)
    shard, others = grid.me, grid.others
    columns_out = depth // shards
    both = NearSums(grid, grad_both, both_from, row_shard(columns_out), *sums)

    def give(turn):
        return remote(out_stage.at[turn], out_from.at[turn], out_send.at[turn], out_recv.at[turn], {"fsdp": others[turn]})

    def keep_tile(place):
        return pltpu.make_async_copy(down_tile, grad_down.at[span(place, 256)], tile_sem)

    line.hello([{"fsdp": other} for other in others])
    loads.start()
    fetch(0).start()
    fetch_grad(0).start()
    scatter.load(0).start()
    line.ready(others)
    gather.start()
    both.start()
    out_sum[...] = jnp.zeros_like(out_sum)
    dkey[...] = jnp.zeros_like(dkey)
    dvalue[...] = jnp.zeros_like(dvalue)

    def unrotated(block, chunk):
        table = span(chunk % (SEQ_LEN // pair), pair)
        return (block * widened(cosine[table, :], width) + turned(block * widened(sine[table, :], width), -1.0)).astype(low)

    def attention(chunk):
        gather.arrive_across(chunk)
        copy = pltpu.make_async_copy(branch_out.at[span(chunk, pair)], branch_chunk, branch_sem)
        copy.start()
        copy.wait()
        out_sum[...] += dot(mixed[span(chunk, pair), :], branch_chunk[...], TN)
        grad = dot(branch_chunk[...], w_out[...], NT).astype(low)
        back_chunk(chunk, pair, grad, qkv, keys_t, mixed, totals, dkey, dvalue, heads_ref, grads_ref, acc, inner_ref)
        qkv_grad[span(chunk, pair), pl.ds(0, width)] = unrotated(acc[...].T * HEAD_DIM**-0.5, chunk)

    def close():
        def part(chunk, carry):
            here = span(chunk, pair)
            qkv_grad[here, pl.ds(width, width)] = unrotated(dkey[here, :], chunk)
            qkv_grad[here, pl.ds(2 * width, width)] = dvalue[here, :].astype(low)
            return carry

        lax.fori_loop(0, chips, part, 0)

    def step(index, carry):
        @pl.when(index == 0)
        def _():
            loads.wait(*range(7))
            gather.keep().wait()

        @pl.when(index < chips)
        def _():
            scatter.free(index)
            scatter.share(index).start()

        @pl.when(index == chips)
        def _():
            for turn in range(shards - 1):
                out_stage[turn] = out_sum[:, span(others[turn], columns_out)].astype(low)
                give(turn).start()
            close()

        def due(done, carry):
            target = line.target(done)
            distance = jnp.where(target > line.chip, target - line.chip, line.chip - target)

            @pl.when(distance == chips - index)
            def _():
                scatter.step(done)

            return carry

        lax.fori_loop(0, chips, due, 0)

        @pl.when(jnp.logical_and(index >= 1, index < chips))
        def _():
            gather.step(index)

        @pl.when(index == 1)
        def _():
            both.start_plain()

        @pl.when(index == 2)
        def _():
            both.join()

        @pl.when(index < chips)
        def _():
            attention(line.target(chips - 1 - index))

        def weights(turn, carry):
            fetch(turn).wait()
            fetch_grad(turn).wait()

            def tile(place, carry):
                here = span(place, 256)
                part = dot(inner_chunk[:, here], grad_chunk[...], TN)

                @pl.when(turn == 0)
                def _():
                    down_sum[here, :] = part

                @pl.when(turn > 0)
                def _():
                    down_sum[here, :] += part

                @pl.when(turn == chips - 1)
                def _():
                    @pl.when(place > 0)
                    def _():
                        keep_tile(place - 1).wait()

                    down_tile[...] = down_sum[here, :].astype(low)
                    keep_tile(place).start()

                return carry

            lax.fori_loop(0, down_sum.shape[0] // 256, tile, 0)

            @pl.when(turn < chips - 1)
            def _():
                fetch(turn + 1).start()
                fetch_grad(turn + 1).start()

            return carry

        lax.fori_loop(jnp.where(index == 0, 0, index + 1), jnp.minimum(index + 2, chips), weights, 0)
        return carry

    lax.fori_loop(0, chips + 1, step, 0)
    total = out_sum[:, span(shard, columns_out)]
    for turn in range(shards - 1):
        give(turn).wait_recv()
        total = total + out_from[turn].astype(jnp.float32)
    grad_out[...] = total
    for turn in range(shards - 1):
        give(turn).wait_send()
    keep_tile(down_sum.shape[0] // 256 - 1).wait()
    both.finish()
    scatter.finish()
    gather.finish(False)


def back(chips, shards, branch, terms, inner, grads, grad_both, w_out, qkv, keys_t, mixed, totals, cosine, sine):
    rows, depth = branch.shape
    pair = 2 * rows
    group_rows = chips * pair
    width = w_out.shape[0]
    hidden = inner.shape[1]
    heads = width // HEAD_DIM
    shape = jax.ShapeDtypeStruct
    held = (w_out, qkv, keys_t, mixed, totals, cosine, sine)
    return pl.pallas_call(
        lambda *refs: back_kernel(chips, shards, *refs),
        in_specs=[VMEM] + [ANYWHERE] * 11,
        out_specs=[VMEM, ANYWHERE, VMEM, ANYWHERE, VMEM, ANYWHERE],
        out_shape=[
            shape((rows, depth), jnp.float32),
            shape((group_rows, depth), low),
            shape((group_rows, 3 * width), low),
            shape((hidden, depth), low),
            shape((width, depth // shards), jnp.float32),
            shape((shards // 2, depth // shards, grad_both.shape[1]), low),
        ],
        scratch_shapes=Loads.scratch(*held) + [
            pltpu.VMEM((pair, hidden), low),
            pltpu.VMEM((pair, depth), low),
            pltpu.VMEM((hidden, depth), jnp.float32),
            pltpu.VMEM((256, depth), low),
            pltpu.VMEM((width, depth), jnp.float32),
            pltpu.VMEM((shards - 1, width, depth // shards), low),
            pltpu.VMEM((shards - 1, width, depth // shards), low),
            pltpu.VMEM((pair, depth), low),
            pltpu.VMEM((group_rows, width), jnp.float32),
            pltpu.VMEM((group_rows, width), jnp.float32),
            pltpu.VMEM((heads, pair, width), low),
            pltpu.VMEM((heads, pair, width), low),
            pltpu.VMEM((width, pair), jnp.float32),
            pltpu.VMEM((8, pair), jnp.float32),
            DMA, DMA, DMA, DMA, DMA((shards - 1,)), DMA((shards - 1,)),
        ] + NearSums.scratch(shards, depth // shards, grad_both.shape[1]) + HeldScatter.scratch(chips, rows, depth) + Gather.scratch(chips),
        compiler_params=pltpu.CompilerParams(collective_id=4, has_side_effects=True, vmem_limit_bytes=67043328),
        cost_estimate=pl.CostEstimate(flops=1 << 20, bytes_accessed=1 << 20, transcendentals=0),
        name="back",
    )(branch, terms, inner, grads, grad_both, *held)


def spread_kernel(
    chips, shards,
    gain, gain_part, qkv_hbm, weight_hbm, activations_hbm, attn_tokens, grad_down,
    input_part, grad_qkv, gain_sum, down_from,
    qkv_grad, weight, activations, held_sem,
    attn_cols, qkv_stage, qkv_from, gains, gains_tp, gains_fsdp,
    attn_sem, qkv_send, qkv_recv, tp_send, tp_recv, fsdp_send, fsdp_recv, *sems,
):
    line = Line(chips)
    size = 2 * chips
    rows, depth = input_part.shape
    pair = 2 * rows
    grid = Grid(shards)
    shard = grid.me
    columns = depth // shards
    loads = Loads((qkv_hbm, weight_hbm, activations_hbm), (qkv_grad, weight, activations, held_sem))
    down = NearSums(grid, grad_down, down_from, column_shard(grad_down.shape[0], columns), *sems[:7])
    scatter = Scatter(line, input_part, *sems[7:])

    def peer(turn):
        return (shard + 1 + turn) % shards

    def fetch(turn):
        return pltpu.make_async_copy(attn_tokens.at[:, span(peer(turn), columns)], attn_cols.at[turn % 2], attn_sem.at[turn % 2])

    def give(turn):
        return remote(qkv_stage.at[turn], qkv_from.at[turn], qkv_send.at[turn], qkv_recv.at[turn], {"fsdp": peer(turn)})

    def tell_tp(ahead):
        return remote(gains, gains_tp.at[line.me], tp_send.at[ahead - 1], tp_recv.at[line.me], {"tp": (line.me + ahead) % size})

    def tell_fsdp(ahead):
        return remote(gains, gains_fsdp.at[shard], fsdp_send.at[ahead - 1], fsdp_recv.at[shard], {"fsdp": (shard + ahead) % shards})

    for ahead in range(1, size):
        hello({"tp": (line.me + ahead) % size})
    for ahead in range(1, shards):
        hello({"fsdp": (shard + ahead) % shards})
    loads.start()
    fetch(0).start()
    loads.wait(0, 1)
    pl.semaphore_wait(pltpu.get_barrier_semaphore(), size - 1 + shards - 1)
    down.start()

    def weights(turn, carry):
        @pl.when(turn < shards - 1)
        def _():
            fetch(turn + 1).start()

        fetch(turn).wait()
        part = dot(attn_cols[turn % 2], qkv_grad[...], TN)

        @pl.when(turn < shards - 1)
        def _():
            qkv_stage[turn] = part.astype(low)
            give(turn).start()

        @pl.when(turn == shards - 1)
        def _():
            grad_qkv[...] = part

        return carry

    def step(index, carry):
        @pl.when(index < chips)
        def _():
            here = span(line.target(index), pair)
            scatter.free(index)

            def tile(place, carry):
                there = span(place, 512)
                scatter.term[index % 2, :, there] = dot(qkv_grad[here, :], weight[there, :], NT).astype(low)
                return carry

            lax.fori_loop(0, depth // 512, tile, 0)
            scatter.share(index).start()

        @pl.when(index == 1)
        def _():
            down.start_plain()

        @pl.when(index == 2)
        def _():
            down.join()

        def phase(which, carry):
            done = jnp.maximum(index - 1, 0)
            late = line.fed(line.target(done))
            turn = jnp.logical_or(jnp.logical_and(which == 0, jnp.logical_not(late)), jnp.logical_and(which == 2, late))

            @pl.when(jnp.logical_and(index >= 1, turn))
            def _():
                scatter.step(done)

            @pl.when(jnp.logical_and(which == 1, index < 2))
            def _():
                lax.fori_loop(index, jnp.where(index == 0, 1, shards), weights, 0)

            return carry

        lax.fori_loop(0, 3, phase, 0)
        return carry

    lax.fori_loop(0, chips + 1, step, 0)
    gains[0:1, :] = jnp.zeros((1, depth), jnp.float32)
    gains[1:2, :] = gain_part[...]

    def norm(here):
        part, grad = norm_back(activations[here, :], gain[...], input_part[here, :])
        input_part[here, :] = part
        gains[0:1, :] += grad

    loads.wait(2)
    by_rows(rows, norm)

    gains_tp[line.me] = gains[...]
    for ahead in range(1, size):
        tell_tp(ahead).start()
    for turn in range(shards - 1):
        give(turn).wait_recv()
        grad_qkv[...] += qkv_from[turn].astype(jnp.float32)
    for ahead in range(1, size):
        source = (line.me + ahead) % size
        remote(gains, gains_tp.at[source], tp_send.at[0], tp_recv.at[source], {"tp": source}).wait_recv()
    total = gains_tp[0]
    for source in range(1, size):
        total = total + gains_tp[source]
    for ahead in range(1, size):
        tell_tp(ahead).wait_send()
    gains[...] = total
    gains_fsdp[shard] = total
    for ahead in range(1, shards):
        tell_fsdp(ahead).start()
    for ahead in range(1, shards):
        source = (shard + ahead) % shards
        remote(gains, gains_fsdp.at[source], fsdp_send.at[0], fsdp_recv.at[source], {"fsdp": source}).wait_recv()
    total = gains_fsdp[0]
    for source in range(1, shards):
        total = total + gains_fsdp[source]
    gain_sum[...] = total
    for ahead in range(1, shards):
        tell_fsdp(ahead).wait_send()
    for turn in range(shards - 1):
        give(turn).wait_send()
    down.finish()
    scatter.finish()


def spread(chips, shards, qkv_grad, weight, activations, gain, gain_part, attn_tokens, grad_down):
    group_rows = qkv_grad.shape[0]
    rows, depth = activations.shape
    width = qkv_grad.shape[1] // 3
    columns = depth // shards
    size = 2 * chips
    shape = jax.ShapeDtypeStruct
    return pl.pallas_call(
        lambda *refs: spread_kernel(chips, shards, *refs),
        in_specs=[VMEM] * 2 + [ANYWHERE] * 5,
        out_specs=[VMEM] * 3 + [ANYWHERE],
        out_shape=[
            shape((rows, depth), jnp.float32),
            shape((columns, 3 * width), jnp.float32),
            shape((2, depth), jnp.float32),
            shape((shards // 2, grad_down.shape[0], columns), low),
        ],
        scratch_shapes=Loads.scratch(qkv_grad, weight, activations) + [
            pltpu.VMEM((2, group_rows, columns), low),
            pltpu.VMEM((shards - 1, columns, 3 * width), low),
            pltpu.VMEM((shards - 1, columns, 3 * width), low),
            pltpu.VMEM((2, depth), jnp.float32),
            pltpu.VMEM((size, 2, depth), jnp.float32),
            pltpu.VMEM((shards, 2, depth), jnp.float32),
            DMA((2,)), DMA((shards - 1,)), DMA((shards - 1,)),
            DMA((size - 1,)), DMA((size,)), DMA((shards - 1,)), DMA((shards,)),
        ] + NearSums.scratch(shards, grad_down.shape[0], columns) + Scatter.scratch(chips, rows, depth),
        compiler_params=pltpu.CompilerParams(collective_id=5, has_side_effects=True, vmem_limit_bytes=63 << 20),
        cost_estimate=pl.CostEstimate(flops=1 << 20, bytes_accessed=1 << 20, transcendentals=0),
        name="spread",
    )(gain, gain_part, qkv_grad, weight, activations, attn_tokens, grad_down)


def chip_at(place, chips):
    return jnp.where(2 * place < chips, 2 * place, 2 * (chips - 1 - place) + 1)


def place_of(chip, chips):
    return jnp.where(chip % 2 == 0, chip // 2, chips - 1 - chip // 2)


def feed_kernel(
    chips, shards,
    gain, hidden_hbm, cotangent_hbm, tokens, grads_hbm, w_gate, w_up, w_down, gate_all, up_all, down_near, down_far,
    hidden_grad, branch, gain_part, inner_out, grad_both, down_out,
    hidden_state, cotangent, state_sem, down_tile, down_sem, tokens_all, gate_w, up_w, down_w, grads, inner, gate_grad, up_grad, term, from_core, from_ring, total, tile_gate, tile_up,
    load_sem, own_sem, grad_sem, store_sem, tile_sem,
    ring_send, ring_recv, core_send, core_recv, share_send, share_recv, total_send, total_recv,
):
    rows, depth = hidden_grad.shape
    pair = 2 * rows
    width = gate_w.shape[1]
    me = lax.axis_index("tp")
    chip, core = me // 2, me % 2
    place = place_of(chip, chips)
    following = {"tp": 2 * chip_at((place + 1) % chips, chips) + core}
    before = {"tp": 2 * chip_at((place + chips - 1) % chips, chips) + core}
    partner = {"tp": 2 * chip + 1 - core}

    grid = Grid(shards)
    rows_of, columns_of = row_shard(w_gate.shape[0]), column_shard(*w_down.shape)

    def load(array, source, shard, whole):
        at = columns_of if array == 2 else rows_of
        target = at((gate_w, up_w, down_w)[array], shard, None)
        return pltpu.make_async_copy(at(source, shard, None) if whole else source, target, load_sem.at[array, shard])

    def load_weights():
        for shard in range(shards):
            own, near = grid.me == shard, grid.is_near(shard)

            @pl.when(own)
            def _():
                for array, source in enumerate((w_gate, w_up, w_down)):
                    load(array, source, shard, False).start()

            @pl.when(jnp.logical_not(own))
            def _():
                for array, source in enumerate((gate_all, up_all)):
                    load(array, source, shard, True).start()

            @pl.when(jnp.logical_and(near, jnp.logical_not(own)))
            def _():
                load(2, down_near, shard, True).start()

            @pl.when(jnp.logical_not(near))
            def _():
                load(2, down_far, shard, True).start()

    own = pltpu.make_async_copy(tokens, tokens_all.at[span(me, rows)], own_sem)
    states = Loads((hidden_hbm, cotangent_hbm), (hidden_state, cotangent, state_sem))

    def source(slot):
        return chip_at((place + chips - slot) % chips, chips)

    def fetch(slot):
        return pltpu.make_async_copy(grads_hbm.at[span(source(slot), pair)], grads.at[slot % 2], grad_sem.at[slot % 2])

    def block(slot):
        return tokens_all.at[span(2 * source(slot) + core, rows)]

    def to_ring(slot):
        return remote(block(slot), block(slot), ring_send.at[slot], ring_recv.at[slot], following)

    def to_core(slot):
        return remote(block(slot), block(slot), core_send.at[slot], core_recv.at[slot], partner)

    def store(slot):
        return pltpu.make_async_copy(inner.at[slot], inner_out.at[span(source(slot), pair)], store_sem.at[slot])

    def keep_down(slot, tile):
        there = down_out.at[span(source(slot), pair), span(tile, 256)]
        return pltpu.make_async_copy(down_tile.at[tile % 2], there, down_sem.at[tile % 2])

    def down_term(slot, carry):
        def tile(index, carry):
            @pl.when(index > 1)
            def _():
                keep_down(slot, index - 2).wait()

            down_tile[index % 2] = dot(inner[slot], down_w[:, span(index, 256)]).astype(low)
            keep_down(slot, index).start()
            return carry

        lax.fori_loop(0, depth // 256, tile, 0)
        for index in range(depth // 256 - 2, depth // 256):
            keep_down(slot, index).wait()
        return carry

    def share(slot):
        place = jnp.where(slot == 0, 0, 1 + slot % 2)
        return remote(term.at[span(1 - core, rows)], from_core.at[place], share_send, share_recv.at[place], partner)

    def pass_on(slot):
        return remote(total.at[slot % 2], from_ring.at[slot - 1], total_send.at[slot % 2], total_recv.at[slot - 1], following)

    for device in (following, before, partner):
        hello(device)
    own.start()
    fetch(0).start()
    load_weights()
    own.wait()
    pl.semaphore_wait(pltpu.get_barrier_semaphore(), 3)

    def step(slot, carry):
        here = slot % 2
        wide_rows = span(source(slot), pair)
        mine = span(core, rows)

        @pl.when(slot > 0)
        def _():
            to_ring(slot - 1).wait_recv()

        @pl.when(slot < chips - 1)
        def _():
            to_ring(slot).start()
            fetch(slot + 1).start()

        to_core(slot).start()

        @pl.when(slot == 0)
        def _():
            for shard in range(shards):
                for array, source in enumerate((gate_all, up_all, down_near)):
                    load(array, source, shard, True).wait()

        @pl.when(slot == 1)
        def _():
            states.start()

        to_core(slot).wait_recv()
        fetch(slot).wait()

        def narrow(tile, carry):
            columns = span(tile, 256)
            token = tokens_all[wide_rows, :]
            gate = dot(token, gate_w[:, columns])
            up = dot(token, up_w[:, columns])
            grad = dot(grads[here], down_w[columns, :], NT)
            squash = jax.nn.sigmoid(gate)
            act = gate * squash
            inner[slot, :, columns] = (act * up).astype(low)
            up_grad[wide_rows, columns] = (grad * act).astype(low)
            gate_grad[wide_rows, columns] = (grad * up * squash * (1.0 + gate * (1.0 - squash))).astype(low)
            return carry

        lax.fori_loop(0, width // 256, narrow, 0)
        store(slot).start()

        @pl.when(slot > 0)
        def _():
            share(slot - 1).wait_send()

        def wide(tile, carry):
            columns = span(tile, 256)
            part = dot(gate_grad[wide_rows, :], gate_w[columns, :], NT) + dot(up_grad[wide_rows, :], up_w[columns, :], NT)
            term[:, columns] = part.astype(low)
            return carry

        lax.fori_loop(0, depth // 256, wide, 0)
        share(slot).start()

        @pl.when(slot == 0)
        def _():
            hidden_grad[...] = term[mine, :].astype(jnp.float32)

        middle = jnp.logical_and(slot >= 2, slot < chips - 1)
        lax.fori_loop(jnp.where(slot == 2, 0, slot), jnp.where(middle, slot + 1, 0), down_term, 0)

        @pl.when(slot > 0)
        def _():
            share(slot).wait_recv()

            @pl.when(slot > 2)
            def _():
                pass_on(slot - 2).wait_send()

            @pl.when(slot == 1)
            def _():
                total[here] = (term[mine, :].astype(jnp.float32) + from_core[1 + here].astype(jnp.float32)).astype(low)

            @pl.when(slot > 1)
            def _():
                pass_on(slot - 1).wait_recv()
                total[here] = (term[mine, :].astype(jnp.float32) + from_core[1 + here].astype(jnp.float32) + from_ring[slot - 2].astype(jnp.float32)).astype(low)

            pass_on(slot).start()

        return carry

    lax.fori_loop(0, chips, step, 0)

    def tiles(index):
        there = span(index, 256)
        return (
            pltpu.make_async_copy(tile_gate.at[index % 2], grad_both.at[there, pl.ds(0, width)], tile_sem.at[0, index % 2]),
            pltpu.make_async_copy(tile_up.at[index % 2], grad_both.at[there, pl.ds(width, width)], tile_sem.at[1, index % 2]),
        )

    def weights(index, carry):
        @pl.when(index > 1)
        def _():
            for copy in tiles(index - 2):
                copy.wait()

        token = tokens_all[:, span(index, 256)]
        tile_gate[index % 2] = dot(token, gate_grad[...], TN).astype(low)
        tile_up[index % 2] = dot(token, up_grad[...], TN).astype(low)
        for copy in tiles(index):
            copy.start()
        return carry

    lax.fori_loop(0 if chips < 4 else chips - 1, chips, down_term, 0)
    lax.fori_loop(0, depth // 256, weights, 0)
    states.wait(0, 1)
    share(0).wait_recv()
    pass_on(chips - 1).wait_recv()
    gain_part[...] = jnp.zeros_like(gain_part)

    def norm(here):
        grad = hidden_grad[here, :] + from_core[0, here, :].astype(jnp.float32) + from_ring[chips - 2, here, :].astype(jnp.float32)
        part, gain_grad = norm_back(hidden_state[here, :], gain[...], grad)
        full = cotangent[here, :] + part
        hidden_grad[here, :] = full
        branch[here, :] = full.astype(low)
        gain_part[...] += gain_grad

    by_rows(rows, norm)
    share(chips - 1).wait_send()
    for slot in range(chips):
        to_core(slot).wait_send()
        if slot < chips - 1:
            to_ring(slot).wait_send()
        if slot >= max(1, chips - 2):
            pass_on(slot).wait_send()
        store(slot).wait()
    for index in range(depth // 256 - 2, depth // 256):
        for copy in tiles(index):
            copy.wait()


def feed(chips, shards, hidden_state, cotangent, gain, tokens, grads, w_gate, w_up, w_down, gate_all, up_all, down_near, down_far):
    rows, depth = tokens.shape
    pair = 2 * rows
    group_rows = chips * pair
    width = w_down.shape[0]
    shape = jax.ShapeDtypeStruct
    return pl.pallas_call(
        lambda *refs: feed_kernel(chips, shards, *refs),
        in_specs=[VMEM] + [ANYWHERE] * 11,
        out_specs=[VMEM] * 3 + [ANYWHERE] * 3,
        out_shape=[
            shape((rows, depth), jnp.float32),
            shape((rows, depth), low),
            shape((1, depth), jnp.float32),
            shape((group_rows, width), low),
            shape((depth, 2 * width), low),
            shape((group_rows, depth), low),
        ],
        scratch_shapes=Loads.scratch(hidden_state, cotangent) + [
            pltpu.VMEM((2, pair, 256), low),
            DMA((2,)),
            pltpu.VMEM((group_rows, depth), low),
            pltpu.VMEM((depth, width), low),
            pltpu.VMEM((depth, width), low),
            pltpu.VMEM((width, depth), low),
            pltpu.VMEM((2, pair, depth), low),
            pltpu.VMEM((chips, pair, width), low),
            pltpu.VMEM((group_rows, width), low),
            pltpu.VMEM((group_rows, width), low),
            pltpu.VMEM((pair, depth), low),
            pltpu.VMEM((3, rows, depth), low),
            pltpu.VMEM((chips - 1, rows, depth), low),
            pltpu.VMEM((2, rows, depth), low),
            pltpu.VMEM((2, 256, width), low),
            pltpu.VMEM((2, 256, width), low),
            DMA((3, shards)), DMA, DMA((2,)), DMA((chips,)), DMA((2, 2)),
            DMA((chips,)), DMA((chips,)), DMA((chips,)), DMA((chips,)),
            DMA, DMA((3,)), DMA((2,)), DMA((chips - 1,)),
        ],
        compiler_params=pltpu.CompilerParams(collective_id=3, has_side_effects=True, vmem_limit_bytes=67043328),
        cost_estimate=pl.CostEstimate(flops=16 * group_rows * depth * width, bytes_accessed=10 * group_rows * depth, transcendentals=group_rows * width),
        name="feed",
    )(gain, hidden_state, cotangent, tokens, grads, w_gate, w_up, w_down, gate_all, up_all, down_near, down_far)


def finish_kernel(
    shard_ref, hidden, down, hidden_grad, input_part, both, both_from, grad_down, down_from, grad_qkv, grad_out,
    output, input_grad, query, key, value, out, gate, up, down_out,
):
    output[...] = hidden[...] + down[...]
    input_grad[...] = hidden_grad[...] + input_part[...]
    width = query.shape[1]
    for part, ref in enumerate((query, key, value)):
        ref[...] = grad_qkv[:, pl.ds(part * width, width)]
    out[...] = grad_out[...]
    wide = gate.shape[1]
    for side, ref in enumerate((gate, up)):
        columns = pl.ds(side * wide, wide)
        total = both[:, columns].astype(jnp.float32)
        for turn in range(both_from.shape[0]):
            total = total + both_from[turn, :, columns].astype(jnp.float32)
        ref[...] = total
    total = grad_down[...].astype(jnp.float32)
    for turn in range(down_from.shape[0]):
        total = total + down_from[turn].astype(jnp.float32)
    down_out[...] = total


def finish(shard, hidden, down, hidden_grad, input_part, both, both_from, grad_down, down_from, grad_qkv, grad_out):
    steps = 8
    shape = jax.ShapeDtypeStruct
    columns = down_from.shape[2]
    results = [shape(hidden.shape, jnp.float32)] * 2
    results += [shape((columns, grad_qkv.shape[1] // 3), jnp.float32)] * 3 + [shape(grad_out.shape, jnp.float32)]
    results += [shape((columns, both.shape[1] // 2), jnp.float32)] * 2 + [shape((grad_down.shape[0], columns), jnp.float32)]
    spec = lambda a: pl.BlockSpec((a.shape[0] // steps, a.shape[1]), lambda i, s: (i, 0))
    spec3 = lambda a: pl.BlockSpec((a.shape[0], a.shape[1] // steps, a.shape[2]), lambda i, s: (0, i, 0))
    return pl.pallas_call(
        finish_kernel,
        grid_spec=pltpu.PrefetchScalarGridSpec(
            num_scalar_prefetch=1,
            grid=(steps,),
            in_specs=[
                spec(hidden), spec(down), spec(hidden_grad), spec(input_part),
                pl.BlockSpec((columns // steps, both.shape[1]), lambda i, s: (s[0] * steps + i, 0)),
                spec3(both_from),
                pl.BlockSpec((grad_down.shape[0] // steps, columns), lambda i, s: (i, s[0])),
                spec3(down_from), spec(grad_qkv), spec(grad_out),
            ],
            out_specs=[spec(a) for a in results],
        ),
        out_shape=results,
        name="finish",
    )(shard.reshape(1), hidden, down, hidden_grad, input_part, both, both_from, grad_down, down_from, grad_qkv, grad_out)


def rope_tables():
    half = HEAD_DIM // 2
    positions = jnp.arange(SEQ_LEN, dtype=jnp.int32).astype(jnp.float32)
    column = jnp.arange(half, dtype=jnp.int32)
    inverse = jnp.power(jnp.float32(rope_base), -2.0 * column.astype(jnp.float32) / HEAD_DIM)
    angle = positions[None, :] * inverse[:, None]
    return (jnp.cos(angle), jnp.sin(angle))


def make_body(mesh):
    chips, shards = mesh.shape["tp"] // 2, mesh.shape["fsdp"]

    def body(activations, gain_attn, w_query, w_key, w_value, w_out, gain_mlp, w_gate, w_up, w_down, cotangent):
        gain_attn, gain_mlp = gain_attn[None, :], gain_mlp[None, :]
        seen_attn, w_qkv, full_out, qkv, keys_t, values_t, cosine, sine, down_near = project(
            chips, shards, activations, gain_attn, w_query, w_key, w_value, w_out, *rope_tables(), w_down
        )
        hidden_state, normed_mlp, mixed, totals, seen_grad, gate_all, up_all, down_far = attend(
            chips, shards, qkv, values_t, full_out, activations, cotangent, gain_mlp, w_gate, w_up, down_near
        )
        hidden_grad, branch_grad, gain_part, inner, grad_both, terms = feed(
            chips, shards, hidden_state, cotangent, gain_mlp, normed_mlp, seen_grad,
            w_gate, w_up, w_down, gate_all, up_all, down_near, down_far,
        )
        down, _, qkv_grad, grad_down, grad_out, both_from = back(
            chips, shards, branch_grad, terms, inner, seen_grad, grad_both, full_out, qkv, keys_t, mixed, totals, cosine, sine
        )
        input_part, grad_qkv, gain_sums, down_from = spread(
            chips, shards, qkv_grad, w_qkv, activations, gain_attn, gain_part, seen_attn, grad_down
        )
        output, input_grad, grad_query, grad_key, grad_value, grad_out, grad_gate, grad_up, grad_down = finish(
            lax.axis_index("fsdp"), hidden_state, down, hidden_grad, input_part,
            grad_both, both_from, grad_down, down_from, grad_qkv, grad_out,
        )
        return (
            output, input_grad, gain_sums[0], grad_query, grad_key, grad_value, grad_out, gain_sums[1],
            grad_gate, grad_up, grad_down,
        )

    return body


def solution(mesh):
    tokens = P(("fsdp", "tp"), None)
    column = P("fsdp", "tp")
    row = P("tp", "fsdp")
    in_specs = (tokens, P(), column, column, column, row, P(), column, column, row, tokens)
    out_specs = (tokens, tokens, P(), column, column, column, row, P(), column, column, row)
    return jax.shard_map(make_body(mesh), mesh=mesh, in_specs=in_specs, out_specs=out_specs, check_vma=False)
```

```python
import jax
import jax.numpy as jnp
import numpy as np
from jax import lax
from jax.experimental import pallas as pl
from jax.experimental.pallas import tpu as pltpu
from jax.sharding import PartitionSpec as P

HEAD_DIM = 64
SEQ_LEN = 2048
LANES = 128
rope_base = 130000.0
norm_eps = 1e-05
masked_score = -1e30

NT = (((1,), (1,)), ((), ()))
NN = (((1,), (0,)), ((), ()))
TN = (((0,), (0,)), ((), ()))
MESH = pl.DeviceIdType.MESH
DMA = pltpu.SemaphoreType.DMA
ANYWHERE = pl.BlockSpec(memory_space=pl.ANY)
VMEM = pl.BlockSpec(memory_space=pltpu.VMEM)
low = jnp.bfloat16


def dot(left, right, dims=NN):
    return lax.dot_general(left, right, dims, preferred_element_type=jnp.float32)


def span(index, size):
    return pl.ds(pl.multiple_of(index * size, size), size)


def remote(source, target, send, receive, device):
    return pltpu.make_async_remote_copy(
        src_ref=source, dst_ref=target, send_sem=send, recv_sem=receive,
        device_id=device, device_id_type=MESH,
    )


def hello(device):
    pl.semaphore_signal(pltpu.get_barrier_semaphore(), inc=1, device_id=device, device_id_type=MESH)


class Line:
    def __init__(self, chips):
        self.chips = chips
        self.me = lax.axis_index("tp")
        self.chip, self.core = self.me // 2, self.me % 2
        self.partner = 2 * self.chip + 1 - self.core
        self.has_left, self.has_right = self.chip > 0, self.chip < chips - 1

    def hello(self, more=()):
        hello({"tp": self.partner})

        @pl.when(self.has_left)
        def _():
            hello({"tp": self.me - 2})

        @pl.when(self.has_right)
        def _():
            hello({"tp": self.me + 2})

        for device in more:
            hello(device)

    def ready(self, more=()):
        count = 1 + len(more) + jnp.where(self.has_left, 1, 0) + jnp.where(self.has_right, 1, 0)
        pl.semaphore_wait(pltpu.get_barrier_semaphore(), count)

    def target(self, step):
        after = self.chips - 1 - self.chip
        most, least = jnp.maximum(self.chip, after), jnp.minimum(self.chip, after)
        sign = jnp.where(after >= self.chip, 1, -1)
        late = step - (most - least)
        side = jnp.where(late % 2 == 0, sign, -sign)
        return jnp.where(late < 0, self.chip + sign * (most - step), self.chip + side * (least - late // 2))


    def fed(self, target):
        after, before = jnp.logical_and(target >= self.chip, self.has_left), jnp.logical_and(target <= self.chip, self.has_right)
        return jnp.logical_or(after, before)


class Gather:
    @staticmethod
    def scratch(chips, parts=1):
        return [DMA((2 * chips, parts)), DMA((chips, parts)), DMA((chips, parts)), DMA((chips, parts)), DMA]

    def __init__(self, line, own, out, received, right, left, across, local, parts=1):
        self.line, self.out = line, out
        self.received, self.right, self.left, self.across, self.local = received, right, left, across, local
        self.parts = parts
        self.rows = out.shape[0] // (2 * line.chips * parts)
        self.held = own is None
        self.own = out.at[span(line.me, self.rows * parts)] if self.held else own

    def block(self, index, part):
        return self.out.at[span(index * self.parts + part, self.rows)]

    def mine(self, part):
        return self.own.at[pl.ds(part * self.rows, self.rows)]

    def copy(self, sems, chip, part, device, mine):
        index = 2 * chip + self.line.core
        source = self.mine(part) if mine else self.block(index, part)
        return remote(source, self.block(index, part), sems.at[chip, part], self.received.at[index, part], {"tp": device})

    def keep(self):
        return pltpu.make_async_copy(self.own, self.out.at[span(self.line.me, self.rows * self.parts)], self.local)

    def start(self):
        line = self.line
        if not self.held:
            self.keep().start()
        for part in range(self.parts):
            @pl.when(line.has_right)
            def _():
                self.copy(self.right, line.chip, part, line.me + 2, True).start()

            @pl.when(line.has_left)
            def _():
                self.copy(self.left, line.chip, part, line.me - 2, True).start()

            self.copy(self.across, line.chip, part, line.partner, True).start()

    def arrive(self, index, part):
        remote(self.mine(part), self.block(index, part), self.right.at[0, part], self.received.at[index, part], {"tp": self.line.partner}).wait_recv()

    def arrive_across(self, chip):
        for part in range(self.parts):
            self.arrive(2 * chip + 1 - self.line.core, part)

    def step(self, distance):
        line = self.line
        before, after = line.chip - distance, line.chip + distance
        for part in range(self.parts):
            @pl.when(before >= 0)
            def _():
                self.arrive(2 * before + line.core, part)

                @pl.when(line.has_right)
                def _():
                    self.copy(self.right, before, part, line.me + 2, False).start()

                self.copy(self.across, before, part, line.partner, False).start()

            @pl.when(after < line.chips)
            def _():
                self.arrive(2 * after + line.core, part)

                @pl.when(line.has_left)
                def _():
                    self.copy(self.left, after, part, line.me - 2, False).start()

                self.copy(self.across, after, part, line.partner, False).start()

    def finish(self, arrivals):
        line = self.line
        if arrivals:
            self.keep().wait()
        for chip in range(line.chips):
            if arrivals:
                self.arrive_across(chip)
            for part in range(self.parts):
                self.copy(self.across, chip, part, line.partner, True).wait_send()

                @pl.when(jnp.logical_and(line.has_right, chip <= line.chip))
                def _():
                    self.copy(self.right, chip, part, line.me + 2, True).wait_send()

                @pl.when(jnp.logical_and(line.has_left, chip >= line.chip))
                def _():
                    self.copy(self.left, chip, part, line.me - 2, True).wait_send()


class Scatter:
    @staticmethod
    def scratch(chips, rows, depth):
        slots = chips // 2 + 1
        return [
            pltpu.VMEM((slots, 2 * rows, depth), low),
            pltpu.VMEM((chips, rows, depth), low),
            pltpu.VMEM((chips + 1, rows, depth), low),
            pltpu.VMEM((2, rows, depth), low),
            DMA((slots,)), DMA((chips,)), DMA((2,)), DMA((chips + 1,)),
        ]

    def __init__(self, line, out, term, shares, lines, total, share_send, share_recv, line_send, line_recv):
        self.line, self.out = line, out
        self.term, self.shares, self.lines, self.total = term, shares, lines, total
        self.share_send, self.share_recv, self.line_send, self.line_recv = share_send, share_recv, line_send, line_recv
        self.rows = out.shape[0]
        self.slots = term.shape[0]

    def share(self, step):
        slot = step % self.slots
        source = self.term.at[slot, span(1 - self.line.core, self.rows)]
        return remote(source, self.shares.at[step], self.share_send.at[slot], self.share_recv.at[step], {"tp": self.line.partner})

    def due(self, index, fed):
        def one(step, carry):
            target = self.line.target(step)
            distance = jnp.where(target > self.line.chip, target - self.line.chip, self.line.chip - target)
            turn = True if fed is None else self.line.fed(target) == fed

            @pl.when(jnp.logical_and(distance == self.line.chips - index, turn))
            def _():
                self.step(step)

            return carry

        return one

    def mine(self, step):
        return self.term[step % self.slots, span(self.line.core, self.rows), :]

    def pass_on(self, step):
        line, target = self.line, self.line.target(step)
        onward = target > line.chip
        slot = jnp.where(onward, target, jnp.where(target == line.chip - 1, line.chips, target))
        device = jnp.where(onward, line.me + 2, line.me - 2)
        return remote(self.total.at[step % 2], self.lines.at[slot], self.line_send.at[step % 2], self.line_recv.at[slot], {"tp": device})

    def add(self, slot):
        remote(self.total.at[0], self.lines.at[slot], self.line_send.at[0], self.line_recv.at[slot], {"tp": self.line.partner}).wait_recv()
        self.out[...] += self.lines[slot].astype(jnp.float32)

    def free(self, step):
        @pl.when(step >= self.slots)
        def _():
            self.share(step - self.slots).wait_send()

    def step(self, step):
        line, target = self.line, self.line.target(step)
        self.share(step).wait_recv()
        self.out[...] = self.mine(step).astype(jnp.float32) + self.shares[step].astype(jnp.float32)

        @pl.when(jnp.logical_and(target >= line.chip, line.has_left))
        def _():
            self.add(target)

        @pl.when(jnp.logical_and(target <= line.chip, line.has_right))
        def _():
            self.add(jnp.where(target == line.chip, line.chips, target))

        @pl.when(step < line.chips - 1)
        def _():
            @pl.when(step >= 2)
            def _():
                self.pass_on(step - 2).wait_send()

            self.total[step % 2] = self.out[...].astype(low)
            self.pass_on(step).start()

    def finish(self):
        chips = self.line.chips
        for step in range(max(0, chips - 3), chips - 1):
            self.pass_on(step).wait_send()
        for step in range(max(0, chips - self.slots), chips):
            self.share(step).wait_send()


NORM_ROWS = 64


def normed(value, gain):
    return value * lax.rsqrt(jnp.mean(value * value, axis=-1, keepdims=True) + norm_eps) * gain


def norm_back(value, gain, grad):
    scale = lax.rsqrt(jnp.mean(value * value, axis=-1, keepdims=True) + norm_eps)
    unit = value * scale
    scaled = grad * gain
    return scale * (scaled - unit * jnp.mean(scaled * unit, axis=-1, keepdims=True)), jnp.sum(grad * unit, axis=0, keepdims=True)


def by_rows(rows, work):
    def step(index, carry):
        work(span(index, NORM_ROWS))
        return carry

    lax.fori_loop(0, rows // NORM_ROWS, step, 0)


class Grid:
    def __init__(self, shards):
        self.shards, self.across = shards, shards // 2
        self.me = lax.axis_index("fsdp")
        self.row, self.column = self.me // self.across, self.me % self.across
        self.others = [(self.me + ahead) % shards for ahead in range(1, shards)]
        self.mates = [self.row * self.across + (self.column + ahead) % self.across for ahead in range(1, self.across)]
        self.twin = (1 - self.row) * self.across + self.column
        self.near = self.mates + [self.twin]

    def is_near(self, shard):
        return jnp.logical_or(shard // self.across == self.row, shard % self.across == self.column)


class NearShards:
    scratch = staticmethod(lambda shards: [DMA((shards // 2,)), DMA((shards // 2,))])

    def __init__(self, grid, own, whole, at, send, receive):
        place = at(whole, grid.me, None)
        self.copies = [remote(own, place, send.at[i], receive.at[i], {"fsdp": peer}) for i, peer in enumerate(grid.near)]

    def start(self):
        for copy in self.copies:
            copy.start()

    def arrive(self):
        for copy in self.copies:
            copy.wait_recv()

    def finish(self):
        for copy in self.copies:
            copy.wait_send()


class FarShards:
    scratch = staticmethod(lambda shards: [DMA((2, shards // 2 - 1)), DMA((2, shards // 2 - 1))])

    def __init__(self, grid, near, whole, at, send, receive):
        self.copies = []
        for i, mate in enumerate(grid.mates):
            self.copies.append(remote(at(near, mate, 0), at(whole, mate, 0), send.at[0, i], receive.at[0, i], {"fsdp": grid.twin}))
            self.copies.append(remote(at(near, grid.twin, 1), at(whole, grid.twin, 1), send.at[1, i], receive.at[1, i], {"fsdp": mate}))

    def start(self):
        for copy in self.copies:
            copy.start()

    def finish(self):
        for copy in self.copies:
            copy.wait_recv()
            copy.wait_send()


class NearSums:
    @staticmethod
    def scratch(shards, rows, columns):
        across = shards // 2
        return [
            pltpu.VMEM((2, across - 1, rows // 2, columns), low),
            pltpu.VMEM((across, rows // 2, columns), low),
            DMA((2, across - 1)), DMA((2, across - 1)), DMA((across, 2)), DMA((across, 2)), DMA((across,)),
        ]

    def __init__(self, grid, part, out, at, relay, base, relay_send, relay_recv, near_send, near_recv, load_sem):
        self.relay, self.base = relay, base
        last = grid.across - 1
        half = base.shape[1]

        def near(source, slot, which, peer):
            target = out.at[slot, pl.ds(which * half, half)]
            return remote(source, target, near_send.at[slot, which], near_recv.at[slot, which], {"fsdp": peer})

        self.by_twin, self.by_mate, self.plain, self.joined, self.loads = [], [], [], [], []
        for i, mate in enumerate(grid.mates):
            far = (1 - grid.row) * grid.across + mate % grid.across
            self.by_twin.append(remote(at(part, far, 0), relay.at[0, i], relay_send.at[0, i], relay_recv.at[0, i], {"fsdp": grid.twin}))
            self.by_mate.append(remote(at(part, far, 1), relay.at[1, i], relay_send.at[1, i], relay_recv.at[1, i], {"fsdp": mate}))
            self.plain.append(near(at(part, mate, 1), i, 1, mate))
            self.joined.append(near(relay.at[0, i], i, 0, mate))
            self.loads.append(pltpu.make_async_copy(at(part, mate, 0), base.at[i], load_sem.at[i]))
        self.plain.append(near(at(part, grid.twin, 0), last, 0, grid.twin))
        self.joined.append(near(relay.at[1, 0], last, 1, grid.twin))
        self.loads.append(pltpu.make_async_copy(at(part, grid.twin, 1), base.at[last], load_sem.at[last]))

    def start(self):
        for copy in self.by_twin + self.by_mate + self.loads:
            copy.start()

    def start_plain(self):
        for copy in self.plain:
            copy.start()

    def join(self):
        for copy in self.by_twin + self.by_mate:
            copy.wait_recv()
        for copy in self.loads:
            copy.wait()
        last = self.base.shape[0] - 1
        for i in range(last):
            self.relay[0, i] = (self.base[i].astype(jnp.float32) + self.relay[0, i].astype(jnp.float32)).astype(low)
        total = self.base[last].astype(jnp.float32)
        for i in range(last):
            total = total + self.relay[1, i].astype(jnp.float32)
        self.relay[1, 0] = total.astype(low)
        for copy in self.joined:
            copy.start()

    def finish(self):
        for copy in self.by_twin + self.by_mate:
            copy.wait_send()
        for copy in self.plain + self.joined:
            copy.wait_recv()
            copy.wait_send()


def row_shard(depth):
    def at(ref, shard, half):
        if half is None:
            return ref.at[span(shard, depth)]
        return ref.at[span(2 * shard + half, depth // 2)]

    return at


def column_shard(rows, width):
    def at(ref, shard, half):
        if half is None:
            return ref.at[:, span(shard, width)]
        return ref.at[pl.ds(half * (rows // 2), rows // 2), span(shard, width)]

    return at


class HeldScatter(Scatter):
    @staticmethod
    def scratch(chips, rows, depth):
        return [
            pltpu.VMEM((2, rows, depth), low),
            pltpu.VMEM((chips, rows, depth), low),
            pltpu.VMEM((chips + 1, rows, depth), low),
            pltpu.VMEM((2, rows, depth), low),
            DMA((2,)), DMA((chips,)), DMA((2,)), DMA((chips + 1,)), DMA((2,)),
        ]

    def __init__(self, line, out, held, *refs):
        super().__init__(line, out, *refs[:-1])
        self.held, self.load_sem = held, refs[-1]

    def load(self, step):
        source = self.held.at[span(2 * self.line.target(step) + self.line.core, self.rows)]
        return pltpu.make_async_copy(source, self.term.at[step % 2], self.load_sem.at[step % 2])

    def share(self, step):
        source = self.held.at[span(2 * self.line.target(step) + 1 - self.line.core, self.rows)]
        return remote(source, self.shares.at[step], self.share_send.at[step % 2], self.share_recv.at[step], {"tp": self.line.partner})

    def mine(self, step):
        self.load(step).wait()

        @pl.when(step < self.line.chips - 1)
        def _():
            self.load(step + 1).start()

        return self.term[step % 2]


class Loads:
    @staticmethod
    def scratch(*operands):
        return [pltpu.VMEM(a.shape, a.dtype) for a in operands] + [DMA((len(operands),))]

    def __init__(self, sources, refs):
        self.refs = refs[: len(sources)]
        self.copies = [pltpu.make_async_copy(source, ref, refs[-1].at[i]) for i, (source, ref) in enumerate(zip(sources, self.refs))]

    def start(self):
        for copy in self.copies:
            copy.start()

    def wait(self, *which):
        for i in which:
            self.copies[i].wait()


def turned(block, sign):
    half = HEAD_DIM // 2
    lane = lax.broadcasted_iota(jnp.int32, block.shape, 1)
    width = block.shape[1]
    up = pltpu.roll(block, width - half, 1)
    down = pltpu.roll(block, half, 1)
    return jnp.where(lane % HEAD_DIM < half, -sign * up, sign * down)


def widened(table, width):
    return table if table.shape[1] == width else jnp.concatenate([table] * (width // table.shape[1]), axis=1)


def only_head(block, head):
    lane = lax.broadcasted_iota(jnp.int32, block.shape, 1)
    return jnp.where(lane // HEAD_DIM == head, block, jnp.zeros_like(block))


def causal(tile):
    key = lax.broadcasted_iota(jnp.int32, tile.shape, 0)
    query = lax.broadcasted_iota(jnp.int32, tile.shape, 1)
    return jnp.where(key <= query, tile, masked_score)


def over_keys(chunk, rows, visit):
    start = chunk * rows
    first = start // SEQ_LEN * SEQ_LEN

    def step(index, carry):
        visit(pl.multiple_of(first + index * rows, rows), False)
        return carry

    lax.fori_loop(0, (start - first) // rows, step, 0)
    visit(pl.multiple_of(start, rows), True)


def project_kernel(
    chips, shards,
    gain, inverse, activations_hbm, w_query, w_key, w_value, w_out, w_down,
    tokens_out, weight_out, full_out, qkv_out, keys_out, values_out, cosine_out, sine_out, down_near,
    weight, out_w, qkv, keys_t, values_t, cosine, sine, tokens, activations,
    load_sem, weight_send, weight_recv, weight_keep, table_sem, store_sem, near_send, near_recv, *gather_sems,
):
    line = Line(chips)
    rows = activations.shape[0]
    depth, width = w_query.shape
    grid = Grid(shards)
    shard, others = grid.me, grid.others
    gather = Gather(line, None, tokens, *gather_sems, parts=2)
    down = NearShards(grid, w_down, down_near, column_shard(*w_down.shape), near_send, near_recv)
    parts = (w_query, w_key, w_value, w_out)

    def place(part):
        if part == 3:
            return out_w.at[:, span(shard, depth)]
        return weight.at[span(shard, depth), pl.ds(part * width, width)]

    def give(ahead, part):
        return remote(parts[part], place(part), weight_send.at[ahead, part], weight_recv.at[ahead, part], {"fsdp": others[ahead]})

    def keep(part):
        return pltpu.make_async_copy(parts[part], place(part), weight_keep.at[part])

    tables = [
        pltpu.make_async_copy(source, out, table_sem.at[i])
        for i, (source, out) in enumerate(((cosine, cosine_out), (sine, sine_out), (weight, weight_out), (out_w, full_out)))
    ]

    def stores(index):
        here = span(index, rows)
        return [
            pltpu.make_async_copy(qkv.at[here], qkv_out.at[here], store_sem.at[0, index]),
            pltpu.make_async_copy(keys_t.at[:, here], keys_out.at[:, here], store_sem.at[1, index]),
            pltpu.make_async_copy(values_t.at[:, here], values_out.at[:, here], store_sem.at[2, index]),
            pltpu.make_async_copy(tokens.at[here], tokens_out.at[here], store_sem.at[3, index]),
        ]

    def norm(index, carry):
        there = span(line.me * (rows // NORM_ROWS) + index, NORM_ROWS)
        tokens[there, :] = normed(activations[span(index, NORM_ROWS), :], gain[...]).astype(low)
        return carry

    load = pltpu.make_async_copy(activations_hbm, activations, load_sem)
    load.start()
    line.hello([{"fsdp": other} for other in others])
    load.wait()
    lax.fori_loop(0, rows // NORM_ROWS, norm, 0)
    line.ready(others)
    gather.start()
    for part in range(4):
        keep(part).start()
        for ahead in range(shards - 1):
            give(ahead, part).start()
    position = lax.broadcasted_iota(jnp.int32, (inverse.shape[0], SEQ_LEN), 1).astype(jnp.float32)
    angle = position * inverse[...]
    for table, turn in ((cosine, jnp.cos(angle).T), (sine, jnp.sin(angle).T)):
        table[...] = jnp.concatenate([turn] * (LANES // turn.shape[1]), axis=1)
    for copy in tables[:2]:
        copy.start()

    def project(index):
        here = span(index, rows)
        table = span(index % (SEQ_LEN // rows), rows)
        for part in range(3):
            columns = pl.ds(part * width, width)
            block = dot(tokens[here, :], weight[:, columns])
            if part < 2:
                block = block * widened(cosine[table, :], width) + turned(block, 1.0) * widened(sine[table, :], width)
            qkv[here, columns] = block.astype(low)
            if part:
                (keys_t, values_t)[part - 1][:, here] = block.T.astype(low)
        for copy in stores(index):
            copy.start()

    def step(index, carry):
        @pl.when(jnp.logical_and(index >= 1, index < chips))
        def _():
            gather.step(index)

        @pl.when(index == 2)
        def _():
            for part in range(4):
                keep(part).wait()
                for ahead in range(shards - 1):
                    give(ahead, part).wait_recv()
            for copy in tables[2:]:
                copy.start()
            down.start()

        def side(turn, carry):
            distance, which, across = index - 1, turn % 3, turn // 3
            chip = jnp.where(which == 0, line.chip - distance, jnp.where(which == 1, line.chip + distance, line.chip))
            there = jnp.logical_and(chip >= 0, chip < chips)

            @pl.when(jnp.logical_and(there, jnp.logical_and(index >= 2, jnp.logical_or(which < 2, index == 2))))
            def _():
                @pl.when(across == 1)
                def _():
                    gather.arrive_across(chip)

                project(2 * chip + jnp.where(across == 1, 1 - line.core, line.core))

            return carry

        lax.fori_loop(0, 6, side, 0)
        return carry

    lax.fori_loop(0, chips + 1, step, 0)
    gather.finish(False)
    for part in range(4):
        for ahead in range(shards - 1):
            give(ahead, part).wait_send()
    for copy in tables:
        copy.wait()
    for index in range(2 * chips):
        for copy in stores(index):
            copy.wait()
    down.arrive()
    down.finish()


def project(chips, shards, activations, gain, w_query, w_key, w_value, w_out, inverse, w_down):
    rows, depth = activations.shape
    group_rows = 2 * chips * rows
    width = w_query.shape[1]
    shape = jax.ShapeDtypeStruct
    held = [
        shape((depth, 3 * width), low),
        shape((width, depth), low),
        shape((group_rows, 3 * width), low),
        shape((width, group_rows), low),
        shape((width, group_rows), low),
        shape((SEQ_LEN, LANES), jnp.float32),
        shape((SEQ_LEN, LANES), jnp.float32),
    ]
    return pl.pallas_call(
        lambda *refs: project_kernel(chips, shards, *refs),
        in_specs=[VMEM] * 2 + [ANYWHERE] * 6,
        out_specs=[ANYWHERE] * 9,
        out_shape=[shape((group_rows, depth), low)] + held + [shape((w_down.shape[0], depth), low)],
        scratch_shapes=[pltpu.VMEM(a.shape, a.dtype) for a in held] + [
            pltpu.VMEM((group_rows, depth), low),
            pltpu.VMEM((rows, depth), jnp.float32),
            DMA, DMA((shards - 1, 4)), DMA((shards - 1, 4)), DMA((4,)), DMA((4,)), DMA((4, 2 * chips)),
        ] + NearShards.scratch(shards) + Gather.scratch(chips, 2),
        compiler_params=pltpu.CompilerParams(collective_id=1, has_side_effects=True, vmem_limit_bytes=63 << 20),
        cost_estimate=pl.CostEstimate(flops=6 * group_rows * depth * width, bytes_accessed=4 * group_rows * depth, transcendentals=0),
        name="project",
    )(gain, inverse, activations, w_query, w_key, w_value, w_out, w_down)


def attend_chunk(chunk, rows, qkv, values_t, heads_ref, acc, out, top_ref, sum_ref):
    width = acc.shape[0]
    heads = width // HEAD_DIM
    scaled = qkv[span(chunk, rows), pl.ds(0, width)] * low(HEAD_DIM**-0.5)
    for head in range(heads):
        heads_ref[head] = only_head(scaled, head)
    acc[...] = jnp.zeros_like(acc)
    top_ref[...] = jnp.full_like(top_ref, masked_score)
    sum_ref[...] = jnp.zeros_like(sum_ref)

    def visit(offset, diagonal):
        key_block = qkv[pl.ds(offset, rows), pl.ds(width, width)]
        for head in range(heads):
            feature = pl.ds(head * HEAD_DIM, HEAD_DIM)
            one = pl.ds(head, 1)
            scores = dot(key_block, heads_ref[head], NT)
            if diagonal:
                scores = causal(scores)
            old = top_ref[one, :]
            top = jnp.maximum(old, jnp.max(scores, axis=0, keepdims=True))
            shrink = jnp.exp(old - top)
            weights = jnp.exp(scores - top)
            top_ref[one, :] = top
            sum_ref[one, :] = sum_ref[one, :] * shrink + jnp.sum(weights, axis=0, keepdims=True)
            acc[feature, :] = acc[feature, :] * shrink + dot(values_t[feature, pl.ds(offset, rows)], weights.astype(low))

    over_keys(chunk, rows, visit)
    for head in range(heads):
        feature = pl.ds(head * HEAD_DIM, HEAD_DIM)
        acc[feature, :] = acc[feature, :] / sum_ref[pl.ds(head, 1), :]
    out[...] = acc[...].T.astype(low)


def attend_kernel(
    chips, shards,
    gain, *refs,
):
    sources, (w_gate, w_up, down_near) = refs[:5], refs[5:8]
    hidden, tokens, mixed, totals, grads_out, gate_all, up_all, down_far = refs[8:16]
    loads = Loads(sources, refs[16:22])
    cotangent, qkv, values_t, w_out, activations = loads.refs
    heads_ref, acc, out, top_ref, sum_ref, grads = refs[22:28]
    loads.start()
    line = Line(chips)
    grid = Grid(shards)
    rows_of = row_shard(w_gate.shape[0])
    line.hello([{"fsdp": peer} for peer in grid.near])
    down = FarShards(grid, down_near, down_far, column_shard(down_near.shape[0], down_near.shape[1] // shards), *refs[28:30])
    gate_near, gate_far = NearShards(grid, w_gate, gate_all, rows_of, *refs[30:32]), FarShards(grid, gate_all, gate_all, rows_of, *refs[32:34])
    up_near, up_far = NearShards(grid, w_up, up_all, rows_of, *refs[34:36]), FarShards(grid, up_all, up_all, rows_of, *refs[36:38])
    sems = refs[38:]
    rows, depth = hidden.shape
    pair = 2 * rows
    scatter = Scatter(line, hidden, *sems[:8])
    loads.wait(0)
    grads[...] = cotangent[...].astype(low)
    gather = Gather(line, grads, grads_out, *sems[8:])
    line.ready(grid.near)
    gather.start()
    gate_near.start()
    down.start()
    loads.wait(1, 2, 3, 4)

    def term(index):
        chunk = line.target(index)
        attend_chunk(chunk, pair, qkv, values_t, heads_ref, acc, out, top_ref, sum_ref)
        mixed[span(chunk, pair), :] = out[...]
        totals[:, span(chunk, pair)] = top_ref[...] + jnp.log(sum_ref[...])
        scatter.free(index)

        def tile(place, carry):
            columns = span(place, 512)
            scatter.term[index % scatter.slots, :, columns] = dot(out[...], w_out[:, columns]).astype(low)
            return carry

        lax.fori_loop(0, depth // 512, tile, 0)
        scatter.share(index).start()

    def step(index, carry):
        def phase(which, carry):
            @pl.when(jnp.logical_and(which == 1, index < chips))
            def _():
                term(index)

            lax.fori_loop(0, jnp.where(which == 1, 0, chips), scatter.due(index, which == 2), 0)
            return carry

        lax.fori_loop(0, 3, phase, 0)

        @pl.when(jnp.logical_and(index >= 1, index < chips))
        def _():
            gather.step(index)

        @pl.when(index == 1)
        def _():
            up_near.start()

        @pl.when(index == min(2, chips))
        def _():
            gate_near.arrive()
            gate_far.start()

        @pl.when(index == min(3, chips))
        def _():
            up_near.arrive()
            up_far.start()

        return carry

    lax.fori_loop(0, chips + 1, step, 0)

    def norm(here):
        state = activations[here, :] + hidden[here, :]
        hidden[here, :] = state
        tokens[here, :] = normed(state, gain[...]).astype(low)

    by_rows(rows, norm)
    scatter.finish()
    gather.finish(True)
    for near in (gate_near, up_near):
        near.finish()
    for far in (down, gate_far, up_far):
        far.finish()


def attend(chips, shards, qkv, values_t, w_out, activations, cotangent, gain, w_gate, w_up, down_near):
    rows, depth = activations.shape
    pair = 2 * rows
    group_rows = chips * pair
    width = w_out.shape[0]
    heads = width // HEAD_DIM
    shape = jax.ShapeDtypeStruct
    return pl.pallas_call(
        lambda *refs: attend_kernel(chips, shards, *refs),
        in_specs=[VMEM] + [ANYWHERE] * 8,
        out_specs=[VMEM] * 4 + [ANYWHERE] * 4,
        out_shape=[
            shape((rows, depth), jnp.float32),
            shape((rows, depth), low),
            shape((group_rows, width), low),
            shape((heads, group_rows), jnp.float32),
            shape((group_rows, depth), low),
            shape((depth, w_gate.shape[1]), low),
            shape((depth, w_gate.shape[1]), low),
            shape(down_near.shape, low),
        ],
        scratch_shapes=Loads.scratch(cotangent, qkv, values_t, w_out, activations) + [
            pltpu.VMEM((heads, pair, width), low),
            pltpu.VMEM((width, pair), jnp.float32),
            pltpu.VMEM((pair, width), low),
            pltpu.VMEM((heads, pair), jnp.float32),
            pltpu.VMEM((heads, pair), jnp.float32),
            pltpu.VMEM((rows, depth), low),
        ] + FarShards.scratch(shards) + (NearShards.scratch(shards) + FarShards.scratch(shards)) * 2 + Scatter.scratch(chips, rows, depth) + Gather.scratch(chips),
        compiler_params=pltpu.CompilerParams(collective_id=2, has_side_effects=True, vmem_limit_bytes=63 << 20),
        cost_estimate=pl.CostEstimate(flops=2 * group_rows * (SEQ_LEN + depth) * width, bytes_accessed=4 * group_rows * depth, transcendentals=group_rows * SEQ_LEN * heads // 2),
        name="attend",
    )(gain, cotangent, qkv, values_t, w_out, activations, w_gate, w_up, down_near)


def back_chunk(chunk, rows, grad, qkv, keys_t, mixed, totals, dkey, dvalue, heads_ref, grads_ref, acc, inner_ref):
    width = acc.shape[0]
    heads = width // HEAD_DIM
    here = span(chunk, rows)
    scaled = qkv[here, pl.ds(0, width)] * low(HEAD_DIM**-0.5)
    product = grad.astype(jnp.float32) * mixed[here, :].astype(jnp.float32)
    shape = (inner_ref.shape[0], width)
    pick = (lax.broadcasted_iota(jnp.int32, shape, 1) // HEAD_DIM == lax.broadcasted_iota(jnp.int32, shape, 0)).astype(jnp.float32)
    inner_ref[...] = lax.dot_general(pick, product, NT, precision=lax.Precision.HIGHEST, preferred_element_type=jnp.float32)
    for head in range(heads):
        heads_ref[head] = only_head(scaled, head)
        grads_ref[head] = only_head(grad, head)
    acc[...] = jnp.zeros_like(acc)

    def visit(offset, diagonal):
        keys = pl.ds(offset, rows)
        key_block = qkv[keys, pl.ds(width, width)]
        value_block = qkv[keys, pl.ds(2 * width, width)]
        key_sum, value_sum = dkey[keys, :], dvalue[keys, :]
        for head in range(heads):
            feature = pl.ds(head * HEAD_DIM, HEAD_DIM)
            scores = dot(key_block, heads_ref[head], NT)
            if diagonal:
                scores = causal(scores)
            probs = jnp.exp(scores - totals[pl.ds(head, 1), here])
            dprobs = dot(value_block, grads_ref[head], NT)
            dscores = (probs * (dprobs - inner_ref[pl.ds(head, 1), :])).astype(low)
            value_sum = value_sum + dot(probs.astype(low), grads_ref[head])
            key_sum = key_sum + dot(dscores, heads_ref[head])
            acc[feature, :] = acc[feature, :] + dot(keys_t[feature, keys], dscores)
        dkey[keys, :] = key_sum
        dvalue[keys, :] = value_sum

    over_keys(chunk, rows, visit)


def back_kernel(
    chips, shards,
    branch, terms, inner, grads, grad_both, *refs,
):
    sources, (down, branch_out, qkv_grad, grad_down, grad_out, both_from) = refs[:7], refs[7:13]
    loads = Loads(sources, refs[13:21])
    w_out, qkv, keys_t, mixed, totals, cosine, sine = loads.refs
    inner_chunk, grad_chunk, down_sum, down_tile, out_sum, out_stage, out_from, branch_chunk, dkey, dvalue = refs[21:31]
    heads_ref, grads_ref, acc, inner_ref, inner_sem, grad_sem, branch_sem, tile_sem, out_send, out_recv = refs[31:41]
    sums = refs[41:48]
    sems = refs[48:]
    line = Line(chips)
    rows, depth = down.shape
    pair = 2 * rows
    width = w_out.shape[0]
    scatter = HeldScatter(line, down, terms, *sems[:9])
    gather = Gather(line, branch, branch_out, *sems[9:])

    def fetch(step):
        return pltpu.make_async_copy(inner.at[span(line.target(step), pair)], inner_chunk, inner_sem)

    def fetch_grad(step):
        return pltpu.make_async_copy(grads.at[span(line.target(step), pair)], grad_chunk, grad_sem)

    grid = Grid(shards)
    shard, others = grid.me, grid.others
    columns_out = depth // shards
    both = NearSums(grid, grad_both, both_from, row_shard(columns_out), *sums)

    def give(turn):
        return remote(out_stage.at[turn], out_from.at[turn], out_send.at[turn], out_recv.at[turn], {"fsdp": others[turn]})

    def keep_tile(place):
        return pltpu.make_async_copy(down_tile, grad_down.at[span(place, 256)], tile_sem)

    line.hello([{"fsdp": other} for other in others])
    loads.start()
    fetch(0).start()
    fetch_grad(0).start()
    scatter.load(0).start()
    line.ready(others)
    gather.start()
    both.start()
    out_sum[...] = jnp.zeros_like(out_sum)
    dkey[...] = jnp.zeros_like(dkey)
    dvalue[...] = jnp.zeros_like(dvalue)

    def unrotated(block, chunk):
        table = span(chunk % (SEQ_LEN // pair), pair)
        return (block * widened(cosine[table, :], width) + turned(block * widened(sine[table, :], width), -1.0)).astype(low)

    def attention(chunk):
        gather.arrive_across(chunk)
        copy = pltpu.make_async_copy(branch_out.at[span(chunk, pair)], branch_chunk, branch_sem)
        copy.start()
        copy.wait()
        out_sum[...] += dot(mixed[span(chunk, pair), :], branch_chunk[...], TN)
        grad = dot(branch_chunk[...], w_out[...], NT).astype(low)
        back_chunk(chunk, pair, grad, qkv, keys_t, mixed, totals, dkey, dvalue, heads_ref, grads_ref, acc, inner_ref)
        qkv_grad[span(chunk, pair), pl.ds(0, width)] = unrotated(acc[...].T * HEAD_DIM**-0.5, chunk)

    def close():
        def part(chunk, carry):
            here = span(chunk, pair)
            qkv_grad[here, pl.ds(width, width)] = unrotated(dkey[here, :], chunk)
            qkv_grad[here, pl.ds(2 * width, width)] = dvalue[here, :].astype(low)
            return carry

        lax.fori_loop(0, chips, part, 0)

    def step(index, carry):
        @pl.when(index == 0)
        def _():
            loads.wait(*range(7))
            gather.keep().wait()

        @pl.when(index < chips)
        def _():
            scatter.free(index)
            scatter.share(index).start()

        @pl.when(index == chips)
        def _():
            for turn in range(shards - 1):
                out_stage[turn] = out_sum[:, span(others[turn], columns_out)].astype(low)
                give(turn).start()
            close()

        lax.fori_loop(0, chips, scatter.due(index, None), 0)

        @pl.when(jnp.logical_and(index >= 1, index < chips))
        def _():
            gather.step(index)

        @pl.when(index == 1)
        def _():
            both.start_plain()

        @pl.when(index == 2)
        def _():
            both.join()

        @pl.when(index < chips)
        def _():
            attention(line.target(chips - 1 - index))

        def weights(turn, carry):
            fetch(turn).wait()
            fetch_grad(turn).wait()

            def tile(place, carry):
                here = span(place, 256)
                part = dot(inner_chunk[:, here], grad_chunk[...], TN)

                @pl.when(turn == 0)
                def _():
                    down_sum[here, :] = part

                @pl.when(turn > 0)
                def _():
                    down_sum[here, :] += part

                @pl.when(turn == chips - 1)
                def _():
                    @pl.when(place > 0)
                    def _():
                        keep_tile(place - 1).wait()

                    down_tile[...] = down_sum[here, :].astype(low)
                    keep_tile(place).start()

                return carry

            lax.fori_loop(0, down_sum.shape[0] // 256, tile, 0)

            @pl.when(turn < chips - 1)
            def _():
                fetch(turn + 1).start()
                fetch_grad(turn + 1).start()

            return carry

        lax.fori_loop(jnp.where(index == 0, 0, index + 1), jnp.minimum(index + 2, chips), weights, 0)
        return carry

    lax.fori_loop(0, chips + 1, step, 0)
    total = out_sum[:, span(shard, columns_out)]
    for turn in range(shards - 1):
        give(turn).wait_recv()
        total = total + out_from[turn].astype(jnp.float32)
    grad_out[...] = total
    for turn in range(shards - 1):
        give(turn).wait_send()
    keep_tile(down_sum.shape[0] // 256 - 1).wait()
    both.finish()
    scatter.finish()
    gather.finish(False)


def back(chips, shards, branch, terms, inner, grads, grad_both, w_out, qkv, keys_t, mixed, totals, cosine, sine):
    rows, depth = branch.shape
    pair = 2 * rows
    group_rows = chips * pair
    width = w_out.shape[0]
    hidden = inner.shape[1]
    heads = width // HEAD_DIM
    shape = jax.ShapeDtypeStruct
    held = (w_out, qkv, keys_t, mixed, totals, cosine, sine)
    return pl.pallas_call(
        lambda *refs: back_kernel(chips, shards, *refs),
        in_specs=[VMEM] + [ANYWHERE] * 11,
        out_specs=[VMEM, ANYWHERE, VMEM, ANYWHERE, VMEM, ANYWHERE],
        out_shape=[
            shape((rows, depth), jnp.float32),
            shape((group_rows, depth), low),
            shape((group_rows, 3 * width), low),
            shape((hidden, depth), low),
            shape((width, depth // shards), jnp.float32),
            shape((shards // 2, depth // shards, grad_both.shape[1]), low),
        ],
        scratch_shapes=Loads.scratch(*held) + [
            pltpu.VMEM((pair, hidden), low),
            pltpu.VMEM((pair, depth), low),
            pltpu.VMEM((hidden, depth), jnp.float32),
            pltpu.VMEM((256, depth), low),
            pltpu.VMEM((width, depth), jnp.float32),
            pltpu.VMEM((shards - 1, width, depth // shards), low),
            pltpu.VMEM((shards - 1, width, depth // shards), low),
            pltpu.VMEM((pair, depth), low),
            pltpu.VMEM((group_rows, width), jnp.float32),
            pltpu.VMEM((group_rows, width), jnp.float32),
            pltpu.VMEM((heads, pair, width), low),
            pltpu.VMEM((heads, pair, width), low),
            pltpu.VMEM((width, pair), jnp.float32),
            pltpu.VMEM((8, pair), jnp.float32),
            DMA, DMA, DMA, DMA, DMA((shards - 1,)), DMA((shards - 1,)),
        ] + NearSums.scratch(shards, depth // shards, grad_both.shape[1]) + HeldScatter.scratch(chips, rows, depth) + Gather.scratch(chips),
        compiler_params=pltpu.CompilerParams(collective_id=4, has_side_effects=True, vmem_limit_bytes=67043328),
        cost_estimate=pl.CostEstimate(flops=1 << 20, bytes_accessed=1 << 20, transcendentals=0),
        name="back",
    )(branch, terms, inner, grads, grad_both, *held)


def spread_kernel(
    chips, shards,
    gain, gain_part, qkv_hbm, weight_hbm, activations_hbm, attn_tokens, grad_down,
    input_part, grad_qkv, gain_sum, down_from,
    qkv_grad, weight, activations, held_sem,
    attn_cols, qkv_stage, qkv_from, gains, gains_tp, gains_fsdp,
    attn_sem, qkv_send, qkv_recv, tp_send, tp_recv, fsdp_send, fsdp_recv, *sems,
):
    line = Line(chips)
    size = 2 * chips
    rows, depth = input_part.shape
    pair = 2 * rows
    grid = Grid(shards)
    shard = grid.me
    columns = depth // shards
    loads = Loads((qkv_hbm, weight_hbm, activations_hbm), (qkv_grad, weight, activations, held_sem))
    down = NearSums(grid, grad_down, down_from, column_shard(grad_down.shape[0], columns), *sems[:7])
    scatter = Scatter(line, input_part, *sems[7:])

    def peer(turn):
        return (shard + 1 + turn) % shards

    def fetch(turn):
        return pltpu.make_async_copy(attn_tokens.at[:, span(peer(turn), columns)], attn_cols.at[turn % 2], attn_sem.at[turn % 2])

    def give(turn):
        return remote(qkv_stage.at[turn], qkv_from.at[turn], qkv_send.at[turn], qkv_recv.at[turn], {"fsdp": peer(turn)})

    def tell_tp(ahead):
        return remote(gains, gains_tp.at[line.me], tp_send.at[ahead - 1], tp_recv.at[line.me], {"tp": (line.me + ahead) % size})

    def tell_fsdp(ahead):
        return remote(gains, gains_fsdp.at[shard], fsdp_send.at[ahead - 1], fsdp_recv.at[shard], {"fsdp": (shard + ahead) % shards})

    for ahead in range(1, size):
        hello({"tp": (line.me + ahead) % size})
    for ahead in range(1, shards):
        hello({"fsdp": (shard + ahead) % shards})
    loads.start()
    fetch(0).start()
    loads.wait(0, 1)
    pl.semaphore_wait(pltpu.get_barrier_semaphore(), size - 1 + shards - 1)
    down.start()

    def weights(turn, carry):
        @pl.when(turn < shards - 1)
        def _():
            fetch(turn + 1).start()

        fetch(turn).wait()
        part = dot(attn_cols[turn % 2], qkv_grad[...], TN)

        @pl.when(turn < shards - 1)
        def _():
            qkv_stage[turn] = part.astype(low)
            give(turn).start()

        @pl.when(turn == shards - 1)
        def _():
            grad_qkv[...] = part

        return carry

    def term(index):
        scatter.free(index)
        here = span(line.target(index), pair)

        def tile(place, carry):
            there = span(place, 512)
            scatter.term[index % scatter.slots, :, there] = dot(qkv_grad[here, :], weight[there, :], NT).astype(low)
            return carry

        lax.fori_loop(0, depth // 512, tile, 0)
        scatter.share(index).start()

    def step(index, carry):
        def phase(which, carry):
            @pl.when(jnp.logical_and(which == 1, index < chips))
            def _():
                term(index)

            @pl.when(jnp.logical_and(which == 2, index < 2))
            def _():
                lax.fori_loop(index, jnp.where(index == 0, 1, shards), weights, 0)

            @pl.when(jnp.logical_and(which == 2, index == 1))
            def _():
                down.start_plain()

            @pl.when(jnp.logical_and(which == 2, index == 2))
            def _():
                down.join()

            outer = jnp.logical_or(which == 0, which == 3)
            lax.fori_loop(0, jnp.where(outer, chips, 0), scatter.due(index, which == 3), 0)
            return carry

        lax.fori_loop(0, 4, phase, 0)
        return carry

    lax.fori_loop(0, chips + 1, step, 0)
    gains[0:1, :] = jnp.zeros((1, depth), jnp.float32)
    gains[1:2, :] = gain_part[...]

    def norm(here):
        part, grad = norm_back(activations[here, :], gain[...], input_part[here, :])
        input_part[here, :] = part
        gains[0:1, :] += grad

    loads.wait(2)
    by_rows(rows, norm)

    gains_tp[line.me] = gains[...]
    for ahead in range(1, size):
        tell_tp(ahead).start()
    for turn in range(shards - 1):
        give(turn).wait_recv()
        grad_qkv[...] += qkv_from[turn].astype(jnp.float32)
    for ahead in range(1, size):
        source = (line.me + ahead) % size
        remote(gains, gains_tp.at[source], tp_send.at[0], tp_recv.at[source], {"tp": source}).wait_recv()
    total = gains_tp[0]
    for source in range(1, size):
        total = total + gains_tp[source]
    for ahead in range(1, size):
        tell_tp(ahead).wait_send()
    gains[...] = total
    gains_fsdp[shard] = total
    for ahead in range(1, shards):
        tell_fsdp(ahead).start()
    for ahead in range(1, shards):
        source = (shard + ahead) % shards
        remote(gains, gains_fsdp.at[source], fsdp_send.at[0], fsdp_recv.at[source], {"fsdp": source}).wait_recv()
    total = gains_fsdp[0]
    for source in range(1, shards):
        total = total + gains_fsdp[source]
    gain_sum[...] = total
    for ahead in range(1, shards):
        tell_fsdp(ahead).wait_send()
    for turn in range(shards - 1):
        give(turn).wait_send()
    down.finish()
    scatter.finish()


def spread(chips, shards, qkv_grad, weight, activations, gain, gain_part, attn_tokens, grad_down):
    group_rows = qkv_grad.shape[0]
    rows, depth = activations.shape
    width = qkv_grad.shape[1] // 3
    columns = depth // shards
    size = 2 * chips
    shape = jax.ShapeDtypeStruct
    return pl.pallas_call(
        lambda *refs: spread_kernel(chips, shards, *refs),
        in_specs=[VMEM] * 2 + [ANYWHERE] * 5,
        out_specs=[VMEM] * 3 + [ANYWHERE],
        out_shape=[
            shape((rows, depth), jnp.float32),
            shape((columns, 3 * width), jnp.float32),
            shape((2, depth), jnp.float32),
            shape((shards // 2, grad_down.shape[0], columns), low),
        ],
        scratch_shapes=Loads.scratch(qkv_grad, weight, activations) + [
            pltpu.VMEM((2, group_rows, columns), low),
            pltpu.VMEM((shards - 1, columns, 3 * width), low),
            pltpu.VMEM((shards - 1, columns, 3 * width), low),
            pltpu.VMEM((2, depth), jnp.float32),
            pltpu.VMEM((size, 2, depth), jnp.float32),
            pltpu.VMEM((shards, 2, depth), jnp.float32),
            DMA((2,)), DMA((shards - 1,)), DMA((shards - 1,)),
            DMA((size - 1,)), DMA((size,)), DMA((shards - 1,)), DMA((shards,)),
        ] + NearSums.scratch(shards, grad_down.shape[0], columns) + Scatter.scratch(chips, rows, depth),
        compiler_params=pltpu.CompilerParams(collective_id=5, has_side_effects=True, vmem_limit_bytes=63 << 20),
        cost_estimate=pl.CostEstimate(flops=1 << 20, bytes_accessed=1 << 20, transcendentals=0),
        name="spread",
    )(gain, gain_part, qkv_grad, weight, activations, attn_tokens, grad_down)


def chip_at(place, chips):
    return jnp.where(2 * place < chips, 2 * place, 2 * (chips - 1 - place) + 1)


def place_of(chip, chips):
    return jnp.where(chip % 2 == 0, chip // 2, chips - 1 - chip // 2)


def feed_kernel(
    chips, shards,
    gain, hidden_hbm, cotangent_hbm, tokens, grads_hbm, w_gate, w_up, w_down, gate_all, up_all, down_near, down_far,
    hidden_grad, branch, gain_part, inner_out, grad_both, down_out,
    hidden_state, cotangent, state_sem, down_tile, down_sem, tokens_all, gate_w, up_w, down_w, grads, inner, gate_grad, up_grad, term, from_core, from_ring, total, tile_gate, tile_up,
    load_sem, own_sem, grad_sem, store_sem, tile_sem,
    ring_send, ring_recv, core_send, core_recv, share_send, share_recv, total_send, total_recv,
):
    rows, depth = hidden_grad.shape
    pair = 2 * rows
    width = gate_w.shape[1]
    me = lax.axis_index("tp")
    chip, core = me // 2, me % 2
    place = place_of(chip, chips)
    following = {"tp": 2 * chip_at((place + 1) % chips, chips) + core}
    before = {"tp": 2 * chip_at((place + chips - 1) % chips, chips) + core}
    partner = {"tp": 2 * chip + 1 - core}

    grid = Grid(shards)
    rows_of, columns_of = row_shard(w_gate.shape[0]), column_shard(*w_down.shape)

    def load(array, source, shard, whole):
        at = columns_of if array == 2 else rows_of
        target = at((gate_w, up_w, down_w)[array], shard, None)
        return pltpu.make_async_copy(at(source, shard, None) if whole else source, target, load_sem.at[array, shard])

    def load_weights():
        for shard in range(shards):
            own, near = grid.me == shard, grid.is_near(shard)

            @pl.when(own)
            def _():
                for array, source in enumerate((w_gate, w_up, w_down)):
                    load(array, source, shard, False).start()

            @pl.when(jnp.logical_not(own))
            def _():
                for array, source in enumerate((gate_all, up_all)):
                    load(array, source, shard, True).start()

            @pl.when(jnp.logical_and(near, jnp.logical_not(own)))
            def _():
                load(2, down_near, shard, True).start()

            @pl.when(jnp.logical_not(near))
            def _():
                load(2, down_far, shard, True).start()

    own = pltpu.make_async_copy(tokens, tokens_all.at[span(me, rows)], own_sem)
    states = Loads((hidden_hbm, cotangent_hbm), (hidden_state, cotangent, state_sem))

    def source(slot):
        return chip_at((place + chips - slot) % chips, chips)

    def fetch(slot):
        return pltpu.make_async_copy(grads_hbm.at[span(source(slot), pair)], grads.at[slot % 2], grad_sem.at[slot % 2])

    def block(slot):
        return tokens_all.at[span(2 * source(slot) + core, rows)]

    def to_ring(slot):
        return remote(block(slot), block(slot), ring_send.at[slot], ring_recv.at[slot], following)

    def to_core(slot):
        return remote(block(slot), block(slot), core_send.at[slot], core_recv.at[slot], partner)

    def store(slot):
        return pltpu.make_async_copy(inner.at[slot], inner_out.at[span(source(slot), pair)], store_sem.at[slot])

    def keep_down(slot, tile):
        there = down_out.at[span(source(slot), pair), span(tile, 256)]
        return pltpu.make_async_copy(down_tile.at[tile % 2], there, down_sem.at[tile % 2])

    def down_term(slot, carry):
        def tile(index, carry):
            @pl.when(index > 1)
            def _():
                keep_down(slot, index - 2).wait()

            down_tile[index % 2] = dot(inner[slot], down_w[:, span(index, 256)]).astype(low)
            keep_down(slot, index).start()
            return carry

        lax.fori_loop(0, depth // 256, tile, 0)
        for index in range(depth // 256 - 2, depth // 256):
            keep_down(slot, index).wait()
        return carry

    def share(slot):
        place = jnp.where(slot == 0, 0, 1 + slot % 2)
        return remote(term.at[span(1 - core, rows)], from_core.at[place], share_send, share_recv.at[place], partner)

    def pass_on(slot):
        return remote(total.at[slot % 2], from_ring.at[slot - 1], total_send.at[slot % 2], total_recv.at[slot - 1], following)

    for device in (following, before, partner):
        hello(device)
    own.start()
    fetch(0).start()
    load_weights()
    own.wait()
    pl.semaphore_wait(pltpu.get_barrier_semaphore(), 3)

    def step(slot, carry):
        here = slot % 2
        wide_rows = span(source(slot), pair)
        mine = span(core, rows)

        @pl.when(slot > 0)
        def _():
            to_ring(slot - 1).wait_recv()

        @pl.when(slot < chips - 1)
        def _():
            to_ring(slot).start()
            fetch(slot + 1).start()

        to_core(slot).start()

        @pl.when(slot == 0)
        def _():
            for shard in range(shards):
                for array, source in enumerate((gate_all, up_all, down_near)):
                    load(array, source, shard, True).wait()

        @pl.when(slot == 1)
        def _():
            states.start()

        to_core(slot).wait_recv()
        fetch(slot).wait()

        def narrow(tile, carry):
            columns = span(tile, 256)
            token = tokens_all[wide_rows, :]
            gate = dot(token, gate_w[:, columns])
            up = dot(token, up_w[:, columns])
            grad = dot(grads[here], down_w[columns, :], NT)
            squash = jax.nn.sigmoid(gate)
            act = gate * squash
            inner[slot, :, columns] = (act * up).astype(low)
            up_grad[wide_rows, columns] = (grad * act).astype(low)
            gate_grad[wide_rows, columns] = (grad * up * squash * (1.0 + gate * (1.0 - squash))).astype(low)
            return carry

        lax.fori_loop(0, width // 256, narrow, 0)
        store(slot).start()

        @pl.when(slot > 0)
        def _():
            share(slot - 1).wait_send()

        def wide(tile, carry):
            columns = span(tile, 256)
            part = dot(gate_grad[wide_rows, :], gate_w[columns, :], NT) + dot(up_grad[wide_rows, :], up_w[columns, :], NT)
            term[:, columns] = part.astype(low)
            return carry

        lax.fori_loop(0, depth // 256, wide, 0)
        share(slot).start()

        @pl.when(slot == 0)
        def _():
            hidden_grad[...] = term[mine, :].astype(jnp.float32)

        middle = jnp.logical_and(slot >= 2, slot < chips - 1)
        lax.fori_loop(jnp.where(slot == 2, 0, slot), jnp.where(middle, slot + 1, 0), down_term, 0)

        @pl.when(slot > 0)
        def _():
            share(slot).wait_recv()

            @pl.when(slot > 2)
            def _():
                pass_on(slot - 2).wait_send()

            @pl.when(slot == 1)
            def _():
                total[here] = (term[mine, :].astype(jnp.float32) + from_core[1 + here].astype(jnp.float32)).astype(low)

            @pl.when(slot > 1)
            def _():
                pass_on(slot - 1).wait_recv()
                total[here] = (term[mine, :].astype(jnp.float32) + from_core[1 + here].astype(jnp.float32) + from_ring[slot - 2].astype(jnp.float32)).astype(low)

            pass_on(slot).start()

        return carry

    lax.fori_loop(0, chips, step, 0)

    def tiles(index):
        there = span(index, 256)
        return (
            pltpu.make_async_copy(tile_gate.at[index % 2], grad_both.at[there, pl.ds(0, width)], tile_sem.at[0, index % 2]),
            pltpu.make_async_copy(tile_up.at[index % 2], grad_both.at[there, pl.ds(width, width)], tile_sem.at[1, index % 2]),
        )

    def weights(index, carry):
        @pl.when(index > 1)
        def _():
            for copy in tiles(index - 2):
                copy.wait()

        token = tokens_all[:, span(index, 256)]
        tile_gate[index % 2] = dot(token, gate_grad[...], TN).astype(low)
        tile_up[index % 2] = dot(token, up_grad[...], TN).astype(low)
        for copy in tiles(index):
            copy.start()
        return carry

    lax.fori_loop(0 if chips < 4 else chips - 1, chips, down_term, 0)
    lax.fori_loop(0, depth // 256, weights, 0)
    states.wait(0, 1)
    share(0).wait_recv()
    pass_on(chips - 1).wait_recv()
    gain_part[...] = jnp.zeros_like(gain_part)

    def norm(here):
        grad = hidden_grad[here, :] + from_core[0, here, :].astype(jnp.float32) + from_ring[chips - 2, here, :].astype(jnp.float32)
        part, gain_grad = norm_back(hidden_state[here, :], gain[...], grad)
        full = cotangent[here, :] + part
        hidden_grad[here, :] = full
        branch[here, :] = full.astype(low)
        gain_part[...] += gain_grad

    by_rows(rows, norm)
    share(chips - 1).wait_send()
    for slot in range(chips):
        to_core(slot).wait_send()
        if slot < chips - 1:
            to_ring(slot).wait_send()
        if slot >= max(1, chips - 2):
            pass_on(slot).wait_send()
        store(slot).wait()
    for index in range(depth // 256 - 2, depth // 256):
        for copy in tiles(index):
            copy.wait()


def feed(chips, shards, hidden_state, cotangent, gain, tokens, grads, w_gate, w_up, w_down, gate_all, up_all, down_near, down_far):
    rows, depth = tokens.shape
    pair = 2 * rows
    group_rows = chips * pair
    width = w_down.shape[0]
    shape = jax.ShapeDtypeStruct
    return pl.pallas_call(
        lambda *refs: feed_kernel(chips, shards, *refs),
        in_specs=[VMEM] + [ANYWHERE] * 11,
        out_specs=[VMEM] * 3 + [ANYWHERE] * 3,
        out_shape=[
            shape((rows, depth), jnp.float32),
            shape((rows, depth), low),
            shape((1, depth), jnp.float32),
            shape((group_rows, width), low),
            shape((depth, 2 * width), low),
            shape((group_rows, depth), low),
        ],
        scratch_shapes=Loads.scratch(hidden_state, cotangent) + [
            pltpu.VMEM((2, pair, 256), low),
            DMA((2,)),
            pltpu.VMEM((group_rows, depth), low),
            pltpu.VMEM((depth, width), low),
            pltpu.VMEM((depth, width), low),
            pltpu.VMEM((width, depth), low),
            pltpu.VMEM((2, pair, depth), low),
            pltpu.VMEM((chips, pair, width), low),
            pltpu.VMEM((group_rows, width), low),
            pltpu.VMEM((group_rows, width), low),
            pltpu.VMEM((pair, depth), low),
            pltpu.VMEM((3, rows, depth), low),
            pltpu.VMEM((chips - 1, rows, depth), low),
            pltpu.VMEM((2, rows, depth), low),
            pltpu.VMEM((2, 256, width), low),
            pltpu.VMEM((2, 256, width), low),
            DMA((3, shards)), DMA, DMA((2,)), DMA((chips,)), DMA((2, 2)),
            DMA((chips,)), DMA((chips,)), DMA((chips,)), DMA((chips,)),
            DMA, DMA((3,)), DMA((2,)), DMA((chips - 1,)),
        ],
        compiler_params=pltpu.CompilerParams(collective_id=3, has_side_effects=True, vmem_limit_bytes=67043328),
        cost_estimate=pl.CostEstimate(flops=16 * group_rows * depth * width, bytes_accessed=10 * group_rows * depth, transcendentals=group_rows * width),
        name="feed",
    )(gain, hidden_state, cotangent, tokens, grads, w_gate, w_up, w_down, gate_all, up_all, down_near, down_far)


def finish_kernel(
    shard_ref, hidden, down, hidden_grad, input_part, both, both_from, grad_down, down_from, grad_qkv, grad_out,
    output, input_grad, query, key, value, out, gate, up, down_out,
):
    output[...] = hidden[...] + down[...]
    input_grad[...] = hidden_grad[...] + input_part[...]
    width = query.shape[1]
    for part, ref in enumerate((query, key, value)):
        ref[...] = grad_qkv[:, pl.ds(part * width, width)]
    out[...] = grad_out[...]
    wide = gate.shape[1]
    for side, ref in enumerate((gate, up)):
        columns = pl.ds(side * wide, wide)
        total = both[:, columns].astype(jnp.float32)
        for turn in range(both_from.shape[0]):
            total = total + both_from[turn, :, columns].astype(jnp.float32)
        ref[...] = total
    total = grad_down[...].astype(jnp.float32)
    for turn in range(down_from.shape[0]):
        total = total + down_from[turn].astype(jnp.float32)
    down_out[...] = total


def finish(shard, hidden, down, hidden_grad, input_part, both, both_from, grad_down, down_from, grad_qkv, grad_out):
    steps = 8
    shape = jax.ShapeDtypeStruct
    columns = down_from.shape[2]
    results = [shape(hidden.shape, jnp.float32)] * 2
    results += [shape((columns, grad_qkv.shape[1] // 3), jnp.float32)] * 3 + [shape(grad_out.shape, jnp.float32)]
    results += [shape((columns, both.shape[1] // 2), jnp.float32)] * 2 + [shape((grad_down.shape[0], columns), jnp.float32)]
    spec = lambda a: pl.BlockSpec((a.shape[0] // steps, a.shape[1]), lambda i, s: (i, 0))
    spec3 = lambda a: pl.BlockSpec((a.shape[0], a.shape[1] // steps, a.shape[2]), lambda i, s: (0, i, 0))
    return pl.pallas_call(
        finish_kernel,
        grid_spec=pltpu.PrefetchScalarGridSpec(
            num_scalar_prefetch=1,
            grid=(steps,),
            in_specs=[
                spec(hidden), spec(down), spec(hidden_grad), spec(input_part),
                pl.BlockSpec((columns // steps, both.shape[1]), lambda i, s: (s[0] * steps + i, 0)),
                spec3(both_from),
                pl.BlockSpec((grad_down.shape[0] // steps, columns), lambda i, s: (i, s[0])),
                spec3(down_from), spec(grad_qkv), spec(grad_out),
            ],
            out_specs=[spec(a) for a in results],
        ),
        out_shape=results,
        name="finish",
    )(shard.reshape(1), hidden, down, hidden_grad, input_part, both, both_from, grad_down, down_from, grad_qkv, grad_out)


def rope_frequencies():
    column = np.arange(HEAD_DIM // 2)
    return jnp.asarray((rope_base ** (-2.0 * column / HEAD_DIM)).astype(np.float32)[:, None])


def make_body(mesh):
    chips, shards = mesh.shape["tp"] // 2, mesh.shape["fsdp"]

    def body(activations, gain_attn, w_query, w_key, w_value, w_out, gain_mlp, w_gate, w_up, w_down, cotangent):
        gain_attn, gain_mlp = gain_attn[None, :], gain_mlp[None, :]
        seen_attn, w_qkv, full_out, qkv, keys_t, values_t, cosine, sine, down_near = project(
            chips, shards, activations, gain_attn, w_query, w_key, w_value, w_out, rope_frequencies(), w_down
        )
        hidden_state, normed_mlp, mixed, totals, seen_grad, gate_all, up_all, down_far = attend(
            chips, shards, qkv, values_t, full_out, activations, cotangent, gain_mlp, w_gate, w_up, down_near
        )
        hidden_grad, branch_grad, gain_part, inner, grad_both, terms = feed(
            chips, shards, hidden_state, cotangent, gain_mlp, normed_mlp, seen_grad,
            w_gate, w_up, w_down, gate_all, up_all, down_near, down_far,
        )
        down, _, qkv_grad, grad_down, grad_out, both_from = back(
            chips, shards, branch_grad, terms, inner, seen_grad, grad_both, full_out, qkv, keys_t, mixed, totals, cosine, sine
        )
        input_part, grad_qkv, gain_sums, down_from = spread(
            chips, shards, qkv_grad, w_qkv, activations, gain_attn, gain_part, seen_attn, grad_down
        )
        output, input_grad, grad_query, grad_key, grad_value, grad_out, grad_gate, grad_up, grad_down = finish(
            lax.axis_index("fsdp"), hidden_state, down, hidden_grad, input_part,
            grad_both, both_from, grad_down, down_from, grad_qkv, grad_out,
        )
        return (
            output, input_grad, gain_sums[0], grad_query, grad_key, grad_value, grad_out, gain_sums[1],
            grad_gate, grad_up, grad_down,
        )

    return body


def solution(mesh):
    tokens = P(("fsdp", "tp"), None)
    column = P("fsdp", "tp")
    row = P("tp", "fsdp")
    in_specs = (tokens, P(), column, column, column, row, P(), column, column, row, tokens)
    out_specs = (tokens, tokens, P(), column, column, column, row, P(), column, column, row)
    return jax.shard_map(make_body(mesh), mesh=mesh, in_specs=in_specs, out_specs=out_specs, check_vma=False)
```

```python
import jax
import jax.numpy as jnp
import numpy as np
from jax import lax
from jax.experimental import pallas as pl
from jax.experimental.pallas import tpu as pltpu
from jax.sharding import PartitionSpec as P

HEAD_DIM = 64
SEQ_LEN = 2048
LANES = 128
rope_base = 130000.0
norm_eps = 1e-05
masked_score = -1e30

NT = (((1,), (1,)), ((), ()))
NN = (((1,), (0,)), ((), ()))
TN = (((0,), (0,)), ((), ()))
MESH = pl.DeviceIdType.MESH
DMA = pltpu.SemaphoreType.DMA
ANYWHERE = pl.BlockSpec(memory_space=pl.ANY)
VMEM = pl.BlockSpec(memory_space=pltpu.VMEM)
low = jnp.bfloat16


def dot(left, right, dims=NN):
    return lax.dot_general(left, right, dims, preferred_element_type=jnp.float32)


def span(index, size):
    return pl.ds(pl.multiple_of(index * size, size), size)


def remote(source, target, send, receive, device):
    return pltpu.make_async_remote_copy(
        src_ref=source, dst_ref=target, send_sem=send, recv_sem=receive,
        device_id=device, device_id_type=MESH,
    )


def hello(device):
    pl.semaphore_signal(pltpu.get_barrier_semaphore(), inc=1, device_id=device, device_id_type=MESH)


class Line:
    def __init__(self, chips):
        self.chips = chips
        self.me = lax.axis_index("tp")
        self.chip, self.core = self.me // 2, self.me % 2
        self.partner = 2 * self.chip + 1 - self.core
        self.has_left, self.has_right = self.chip > 0, self.chip < chips - 1

    def hello(self, more=()):
        hello({"tp": self.partner})

        @pl.when(self.has_left)
        def _():
            hello({"tp": self.me - 2})

        @pl.when(self.has_right)
        def _():
            hello({"tp": self.me + 2})

        for device in more:
            hello(device)

    def ready(self, more=()):
        count = 1 + len(more) + jnp.where(self.has_left, 1, 0) + jnp.where(self.has_right, 1, 0)
        pl.semaphore_wait(pltpu.get_barrier_semaphore(), count)

    def target(self, step):
        after = self.chips - 1 - self.chip
        most, least = jnp.maximum(self.chip, after), jnp.minimum(self.chip, after)
        sign = jnp.where(after >= self.chip, 1, -1)
        late = step - (most - least)
        side = jnp.where(late % 2 == 0, sign, -sign)
        return jnp.where(late < 0, self.chip + sign * (most - step), self.chip + side * (least - late // 2))


    def fed(self, target):
        after, before = jnp.logical_and(target >= self.chip, self.has_left), jnp.logical_and(target <= self.chip, self.has_right)
        return jnp.logical_or(after, before)


class Gather:
    @staticmethod
    def scratch(chips, parts=1):
        return [DMA((2 * chips, parts)), DMA((chips, parts)), DMA((chips, parts)), DMA((chips, parts)), DMA]

    def __init__(self, line, own, out, received, right, left, across, local, parts=1):
        self.line, self.out = line, out
        self.received, self.right, self.left, self.across, self.local = received, right, left, across, local
        self.parts = parts
        self.rows = out.shape[0] // (2 * line.chips * parts)
        self.held = own is None
        self.own = out.at[span(line.me, self.rows * parts)] if self.held else own

    def block(self, index, part):
        return self.out.at[span(index * self.parts + part, self.rows)]

    def mine(self, part):
        return self.own.at[pl.ds(part * self.rows, self.rows)]

    def copy(self, sems, chip, part, device, mine):
        index = 2 * chip + self.line.core
        source = self.mine(part) if mine else self.block(index, part)
        return remote(source, self.block(index, part), sems.at[chip, part], self.received.at[index, part], {"tp": device})

    def keep(self):
        return pltpu.make_async_copy(self.own, self.out.at[span(self.line.me, self.rows * self.parts)], self.local)

    def start(self):
        line = self.line
        if not self.held:
            self.keep().start()
        for part in range(self.parts):
            @pl.when(line.has_right)
            def _():
                self.copy(self.right, line.chip, part, line.me + 2, True).start()

            @pl.when(line.has_left)
            def _():
                self.copy(self.left, line.chip, part, line.me - 2, True).start()

            self.copy(self.across, line.chip, part, line.partner, True).start()

    def arrive(self, index, part):
        remote(self.mine(part), self.block(index, part), self.right.at[0, part], self.received.at[index, part], {"tp": self.line.partner}).wait_recv()

    def arrive_across(self, chip):
        for part in range(self.parts):
            self.arrive(2 * chip + 1 - self.line.core, part)

    def step(self, distance):
        line = self.line
        before, after = line.chip - distance, line.chip + distance
        for part in range(self.parts):
            @pl.when(before >= 0)
            def _():
                self.arrive(2 * before + line.core, part)

                @pl.when(line.has_right)
                def _():
                    self.copy(self.right, before, part, line.me + 2, False).start()

                self.copy(self.across, before, part, line.partner, False).start()

            @pl.when(after < line.chips)
            def _():
                self.arrive(2 * after + line.core, part)

                @pl.when(line.has_left)
                def _():
                    self.copy(self.left, after, part, line.me - 2, False).start()

                self.copy(self.across, after, part, line.partner, False).start()

    def finish(self, arrivals):
        line = self.line
        if arrivals:
            self.keep().wait()
        for chip in range(line.chips):
            if arrivals:
                self.arrive_across(chip)
            for part in range(self.parts):
                self.copy(self.across, chip, part, line.partner, True).wait_send()

                @pl.when(jnp.logical_and(line.has_right, chip <= line.chip))
                def _():
                    self.copy(self.right, chip, part, line.me + 2, True).wait_send()

                @pl.when(jnp.logical_and(line.has_left, chip >= line.chip))
                def _():
                    self.copy(self.left, chip, part, line.me - 2, True).wait_send()


class Scatter:
    @staticmethod
    def scratch(chips, rows, depth):
        slots = chips // 2 + 1
        return [
            pltpu.VMEM((slots, 2 * rows, depth), low),
            pltpu.VMEM((chips, rows, depth), low),
            pltpu.VMEM((chips + 1, rows, depth), low),
            pltpu.VMEM((2, rows, depth), low),
            DMA((slots,)), DMA((chips,)), DMA((2,)), DMA((chips + 1,)),
        ]

    def __init__(self, line, out, term, shares, lines, total, share_send, share_recv, line_send, line_recv):
        self.line, self.out = line, out
        self.term, self.shares, self.lines, self.total = term, shares, lines, total
        self.share_send, self.share_recv, self.line_send, self.line_recv = share_send, share_recv, line_send, line_recv
        self.rows = out.shape[0]
        self.slots = term.shape[0]

    def share(self, step):
        slot = step % self.slots
        source = self.term.at[slot, span(1 - self.line.core, self.rows)]
        return remote(source, self.shares.at[step], self.share_send.at[slot], self.share_recv.at[step], {"tp": self.line.partner})

    def due(self, index, fed):
        def one(step, carry):
            target = self.line.target(step)
            distance = jnp.where(target > self.line.chip, target - self.line.chip, self.line.chip - target)
            turn = True if fed is None else self.line.fed(target) == fed

            @pl.when(jnp.logical_and(distance == self.line.chips - index, turn))
            def _():
                self.step(step)

            return carry

        return one

    def mine(self, step):
        return self.term[step % self.slots, span(self.line.core, self.rows), :]

    def pass_on(self, step):
        line, target = self.line, self.line.target(step)
        onward = target > line.chip
        slot = jnp.where(onward, target, jnp.where(target == line.chip - 1, line.chips, target))
        device = jnp.where(onward, line.me + 2, line.me - 2)
        return remote(self.total.at[step % 2], self.lines.at[slot], self.line_send.at[step % 2], self.line_recv.at[slot], {"tp": device})

    def add(self, slot):
        remote(self.total.at[0], self.lines.at[slot], self.line_send.at[0], self.line_recv.at[slot], {"tp": self.line.partner}).wait_recv()
        self.out[...] += self.lines[slot].astype(jnp.float32)

    def free(self, step):
        @pl.when(step >= self.slots)
        def _():
            self.share(step - self.slots).wait_send()

    def step(self, step):
        line, target = self.line, self.line.target(step)
        self.share(step).wait_recv()
        self.out[...] = self.mine(step).astype(jnp.float32) + self.shares[step].astype(jnp.float32)

        @pl.when(jnp.logical_and(target >= line.chip, line.has_left))
        def _():
            self.add(target)

        @pl.when(jnp.logical_and(target <= line.chip, line.has_right))
        def _():
            self.add(jnp.where(target == line.chip, line.chips, target))

        @pl.when(step < line.chips - 1)
        def _():
            @pl.when(step >= 2)
            def _():
                self.pass_on(step - 2).wait_send()

            self.total[step % 2] = self.out[...].astype(low)
            self.pass_on(step).start()

    def finish(self):
        chips = self.line.chips
        for step in range(max(0, chips - 3), chips - 1):
            self.pass_on(step).wait_send()
        for step in range(max(0, chips - self.slots), chips):
            self.share(step).wait_send()


NORM_ROWS = 64


def normed(value, gain):
    return value * lax.rsqrt(jnp.mean(value * value, axis=-1, keepdims=True) + norm_eps) * gain


def norm_back(value, gain, grad):
    scale = lax.rsqrt(jnp.mean(value * value, axis=-1, keepdims=True) + norm_eps)
    unit = value * scale
    scaled = grad * gain
    return scale * (scaled - unit * jnp.mean(scaled * unit, axis=-1, keepdims=True)), jnp.sum(grad * unit, axis=0, keepdims=True)


def by_rows(rows, work, stores=None):
    def step(index, carry):
        work(span(index, NORM_ROWS))
        if stores:
            stores.start(index)
        return carry

    lax.fori_loop(0, rows // NORM_ROWS, step, 0)


class Grid:
    def __init__(self, shards):
        self.shards, self.across = shards, shards // 2
        self.me = lax.axis_index("fsdp")
        self.row, self.column = self.me // self.across, self.me % self.across
        self.others = [(self.me + ahead) % shards for ahead in range(1, shards)]
        self.mates = [self.row * self.across + (self.column + ahead) % self.across for ahead in range(1, self.across)]
        self.twin = (1 - self.row) * self.across + self.column
        self.near = self.mates + [self.twin]

    def is_near(self, shard):
        return jnp.logical_or(shard // self.across == self.row, shard % self.across == self.column)


class NearShards:
    scratch = staticmethod(lambda shards: [DMA((shards // 2,)), DMA((shards // 2,))])

    def __init__(self, grid, own, whole, at, send, receive):
        place = at(whole, grid.me, None)
        self.copies = [remote(own, place, send.at[i], receive.at[i], {"fsdp": peer}) for i, peer in enumerate(grid.near)]

    def start(self):
        for copy in self.copies:
            copy.start()

    def arrive(self):
        for copy in self.copies:
            copy.wait_recv()

    def finish(self):
        for copy in self.copies:
            copy.wait_send()


class FarShards:
    scratch = staticmethod(lambda shards: [DMA((2, shards // 2 - 1)), DMA((2, shards // 2 - 1))])

    def __init__(self, grid, near, whole, at, send, receive):
        self.copies = []
        for i, mate in enumerate(grid.mates):
            self.copies.append(remote(at(near, mate, 0), at(whole, mate, 0), send.at[0, i], receive.at[0, i], {"fsdp": grid.twin}))
            self.copies.append(remote(at(near, grid.twin, 1), at(whole, grid.twin, 1), send.at[1, i], receive.at[1, i], {"fsdp": mate}))

    def start(self):
        for copy in self.copies:
            copy.start()

    def finish(self):
        for copy in self.copies:
            copy.wait_recv()
            copy.wait_send()


class NearSums:
    @staticmethod
    def scratch(shards, rows, columns):
        across = shards // 2
        return [
            pltpu.VMEM((2, across - 1, rows // 2, columns), low),
            pltpu.VMEM((across, rows // 2, columns), low),
            DMA((2, across - 1)), DMA((2, across - 1)), DMA((across, 2)), DMA((across, 2)), DMA((across,)),
        ]

    def __init__(self, grid, part, out, at, relay, base, relay_send, relay_recv, near_send, near_recv, load_sem):
        self.relay, self.base = relay, base
        last = grid.across - 1
        half = base.shape[1]

        def near(source, slot, which, peer):
            target = out.at[slot, pl.ds(which * half, half)]
            return remote(source, target, near_send.at[slot, which], near_recv.at[slot, which], {"fsdp": peer})

        self.by_twin, self.by_mate, self.plain, self.joined, self.loads = [], [], [], [], []
        for i, mate in enumerate(grid.mates):
            far = (1 - grid.row) * grid.across + mate % grid.across
            self.by_twin.append(remote(at(part, far, 0), relay.at[0, i], relay_send.at[0, i], relay_recv.at[0, i], {"fsdp": grid.twin}))
            self.by_mate.append(remote(at(part, far, 1), relay.at[1, i], relay_send.at[1, i], relay_recv.at[1, i], {"fsdp": mate}))
            self.plain.append(near(at(part, mate, 1), i, 1, mate))
            self.joined.append(near(relay.at[0, i], i, 0, mate))
            self.loads.append(pltpu.make_async_copy(at(part, mate, 0), base.at[i], load_sem.at[i]))
        self.plain.append(near(at(part, grid.twin, 0), last, 0, grid.twin))
        self.joined.append(near(relay.at[1, 0], last, 1, grid.twin))
        self.loads.append(pltpu.make_async_copy(at(part, grid.twin, 1), base.at[last], load_sem.at[last]))

    def start(self):
        for copy in self.by_twin + self.by_mate + self.loads:
            copy.start()

    def start_plain(self):
        for copy in self.plain:
            copy.start()

    def join(self):
        for copy in self.by_twin + self.by_mate:
            copy.wait_recv()
        for copy in self.loads:
            copy.wait()
        last = self.base.shape[0] - 1
        for i in range(last):
            self.relay[0, i] = (self.base[i].astype(jnp.float32) + self.relay[0, i].astype(jnp.float32)).astype(low)
        total = self.base[last].astype(jnp.float32)
        for i in range(last):
            total = total + self.relay[1, i].astype(jnp.float32)
        self.relay[1, 0] = total.astype(low)
        for copy in self.joined:
            copy.start()

    def finish(self):
        for copy in self.by_twin + self.by_mate:
            copy.wait_send()
        for copy in self.plain + self.joined:
            copy.wait_recv()
            copy.wait_send()


def row_shard(depth):
    def at(ref, shard, half):
        if half is None:
            return ref.at[span(shard, depth)]
        return ref.at[span(2 * shard + half, depth // 2)]

    return at


def column_shard(rows, width):
    def at(ref, shard, half):
        if half is None:
            return ref.at[:, span(shard, width)]
        return ref.at[pl.ds(half * (rows // 2), rows // 2), span(shard, width)]

    return at


class HeldScatter(Scatter):
    @staticmethod
    def scratch(chips, rows, depth):
        return [
            pltpu.VMEM((2, rows, depth), low),
            pltpu.VMEM((chips, rows, depth), low),
            pltpu.VMEM((chips + 1, rows, depth), low),
            pltpu.VMEM((2, rows, depth), low),
            DMA((2,)), DMA((chips,)), DMA((2,)), DMA((chips + 1,)), DMA((2,)),
        ]

    def __init__(self, line, out, held, *refs):
        super().__init__(line, out, *refs[:-1])
        self.held, self.load_sem = held, refs[-1]

    def load(self, step):
        source = self.held.at[span(2 * self.line.target(step) + self.line.core, self.rows)]
        return pltpu.make_async_copy(source, self.term.at[step % 2], self.load_sem.at[step % 2])

    def share(self, step):
        source = self.held.at[span(2 * self.line.target(step) + 1 - self.line.core, self.rows)]
        return remote(source, self.shares.at[step], self.share_send.at[step % 2], self.share_recv.at[step], {"tp": self.line.partner})

    def mine(self, step):
        self.load(step).wait()

        @pl.when(step < self.line.chips - 1)
        def _():
            self.load(step + 1).start()

        return self.term[step % 2]


class Loads:
    @staticmethod
    def scratch(*operands):
        return [pltpu.VMEM(a.shape, a.dtype) for a in operands] + [DMA((len(operands),))]

    def __init__(self, sources, refs):
        self.refs = refs[: len(sources)]
        self.copies = [pltpu.make_async_copy(source, ref, refs[-1].at[i]) for i, (source, ref) in enumerate(zip(sources, self.refs))]

    def start(self):
        for copy in self.copies:
            copy.start()

    def wait(self, *which):
        for i in which:
            self.copies[i].wait()


class RowStores:
    @staticmethod
    def scratch(size, count, *results):
        return [pltpu.VMEM(a.shape, a.dtype) for a in results] + [DMA((len(results), count))]

    def __init__(self, size, count, refs, outs, sems):
        self.size, self.count, self.refs, self.outs, self.sems = size, count, refs, outs, sems

    def copies(self, index):
        here = span(index, self.size)
        return [pltpu.make_async_copy(a.at[here], b.at[here], self.sems.at[i, index]) for i, (a, b) in enumerate(zip(self.refs, self.outs))]

    def start(self, index):
        for copy in self.copies(index):
            copy.start()

    def wait(self):
        for index in range(self.count):
            for copy in self.copies(index):
                copy.wait()


def turned(block, sign):
    half = HEAD_DIM // 2
    lane = lax.broadcasted_iota(jnp.int32, block.shape, 1)
    width = block.shape[1]
    up = pltpu.roll(block, width - half, 1)
    down = pltpu.roll(block, half, 1)
    return jnp.where(lane % HEAD_DIM < half, -sign * up, sign * down)


def widened(table, width):
    return table if table.shape[1] == width else jnp.concatenate([table] * (width // table.shape[1]), axis=1)


def only_head(block, head):
    lane = lax.broadcasted_iota(jnp.int32, block.shape, 1)
    return jnp.where(lane // HEAD_DIM == head, block, jnp.zeros_like(block))


def causal(tile):
    key = lax.broadcasted_iota(jnp.int32, tile.shape, 0)
    query = lax.broadcasted_iota(jnp.int32, tile.shape, 1)
    return jnp.where(key <= query, tile, masked_score)


def over_keys(chunk, rows, visit):
    start = chunk * rows
    first = start // SEQ_LEN * SEQ_LEN

    def step(index, carry):
        visit(pl.multiple_of(first + index * rows, rows), False)
        return carry

    lax.fori_loop(0, (start - first) // rows, step, 0)
    visit(pl.multiple_of(start, rows), True)


def project_kernel(
    chips, shards,
    gain, inverse, activations_hbm, w_query, w_key, w_value, w_out, w_down,
    tokens_out, weight_out, full_out, qkv_out, keys_out, values_out, cosine_out, sine_out, down_near,
    weight, out_w, qkv, keys_t, values_t, cosine, sine, tokens, activations,
    load_sem, weight_send, weight_recv, weight_keep, table_sem, store_sem, near_send, near_recv, *gather_sems,
):
    line = Line(chips)
    rows = activations.shape[0]
    depth, width = w_query.shape
    grid = Grid(shards)
    shard, others = grid.me, grid.others
    gather = Gather(line, None, tokens, *gather_sems, parts=2)
    down = NearShards(grid, w_down, down_near, column_shard(*w_down.shape), near_send, near_recv)
    parts = (w_query, w_key, w_value, w_out)

    def place(part):
        if part == 3:
            return out_w.at[:, span(shard, depth)]
        return weight.at[span(shard, depth), pl.ds(part * width, width)]

    def give(ahead, part):
        return remote(parts[part], place(part), weight_send.at[ahead, part], weight_recv.at[ahead, part], {"fsdp": others[ahead]})

    def keep(part):
        return pltpu.make_async_copy(parts[part], place(part), weight_keep.at[part])

    tables = [
        pltpu.make_async_copy(source, out, table_sem.at[i])
        for i, (source, out) in enumerate(((cosine, cosine_out), (sine, sine_out), (weight, weight_out), (out_w, full_out)))
    ]

    def stores(index):
        here = span(index, rows)
        return [
            pltpu.make_async_copy(qkv.at[here], qkv_out.at[here], store_sem.at[0, index]),
            pltpu.make_async_copy(keys_t.at[:, here], keys_out.at[:, here], store_sem.at[1, index]),
            pltpu.make_async_copy(values_t.at[:, here], values_out.at[:, here], store_sem.at[2, index]),
            pltpu.make_async_copy(tokens.at[here], tokens_out.at[here], store_sem.at[3, index]),
        ]

    def norm(index, carry):
        there = span(line.me * (rows // NORM_ROWS) + index, NORM_ROWS)
        tokens[there, :] = normed(activations[span(index, NORM_ROWS), :], gain[...]).astype(low)
        return carry

    load = pltpu.make_async_copy(activations_hbm, activations, load_sem)
    load.start()
    line.hello([{"fsdp": other} for other in others])
    load.wait()
    lax.fori_loop(0, rows // NORM_ROWS, norm, 0)
    line.ready(others)
    gather.start()
    for part in range(4):
        keep(part).start()
        for ahead in range(shards - 1):
            give(ahead, part).start()
    position = lax.broadcasted_iota(jnp.int32, (inverse.shape[0], SEQ_LEN), 1).astype(jnp.float32)
    angle = position * inverse[...]
    for table, turn in ((cosine, jnp.cos(angle).T), (sine, jnp.sin(angle).T)):
        table[...] = jnp.concatenate([turn] * (LANES // turn.shape[1]), axis=1)
    for copy in tables[:2]:
        copy.start()

    def project(index):
        here = span(index, rows)
        table = span(index % (SEQ_LEN // rows), rows)
        for part in range(3):
            columns = pl.ds(part * width, width)
            block = dot(tokens[here, :], weight[:, columns])
            if part < 2:
                block = block * widened(cosine[table, :], width) + turned(block, 1.0) * widened(sine[table, :], width)
            qkv[here, columns] = block.astype(low)
            if part:
                (keys_t, values_t)[part - 1][:, here] = block.T.astype(low)
        for copy in stores(index):
            copy.start()

    def step(index, carry):
        @pl.when(jnp.logical_and(index >= 1, index < chips))
        def _():
            gather.step(index)

        @pl.when(index == 2)
        def _():
            for part in range(4):
                keep(part).wait()
                for ahead in range(shards - 1):
                    give(ahead, part).wait_recv()
            for copy in tables[2:]:
                copy.start()
            down.start()

        def side(turn, carry):
            distance, which, across = index - 1, turn % 3, turn // 3
            chip = jnp.where(which == 0, line.chip - distance, jnp.where(which == 1, line.chip + distance, line.chip))
            there = jnp.logical_and(chip >= 0, chip < chips)

            @pl.when(jnp.logical_and(there, jnp.logical_and(index >= 2, jnp.logical_or(which < 2, index == 2))))
            def _():
                @pl.when(across == 1)
                def _():
                    gather.arrive_across(chip)

                project(2 * chip + jnp.where(across == 1, 1 - line.core, line.core))

            return carry

        lax.fori_loop(0, 6, side, 0)
        return carry

    lax.fori_loop(0, chips + 1, step, 0)
    gather.finish(False)
    for part in range(4):
        for ahead in range(shards - 1):
            give(ahead, part).wait_send()
    for copy in tables:
        copy.wait()
    for index in range(2 * chips):
        for copy in stores(index):
            copy.wait()
    down.arrive()
    down.finish()


def project(chips, shards, activations, gain, w_query, w_key, w_value, w_out, inverse, w_down):
    rows, depth = activations.shape
    group_rows = 2 * chips * rows
    width = w_query.shape[1]
    shape = jax.ShapeDtypeStruct
    held = [
        shape((depth, 3 * width), low),
        shape((width, depth), low),
        shape((group_rows, 3 * width), low),
        shape((width, group_rows), low),
        shape((width, group_rows), low),
        shape((SEQ_LEN, LANES), jnp.float32),
        shape((SEQ_LEN, LANES), jnp.float32),
    ]
    return pl.pallas_call(
        lambda *refs: project_kernel(chips, shards, *refs),
        in_specs=[VMEM] * 2 + [ANYWHERE] * 6,
        out_specs=[ANYWHERE] * 9,
        out_shape=[shape((group_rows, depth), low)] + held + [shape((w_down.shape[0], depth), low)],
        scratch_shapes=[pltpu.VMEM(a.shape, a.dtype) for a in held] + [
            pltpu.VMEM((group_rows, depth), low),
            pltpu.VMEM((rows, depth), jnp.float32),
            DMA, DMA((shards - 1, 4)), DMA((shards - 1, 4)), DMA((4,)), DMA((4,)), DMA((4, 2 * chips)),
        ] + NearShards.scratch(shards) + Gather.scratch(chips, 2),
        compiler_params=pltpu.CompilerParams(collective_id=1, has_side_effects=True, vmem_limit_bytes=63 << 20),
        cost_estimate=pl.CostEstimate(flops=6 * group_rows * depth * width, bytes_accessed=4 * group_rows * depth, transcendentals=0),
        name="project",
    )(gain, inverse, activations, w_query, w_key, w_value, w_out, w_down)


def attend_chunk(chunk, rows, qkv, values_t, heads_ref, acc, out, top_ref, sum_ref):
    width = acc.shape[0]
    heads = width // HEAD_DIM
    scaled = qkv[span(chunk, rows), pl.ds(0, width)] * low(HEAD_DIM**-0.5)
    for head in range(heads):
        heads_ref[head] = only_head(scaled, head)
    acc[...] = jnp.zeros_like(acc)
    top_ref[...] = jnp.full_like(top_ref, masked_score)
    sum_ref[...] = jnp.zeros_like(sum_ref)

    def visit(offset, diagonal):
        key_block = qkv[pl.ds(offset, rows), pl.ds(width, width)]
        for head in range(heads):
            feature = pl.ds(head * HEAD_DIM, HEAD_DIM)
            one = pl.ds(head, 1)
            scores = dot(key_block, heads_ref[head], NT)
            if diagonal:
                scores = causal(scores)
            old = top_ref[one, :]
            top = jnp.maximum(old, jnp.max(scores, axis=0, keepdims=True))
            shrink = jnp.exp(old - top)
            weights = jnp.exp(scores - top)
            top_ref[one, :] = top
            sum_ref[one, :] = sum_ref[one, :] * shrink + jnp.sum(weights, axis=0, keepdims=True)
            acc[feature, :] = acc[feature, :] * shrink + dot(values_t[feature, pl.ds(offset, rows)], weights.astype(low))

    over_keys(chunk, rows, visit)
    for head in range(heads):
        feature = pl.ds(head * HEAD_DIM, HEAD_DIM)
        acc[feature, :] = acc[feature, :] / sum_ref[pl.ds(head, 1), :]
    out[...] = acc[...].T.astype(low)


def attend_kernel(
    chips, shards,
    gain, *refs,
):
    sources, (w_gate, w_up, down_near) = refs[:5], refs[5:8]
    hidden_out, tokens_out, mixed_out, totals, grads_out, gate_all, up_all, down_far = refs[8:16]
    hidden, tokens, rows_sem, mixed, mixed_sem = refs[-5:]
    refs = refs[:-5]
    loads = Loads(sources, refs[16:22])
    cotangent, qkv, values_t, w_out, activations = loads.refs
    heads_ref, acc, out, top_ref, sum_ref, grads = refs[22:28]
    loads.start()
    line = Line(chips)
    grid = Grid(shards)
    rows_of = row_shard(w_gate.shape[0])
    line.hello([{"fsdp": peer} for peer in grid.near])
    down = FarShards(grid, down_near, down_far, column_shard(down_near.shape[0], down_near.shape[1] // shards), *refs[28:30])
    gate_near, gate_far = NearShards(grid, w_gate, gate_all, rows_of, *refs[30:32]), FarShards(grid, gate_all, gate_all, rows_of, *refs[32:34])
    up_near, up_far = NearShards(grid, w_up, up_all, rows_of, *refs[34:36]), FarShards(grid, up_all, up_all, rows_of, *refs[36:38])
    sems = refs[38:]
    rows, depth = hidden.shape
    pair = 2 * rows
    states = RowStores(NORM_ROWS, rows // NORM_ROWS, (hidden, tokens), (hidden_out, tokens_out), rows_sem)
    blends = RowStores(pair, chips, (mixed,), (mixed_out,), mixed_sem)
    scatter = Scatter(line, hidden, *sems[:8])
    loads.wait(0)
    grads[...] = cotangent[...].astype(low)
    gather = Gather(line, grads, grads_out, *sems[8:])
    line.ready(grid.near)
    gather.start()
    gate_near.start()
    down.start()
    loads.wait(1, 2, 3, 4)

    def term(index):
        chunk = line.target(index)
        attend_chunk(chunk, pair, qkv, values_t, heads_ref, acc, out, top_ref, sum_ref)
        mixed[span(chunk, pair), :] = out[...]
        blends.start(chunk)
        totals[:, span(chunk, pair)] = top_ref[...] + jnp.log(sum_ref[...])
        scatter.free(index)

        def tile(place, carry):
            columns = span(place, 512)
            scatter.term[index % scatter.slots, :, columns] = dot(out[...], w_out[:, columns]).astype(low)
            return carry

        lax.fori_loop(0, depth // 512, tile, 0)
        scatter.share(index).start()

    def step(index, carry):
        def phase(which, carry):
            @pl.when(jnp.logical_and(which == 1, index < chips))
            def _():
                term(index)

            lax.fori_loop(0, jnp.where(which == 1, 0, chips), scatter.due(index, which == 2), 0)
            return carry

        lax.fori_loop(0, 3, phase, 0)

        @pl.when(jnp.logical_and(index >= 1, index < chips))
        def _():
            gather.step(index)

        @pl.when(index == 1)
        def _():
            up_near.start()

        @pl.when(index == min(2, chips))
        def _():
            gate_near.arrive()
            gate_far.start()

        @pl.when(index == min(3, chips))
        def _():
            up_near.arrive()
            up_far.start()

        return carry

    lax.fori_loop(0, chips + 1, step, 0)

    def norm(here):
        state = activations[here, :] + hidden[here, :]
        hidden[here, :] = state
        tokens[here, :] = normed(state, gain[...]).astype(low)

    by_rows(rows, norm, states)
    scatter.finish()
    gather.finish(True)
    blends.wait()
    states.wait()
    for near in (gate_near, up_near):
        near.finish()
    for far in (down, gate_far, up_far):
        far.finish()


def attend(chips, shards, qkv, values_t, w_out, activations, cotangent, gain, w_gate, w_up, down_near):
    rows, depth = activations.shape
    pair = 2 * rows
    group_rows = chips * pair
    width = w_out.shape[0]
    heads = width // HEAD_DIM
    shape = jax.ShapeDtypeStruct
    stored = [shape((rows, depth), jnp.float32), shape((rows, depth), low), shape((group_rows, width), low)]
    return pl.pallas_call(
        lambda *refs: attend_kernel(chips, shards, *refs),
        in_specs=[VMEM] + [ANYWHERE] * 8,
        out_specs=[ANYWHERE] * 3 + [VMEM] + [ANYWHERE] * 4,
        out_shape=stored + [
            shape((heads, group_rows), jnp.float32),
            shape((group_rows, depth), low),
            shape((depth, w_gate.shape[1]), low),
            shape((depth, w_gate.shape[1]), low),
            shape(down_near.shape, low),
        ],
        scratch_shapes=Loads.scratch(cotangent, qkv, values_t, w_out, activations) + [
            pltpu.VMEM((heads, pair, width), low),
            pltpu.VMEM((width, pair), jnp.float32),
            pltpu.VMEM((pair, width), low),
            pltpu.VMEM((heads, pair), jnp.float32),
            pltpu.VMEM((heads, pair), jnp.float32),
            pltpu.VMEM((rows, depth), low),
        ] + FarShards.scratch(shards) + (NearShards.scratch(shards) + FarShards.scratch(shards)) * 2 + Scatter.scratch(chips, rows, depth) + Gather.scratch(chips)
        + RowStores.scratch(NORM_ROWS, rows // NORM_ROWS, *stored[:2]) + RowStores.scratch(pair, chips, stored[2]),
        compiler_params=pltpu.CompilerParams(collective_id=2, has_side_effects=True, vmem_limit_bytes=63 << 20),
        cost_estimate=pl.CostEstimate(flops=2 * group_rows * (SEQ_LEN + depth) * width, bytes_accessed=4 * group_rows * depth, transcendentals=group_rows * SEQ_LEN * heads // 2),
        name="attend",
    )(gain, cotangent, qkv, values_t, w_out, activations, w_gate, w_up, down_near)


def back_chunk(chunk, rows, grad, qkv, keys_t, mixed, totals, dkey, dvalue, heads_ref, grads_ref, acc, inner_ref):
    width = acc.shape[0]
    heads = width // HEAD_DIM
    here = span(chunk, rows)
    scaled = qkv[here, pl.ds(0, width)] * low(HEAD_DIM**-0.5)
    product = grad.astype(jnp.float32) * mixed[here, :].astype(jnp.float32)
    shape = (inner_ref.shape[0], width)
    pick = (lax.broadcasted_iota(jnp.int32, shape, 1) // HEAD_DIM == lax.broadcasted_iota(jnp.int32, shape, 0)).astype(jnp.float32)
    inner_ref[...] = lax.dot_general(pick, product, NT, precision=lax.Precision.HIGHEST, preferred_element_type=jnp.float32)
    for head in range(heads):
        heads_ref[head] = only_head(scaled, head)
        grads_ref[head] = only_head(grad, head)
    acc[...] = jnp.zeros_like(acc)

    def visit(offset, diagonal):
        keys = pl.ds(offset, rows)
        key_block = qkv[keys, pl.ds(width, width)]
        value_block = qkv[keys, pl.ds(2 * width, width)]
        key_sum, value_sum = dkey[keys, :], dvalue[keys, :]
        for head in range(heads):
            feature = pl.ds(head * HEAD_DIM, HEAD_DIM)
            scores = dot(key_block, heads_ref[head], NT)
            if diagonal:
                scores = causal(scores)
            probs = jnp.exp(scores - totals[pl.ds(head, 1), here])
            dprobs = dot(value_block, grads_ref[head], NT)
            dscores = (probs * (dprobs - inner_ref[pl.ds(head, 1), :])).astype(low)
            value_sum = value_sum + dot(probs.astype(low), grads_ref[head])
            key_sum = key_sum + dot(dscores, heads_ref[head])
            acc[feature, :] = acc[feature, :] + dot(keys_t[feature, keys], dscores)
        dkey[keys, :] = key_sum
        dvalue[keys, :] = value_sum

    over_keys(chunk, rows, visit)


def back_kernel(
    chips, shards,
    branch, terms, inner, grads, grad_both, *refs,
):
    sources, (down, branch_out, qkv_out, grad_down, grad_out, both_from) = refs[:7], refs[7:13]
    qkv_grad, qkv_sem = refs[-2:]
    refs = refs[:-2]
    loads = Loads(sources, refs[13:21])
    w_out, qkv, keys_t, mixed, totals, cosine, sine = loads.refs
    inner_chunk, grad_chunk, down_sum, down_tile, out_sum, out_stage, out_from, branch_chunk, dkey, dvalue = refs[21:31]
    heads_ref, grads_ref, acc, inner_ref, inner_sem, grad_sem, branch_sem, tile_sem, out_send, out_recv = refs[31:41]
    sums = refs[41:48]
    sems = refs[48:]
    line = Line(chips)
    rows, depth = down.shape
    pair = 2 * rows
    width = w_out.shape[0]
    results = RowStores(pair, chips, (qkv_grad,), (qkv_out,), qkv_sem)
    scatter = HeldScatter(line, down, terms, *sems[:9])
    gather = Gather(line, branch, branch_out, *sems[9:])

    def fetch(step):
        return pltpu.make_async_copy(inner.at[span(line.target(step), pair)], inner_chunk, inner_sem)

    def fetch_grad(step):
        return pltpu.make_async_copy(grads.at[span(line.target(step), pair)], grad_chunk, grad_sem)

    grid = Grid(shards)
    shard, others = grid.me, grid.others
    columns_out = depth // shards
    both = NearSums(grid, grad_both, both_from, row_shard(columns_out), *sums)

    def give(turn):
        return remote(out_stage.at[turn], out_from.at[turn], out_send.at[turn], out_recv.at[turn], {"fsdp": others[turn]})

    def keep_tile(place):
        return pltpu.make_async_copy(down_tile, grad_down.at[span(place, 256)], tile_sem)

    line.hello([{"fsdp": other} for other in others])
    loads.start()
    fetch(0).start()
    fetch_grad(0).start()
    scatter.load(0).start()
    line.ready(others)
    gather.start()
    both.start()
    out_sum[...] = jnp.zeros_like(out_sum)
    dkey[...] = jnp.zeros_like(dkey)
    dvalue[...] = jnp.zeros_like(dvalue)

    def unrotated(block, chunk):
        table = span(chunk % (SEQ_LEN // pair), pair)
        return (block * widened(cosine[table, :], width) + turned(block * widened(sine[table, :], width), -1.0)).astype(low)

    def attention(chunk):
        gather.arrive_across(chunk)
        copy = pltpu.make_async_copy(branch_out.at[span(chunk, pair)], branch_chunk, branch_sem)
        copy.start()
        copy.wait()
        out_sum[...] += dot(mixed[span(chunk, pair), :], branch_chunk[...], TN)
        grad = dot(branch_chunk[...], w_out[...], NT).astype(low)
        back_chunk(chunk, pair, grad, qkv, keys_t, mixed, totals, dkey, dvalue, heads_ref, grads_ref, acc, inner_ref)
        qkv_grad[span(chunk, pair), pl.ds(0, width)] = unrotated(acc[...].T * HEAD_DIM**-0.5, chunk)

    def close():
        def part(chunk, carry):
            here = span(chunk, pair)
            qkv_grad[here, pl.ds(width, width)] = unrotated(dkey[here, :], chunk)
            qkv_grad[here, pl.ds(2 * width, width)] = dvalue[here, :].astype(low)
            results.start(chunk)
            return carry

        lax.fori_loop(0, chips, part, 0)

    def step(index, carry):
        @pl.when(index == 0)
        def _():
            loads.wait(*range(7))
            gather.keep().wait()

        @pl.when(index < chips)
        def _():
            scatter.free(index)
            scatter.share(index).start()

        @pl.when(index == chips)
        def _():
            for turn in range(shards - 1):
                out_stage[turn] = out_sum[:, span(others[turn], columns_out)].astype(low)
                give(turn).start()
            close()

        lax.fori_loop(0, chips, scatter.due(index, None), 0)

        @pl.when(jnp.logical_and(index >= 1, index < chips))
        def _():
            gather.step(index)

        @pl.when(index == 1)
        def _():
            both.start_plain()

        @pl.when(index == 2)
        def _():
            both.join()

        @pl.when(index < chips)
        def _():
            attention(line.target(chips - 1 - index))

        def weights(turn, carry):
            fetch(turn).wait()
            fetch_grad(turn).wait()

            def tile(place, carry):
                here = span(place, 256)
                part = dot(inner_chunk[:, here], grad_chunk[...], TN)

                @pl.when(turn == 0)
                def _():
                    down_sum[here, :] = part

                @pl.when(turn > 0)
                def _():
                    down_sum[here, :] += part

                @pl.when(turn == chips - 1)
                def _():
                    @pl.when(place > 0)
                    def _():
                        keep_tile(place - 1).wait()

                    down_tile[...] = down_sum[here, :].astype(low)
                    keep_tile(place).start()

                return carry

            lax.fori_loop(0, down_sum.shape[0] // 256, tile, 0)

            @pl.when(turn < chips - 1)
            def _():
                fetch(turn + 1).start()
                fetch_grad(turn + 1).start()

            return carry

        lax.fori_loop(jnp.where(index == 0, 0, index + 1), jnp.minimum(index + 2, chips), weights, 0)
        return carry

    lax.fori_loop(0, chips + 1, step, 0)
    total = out_sum[:, span(shard, columns_out)]
    for turn in range(shards - 1):
        give(turn).wait_recv()
        total = total + out_from[turn].astype(jnp.float32)
    grad_out[...] = total
    for turn in range(shards - 1):
        give(turn).wait_send()
    keep_tile(down_sum.shape[0] // 256 - 1).wait()
    both.finish()
    results.wait()
    scatter.finish()
    gather.finish(False)


def back(chips, shards, branch, terms, inner, grads, grad_both, w_out, qkv, keys_t, mixed, totals, cosine, sine):
    rows, depth = branch.shape
    pair = 2 * rows
    group_rows = chips * pair
    width = w_out.shape[0]
    hidden = inner.shape[1]
    heads = width // HEAD_DIM
    shape = jax.ShapeDtypeStruct
    held = (w_out, qkv, keys_t, mixed, totals, cosine, sine)
    return pl.pallas_call(
        lambda *refs: back_kernel(chips, shards, *refs),
        in_specs=[VMEM] + [ANYWHERE] * 11,
        out_specs=[VMEM, ANYWHERE, ANYWHERE, ANYWHERE, VMEM, ANYWHERE],
        out_shape=[
            shape((rows, depth), jnp.float32),
            shape((group_rows, depth), low),
            shape((group_rows, 3 * width), low),
            shape((hidden, depth), low),
            shape((width, depth // shards), jnp.float32),
            shape((shards // 2, depth // shards, grad_both.shape[1]), low),
        ],
        scratch_shapes=Loads.scratch(*held) + [
            pltpu.VMEM((pair, hidden), low),
            pltpu.VMEM((pair, depth), low),
            pltpu.VMEM((hidden, depth), jnp.float32),
            pltpu.VMEM((256, depth), low),
            pltpu.VMEM((width, depth), jnp.float32),
            pltpu.VMEM((shards - 1, width, depth // shards), low),
            pltpu.VMEM((shards - 1, width, depth // shards), low),
            pltpu.VMEM((pair, depth), low),
            pltpu.VMEM((group_rows, width), jnp.float32),
            pltpu.VMEM((group_rows, width), jnp.float32),
            pltpu.VMEM((heads, pair, width), low),
            pltpu.VMEM((heads, pair, width), low),
            pltpu.VMEM((width, pair), jnp.float32),
            pltpu.VMEM((8, pair), jnp.float32),
            DMA, DMA, DMA, DMA, DMA((shards - 1,)), DMA((shards - 1,)),
        ] + NearSums.scratch(shards, depth // shards, grad_both.shape[1]) + HeldScatter.scratch(chips, rows, depth) + Gather.scratch(chips)
        + RowStores.scratch(pair, chips, shape((group_rows, 3 * width), low)),
        compiler_params=pltpu.CompilerParams(collective_id=4, has_side_effects=True, vmem_limit_bytes=67043328),
        cost_estimate=pl.CostEstimate(flops=1 << 20, bytes_accessed=1 << 20, transcendentals=0),
        name="back",
    )(branch, terms, inner, grads, grad_both, *held)


def spread_kernel(
    chips, shards,
    gain, gain_part, qkv_hbm, weight_hbm, activations_hbm, attn_tokens, grad_down,
    input_out, qkv_out, gain_sum, down_from,
    input_part, rows_sem, grad_qkv, sum_sem, qkv_grad, weight, activations, held_sem,
    attn_cols, qkv_stage, qkv_from, gains, gains_tp, gains_fsdp,
    attn_sem, qkv_send, qkv_recv, tp_send, tp_recv, fsdp_send, fsdp_recv, *sems,
):
    line = Line(chips)
    size = 2 * chips
    rows, depth = input_part.shape
    pair = 2 * rows
    grid = Grid(shards)
    shard = grid.me
    columns = depth // shards
    loads = Loads((qkv_hbm, weight_hbm, activations_hbm), (qkv_grad, weight, activations, held_sem))
    down = NearSums(grid, grad_down, down_from, column_shard(grad_down.shape[0], columns), *sems[:7])
    scatter = Scatter(line, input_part, *sems[7:])

    def peer(turn):
        return (shard + 1 + turn) % shards

    def fetch(turn):
        return pltpu.make_async_copy(attn_tokens.at[:, span(peer(turn), columns)], attn_cols.at[turn % 2], attn_sem.at[turn % 2])

    def give(turn):
        return remote(qkv_stage.at[turn], qkv_from.at[turn], qkv_send.at[turn], qkv_recv.at[turn], {"fsdp": peer(turn)})

    def tell_tp(ahead):
        return remote(gains, gains_tp.at[line.me], tp_send.at[ahead - 1], tp_recv.at[line.me], {"tp": (line.me + ahead) % size})

    def tell_fsdp(ahead):
        return remote(gains, gains_fsdp.at[shard], fsdp_send.at[ahead - 1], fsdp_recv.at[shard], {"fsdp": (shard + ahead) % shards})

    for ahead in range(1, size):
        hello({"tp": (line.me + ahead) % size})
    for ahead in range(1, shards):
        hello({"fsdp": (shard + ahead) % shards})
    loads.start()
    fetch(0).start()
    loads.wait(0, 1)
    pl.semaphore_wait(pltpu.get_barrier_semaphore(), size - 1 + shards - 1)
    down.start()

    def weights(turn, carry):
        @pl.when(turn < shards - 1)
        def _():
            fetch(turn + 1).start()

        fetch(turn).wait()
        part = dot(attn_cols[turn % 2], qkv_grad[...], TN)

        @pl.when(turn < shards - 1)
        def _():
            qkv_stage[turn] = part.astype(low)
            give(turn).start()

        @pl.when(turn == shards - 1)
        def _():
            grad_qkv[...] = part

        return carry

    def term(index):
        scatter.free(index)
        here = span(line.target(index), pair)

        def tile(place, carry):
            there = span(place, 512)
            scatter.term[index % scatter.slots, :, there] = dot(qkv_grad[here, :], weight[there, :], NT).astype(low)
            return carry

        lax.fori_loop(0, depth // 512, tile, 0)
        scatter.share(index).start()

    def step(index, carry):
        def phase(which, carry):
            @pl.when(jnp.logical_and(which == 1, index < chips))
            def _():
                term(index)

            @pl.when(jnp.logical_and(which == 2, index < 2))
            def _():
                lax.fori_loop(index, jnp.where(index == 0, 1, shards), weights, 0)

            @pl.when(jnp.logical_and(which == 2, index == 1))
            def _():
                down.start_plain()

            @pl.when(jnp.logical_and(which == 2, index == 2))
            def _():
                down.join()

            outer = jnp.logical_or(which == 0, which == 3)
            lax.fori_loop(0, jnp.where(outer, chips, 0), scatter.due(index, which == 3), 0)
            return carry

        lax.fori_loop(0, 4, phase, 0)
        return carry

    lax.fori_loop(0, chips + 1, step, 0)
    gains[0:1, :] = jnp.zeros((1, depth), jnp.float32)
    gains[1:2, :] = gain_part[...]

    def norm(here):
        part, grad = norm_back(activations[here, :], gain[...], input_part[here, :])
        input_part[here, :] = part
        gains[0:1, :] += grad

    loads.wait(2)
    results = RowStores(NORM_ROWS, rows // NORM_ROWS, (input_part,), (input_out,), rows_sem)
    by_rows(rows, norm, results)

    gains_tp[line.me] = gains[...]
    for ahead in range(1, size):
        tell_tp(ahead).start()
    for turn in range(shards - 1):
        give(turn).wait_recv()
        grad_qkv[...] += qkv_from[turn].astype(jnp.float32)
    summed = RowStores(columns, 1, (grad_qkv,), (qkv_out,), sum_sem)
    summed.start(0)
    for ahead in range(1, size):
        source = (line.me + ahead) % size
        remote(gains, gains_tp.at[source], tp_send.at[0], tp_recv.at[source], {"tp": source}).wait_recv()
    total = gains_tp[0]
    for source in range(1, size):
        total = total + gains_tp[source]
    for ahead in range(1, size):
        tell_tp(ahead).wait_send()
    gains[...] = total
    gains_fsdp[shard] = total
    for ahead in range(1, shards):
        tell_fsdp(ahead).start()
    for ahead in range(1, shards):
        source = (shard + ahead) % shards
        remote(gains, gains_fsdp.at[source], fsdp_send.at[0], fsdp_recv.at[source], {"fsdp": source}).wait_recv()
    total = gains_fsdp[0]
    for source in range(1, shards):
        total = total + gains_fsdp[source]
    gain_sum[...] = total
    for ahead in range(1, shards):
        tell_fsdp(ahead).wait_send()
    for turn in range(shards - 1):
        give(turn).wait_send()
    down.finish()
    results.wait()
    summed.wait()
    scatter.finish()


def spread(chips, shards, qkv_grad, weight, activations, gain, gain_part, attn_tokens, grad_down):
    group_rows = qkv_grad.shape[0]
    rows, depth = activations.shape
    width = qkv_grad.shape[1] // 3
    columns = depth // shards
    size = 2 * chips
    shape = jax.ShapeDtypeStruct
    stored = [shape((rows, depth), jnp.float32), shape((columns, 3 * width), jnp.float32)]
    return pl.pallas_call(
        lambda *refs: spread_kernel(chips, shards, *refs),
        in_specs=[VMEM] * 2 + [ANYWHERE] * 5,
        out_specs=[ANYWHERE] * 2 + [VMEM, ANYWHERE],
        out_shape=stored + [
            shape((2, depth), jnp.float32),
            shape((shards // 2, grad_down.shape[0], columns), low),
        ],
        scratch_shapes=RowStores.scratch(NORM_ROWS, rows // NORM_ROWS, stored[0]) + RowStores.scratch(columns, 1, stored[1]) + Loads.scratch(qkv_grad, weight, activations) + [
            pltpu.VMEM((2, group_rows, columns), low),
            pltpu.VMEM((shards - 1, columns, 3 * width), low),
            pltpu.VMEM((shards - 1, columns, 3 * width), low),
            pltpu.VMEM((2, depth), jnp.float32),
            pltpu.VMEM((size, 2, depth), jnp.float32),
            pltpu.VMEM((shards, 2, depth), jnp.float32),
            DMA((2,)), DMA((shards - 1,)), DMA((shards - 1,)),
            DMA((size - 1,)), DMA((size,)), DMA((shards - 1,)), DMA((shards,)),
        ] + NearSums.scratch(shards, grad_down.shape[0], columns) + Scatter.scratch(chips, rows, depth),
        compiler_params=pltpu.CompilerParams(collective_id=5, has_side_effects=True, vmem_limit_bytes=63 << 20),
        cost_estimate=pl.CostEstimate(flops=1 << 20, bytes_accessed=1 << 20, transcendentals=0),
        name="spread",
    )(gain, gain_part, qkv_grad, weight, activations, attn_tokens, grad_down)


def chip_at(place, chips):
    return jnp.where(2 * place < chips, 2 * place, 2 * (chips - 1 - place) + 1)


def place_of(chip, chips):
    return jnp.where(chip % 2 == 0, chip // 2, chips - 1 - chip // 2)


def feed_kernel(
    chips, shards,
    gain, hidden_hbm, cotangent_hbm, tokens, grads_hbm, w_gate, w_up, w_down, gate_all, up_all, down_near, down_far,
    hidden_grad_out, branch_out, gain_part, inner_out, grad_both, down_out,
    hidden_grad, branch, rows_sem, hidden_state, cotangent, state_sem, down_tile, down_sem, tokens_all, gate_w, up_w, down_w, grads, inner, gate_grad, up_grad, term, from_core, from_ring, total, tile_gate, tile_up,
    load_sem, own_sem, grad_sem, store_sem, tile_sem,
    ring_send, ring_recv, core_send, core_recv, share_send, share_recv, total_send, total_recv,
):
    rows, depth = hidden_grad.shape
    pair = 2 * rows
    width = gate_w.shape[1]
    me = lax.axis_index("tp")
    chip, core = me // 2, me % 2
    place = place_of(chip, chips)
    following = {"tp": 2 * chip_at((place + 1) % chips, chips) + core}
    before = {"tp": 2 * chip_at((place + chips - 1) % chips, chips) + core}
    partner = {"tp": 2 * chip + 1 - core}

    grid = Grid(shards)
    part = w_gate.shape[0]

    def load(array, source, shard, tile, whole):
        cut = span(tile, 256)
        if array == 2:
            place = lambda ref: ref.at[cut, span(shard, part)]
            own = lambda ref: ref.at[cut]
        else:
            place = lambda ref: ref.at[span(shard, part), cut]
            own = lambda ref: ref.at[:, cut]
        target = place((gate_w, up_w, down_w)[array])
        return pltpu.make_async_copy(place(source) if whole else own(source), target, load_sem.at[array, shard, tile])

    def load_weights(tile, carry):
        for shard in range(shards):
            own, near = grid.me == shard, grid.is_near(shard)

            @pl.when(own)
            def _():
                for array, source in enumerate((w_gate, w_up, w_down)):
                    load(array, source, shard, tile, False).start()

            @pl.when(jnp.logical_not(own))
            def _():
                for array, source in enumerate((gate_all, up_all)):
                    load(array, source, shard, tile, True).start()

            @pl.when(jnp.logical_and(near, jnp.logical_not(own)))
            def _():
                load(2, down_near, shard, tile, True).start()

            @pl.when(jnp.logical_not(near))
            def _():
                load(2, down_far, shard, tile, True).start()

        return carry

    own = pltpu.make_async_copy(tokens, tokens_all.at[span(me, rows)], own_sem)
    states = Loads((hidden_hbm, cotangent_hbm), (hidden_state, cotangent, state_sem))

    def source(slot):
        return chip_at((place + chips - slot) % chips, chips)

    def fetch(slot):
        return pltpu.make_async_copy(grads_hbm.at[span(source(slot), pair)], grads.at[slot % 2], grad_sem.at[slot % 2])

    def block(slot):
        return tokens_all.at[span(2 * source(slot) + core, rows)]

    def to_ring(slot):
        return remote(block(slot), block(slot), ring_send.at[slot], ring_recv.at[slot], following)

    def to_core(slot):
        return remote(block(slot), block(slot), core_send.at[slot], core_recv.at[slot], partner)

    def store(slot):
        return pltpu.make_async_copy(inner.at[slot], inner_out.at[span(source(slot), pair)], store_sem.at[slot])

    def keep_down(slot, tile):
        there = down_out.at[span(source(slot), pair), span(tile, 256)]
        return pltpu.make_async_copy(down_tile.at[tile % 2], there, down_sem.at[tile % 2])

    def down_term(slot, carry):
        def tile(index, carry):
            @pl.when(index > 1)
            def _():
                keep_down(slot, index - 2).wait()

            down_tile[index % 2] = dot(inner[slot], down_w[:, span(index, 256)]).astype(low)
            keep_down(slot, index).start()
            return carry

        lax.fori_loop(0, depth // 256, tile, 0)
        for index in range(depth // 256 - 2, depth // 256):
            keep_down(slot, index).wait()
        return carry

    def share(slot):
        place = jnp.where(slot == 0, 0, 1 + slot % 2)
        return remote(term.at[span(1 - core, rows)], from_core.at[place], share_send, share_recv.at[place], partner)

    def pass_on(slot):
        return remote(total.at[slot % 2], from_ring.at[slot - 1], total_send.at[slot % 2], total_recv.at[slot - 1], following)

    for device in (following, before, partner):
        hello(device)
    own.start()
    fetch(0).start()
    lax.fori_loop(0, width // 256, load_weights, 0)
    own.wait()
    pl.semaphore_wait(pltpu.get_barrier_semaphore(), 3)

    def step(slot, carry):
        here = slot % 2
        wide_rows = span(source(slot), pair)
        mine = span(core, rows)

        @pl.when(slot > 0)
        def _():
            to_ring(slot - 1).wait_recv()

        @pl.when(slot < chips - 1)
        def _():
            to_ring(slot).start()
            fetch(slot + 1).start()

        to_core(slot).start()

        @pl.when(slot == 1)
        def _():
            states.start()

        to_core(slot).wait_recv()
        fetch(slot).wait()

        def narrow(tile, carry):
            columns = span(tile, 256)

            @pl.when(slot == 0)
            def _():
                for shard in range(shards):
                    for array, source in enumerate((gate_all, up_all, down_near)):
                        load(array, source, shard, tile, True).wait()

            token = tokens_all[wide_rows, :]
            gate = dot(token, gate_w[:, columns])
            up = dot(token, up_w[:, columns])
            grad = dot(grads[here], down_w[columns, :], NT)
            squash = jax.nn.sigmoid(gate)
            act = gate * squash
            inner[slot, :, columns] = (act * up).astype(low)
            up_grad[wide_rows, columns] = (grad * act).astype(low)
            gate_grad[wide_rows, columns] = (grad * up * squash * (1.0 + gate * (1.0 - squash))).astype(low)
            return carry

        lax.fori_loop(0, width // 256, narrow, 0, unroll=2)
        store(slot).start()

        @pl.when(slot > 0)
        def _():
            share(slot - 1).wait_send()

        def wide(tile, carry):
            columns = span(tile, 256)
            part = dot(gate_grad[wide_rows, :], gate_w[columns, :], NT) + dot(up_grad[wide_rows, :], up_w[columns, :], NT)
            term[:, columns] = part.astype(low)
            return carry

        lax.fori_loop(0, depth // 256, wide, 0)
        share(slot).start()

        @pl.when(slot == 0)
        def _():
            hidden_grad[...] = term[mine, :].astype(jnp.float32)

        middle = jnp.logical_and(slot >= 2, slot < chips - 1)
        lax.fori_loop(jnp.where(slot == 2, 0, slot), jnp.where(middle, slot + 1, 0), down_term, 0)

        @pl.when(slot > 0)
        def _():
            share(slot).wait_recv()

            @pl.when(slot > 2)
            def _():
                pass_on(slot - 2).wait_send()

            @pl.when(slot == 1)
            def _():
                total[here] = (term[mine, :].astype(jnp.float32) + from_core[1 + here].astype(jnp.float32)).astype(low)

            @pl.when(slot > 1)
            def _():
                pass_on(slot - 1).wait_recv()
                total[here] = (term[mine, :].astype(jnp.float32) + from_core[1 + here].astype(jnp.float32) + from_ring[slot - 2].astype(jnp.float32)).astype(low)

            pass_on(slot).start()

        return carry

    lax.fori_loop(0, chips, step, 0)

    def tiles(index):
        there = span(index, 256)
        return (
            pltpu.make_async_copy(tile_gate.at[index % 2], grad_both.at[there, pl.ds(0, width)], tile_sem.at[0, index % 2]),
            pltpu.make_async_copy(tile_up.at[index % 2], grad_both.at[there, pl.ds(width, width)], tile_sem.at[1, index % 2]),
        )

    def weights(index, carry):
        @pl.when(index > 1)
        def _():
            for copy in tiles(index - 2):
                copy.wait()

        token = tokens_all[:, span(index, 256)]
        tile_gate[index % 2] = dot(token, gate_grad[...], TN).astype(low)
        tile_up[index % 2] = dot(token, up_grad[...], TN).astype(low)
        for copy in tiles(index):
            copy.start()
        return carry

    lax.fori_loop(0 if chips < 4 else chips - 1, chips, down_term, 0)
    lax.fori_loop(0, depth // 256, weights, 0)
    states.wait(0, 1)
    share(0).wait_recv()
    pass_on(chips - 1).wait_recv()
    gain_part[...] = jnp.zeros_like(gain_part)

    def norm(here):
        grad = hidden_grad[here, :] + from_core[0, here, :].astype(jnp.float32) + from_ring[chips - 2, here, :].astype(jnp.float32)
        part, gain_grad = norm_back(hidden_state[here, :], gain[...], grad)
        full = cotangent[here, :] + part
        hidden_grad[here, :] = full
        branch[here, :] = full.astype(low)
        gain_part[...] += gain_grad

    results = RowStores(NORM_ROWS, rows // NORM_ROWS, (hidden_grad, branch), (hidden_grad_out, branch_out), rows_sem)
    by_rows(rows, norm, results)
    share(chips - 1).wait_send()
    for slot in range(chips):
        to_core(slot).wait_send()
        if slot < chips - 1:
            to_ring(slot).wait_send()
        if slot >= max(1, chips - 2):
            pass_on(slot).wait_send()
        store(slot).wait()
    for index in range(depth // 256 - 2, depth // 256):
        for copy in tiles(index):
            copy.wait()
    results.wait()


def feed(chips, shards, hidden_state, cotangent, gain, tokens, grads, w_gate, w_up, w_down, gate_all, up_all, down_near, down_far):
    rows, depth = tokens.shape
    pair = 2 * rows
    group_rows = chips * pair
    width = w_down.shape[0]
    shape = jax.ShapeDtypeStruct
    stored = [shape((rows, depth), jnp.float32), shape((rows, depth), low)]
    return pl.pallas_call(
        lambda *refs: feed_kernel(chips, shards, *refs),
        in_specs=[VMEM] + [ANYWHERE] * 11,
        out_specs=[ANYWHERE] * 2 + [VMEM] + [ANYWHERE] * 3,
        out_shape=stored + [
            shape((1, depth), jnp.float32),
            shape((group_rows, width), low),
            shape((depth, 2 * width), low),
            shape((group_rows, depth), low),
        ],
        scratch_shapes=RowStores.scratch(NORM_ROWS, rows // NORM_ROWS, *stored) + Loads.scratch(hidden_state, cotangent) + [
            pltpu.VMEM((2, pair, 256), low),
            DMA((2,)),
            pltpu.VMEM((group_rows, depth), low),
            pltpu.VMEM((depth, width), low),
            pltpu.VMEM((depth, width), low),
            pltpu.VMEM((width, depth), low),
            pltpu.VMEM((2, pair, depth), low),
            pltpu.VMEM((chips, pair, width), low),
            pltpu.VMEM((group_rows, width), low),
            pltpu.VMEM((group_rows, width), low),
            pltpu.VMEM((pair, depth), low),
            pltpu.VMEM((3, rows, depth), low),
            pltpu.VMEM((chips - 1, rows, depth), low),
            pltpu.VMEM((2, rows, depth), low),
            pltpu.VMEM((2, 256, width), low),
            pltpu.VMEM((2, 256, width), low),
            DMA((3, shards, width // 256)), DMA, DMA((2,)), DMA((chips,)), DMA((2, 2)),
            DMA((chips,)), DMA((chips,)), DMA((chips,)), DMA((chips,)),
            DMA, DMA((3,)), DMA((2,)), DMA((chips - 1,)),
        ],
        compiler_params=pltpu.CompilerParams(collective_id=3, has_side_effects=True, vmem_limit_bytes=67043328),
        cost_estimate=pl.CostEstimate(flops=16 * group_rows * depth * width, bytes_accessed=10 * group_rows * depth, transcendentals=group_rows * width),
        name="feed",
    )(gain, hidden_state, cotangent, tokens, grads, w_gate, w_up, w_down, gate_all, up_all, down_near, down_far)


def finish_kernel(
    shard_ref, hidden, down, hidden_grad, input_part, both, both_from, grad_down, down_from, grad_qkv, grad_out, gains,
    output, input_grad, query, key, value, out, gate, up, down_out, gain_attn, gain_mlp,
):
    gain_attn[...] = gains[0:1, :]
    gain_mlp[...] = gains[1:2, :]
    output[...] = hidden[...] + down[...]
    input_grad[...] = hidden_grad[...] + input_part[...]
    width = query.shape[1]
    for part, ref in enumerate((query, key, value)):
        ref[...] = grad_qkv[:, pl.ds(part * width, width)]
    out[...] = grad_out[...]
    wide = gate.shape[1]
    for side, ref in enumerate((gate, up)):
        columns = pl.ds(side * wide, wide)
        total = both[:, columns].astype(jnp.float32)
        for turn in range(both_from.shape[0]):
            total = total + both_from[turn, :, columns].astype(jnp.float32)
        ref[...] = total
    total = grad_down[...].astype(jnp.float32)
    for turn in range(down_from.shape[0]):
        total = total + down_from[turn].astype(jnp.float32)
    down_out[...] = total


def finish(shard, hidden, down, hidden_grad, input_part, both, both_from, grad_down, down_from, grad_qkv, grad_out, gains):
    steps = 8
    shape = jax.ShapeDtypeStruct
    columns = down_from.shape[2]
    results = [shape(hidden.shape, jnp.float32)] * 2
    results += [shape((columns, grad_qkv.shape[1] // 3), jnp.float32)] * 3 + [shape(grad_out.shape, jnp.float32)]
    results += [shape((columns, both.shape[1] // 2), jnp.float32)] * 2 + [shape((grad_down.shape[0], columns), jnp.float32)]
    spec = lambda a: pl.BlockSpec((a.shape[0] // steps, a.shape[1]), lambda i, s: (i, 0))
    spec3 = lambda a: pl.BlockSpec((a.shape[0], a.shape[1] // steps, a.shape[2]), lambda i, s: (0, i, 0))
    return pl.pallas_call(
        finish_kernel,
        grid_spec=pltpu.PrefetchScalarGridSpec(
            num_scalar_prefetch=1,
            grid=(steps,),
            in_specs=[
                spec(hidden), spec(down), spec(hidden_grad), spec(input_part),
                pl.BlockSpec((columns // steps, both.shape[1]), lambda i, s: (s[0] * steps + i, 0)),
                spec3(both_from),
                pl.BlockSpec((grad_down.shape[0] // steps, columns), lambda i, s: (i, s[0])),
                spec3(down_from), spec(grad_qkv), spec(grad_out),
                pl.BlockSpec(gains.shape, lambda i, s: (0, 0)),
            ],
            out_specs=[spec(a) for a in results] + [pl.BlockSpec((1, gains.shape[1]), lambda i, s: (0, 0))] * 2,
        ),
        out_shape=results + [shape((1, gains.shape[1]), jnp.float32)] * 2,
        name="finish",
    )(shard.reshape(1), hidden, down, hidden_grad, input_part, both, both_from, grad_down, down_from, grad_qkv, grad_out, gains)


def rope_frequencies():
    column = np.arange(HEAD_DIM // 2)
    return jnp.asarray((rope_base ** (-2.0 * column / HEAD_DIM)).astype(np.float32)[:, None])


def make_body(mesh):
    chips, shards = mesh.shape["tp"] // 2, mesh.shape["fsdp"]

    def body(activations, gain_attn, w_query, w_key, w_value, w_out, gain_mlp, w_gate, w_up, w_down, cotangent):
        gain_attn, gain_mlp = gain_attn[None, :], gain_mlp[None, :]
        seen_attn, w_qkv, full_out, qkv, keys_t, values_t, cosine, sine, down_near = project(
            chips, shards, activations, gain_attn, w_query, w_key, w_value, w_out, rope_frequencies(), w_down
        )
        hidden_state, normed_mlp, mixed, totals, seen_grad, gate_all, up_all, down_far = attend(
            chips, shards, qkv, values_t, full_out, activations, cotangent, gain_mlp, w_gate, w_up, down_near
        )
        hidden_grad, branch_grad, gain_part, inner, grad_both, terms = feed(
            chips, shards, hidden_state, cotangent, gain_mlp, normed_mlp, seen_grad,
            w_gate, w_up, w_down, gate_all, up_all, down_near, down_far,
        )
        down, _, qkv_grad, grad_down, grad_out, both_from = back(
            chips, shards, branch_grad, terms, inner, seen_grad, grad_both, full_out, qkv, keys_t, mixed, totals, cosine, sine
        )
        input_part, grad_qkv, gain_sums, down_from = spread(
            chips, shards, qkv_grad, w_qkv, activations, gain_attn, gain_part, seen_attn, grad_down
        )
        output, input_grad, grad_query, grad_key, grad_value, grad_out, grad_gate, grad_up, grad_down, gain_attn, gain_mlp = finish(
            lax.axis_index("fsdp"), hidden_state, down, hidden_grad, input_part,
            grad_both, both_from, grad_down, down_from, grad_qkv, grad_out, gain_sums,
        )
        return (
            output, input_grad, gain_attn[0], grad_query, grad_key, grad_value, grad_out, gain_mlp[0],
            grad_gate, grad_up, grad_down,
        )

    return body


def solution(mesh):
    tokens = P(("fsdp", "tp"), None)
    column = P("fsdp", "tp")
    row = P("tp", "fsdp")
    in_specs = (tokens, P(), column, column, column, row, P(), column, column, row, tokens)
    out_specs = (tokens, tokens, P(), column, column, column, row, P(), column, column, row)
    return jax.shard_map(make_body(mesh), mesh=mesh, in_specs=in_specs, out_specs=out_specs, check_vma=False)
```

```python
import jax
import jax.numpy as jnp
import numpy as np
from jax import lax
from jax.experimental import pallas as pl
from jax.experimental.pallas import tpu as pltpu
from jax.sharding import PartitionSpec as P

HEAD_DIM = 64
SEQ_LEN = 2048
LANES = 128
rope_base = 130000.0
norm_eps = 1e-05
masked_score = -1e30

NT = (((1,), (1,)), ((), ()))
NN = (((1,), (0,)), ((), ()))
TN = (((0,), (0,)), ((), ()))
MESH = pl.DeviceIdType.MESH
DMA = pltpu.SemaphoreType.DMA
ANYWHERE = pl.BlockSpec(memory_space=pl.ANY)
VMEM = pl.BlockSpec(memory_space=pltpu.VMEM)
low = jnp.bfloat16


def dot(left, right, dims=NN):
    return lax.dot_general(left, right, dims, preferred_element_type=jnp.float32)


def span(index, size):
    return pl.ds(pl.multiple_of(index * size, size), size)


def remote(source, target, send, receive, device):
    return pltpu.make_async_remote_copy(
        src_ref=source, dst_ref=target, send_sem=send, recv_sem=receive,
        device_id=device, device_id_type=MESH,
    )


def hello(device):
    pl.semaphore_signal(pltpu.get_barrier_semaphore(), inc=1, device_id=device, device_id_type=MESH)


class Line:
    def __init__(self, chips):
        self.chips = chips
        self.me = lax.axis_index("tp")
        self.chip, self.core = self.me // 2, self.me % 2
        self.partner = 2 * self.chip + 1 - self.core
        self.has_left, self.has_right = self.chip > 0, self.chip < chips - 1

    def hello(self, more=()):
        hello({"tp": self.partner})

        @pl.when(self.has_left)
        def _():
            hello({"tp": self.me - 2})

        @pl.when(self.has_right)
        def _():
            hello({"tp": self.me + 2})

        for device in more:
            hello(device)

    def ready(self, more=()):
        count = 1 + len(more) + jnp.where(self.has_left, 1, 0) + jnp.where(self.has_right, 1, 0)
        pl.semaphore_wait(pltpu.get_barrier_semaphore(), count)

    def target(self, step):
        after = self.chips - 1 - self.chip
        most, least = jnp.maximum(self.chip, after), jnp.minimum(self.chip, after)
        sign = jnp.where(after >= self.chip, 1, -1)
        late = step - (most - least)
        side = jnp.where(late % 2 == 0, sign, -sign)
        return jnp.where(late < 0, self.chip + sign * (most - step), self.chip + side * (least - late // 2))


    def fed(self, target):
        after, before = jnp.logical_and(target >= self.chip, self.has_left), jnp.logical_and(target <= self.chip, self.has_right)
        return jnp.logical_or(after, before)


class Gather:
    @staticmethod
    def scratch(chips, parts=1):
        return [DMA((2 * chips, parts)), DMA((chips, parts)), DMA((chips, parts)), DMA((chips, parts)), DMA]

    def __init__(self, line, own, out, received, right, left, across, local, parts=1):
        self.line, self.out = line, out
        self.received, self.right, self.left, self.across, self.local = received, right, left, across, local
        self.parts = parts
        self.rows = out.shape[0] // (2 * line.chips * parts)
        self.held = own is None
        self.own = out.at[span(line.me, self.rows * parts)] if self.held else own

    def block(self, index, part):
        return self.out.at[span(index * self.parts + part, self.rows)]

    def mine(self, part):
        return self.own.at[pl.ds(part * self.rows, self.rows)]

    def copy(self, sems, chip, part, device, mine):
        index = 2 * chip + self.line.core
        source = self.mine(part) if mine else self.block(index, part)
        return remote(source, self.block(index, part), sems.at[chip, part], self.received.at[index, part], {"tp": device})

    def keep(self):
        return pltpu.make_async_copy(self.own, self.out.at[span(self.line.me, self.rows * self.parts)], self.local)

    def start(self):
        line = self.line
        if not self.held:
            self.keep().start()
        for part in range(self.parts):
            @pl.when(line.has_right)
            def _():
                self.copy(self.right, line.chip, part, line.me + 2, True).start()

            @pl.when(line.has_left)
            def _():
                self.copy(self.left, line.chip, part, line.me - 2, True).start()

            self.copy(self.across, line.chip, part, line.partner, True).start()

    def arrive(self, index, part):
        remote(self.mine(part), self.block(index, part), self.right.at[0, part], self.received.at[index, part], {"tp": self.line.partner}).wait_recv()

    def arrive_across(self, chip):
        for part in range(self.parts):
            self.arrive(2 * chip + 1 - self.line.core, part)

    def step(self, distance):
        line = self.line
        before, after = line.chip - distance, line.chip + distance
        for part in range(self.parts):
            @pl.when(before >= 0)
            def _():
                self.arrive(2 * before + line.core, part)

                @pl.when(line.has_right)
                def _():
                    self.copy(self.right, before, part, line.me + 2, False).start()

                self.copy(self.across, before, part, line.partner, False).start()

            @pl.when(after < line.chips)
            def _():
                self.arrive(2 * after + line.core, part)

                @pl.when(line.has_left)
                def _():
                    self.copy(self.left, after, part, line.me - 2, False).start()

                self.copy(self.across, after, part, line.partner, False).start()

    def finish(self, arrivals):
        line = self.line
        if arrivals:
            self.keep().wait()
        for chip in range(line.chips):
            if arrivals:
                self.arrive_across(chip)
            for part in range(self.parts):
                self.copy(self.across, chip, part, line.partner, True).wait_send()

                @pl.when(jnp.logical_and(line.has_right, chip <= line.chip))
                def _():
                    self.copy(self.right, chip, part, line.me + 2, True).wait_send()

                @pl.when(jnp.logical_and(line.has_left, chip >= line.chip))
                def _():
                    self.copy(self.left, chip, part, line.me - 2, True).wait_send()


class Scatter:
    @staticmethod
    def scratch(chips, rows, depth):
        slots = chips // 2 + 1
        return [
            pltpu.VMEM((slots, 2 * rows, depth), low),
            pltpu.VMEM((chips, rows, depth), low),
            pltpu.VMEM((chips + 1, rows, depth), low),
            pltpu.VMEM((2, rows, depth), low),
            DMA((slots,)), DMA((chips,)), DMA((2,)), DMA((chips + 1,)),
        ]

    def __init__(self, line, out, term, shares, lines, total, share_send, share_recv, line_send, line_recv):
        self.line, self.out = line, out
        self.term, self.shares, self.lines, self.total = term, shares, lines, total
        self.share_send, self.share_recv, self.line_send, self.line_recv = share_send, share_recv, line_send, line_recv
        self.rows = out.shape[0]
        self.slots = term.shape[0]

    def share(self, step):
        slot = step % self.slots
        source = self.term.at[slot, span(1 - self.line.core, self.rows)]
        return remote(source, self.shares.at[step], self.share_send.at[slot], self.share_recv.at[step], {"tp": self.line.partner})

    def due(self, index, fed):
        def one(step, carry):
            target = self.line.target(step)
            distance = jnp.where(target > self.line.chip, target - self.line.chip, self.line.chip - target)
            turn = True if fed is None else self.line.fed(target) == fed

            @pl.when(jnp.logical_and(distance == self.line.chips - index, turn))
            def _():
                self.step(step)

            return carry

        return one

    def mine(self, step):
        return self.term[step % self.slots, span(self.line.core, self.rows), :]

    def pass_on(self, step):
        line, target = self.line, self.line.target(step)
        onward = target > line.chip
        slot = jnp.where(onward, target, jnp.where(target == line.chip - 1, line.chips, target))
        device = jnp.where(onward, line.me + 2, line.me - 2)
        return remote(self.total.at[step % 2], self.lines.at[slot], self.line_send.at[step % 2], self.line_recv.at[slot], {"tp": device})

    def add(self, slot):
        remote(self.total.at[0], self.lines.at[slot], self.line_send.at[0], self.line_recv.at[slot], {"tp": self.line.partner}).wait_recv()
        self.out[...] += self.lines[slot].astype(jnp.float32)

    def free(self, step):
        @pl.when(step >= self.slots)
        def _():
            self.share(step - self.slots).wait_send()

    def step(self, step):
        line, target = self.line, self.line.target(step)
        self.share(step).wait_recv()
        self.out[...] = self.mine(step).astype(jnp.float32) + self.shares[step].astype(jnp.float32)

        @pl.when(jnp.logical_and(target >= line.chip, line.has_left))
        def _():
            self.add(target)

        @pl.when(jnp.logical_and(target <= line.chip, line.has_right))
        def _():
            self.add(jnp.where(target == line.chip, line.chips, target))

        @pl.when(step < line.chips - 1)
        def _():
            @pl.when(step >= 2)
            def _():
                self.pass_on(step - 2).wait_send()

            self.total[step % 2] = self.out[...].astype(low)
            self.pass_on(step).start()

    def finish(self):
        chips = self.line.chips
        for step in range(max(0, chips - 3), chips - 1):
            self.pass_on(step).wait_send()
        for step in range(max(0, chips - self.slots), chips):
            self.share(step).wait_send()


NORM_ROWS = 64


def normed(value, gain):
    return value * lax.rsqrt(jnp.mean(value * value, axis=-1, keepdims=True) + norm_eps) * gain


def norm_back(value, gain, grad):
    scale = lax.rsqrt(jnp.mean(value * value, axis=-1, keepdims=True) + norm_eps)
    unit = value * scale
    scaled = grad * gain
    return scale * (scaled - unit * jnp.mean(scaled * unit, axis=-1, keepdims=True)), jnp.sum(grad * unit, axis=0, keepdims=True)


def by_rows(rows, work, stores=None):
    def step(index, carry):
        work(span(index, NORM_ROWS))
        if stores:
            stores.start(index)
        return carry

    lax.fori_loop(0, rows // NORM_ROWS, step, 0)


class Grid:
    def __init__(self, shards):
        self.shards, self.across = shards, shards // 2
        self.me = lax.axis_index("fsdp")
        self.row, self.column = self.me // self.across, self.me % self.across
        self.others = [(self.me + ahead) % shards for ahead in range(1, shards)]
        self.mates = [self.row * self.across + (self.column + ahead) % self.across for ahead in range(1, self.across)]
        self.twin = (1 - self.row) * self.across + self.column
        self.near = self.mates + [self.twin]

    def is_near(self, shard):
        return jnp.logical_or(shard // self.across == self.row, shard % self.across == self.column)


class NearShards:
    scratch = staticmethod(lambda shards: [DMA((shards // 2,)), DMA((shards // 2,))])

    def __init__(self, grid, own, whole, at, send, receive):
        place = at(whole, grid.me, None)
        self.copies = [remote(own, place, send.at[i], receive.at[i], {"fsdp": peer}) for i, peer in enumerate(grid.near)]

    def start(self):
        for copy in self.copies:
            copy.start()

    def arrive(self):
        for copy in self.copies:
            copy.wait_recv()

    def finish(self):
        for copy in self.copies:
            copy.wait_send()


class FarShards:
    scratch = staticmethod(lambda shards: [DMA((2, shards // 2 - 1)), DMA((2, shards // 2 - 1))])

    def __init__(self, grid, near, whole, at, send, receive):
        self.copies = []
        for i, mate in enumerate(grid.mates):
            self.copies.append(remote(at(near, mate, 0), at(whole, mate, 0), send.at[0, i], receive.at[0, i], {"fsdp": grid.twin}))
            self.copies.append(remote(at(near, grid.twin, 1), at(whole, grid.twin, 1), send.at[1, i], receive.at[1, i], {"fsdp": mate}))

    def start(self):
        for copy in self.copies:
            copy.start()

    def finish(self):
        for copy in self.copies:
            copy.wait_recv()
            copy.wait_send()


class NearSums:
    @staticmethod
    def scratch(shards, rows, columns):
        across = shards // 2
        return [
            pltpu.VMEM((2, across - 1, rows // 2, columns), low),
            pltpu.VMEM((across, rows // 2, columns), low),
            DMA((2, across - 1)), DMA((2, across - 1)), DMA((across, 2)), DMA((across, 2)), DMA((across,)),
        ]

    def __init__(self, grid, part, out, at, relay, base, relay_send, relay_recv, near_send, near_recv, load_sem):
        self.relay, self.base = relay, base
        last = grid.across - 1
        half = base.shape[1]

        def near(source, slot, which, peer):
            target = out.at[slot, pl.ds(which * half, half)]
            return remote(source, target, near_send.at[slot, which], near_recv.at[slot, which], {"fsdp": peer})

        self.by_twin, self.by_mate, self.plain, self.joined, self.loads = [], [], [], [], []
        for i, mate in enumerate(grid.mates):
            far = (1 - grid.row) * grid.across + mate % grid.across
            self.by_twin.append(remote(at(part, far, 0), relay.at[0, i], relay_send.at[0, i], relay_recv.at[0, i], {"fsdp": grid.twin}))
            self.by_mate.append(remote(at(part, far, 1), relay.at[1, i], relay_send.at[1, i], relay_recv.at[1, i], {"fsdp": mate}))
            self.plain.append(near(at(part, mate, 1), i, 1, mate))
            self.joined.append(near(relay.at[0, i], i, 0, mate))
            self.loads.append(pltpu.make_async_copy(at(part, mate, 0), base.at[i], load_sem.at[i]))
        self.plain.append(near(at(part, grid.twin, 0), last, 0, grid.twin))
        self.joined.append(near(relay.at[1, 0], last, 1, grid.twin))
        self.loads.append(pltpu.make_async_copy(at(part, grid.twin, 1), base.at[last], load_sem.at[last]))

    def start(self):
        for copy in self.by_twin + self.by_mate + self.loads:
            copy.start()

    def start_plain(self):
        for copy in self.plain:
            copy.start()

    def join(self):
        for copy in self.by_twin + self.by_mate:
            copy.wait_recv()
        for copy in self.loads:
            copy.wait()
        last = self.base.shape[0] - 1
        for i in range(last):
            self.relay[0, i] = (self.base[i].astype(jnp.float32) + self.relay[0, i].astype(jnp.float32)).astype(low)
        total = self.base[last].astype(jnp.float32)
        for i in range(last):
            total = total + self.relay[1, i].astype(jnp.float32)
        self.relay[1, 0] = total.astype(low)
        for copy in self.joined:
            copy.start()

    def finish(self):
        for copy in self.by_twin + self.by_mate:
            copy.wait_send()
        for copy in self.plain + self.joined:
            copy.wait_recv()
            copy.wait_send()


def row_shard(depth):
    def at(ref, shard, half):
        if half is None:
            return ref.at[span(shard, depth)]
        return ref.at[span(2 * shard + half, depth // 2)]

    return at


def column_shard(rows, width):
    def at(ref, shard, half):
        if half is None:
            return ref.at[:, span(shard, width)]
        return ref.at[pl.ds(half * (rows // 2), rows // 2), span(shard, width)]

    return at


class HeldScatter(Scatter):
    @staticmethod
    def scratch(chips, rows, depth):
        return [
            pltpu.VMEM((2, rows, depth), low),
            pltpu.VMEM((chips, rows, depth), low),
            pltpu.VMEM((chips + 1, rows, depth), low),
            pltpu.VMEM((2, rows, depth), low),
            DMA((2,)), DMA((chips,)), DMA((2,)), DMA((chips + 1,)), DMA((2,)),
        ]

    def __init__(self, line, out, held, *refs):
        super().__init__(line, out, *refs[:-1])
        self.held, self.load_sem = held, refs[-1]

    def load(self, step):
        source = self.held.at[span(2 * self.line.target(step) + self.line.core, self.rows)]
        return pltpu.make_async_copy(source, self.term.at[step % 2], self.load_sem.at[step % 2])

    def share(self, step):
        source = self.held.at[span(2 * self.line.target(step) + 1 - self.line.core, self.rows)]
        return remote(source, self.shares.at[step], self.share_send.at[step % 2], self.share_recv.at[step], {"tp": self.line.partner})

    def mine(self, step):
        self.load(step).wait()

        @pl.when(step < self.line.chips - 1)
        def _():
            self.load(step + 1).start()

        return self.term[step % 2]


class Loads:
    @staticmethod
    def scratch(*operands):
        return [pltpu.VMEM(a.shape, a.dtype) for a in operands] + [DMA((len(operands),))]

    def __init__(self, sources, refs):
        self.refs = refs[: len(sources)]
        self.copies = [pltpu.make_async_copy(source, ref, refs[-1].at[i]) for i, (source, ref) in enumerate(zip(sources, self.refs))]

    def start(self):
        for copy in self.copies:
            copy.start()

    def wait(self, *which):
        for i in which:
            self.copies[i].wait()


class RowStores:
    @staticmethod
    def scratch(size, count, *results):
        return [pltpu.VMEM(a.shape, a.dtype) for a in results] + [DMA((len(results), count))]

    def __init__(self, size, count, refs, outs, sems):
        self.size, self.count, self.refs, self.outs, self.sems = size, count, refs, outs, sems

    def copies(self, index):
        here = span(index, self.size)
        return [pltpu.make_async_copy(a.at[here], b.at[here], self.sems.at[i, index]) for i, (a, b) in enumerate(zip(self.refs, self.outs))]

    def start(self, index):
        for copy in self.copies(index):
            copy.start()

    def wait(self):
        for index in range(self.count):
            for copy in self.copies(index):
                copy.wait()


def turned(block, sign):
    half = HEAD_DIM // 2
    lane = lax.broadcasted_iota(jnp.int32, block.shape, 1)
    width = block.shape[1]
    up = pltpu.roll(block, width - half, 1)
    down = pltpu.roll(block, half, 1)
    return jnp.where(lane % HEAD_DIM < half, -sign * up, sign * down)


def widened(table, width):
    return table if table.shape[1] == width else jnp.concatenate([table] * (width // table.shape[1]), axis=1)


def only_head(block, head):
    lane = lax.broadcasted_iota(jnp.int32, block.shape, 1)
    return jnp.where(lane // HEAD_DIM == head, block, jnp.zeros_like(block))


def causal(tile):
    key = lax.broadcasted_iota(jnp.int32, tile.shape, 0)
    query = lax.broadcasted_iota(jnp.int32, tile.shape, 1)
    return jnp.where(key <= query, tile, masked_score)


def over_keys(chunk, rows, visit):
    start = chunk * rows
    first = start // SEQ_LEN * SEQ_LEN

    def step(index, carry):
        visit(pl.multiple_of(first + index * rows, rows), False)
        return carry

    lax.fori_loop(0, (start - first) // rows, step, 0)
    visit(pl.multiple_of(start, rows), True)


def project_kernel(
    chips, shards,
    gain, inverse, activations_hbm, w_query, w_key, w_value, w_out, w_down,
    tokens_out, weight_out, full_out, qkv_out, keys_out, values_out, cosine_out, sine_out, down_near,
    weight, out_w, qkv, keys_t, values_t, cosine, sine, tokens, activations,
    load_sem, weight_send, weight_recv, weight_keep, table_sem, store_sem, near_send, near_recv, *gather_sems,
):
    line = Line(chips)
    rows = activations.shape[0]
    depth, width = w_query.shape
    grid = Grid(shards)
    shard, others = grid.me, grid.others
    gather = Gather(line, None, tokens, *gather_sems, parts=2)
    down = NearShards(grid, w_down, down_near, column_shard(*w_down.shape), near_send, near_recv)
    parts = (w_query, w_key, w_value, w_out)

    def place(part):
        if part == 3:
            return out_w.at[:, span(shard, depth)]
        return weight.at[span(shard, depth), pl.ds(part * width, width)]

    def give(ahead, part):
        return remote(parts[part], place(part), weight_send.at[ahead, part], weight_recv.at[ahead, part], {"fsdp": others[ahead]})

    def keep(part):
        return pltpu.make_async_copy(parts[part], place(part), weight_keep.at[part])

    tables = [
        pltpu.make_async_copy(source, out, table_sem.at[i])
        for i, (source, out) in enumerate(((cosine, cosine_out), (sine, sine_out), (weight, weight_out), (out_w, full_out)))
    ]

    def stores(index):
        here = span(index, rows)
        return [
            pltpu.make_async_copy(qkv.at[here], qkv_out.at[here], store_sem.at[0, index]),
            pltpu.make_async_copy(keys_t.at[:, here], keys_out.at[:, here], store_sem.at[1, index]),
            pltpu.make_async_copy(values_t.at[:, here], values_out.at[:, here], store_sem.at[2, index]),
            pltpu.make_async_copy(tokens.at[here], tokens_out.at[here], store_sem.at[3, index]),
        ]

    def norm(index, carry):
        there = span(line.me * (rows // NORM_ROWS) + index, NORM_ROWS)
        tokens[there, :] = normed(activations[span(index, NORM_ROWS), :], gain[...]).astype(low)
        return carry

    load = pltpu.make_async_copy(activations_hbm, activations, load_sem)
    load.start()
    line.hello([{"fsdp": other} for other in others])
    load.wait()
    lax.fori_loop(0, rows // NORM_ROWS, norm, 0)
    line.ready(others)
    gather.start()
    for part in range(4):
        keep(part).start()
        for ahead in range(shards - 1):
            give(ahead, part).start()
    position = lax.broadcasted_iota(jnp.int32, (inverse.shape[0], SEQ_LEN), 1).astype(jnp.float32)
    angle = position * inverse[...]
    for table, turn in ((cosine, jnp.cos(angle).T), (sine, jnp.sin(angle).T)):
        table[...] = jnp.concatenate([turn] * (LANES // turn.shape[1]), axis=1)
    for copy in tables[:2]:
        copy.start()

    def project(index):
        here = span(index, rows)
        table = span(index % (SEQ_LEN // rows), rows)
        for part in range(3):
            columns = pl.ds(part * width, width)
            block = dot(tokens[here, :], weight[:, columns])
            if part < 2:
                block = block * widened(cosine[table, :], width) + turned(block, 1.0) * widened(sine[table, :], width)
            qkv[here, columns] = block.astype(low)
            if part:
                (keys_t, values_t)[part - 1][:, here] = block.T.astype(low)
        for copy in stores(index):
            copy.start()

    def step(index, carry):
        @pl.when(jnp.logical_and(index >= 1, index < chips))
        def _():
            gather.step(index)

        @pl.when(index == 2)
        def _():
            for part in range(4):
                keep(part).wait()
                for ahead in range(shards - 1):
                    give(ahead, part).wait_recv()
            for copy in tables[2:]:
                copy.start()
            down.start()

        def side(turn, carry):
            distance, which, across = index - 1, turn % 3, turn // 3
            chip = jnp.where(which == 0, line.chip - distance, jnp.where(which == 1, line.chip + distance, line.chip))
            there = jnp.logical_and(chip >= 0, chip < chips)

            @pl.when(jnp.logical_and(there, jnp.logical_and(index >= 2, jnp.logical_or(which < 2, index == 2))))
            def _():
                @pl.when(across == 1)
                def _():
                    gather.arrive_across(chip)

                project(2 * chip + jnp.where(across == 1, 1 - line.core, line.core))

            return carry

        lax.fori_loop(0, 6, side, 0)
        return carry

    lax.fori_loop(0, chips + 1, step, 0)
    gather.finish(False)
    for part in range(4):
        for ahead in range(shards - 1):
            give(ahead, part).wait_send()
    for copy in tables:
        copy.wait()
    for index in range(2 * chips):
        for copy in stores(index):
            copy.wait()
    down.arrive()
    down.finish()


def project(chips, shards, activations, gain, w_query, w_key, w_value, w_out, inverse, w_down):
    rows, depth = activations.shape
    group_rows = 2 * chips * rows
    width = w_query.shape[1]
    shape = jax.ShapeDtypeStruct
    held = [
        shape((depth, 3 * width), low),
        shape((width, depth), low),
        shape((group_rows, 3 * width), low),
        shape((width, group_rows), low),
        shape((width, group_rows), low),
        shape((SEQ_LEN, LANES), jnp.float32),
        shape((SEQ_LEN, LANES), jnp.float32),
    ]
    return pl.pallas_call(
        lambda *refs: project_kernel(chips, shards, *refs),
        in_specs=[VMEM] * 2 + [ANYWHERE] * 6,
        out_specs=[ANYWHERE] * 9,
        out_shape=[shape((group_rows, depth), low)] + held + [shape((w_down.shape[0], depth), low)],
        scratch_shapes=[pltpu.VMEM(a.shape, a.dtype) for a in held] + [
            pltpu.VMEM((group_rows, depth), low),
            pltpu.VMEM((rows, depth), jnp.float32),
            DMA, DMA((shards - 1, 4)), DMA((shards - 1, 4)), DMA((4,)), DMA((4,)), DMA((4, 2 * chips)),
        ] + NearShards.scratch(shards) + Gather.scratch(chips, 2),
        compiler_params=pltpu.CompilerParams(collective_id=1, has_side_effects=True, vmem_limit_bytes=63 << 20),
        cost_estimate=pl.CostEstimate(flops=6 * group_rows * depth * width, bytes_accessed=4 * group_rows * depth, transcendentals=0),
        name="project",
    )(gain, inverse, activations, w_query, w_key, w_value, w_out, w_down)


def attend_chunk(chunk, rows, qkv, values_t, heads_ref, acc, out, top_ref, sum_ref):
    width = acc.shape[0]
    heads = width // HEAD_DIM
    scaled = qkv[span(chunk, rows), pl.ds(0, width)] * low(HEAD_DIM**-0.5)
    for head in range(heads):
        heads_ref[head] = only_head(scaled, head)
    acc[...] = jnp.zeros_like(acc)
    top_ref[...] = jnp.full_like(top_ref, masked_score)
    sum_ref[...] = jnp.zeros_like(sum_ref)

    def visit(offset, diagonal):
        key_block = qkv[pl.ds(offset, rows), pl.ds(width, width)]
        for head in range(heads):
            feature = pl.ds(head * HEAD_DIM, HEAD_DIM)
            one = pl.ds(head, 1)
            scores = dot(key_block, heads_ref[head], NT)
            if diagonal:
                scores = causal(scores)
            old = top_ref[one, :]
            top = jnp.maximum(old, jnp.max(scores, axis=0, keepdims=True))
            shrink = jnp.exp(old - top)
            weights = jnp.exp(scores - top)
            top_ref[one, :] = top
            sum_ref[one, :] = sum_ref[one, :] * shrink + jnp.sum(weights, axis=0, keepdims=True)
            acc[feature, :] = acc[feature, :] * shrink + dot(values_t[feature, pl.ds(offset, rows)], weights.astype(low))

    over_keys(chunk, rows, visit)
    for head in range(heads):
        feature = pl.ds(head * HEAD_DIM, HEAD_DIM)
        acc[feature, :] = acc[feature, :] / sum_ref[pl.ds(head, 1), :]
    out[...] = acc[...].T.astype(low)


def attend_kernel(
    chips, shards,
    gain, *refs,
):
    sources, (w_gate, w_up, down_near) = refs[:5], refs[5:8]
    hidden_out, tokens_out, mixed_out, totals, grads_out, gate_all, up_all, down_far = refs[8:16]
    hidden, tokens, rows_sem, mixed, mixed_sem = refs[-5:]
    refs = refs[:-5]
    loads = Loads(sources, refs[16:22])
    cotangent, qkv, values_t, w_out, activations = loads.refs
    heads_ref, acc, out, top_ref, sum_ref, grads = refs[22:28]
    loads.start()
    line = Line(chips)
    grid = Grid(shards)
    rows_of = row_shard(w_gate.shape[0])
    line.hello([{"fsdp": peer} for peer in grid.near])
    down = FarShards(grid, down_near, down_far, column_shard(down_near.shape[0], down_near.shape[1] // shards), *refs[28:30])
    gate_near, gate_far = NearShards(grid, w_gate, gate_all, rows_of, *refs[30:32]), FarShards(grid, gate_all, gate_all, rows_of, *refs[32:34])
    up_near, up_far = NearShards(grid, w_up, up_all, rows_of, *refs[34:36]), FarShards(grid, up_all, up_all, rows_of, *refs[36:38])
    sems = refs[38:]
    rows, depth = hidden.shape
    pair = 2 * rows
    states = RowStores(NORM_ROWS, rows // NORM_ROWS, (hidden, tokens), (hidden_out, tokens_out), rows_sem)
    blends = RowStores(pair, chips, (mixed,), (mixed_out,), mixed_sem)
    scatter = Scatter(line, hidden, *sems[:8])
    loads.wait(0)
    grads[...] = cotangent[...].astype(low)
    gather = Gather(line, grads, grads_out, *sems[8:])
    line.ready(grid.near)
    gather.start()
    gate_near.start()
    down.start()
    loads.wait(1, 2, 3, 4)

    def term(index):
        chunk = line.target(index)
        attend_chunk(chunk, pair, qkv, values_t, heads_ref, acc, out, top_ref, sum_ref)
        mixed[span(chunk, pair), :] = out[...]
        blends.start(chunk)
        totals[:, span(chunk, pair)] = top_ref[...] + jnp.log(sum_ref[...])
        scatter.free(index)

        def tile(place, carry):
            columns = span(place, 512)
            scatter.term[index % scatter.slots, :, columns] = dot(out[...], w_out[:, columns]).astype(low)
            return carry

        lax.fori_loop(0, depth // 512, tile, 0)
        scatter.share(index).start()

    def step(index, carry):
        def phase(which, carry):
            @pl.when(jnp.logical_and(which == 1, index < chips))
            def _():
                term(index)

            lax.fori_loop(0, jnp.where(which == 1, 0, chips), scatter.due(index, which == 2), 0)
            return carry

        lax.fori_loop(0, 3, phase, 0)

        @pl.when(jnp.logical_and(index >= 1, index < chips))
        def _():
            gather.step(index)

        @pl.when(index == 1)
        def _():
            up_near.start()

        @pl.when(index == min(2, chips))
        def _():
            gate_near.arrive()
            gate_far.start()

        @pl.when(index == min(3, chips))
        def _():
            up_near.arrive()
            up_far.start()

        return carry

    lax.fori_loop(0, chips + 1, step, 0)

    def norm(here):
        state = activations[here, :] + hidden[here, :]
        hidden[here, :] = state
        tokens[here, :] = normed(state, gain[...]).astype(low)

    by_rows(rows, norm, states)
    scatter.finish()
    gather.finish(True)
    blends.wait()
    states.wait()
    for near in (gate_near, up_near):
        near.finish()
    for far in (down, gate_far, up_far):
        far.finish()


def attend(chips, shards, qkv, values_t, w_out, activations, cotangent, gain, w_gate, w_up, down_near):
    rows, depth = activations.shape
    pair = 2 * rows
    group_rows = chips * pair
    width = w_out.shape[0]
    heads = width // HEAD_DIM
    shape = jax.ShapeDtypeStruct
    stored = [shape((rows, depth), jnp.float32), shape((rows, depth), low), shape((group_rows, width), low)]
    return pl.pallas_call(
        lambda *refs: attend_kernel(chips, shards, *refs),
        in_specs=[VMEM] + [ANYWHERE] * 8,
        out_specs=[ANYWHERE] * 3 + [VMEM] + [ANYWHERE] * 4,
        out_shape=stored + [
            shape((heads, group_rows), jnp.float32),
            shape((group_rows, depth), low),
            shape((depth, w_gate.shape[1]), low),
            shape((depth, w_gate.shape[1]), low),
            shape(down_near.shape, low),
        ],
        scratch_shapes=Loads.scratch(cotangent, qkv, values_t, w_out, activations) + [
            pltpu.VMEM((heads, pair, width), low),
            pltpu.VMEM((width, pair), jnp.float32),
            pltpu.VMEM((pair, width), low),
            pltpu.VMEM((heads, pair), jnp.float32),
            pltpu.VMEM((heads, pair), jnp.float32),
            pltpu.VMEM((rows, depth), low),
        ] + FarShards.scratch(shards) + (NearShards.scratch(shards) + FarShards.scratch(shards)) * 2 + Scatter.scratch(chips, rows, depth) + Gather.scratch(chips)
        + RowStores.scratch(NORM_ROWS, rows // NORM_ROWS, *stored[:2]) + RowStores.scratch(pair, chips, stored[2]),
        compiler_params=pltpu.CompilerParams(collective_id=2, has_side_effects=True, vmem_limit_bytes=63 << 20),
        cost_estimate=pl.CostEstimate(flops=2 * group_rows * (SEQ_LEN + depth) * width, bytes_accessed=4 * group_rows * depth, transcendentals=group_rows * SEQ_LEN * heads // 2),
        name="attend",
    )(gain, cotangent, qkv, values_t, w_out, activations, w_gate, w_up, down_near)


def back_chunk(chunk, rows, grad, qkv, keys_t, mixed, totals, dkey, dvalue, heads_ref, grads_ref, acc, inner_ref):
    width = acc.shape[0]
    heads = width // HEAD_DIM
    here = span(chunk, rows)
    scaled = qkv[here, pl.ds(0, width)] * low(HEAD_DIM**-0.5)
    product = grad.astype(jnp.float32) * mixed[here, :].astype(jnp.float32)
    shape = (inner_ref.shape[0], width)
    pick = (lax.broadcasted_iota(jnp.int32, shape, 1) // HEAD_DIM == lax.broadcasted_iota(jnp.int32, shape, 0)).astype(jnp.float32)
    inner_ref[...] = lax.dot_general(pick, product, NT, precision=lax.Precision.HIGHEST, preferred_element_type=jnp.float32)
    for head in range(heads):
        heads_ref[head] = only_head(scaled, head)
        grads_ref[head] = only_head(grad, head)
    acc[...] = jnp.zeros_like(acc)

    def visit(offset, diagonal):
        keys = pl.ds(offset, rows)
        key_block = qkv[keys, pl.ds(width, width)]
        value_block = qkv[keys, pl.ds(2 * width, width)]
        key_sum, value_sum = dkey[keys, :], dvalue[keys, :]
        for head in range(heads):
            feature = pl.ds(head * HEAD_DIM, HEAD_DIM)
            scores = dot(key_block, heads_ref[head], NT)
            if diagonal:
                scores = causal(scores)
            probs = jnp.exp(scores - totals[pl.ds(head, 1), here])
            dprobs = dot(value_block, grads_ref[head], NT)
            dscores = (probs * (dprobs - inner_ref[pl.ds(head, 1), :])).astype(low)
            value_sum = value_sum + dot(probs.astype(low), grads_ref[head])
            key_sum = key_sum + dot(dscores, heads_ref[head])
            acc[feature, :] = acc[feature, :] + dot(keys_t[feature, keys], dscores)
        dkey[keys, :] = key_sum
        dvalue[keys, :] = value_sum

    over_keys(chunk, rows, visit)


def back_kernel(
    chips, shards,
    branch, terms, inner, grads, grad_both, *refs,
):
    sources, (down, branch_out, qkv_out, grad_down, grad_out, both_from) = refs[:7], refs[7:13]
    qkv_grad, qkv_sem = refs[-2:]
    refs = refs[:-2]
    loads = Loads(sources, refs[13:21])
    w_out, qkv, keys_t, mixed, totals, cosine, sine = loads.refs
    inner_chunk, grad_chunk, down_sum, down_tile, out_sum, out_stage, out_from, branch_chunk, dkey, dvalue = refs[21:31]
    heads_ref, grads_ref, acc, inner_ref, inner_sem, grad_sem, branch_sem, tile_sem, out_send, out_recv = refs[31:41]
    sums = refs[41:48]
    sems = refs[48:]
    line = Line(chips)
    rows, depth = down.shape
    pair = 2 * rows
    width = w_out.shape[0]
    results = RowStores(pair, chips, (qkv_grad,), (qkv_out,), qkv_sem)
    scatter = HeldScatter(line, down, terms, *sems[:9])
    gather = Gather(line, branch, branch_out, *sems[9:], parts=2)

    def fetch(step):
        return pltpu.make_async_copy(inner.at[span(line.target(step), pair)], inner_chunk, inner_sem)

    def fetch_grad(step):
        return pltpu.make_async_copy(grads.at[span(line.target(step), pair)], grad_chunk, grad_sem)

    grid = Grid(shards)
    shard, others = grid.me, grid.others
    columns_out = depth // shards
    both = NearSums(grid, grad_both, both_from, row_shard(columns_out), *sums)

    def give(turn):
        return remote(out_stage.at[turn], out_from.at[turn], out_send.at[turn], out_recv.at[turn], {"fsdp": others[turn]})

    def keep_tile(place):
        return pltpu.make_async_copy(down_tile, grad_down.at[span(place, 256)], tile_sem)

    line.hello([{"fsdp": other} for other in others])
    loads.start()
    fetch(0).start()
    fetch_grad(0).start()
    scatter.load(0).start()
    line.ready(others)
    gather.start()
    both.start()
    out_sum[...] = jnp.zeros_like(out_sum)
    dkey[...] = jnp.zeros_like(dkey)
    dvalue[...] = jnp.zeros_like(dvalue)

    def unrotated(block, chunk):
        table = span(chunk % (SEQ_LEN // pair), pair)
        return (block * widened(cosine[table, :], width) + turned(block * widened(sine[table, :], width), -1.0)).astype(low)

    def attention(chunk):
        gather.arrive_across(chunk)
        copy = pltpu.make_async_copy(branch_out.at[span(chunk, pair)], branch_chunk, branch_sem)
        copy.start()
        copy.wait()
        out_sum[...] += dot(mixed[span(chunk, pair), :], branch_chunk[...], TN)
        grad = dot(branch_chunk[...], w_out[...], NT).astype(low)
        back_chunk(chunk, pair, grad, qkv, keys_t, mixed, totals, dkey, dvalue, heads_ref, grads_ref, acc, inner_ref)
        qkv_grad[span(chunk, pair), pl.ds(0, width)] = unrotated(acc[...].T * HEAD_DIM**-0.5, chunk)

    def close():
        def part(chunk, carry):
            here = span(chunk, pair)
            qkv_grad[here, pl.ds(width, width)] = unrotated(dkey[here, :], chunk)
            qkv_grad[here, pl.ds(2 * width, width)] = dvalue[here, :].astype(low)
            results.start(chunk)
            return carry

        lax.fori_loop(0, chips, part, 0)

    def step(index, carry):
        @pl.when(index == 0)
        def _():
            loads.wait(*range(7))
            gather.keep().wait()

        @pl.when(index < chips)
        def _():
            scatter.free(index)
            scatter.share(index).start()

        @pl.when(index == chips)
        def _():
            for turn in range(shards - 1):
                out_stage[turn] = out_sum[:, span(others[turn], columns_out)].astype(low)
                give(turn).start()
            close()

        lax.fori_loop(0, chips, scatter.due(index, None), 0)

        @pl.when(jnp.logical_and(index >= 1, index < chips))
        def _():
            gather.step(index)

        @pl.when(index == 1)
        def _():
            both.start_plain()

        @pl.when(index == 2)
        def _():
            both.join()

        @pl.when(index < chips)
        def _():
            attention(line.target(chips - 1 - index))

        def weights(turn, carry):
            fetch(turn).wait()
            fetch_grad(turn).wait()

            def tile(place, carry):
                here = span(place, 256)
                part = dot(inner_chunk[:, here], grad_chunk[...], TN)

                @pl.when(turn == 0)
                def _():
                    down_sum[here, :] = part

                @pl.when(turn > 0)
                def _():
                    down_sum[here, :] += part

                @pl.when(turn == chips - 1)
                def _():
                    @pl.when(place > 0)
                    def _():
                        keep_tile(place - 1).wait()

                    down_tile[...] = down_sum[here, :].astype(low)
                    keep_tile(place).start()

                return carry

            lax.fori_loop(0, down_sum.shape[0] // 256, tile, 0)

            @pl.when(turn < chips - 1)
            def _():
                fetch(turn + 1).start()
                fetch_grad(turn + 1).start()

            return carry

        lax.fori_loop(jnp.where(index == 0, 0, index + 1), jnp.minimum(index + 2, chips), weights, 0)
        return carry

    lax.fori_loop(0, chips + 1, step, 0)
    total = out_sum[:, span(shard, columns_out)]
    for turn in range(shards - 1):
        give(turn).wait_recv()
        total = total + out_from[turn].astype(jnp.float32)
    grad_out[...] = total
    for turn in range(shards - 1):
        give(turn).wait_send()
    keep_tile(down_sum.shape[0] // 256 - 1).wait()
    both.finish()
    results.wait()
    scatter.finish()
    gather.finish(False)


def back(chips, shards, branch, terms, inner, grads, grad_both, w_out, qkv, keys_t, mixed, totals, cosine, sine):
    rows, depth = branch.shape
    pair = 2 * rows
    group_rows = chips * pair
    width = w_out.shape[0]
    hidden = inner.shape[1]
    heads = width // HEAD_DIM
    shape = jax.ShapeDtypeStruct
    held = (w_out, qkv, keys_t, mixed, totals, cosine, sine)
    return pl.pallas_call(
        lambda *refs: back_kernel(chips, shards, *refs),
        in_specs=[VMEM] + [ANYWHERE] * 11,
        out_specs=[VMEM, ANYWHERE, ANYWHERE, ANYWHERE, VMEM, ANYWHERE],
        out_shape=[
            shape((rows, depth), jnp.float32),
            shape((group_rows, depth), low),
            shape((group_rows, 3 * width), low),
            shape((hidden, depth), low),
            shape((width, depth // shards), jnp.float32),
            shape((shards // 2, depth // shards, grad_both.shape[1]), low),
        ],
        scratch_shapes=Loads.scratch(*held) + [
            pltpu.VMEM((pair, hidden), low),
            pltpu.VMEM((pair, depth), low),
            pltpu.VMEM((hidden, depth), jnp.float32),
            pltpu.VMEM((256, depth), low),
            pltpu.VMEM((width, depth), jnp.float32),
            pltpu.VMEM((shards - 1, width, depth // shards), low),
            pltpu.VMEM((shards - 1, width, depth // shards), low),
            pltpu.VMEM((pair, depth), low),
            pltpu.VMEM((group_rows, width), jnp.float32),
            pltpu.VMEM((group_rows, width), jnp.float32),
            pltpu.VMEM((heads, pair, width), low),
            pltpu.VMEM((heads, pair, width), low),
            pltpu.VMEM((width, pair), jnp.float32),
            pltpu.VMEM((8, pair), jnp.float32),
            DMA, DMA, DMA, DMA, DMA((shards - 1,)), DMA((shards - 1,)),
        ] + NearSums.scratch(shards, depth // shards, grad_both.shape[1]) + HeldScatter.scratch(chips, rows, depth) + Gather.scratch(chips, 2)
        + RowStores.scratch(pair, chips, shape((group_rows, 3 * width), low)),
        compiler_params=pltpu.CompilerParams(collective_id=4, has_side_effects=True, vmem_limit_bytes=67043328),
        cost_estimate=pl.CostEstimate(flops=1 << 20, bytes_accessed=1 << 20, transcendentals=0),
        name="back",
    )(branch, terms, inner, grads, grad_both, *held)


def spread_kernel(
    chips, shards,
    gain, gain_part, qkv_hbm, weight_hbm, activations_hbm, attn_tokens, grad_down,
    input_out, qkv_out, gain_sum, down_from,
    input_part, rows_sem, grad_qkv, sum_sem, qkv_grad, weight, activations, held_sem,
    attn_cols, qkv_stage, qkv_from, gains, gains_tp, gains_fsdp,
    attn_sem, qkv_send, qkv_recv, tp_send, tp_recv, fsdp_send, fsdp_recv, *sems,
):
    line = Line(chips)
    size = 2 * chips
    rows, depth = input_part.shape
    pair = 2 * rows
    grid = Grid(shards)
    shard = grid.me
    columns = depth // shards
    loads = Loads((qkv_hbm, weight_hbm, activations_hbm), (qkv_grad, weight, activations, held_sem))
    down = NearSums(grid, grad_down, down_from, column_shard(grad_down.shape[0], columns), *sems[:7])
    scatter = Scatter(line, input_part, *sems[7:])

    def peer(turn):
        return (shard + 1 + turn) % shards

    def fetch(turn):
        return pltpu.make_async_copy(attn_tokens.at[:, span(peer(turn), columns)], attn_cols.at[turn % 2], attn_sem.at[turn % 2])

    def give(turn):
        return remote(qkv_stage.at[turn], qkv_from.at[turn], qkv_send.at[turn], qkv_recv.at[turn], {"fsdp": peer(turn)})

    def tell_tp(ahead):
        return remote(gains, gains_tp.at[line.me], tp_send.at[ahead - 1], tp_recv.at[line.me], {"tp": (line.me + ahead) % size})

    def tell_fsdp(ahead):
        return remote(gains, gains_fsdp.at[shard], fsdp_send.at[ahead - 1], fsdp_recv.at[shard], {"fsdp": (shard + ahead) % shards})

    for ahead in range(1, size):
        hello({"tp": (line.me + ahead) % size})
    for ahead in range(1, shards):
        hello({"fsdp": (shard + ahead) % shards})
    loads.start()
    fetch(0).start()
    loads.wait(0, 1)
    pl.semaphore_wait(pltpu.get_barrier_semaphore(), size - 1 + shards - 1)
    down.start()

    def weights(turn, carry):
        @pl.when(turn < shards - 1)
        def _():
            fetch(turn + 1).start()

        fetch(turn).wait()
        part = dot(attn_cols[turn % 2], qkv_grad[...], TN)

        @pl.when(turn < shards - 1)
        def _():
            qkv_stage[turn] = part.astype(low)
            give(turn).start()

        @pl.when(turn == shards - 1)
        def _():
            grad_qkv[...] = part

        return carry

    def term(index):
        scatter.free(index)
        here = span(line.target(index), pair)

        def tile(place, carry):
            there = span(place, 512)
            scatter.term[index % scatter.slots, :, there] = dot(qkv_grad[here, :], weight[there, :], NT).astype(low)
            return carry

        lax.fori_loop(0, depth // 512, tile, 0)
        scatter.share(index).start()

    def step(index, carry):
        def phase(which, carry):
            @pl.when(jnp.logical_and(which == 1, index < chips))
            def _():
                term(index)

            @pl.when(jnp.logical_and(which == 2, index < 2))
            def _():
                lax.fori_loop(index, jnp.where(index == 0, 1, shards), weights, 0)

            @pl.when(jnp.logical_and(which == 2, index == 1))
            def _():
                down.start_plain()

            @pl.when(jnp.logical_and(which == 2, index == 2))
            def _():
                down.join()

            outer = jnp.logical_or(which == 0, which == 3)
            lax.fori_loop(0, jnp.where(outer, chips, 0), scatter.due(index, which == 3), 0)
            return carry

        lax.fori_loop(0, 4, phase, 0)
        return carry

    lax.fori_loop(0, chips + 1, step, 0)
    gains[0:1, :] = jnp.zeros((1, depth), jnp.float32)
    gains[1:2, :] = gain_part[...]

    def norm(here):
        part, grad = norm_back(activations[here, :], gain[...], input_part[here, :])
        input_part[here, :] = part
        gains[0:1, :] += grad

    loads.wait(2)
    results = RowStores(NORM_ROWS, rows // NORM_ROWS, (input_part,), (input_out,), rows_sem)
    by_rows(rows, norm, results)

    gains_tp[line.me] = gains[...]
    for ahead in range(1, size):
        tell_tp(ahead).start()
    for turn in range(shards - 1):
        give(turn).wait_recv()
        grad_qkv[...] += qkv_from[turn].astype(jnp.float32)
    summed = RowStores(columns, 1, (grad_qkv,), (qkv_out,), sum_sem)
    summed.start(0)
    for ahead in range(1, size):
        source = (line.me + ahead) % size
        remote(gains, gains_tp.at[source], tp_send.at[0], tp_recv.at[source], {"tp": source}).wait_recv()
    total = gains_tp[0]
    for source in range(1, size):
        total = total + gains_tp[source]
    for ahead in range(1, size):
        tell_tp(ahead).wait_send()
    gains[...] = total
    gains_fsdp[shard] = total
    for ahead in range(1, shards):
        tell_fsdp(ahead).start()
    for ahead in range(1, shards):
        source = (shard + ahead) % shards
        remote(gains, gains_fsdp.at[source], fsdp_send.at[0], fsdp_recv.at[source], {"fsdp": source}).wait_recv()
    total = gains_fsdp[0]
    for source in range(1, shards):
        total = total + gains_fsdp[source]
    gain_sum[...] = total
    for ahead in range(1, shards):
        tell_fsdp(ahead).wait_send()
    for turn in range(shards - 1):
        give(turn).wait_send()
    down.finish()
    results.wait()
    summed.wait()
    scatter.finish()


def spread(chips, shards, qkv_grad, weight, activations, gain, gain_part, attn_tokens, grad_down):
    group_rows = qkv_grad.shape[0]
    rows, depth = activations.shape
    width = qkv_grad.shape[1] // 3
    columns = depth // shards
    size = 2 * chips
    shape = jax.ShapeDtypeStruct
    stored = [shape((rows, depth), jnp.float32), shape((columns, 3 * width), jnp.float32)]
    return pl.pallas_call(
        lambda *refs: spread_kernel(chips, shards, *refs),
        in_specs=[VMEM] * 2 + [ANYWHERE] * 5,
        out_specs=[ANYWHERE] * 2 + [VMEM, ANYWHERE],
        out_shape=stored + [
            shape((2, depth), jnp.float32),
            shape((shards // 2, grad_down.shape[0], columns), low),
        ],
        scratch_shapes=RowStores.scratch(NORM_ROWS, rows // NORM_ROWS, stored[0]) + RowStores.scratch(columns, 1, stored[1]) + Loads.scratch(qkv_grad, weight, activations) + [
            pltpu.VMEM((2, group_rows, columns), low),
            pltpu.VMEM((shards - 1, columns, 3 * width), low),
            pltpu.VMEM((shards - 1, columns, 3 * width), low),
            pltpu.VMEM((2, depth), jnp.float32),
            pltpu.VMEM((size, 2, depth), jnp.float32),
            pltpu.VMEM((shards, 2, depth), jnp.float32),
            DMA((2,)), DMA((shards - 1,)), DMA((shards - 1,)),
            DMA((size - 1,)), DMA((size,)), DMA((shards - 1,)), DMA((shards,)),
        ] + NearSums.scratch(shards, grad_down.shape[0], columns) + Scatter.scratch(chips, rows, depth),
        compiler_params=pltpu.CompilerParams(collective_id=5, has_side_effects=True, vmem_limit_bytes=63 << 20),
        cost_estimate=pl.CostEstimate(flops=1 << 20, bytes_accessed=1 << 20, transcendentals=0),
        name="spread",
    )(gain, gain_part, qkv_grad, weight, activations, attn_tokens, grad_down)


def chip_at(place, chips):
    return jnp.where(2 * place < chips, 2 * place, 2 * (chips - 1 - place) + 1)


def place_of(chip, chips):
    return jnp.where(chip % 2 == 0, chip // 2, chips - 1 - chip // 2)


def feed_kernel(
    chips, shards,
    gain, hidden_hbm, cotangent_hbm, tokens, grads_hbm, w_gate, w_up, w_down, gate_all, up_all, down_near, down_far,
    hidden_grad_out, branch_out, gain_part, inner_out, grad_both, down_out,
    hidden_grad, branch, rows_sem, hidden_state, cotangent, state_sem, down_tile, down_sem, tokens_all, gate_w, up_w, down_w, grads, inner, gate_grad, up_grad, term, from_core, from_ring, total, tile_gate, tile_up,
    load_sem, own_sem, grad_sem, store_sem, tile_sem,
    ring_send, ring_recv, core_send, core_recv, share_send, share_recv, total_send, total_recv,
):
    rows, depth = hidden_grad.shape
    pair = 2 * rows
    width = gate_w.shape[1]
    me = lax.axis_index("tp")
    chip, core = me // 2, me % 2
    place = place_of(chip, chips)
    following = {"tp": 2 * chip_at((place + 1) % chips, chips) + core}
    before = {"tp": 2 * chip_at((place + chips - 1) % chips, chips) + core}
    partner = {"tp": 2 * chip + 1 - core}

    grid = Grid(shards)
    part = w_gate.shape[0]

    def load(array, source, shard, tile, whole):
        cut = span(tile, 256)
        if array == 2:
            place = lambda ref: ref.at[cut, span(shard, part)]
            own = lambda ref: ref.at[cut]
        else:
            place = lambda ref: ref.at[span(shard, part), cut]
            own = lambda ref: ref.at[:, cut]
        target = place((gate_w, up_w, down_w)[array])
        return pltpu.make_async_copy(place(source) if whole else own(source), target, load_sem.at[array, shard, tile])

    def load_weights(tile, carry):
        for shard in range(shards):
            own, near = grid.me == shard, grid.is_near(shard)

            @pl.when(own)
            def _():
                for array, source in enumerate((w_gate, w_up, w_down)):
                    load(array, source, shard, tile, False).start()

            @pl.when(jnp.logical_not(own))
            def _():
                for array, source in enumerate((gate_all, up_all)):
                    load(array, source, shard, tile, True).start()

            @pl.when(jnp.logical_and(near, jnp.logical_not(own)))
            def _():
                load(2, down_near, shard, tile, True).start()

            @pl.when(jnp.logical_not(near))
            def _():
                load(2, down_far, shard, tile, True).start()

        return carry

    own = pltpu.make_async_copy(tokens, tokens_all.at[span(me, rows)], own_sem)
    states = Loads((hidden_hbm, cotangent_hbm), (hidden_state, cotangent, state_sem))

    def source(slot):
        return chip_at((place + chips - slot) % chips, chips)

    def fetch(slot):
        return pltpu.make_async_copy(grads_hbm.at[span(source(slot), pair)], grads.at[slot % 2], grad_sem.at[slot % 2])

    def block(slot):
        return tokens_all.at[span(2 * source(slot) + core, rows)]

    def to_ring(slot):
        return remote(block(slot), block(slot), ring_send.at[slot], ring_recv.at[slot], following)

    def to_core(slot):
        return remote(block(slot), block(slot), core_send.at[slot], core_recv.at[slot], partner)

    def store(slot):
        return pltpu.make_async_copy(inner.at[slot], inner_out.at[span(source(slot), pair)], store_sem.at[slot])

    def keep_down(slot, tile):
        there = down_out.at[span(source(slot), pair), span(tile, 256)]
        return pltpu.make_async_copy(down_tile.at[tile % 2], there, down_sem.at[tile % 2])

    def down_term(slot, carry):
        def tile(index, carry):
            @pl.when(index > 1)
            def _():
                keep_down(slot, index - 2).wait()

            down_tile[index % 2] = dot(inner[slot], down_w[:, span(index, 256)]).astype(low)
            keep_down(slot, index).start()
            return carry

        lax.fori_loop(0, depth // 256, tile, 0)
        for index in range(depth // 256 - 2, depth // 256):
            keep_down(slot, index).wait()
        return carry

    def share(slot):
        place = jnp.where(slot == 0, 0, 1 + slot % 2)
        return remote(term.at[span(1 - core, rows)], from_core.at[place], share_send, share_recv.at[place], partner)

    def pass_on(slot):
        return remote(total.at[slot % 2], from_ring.at[slot - 1], total_send.at[slot % 2], total_recv.at[slot - 1], following)

    for device in (following, before, partner):
        hello(device)
    own.start()
    fetch(0).start()
    lax.fori_loop(0, width // 256, load_weights, 0)
    own.wait()
    pl.semaphore_wait(pltpu.get_barrier_semaphore(), 3)

    def step(slot, carry):
        here = slot % 2
        wide_rows = span(source(slot), pair)
        mine = span(core, rows)

        @pl.when(slot > 0)
        def _():
            to_ring(slot - 1).wait_recv()

        @pl.when(slot < chips - 1)
        def _():
            to_ring(slot).start()
            fetch(slot + 1).start()

        to_core(slot).start()

        @pl.when(slot == 1)
        def _():
            states.start()

        to_core(slot).wait_recv()
        fetch(slot).wait()

        def narrow(tile, carry):
            columns = span(tile, 256)

            @pl.when(slot == 0)
            def _():
                for shard in range(shards):
                    for array, source in enumerate((gate_all, up_all, down_near)):
                        load(array, source, shard, tile, True).wait()

            token = tokens_all[wide_rows, :]
            gate = dot(token, gate_w[:, columns])
            up = dot(token, up_w[:, columns])
            grad = dot(grads[here], down_w[columns, :], NT)
            squash = jax.nn.sigmoid(gate)
            act = gate * squash
            inner[slot, :, columns] = (act * up).astype(low)
            up_grad[wide_rows, columns] = (grad * act).astype(low)
            gate_grad[wide_rows, columns] = (grad * up * squash * (1.0 + gate * (1.0 - squash))).astype(low)
            return carry

        lax.fori_loop(0, width // 256, narrow, 0, unroll=2)
        store(slot).start()

        @pl.when(slot > 0)
        def _():
            share(slot - 1).wait_send()

        def wide(tile, carry):
            columns = span(tile, 256)
            part = dot(gate_grad[wide_rows, :], gate_w[columns, :], NT) + dot(up_grad[wide_rows, :], up_w[columns, :], NT)
            term[:, columns] = part.astype(low)
            return carry

        lax.fori_loop(0, depth // 256, wide, 0)
        share(slot).start()

        @pl.when(slot == 0)
        def _():
            hidden_grad[...] = term[mine, :].astype(jnp.float32)

        middle = jnp.logical_and(slot >= 2, slot < chips - 1)
        lax.fori_loop(jnp.where(slot == 2, 0, slot), jnp.where(middle, slot + 1, 0), down_term, 0)

        @pl.when(slot > 0)
        def _():
            share(slot).wait_recv()

            @pl.when(slot > 2)
            def _():
                pass_on(slot - 2).wait_send()

            @pl.when(slot == 1)
            def _():
                total[here] = (term[mine, :].astype(jnp.float32) + from_core[1 + here].astype(jnp.float32)).astype(low)

            @pl.when(slot > 1)
            def _():
                pass_on(slot - 1).wait_recv()
                total[here] = (term[mine, :].astype(jnp.float32) + from_core[1 + here].astype(jnp.float32) + from_ring[slot - 2].astype(jnp.float32)).astype(low)

            pass_on(slot).start()

        return carry

    lax.fori_loop(0, chips, step, 0)

    def tiles(index):
        there = span(index, 256)
        return (
            pltpu.make_async_copy(tile_gate.at[index % 2], grad_both.at[there, pl.ds(0, width)], tile_sem.at[0, index % 2]),
            pltpu.make_async_copy(tile_up.at[index % 2], grad_both.at[there, pl.ds(width, width)], tile_sem.at[1, index % 2]),
        )

    def weights(index, carry):
        @pl.when(index > 1)
        def _():
            for copy in tiles(index - 2):
                copy.wait()

        token = tokens_all[:, span(index, 256)]
        tile_gate[index % 2] = dot(token, gate_grad[...], TN).astype(low)
        tile_up[index % 2] = dot(token, up_grad[...], TN).astype(low)
        for copy in tiles(index):
            copy.start()
        return carry

    lax.fori_loop(0 if chips < 4 else chips - 1, chips, down_term, 0)
    lax.fori_loop(0, depth // 256, weights, 0)
    states.wait(0, 1)
    share(0).wait_recv()
    pass_on(chips - 1).wait_recv()
    gain_part[...] = jnp.zeros_like(gain_part)

    def norm(here):
        grad = hidden_grad[here, :] + from_core[0, here, :].astype(jnp.float32) + from_ring[chips - 2, here, :].astype(jnp.float32)
        part, gain_grad = norm_back(hidden_state[here, :], gain[...], grad)
        full = cotangent[here, :] + part
        hidden_grad[here, :] = full
        branch[here, :] = full.astype(low)
        gain_part[...] += gain_grad

    results = RowStores(NORM_ROWS, rows // NORM_ROWS, (hidden_grad, branch), (hidden_grad_out, branch_out), rows_sem)
    by_rows(rows, norm, results)
    share(chips - 1).wait_send()
    for slot in range(chips):
        to_core(slot).wait_send()
        if slot < chips - 1:
            to_ring(slot).wait_send()
        if slot >= max(1, chips - 2):
            pass_on(slot).wait_send()
        store(slot).wait()
    for index in range(depth // 256 - 2, depth // 256):
        for copy in tiles(index):
            copy.wait()
    results.wait()


def feed(chips, shards, hidden_state, cotangent, gain, tokens, grads, w_gate, w_up, w_down, gate_all, up_all, down_near, down_far):
    rows, depth = tokens.shape
    pair = 2 * rows
    group_rows = chips * pair
    width = w_down.shape[0]
    shape = jax.ShapeDtypeStruct
    stored = [shape((rows, depth), jnp.float32), shape((rows, depth), low)]
    return pl.pallas_call(
        lambda *refs: feed_kernel(chips, shards, *refs),
        in_specs=[VMEM] + [ANYWHERE] * 11,
        out_specs=[ANYWHERE] * 2 + [VMEM] + [ANYWHERE] * 3,
        out_shape=stored + [
            shape((1, depth), jnp.float32),
            shape((group_rows, width), low),
            shape((depth, 2 * width), low),
            shape((group_rows, depth), low),
        ],
        scratch_shapes=RowStores.scratch(NORM_ROWS, rows // NORM_ROWS, *stored) + Loads.scratch(hidden_state, cotangent) + [
            pltpu.VMEM((2, pair, 256), low),
            DMA((2,)),
            pltpu.VMEM((group_rows, depth), low),
            pltpu.VMEM((depth, width), low),
            pltpu.VMEM((depth, width), low),
            pltpu.VMEM((width, depth), low),
            pltpu.VMEM((2, pair, depth), low),
            pltpu.VMEM((chips, pair, width), low),
            pltpu.VMEM((group_rows, width), low),
            pltpu.VMEM((group_rows, width), low),
            pltpu.VMEM((pair, depth), low),
            pltpu.VMEM((3, rows, depth), low),
            pltpu.VMEM((chips - 1, rows, depth), low),
            pltpu.VMEM((2, rows, depth), low),
            pltpu.VMEM((2, 256, width), low),
            pltpu.VMEM((2, 256, width), low),
            DMA((3, shards, width // 256)), DMA, DMA((2,)), DMA((chips,)), DMA((2, 2)),
            DMA((chips,)), DMA((chips,)), DMA((chips,)), DMA((chips,)),
            DMA, DMA((3,)), DMA((2,)), DMA((chips - 1,)),
        ],
        compiler_params=pltpu.CompilerParams(collective_id=3, has_side_effects=True, vmem_limit_bytes=67043328),
        cost_estimate=pl.CostEstimate(flops=16 * group_rows * depth * width, bytes_accessed=10 * group_rows * depth, transcendentals=group_rows * width),
        name="feed",
    )(gain, hidden_state, cotangent, tokens, grads, w_gate, w_up, w_down, gate_all, up_all, down_near, down_far)


def finish_kernel(
    shard_ref, hidden, down, hidden_grad, input_part, both, both_from, grad_down, down_from, grad_qkv, grad_out, gains,
    output, input_grad, query, key, value, out, gate, up, down_out, gain_attn, gain_mlp,
):
    gain_attn[...] = gains[0:1, :]
    gain_mlp[...] = gains[1:2, :]
    output[...] = hidden[...] + down[...]
    input_grad[...] = hidden_grad[...] + input_part[...]
    width = query.shape[1]
    for part, ref in enumerate((query, key, value)):
        ref[...] = grad_qkv[:, pl.ds(part * width, width)]
    out[...] = grad_out[...]
    wide = gate.shape[1]
    for side, ref in enumerate((gate, up)):
        columns = pl.ds(side * wide, wide)
        total = both[:, columns].astype(jnp.float32)
        for turn in range(both_from.shape[0]):
            total = total + both_from[turn, :, columns].astype(jnp.float32)
        ref[...] = total
    total = grad_down[...].astype(jnp.float32)
    for turn in range(down_from.shape[0]):
        total = total + down_from[turn].astype(jnp.float32)
    down_out[...] = total


def finish(shard, hidden, down, hidden_grad, input_part, both, both_from, grad_down, down_from, grad_qkv, grad_out, gains):
    steps = 4
    shape = jax.ShapeDtypeStruct
    columns = down_from.shape[2]
    results = [shape(hidden.shape, jnp.float32)] * 2
    results += [shape((columns, grad_qkv.shape[1] // 3), jnp.float32)] * 3 + [shape(grad_out.shape, jnp.float32)]
    results += [shape((columns, both.shape[1] // 2), jnp.float32)] * 2 + [shape((grad_down.shape[0], columns), jnp.float32)]
    spec = lambda a: pl.BlockSpec((a.shape[0] // steps, a.shape[1]), lambda i, s: (i, 0))
    spec3 = lambda a: pl.BlockSpec((a.shape[0], a.shape[1] // steps, a.shape[2]), lambda i, s: (0, i, 0))
    return pl.pallas_call(
        finish_kernel,
        grid_spec=pltpu.PrefetchScalarGridSpec(
            num_scalar_prefetch=1,
            grid=(steps,),
            in_specs=[
                spec(hidden), spec(down), spec(hidden_grad), spec(input_part),
                pl.BlockSpec((columns // steps, both.shape[1]), lambda i, s: (s[0] * steps + i, 0)),
                spec3(both_from),
                pl.BlockSpec((grad_down.shape[0] // steps, columns), lambda i, s: (i, s[0])),
                spec3(down_from), spec(grad_qkv), spec(grad_out),
                pl.BlockSpec(gains.shape, lambda i, s: (0, 0)),
            ],
            out_specs=[spec(a) for a in results] + [pl.BlockSpec((1, gains.shape[1]), lambda i, s: (0, 0))] * 2,
        ),
        out_shape=results + [shape((1, gains.shape[1]), jnp.float32)] * 2,
        name="finish",
    )(shard.reshape(1), hidden, down, hidden_grad, input_part, both, both_from, grad_down, down_from, grad_qkv, grad_out, gains)


def rope_frequencies():
    column = np.arange(HEAD_DIM // 2)
    return jnp.asarray((rope_base ** (-2.0 * column / HEAD_DIM)).astype(np.float32)[:, None])


def make_body(mesh):
    chips, shards = mesh.shape["tp"] // 2, mesh.shape["fsdp"]

    def body(activations, gain_attn, w_query, w_key, w_value, w_out, gain_mlp, w_gate, w_up, w_down, cotangent):
        gain_attn, gain_mlp = gain_attn[None, :], gain_mlp[None, :]
        seen_attn, w_qkv, full_out, qkv, keys_t, values_t, cosine, sine, down_near = project(
            chips, shards, activations, gain_attn, w_query, w_key, w_value, w_out, rope_frequencies(), w_down
        )
        hidden_state, normed_mlp, mixed, totals, seen_grad, gate_all, up_all, down_far = attend(
            chips, shards, qkv, values_t, full_out, activations, cotangent, gain_mlp, w_gate, w_up, down_near
        )
        hidden_grad, branch_grad, gain_part, inner, grad_both, terms = feed(
            chips, shards, hidden_state, cotangent, gain_mlp, normed_mlp, seen_grad,
            w_gate, w_up, w_down, gate_all, up_all, down_near, down_far,
        )
        down, _, qkv_grad, grad_down, grad_out, both_from = back(
            chips, shards, branch_grad, terms, inner, seen_grad, grad_both, full_out, qkv, keys_t, mixed, totals, cosine, sine
        )
        input_part, grad_qkv, gain_sums, down_from = spread(
            chips, shards, qkv_grad, w_qkv, activations, gain_attn, gain_part, seen_attn, grad_down
        )
        output, input_grad, grad_query, grad_key, grad_value, grad_out, grad_gate, grad_up, grad_down, gain_attn, gain_mlp = finish(
            lax.axis_index("fsdp"), hidden_state, down, hidden_grad, input_part,
            grad_both, both_from, grad_down, down_from, grad_qkv, grad_out, gain_sums,
        )
        return (
            output, input_grad, gain_attn[0], grad_query, grad_key, grad_value, grad_out, gain_mlp[0],
            grad_gate, grad_up, grad_down,
        )

    return body


def solution(mesh):
    tokens = P(("fsdp", "tp"), None)
    column = P("fsdp", "tp")
    row = P("tp", "fsdp")
    in_specs = (tokens, P(), column, column, column, row, P(), column, column, row, tokens)
    out_specs = (tokens, tokens, P(), column, column, column, row, P(), column, column, row)
    return jax.shard_map(make_body(mesh), mesh=mesh, in_specs=in_specs, out_specs=out_specs, check_vma=False)
```

```python
import jax
import jax.numpy as jnp
import numpy as np
from jax import lax
from jax.experimental import pallas as pl
from jax.experimental.pallas import tpu as pltpu
from jax.sharding import PartitionSpec as P

HEAD_DIM = 64
SEQ_LEN = 2048
LANES = 128
rope_base = 130000.0
norm_eps = 1e-05
masked_score = -1e30

NT = (((1,), (1,)), ((), ()))
NN = (((1,), (0,)), ((), ()))
TN = (((0,), (0,)), ((), ()))
MESH = pl.DeviceIdType.MESH
DMA = pltpu.SemaphoreType.DMA
ANYWHERE = pl.BlockSpec(memory_space=pl.ANY)
VMEM = pl.BlockSpec(memory_space=pltpu.VMEM)
low = jnp.bfloat16


def dot(left, right, dims=NN):
    return lax.dot_general(left, right, dims, preferred_element_type=jnp.float32)


def span(index, size):
    return pl.ds(pl.multiple_of(index * size, size), size)


def remote(source, target, send, receive, device):
    return pltpu.make_async_remote_copy(
        src_ref=source, dst_ref=target, send_sem=send, recv_sem=receive,
        device_id=device, device_id_type=MESH,
    )


def hello(device):
    pl.semaphore_signal(pltpu.get_barrier_semaphore(), inc=1, device_id=device, device_id_type=MESH)


class Line:
    def __init__(self, chips):
        self.chips = chips
        self.me = lax.axis_index("tp")
        self.chip, self.core = self.me // 2, self.me % 2
        self.partner = 2 * self.chip + 1 - self.core
        self.has_left, self.has_right = self.chip > 0, self.chip < chips - 1

    def hello(self, more=()):
        hello({"tp": self.partner})

        @pl.when(self.has_left)
        def _():
            hello({"tp": self.me - 2})

        @pl.when(self.has_right)
        def _():
            hello({"tp": self.me + 2})

        for device in more:
            hello(device)

    def ready(self, more=()):
        count = 1 + len(more) + jnp.where(self.has_left, 1, 0) + jnp.where(self.has_right, 1, 0)
        pl.semaphore_wait(pltpu.get_barrier_semaphore(), count)

    def target(self, step):
        after = self.chips - 1 - self.chip
        most, least = jnp.maximum(self.chip, after), jnp.minimum(self.chip, after)
        sign = jnp.where(after >= self.chip, 1, -1)
        late = step - (most - least)
        side = jnp.where(late % 2 == 0, sign, -sign)
        return jnp.where(late < 0, self.chip + sign * (most - step), self.chip + side * (least - late // 2))


    def fed(self, target):
        after, before = jnp.logical_and(target >= self.chip, self.has_left), jnp.logical_and(target <= self.chip, self.has_right)
        return jnp.logical_or(after, before)


class Gather:
    @staticmethod
    def scratch(chips, parts=1):
        return [DMA((2 * chips, parts)), DMA((chips, parts)), DMA((chips, parts)), DMA((chips, parts)), DMA]

    def __init__(self, line, own, out, received, right, left, across, local, parts=1):
        self.line, self.out = line, out
        self.received, self.right, self.left, self.across, self.local = received, right, left, across, local
        self.parts = parts
        self.rows = out.shape[0] // (2 * line.chips * parts)
        self.held = own is None
        self.own = out.at[span(line.me, self.rows * parts)] if self.held else own

    def block(self, index, part):
        return self.out.at[span(index * self.parts + part, self.rows)]

    def mine(self, part):
        return self.own.at[pl.ds(part * self.rows, self.rows)]

    def copy(self, sems, chip, part, device, mine):
        index = 2 * chip + self.line.core
        source = self.mine(part) if mine else self.block(index, part)
        return remote(source, self.block(index, part), sems.at[chip, part], self.received.at[index, part], {"tp": device})

    def keep(self):
        return pltpu.make_async_copy(self.own, self.out.at[span(self.line.me, self.rows * self.parts)], self.local)

    def start(self):
        line = self.line
        if not self.held:
            self.keep().start()
        for part in range(self.parts):
            @pl.when(line.has_right)
            def _():
                self.copy(self.right, line.chip, part, line.me + 2, True).start()

            @pl.when(line.has_left)
            def _():
                self.copy(self.left, line.chip, part, line.me - 2, True).start()

            self.copy(self.across, line.chip, part, line.partner, True).start()

    def arrive(self, index, part):
        remote(self.mine(part), self.block(index, part), self.right.at[0, part], self.received.at[index, part], {"tp": self.line.partner}).wait_recv()

    def arrive_across(self, chip):
        for part in range(self.parts):
            self.arrive(2 * chip + 1 - self.line.core, part)

    def step(self, distance):
        line = self.line
        before, after = line.chip - distance, line.chip + distance
        for part in range(self.parts):
            @pl.when(before >= 0)
            def _():
                self.arrive(2 * before + line.core, part)

                @pl.when(line.has_right)
                def _():
                    self.copy(self.right, before, part, line.me + 2, False).start()

                self.copy(self.across, before, part, line.partner, False).start()

            @pl.when(after < line.chips)
            def _():
                self.arrive(2 * after + line.core, part)

                @pl.when(line.has_left)
                def _():
                    self.copy(self.left, after, part, line.me - 2, False).start()

                self.copy(self.across, after, part, line.partner, False).start()

    def finish(self, arrivals):
        line = self.line
        if arrivals:
            self.keep().wait()
        for chip in range(line.chips):
            if arrivals:
                self.arrive_across(chip)
            for part in range(self.parts):
                self.copy(self.across, chip, part, line.partner, True).wait_send()

                @pl.when(jnp.logical_and(line.has_right, chip <= line.chip))
                def _():
                    self.copy(self.right, chip, part, line.me + 2, True).wait_send()

                @pl.when(jnp.logical_and(line.has_left, chip >= line.chip))
                def _():
                    self.copy(self.left, chip, part, line.me - 2, True).wait_send()


class Scatter:
    @staticmethod
    def scratch(chips, rows, depth):
        slots = chips // 2 + 1
        return [
            pltpu.VMEM((slots, 2 * rows, depth), low),
            pltpu.VMEM((chips, rows, depth), low),
            pltpu.VMEM((chips + 1, rows, depth), low),
            pltpu.VMEM((2, rows, depth), low),
            DMA((slots,)), DMA((chips,)), DMA((2,)), DMA((chips + 1,)),
        ]

    def __init__(self, line, out, term, shares, lines, total, share_send, share_recv, line_send, line_recv):
        self.line, self.out = line, out
        self.term, self.shares, self.lines, self.total = term, shares, lines, total
        self.share_send, self.share_recv, self.line_send, self.line_recv = share_send, share_recv, line_send, line_recv
        self.rows = out.shape[0]
        self.slots = term.shape[0]

    def share(self, step):
        slot = step % self.slots
        source = self.term.at[slot, span(1 - self.line.core, self.rows)]
        return remote(source, self.shares.at[step], self.share_send.at[slot], self.share_recv.at[step], {"tp": self.line.partner})

    def due(self, index, fed):
        def one(step, carry):
            target = self.line.target(step)
            distance = jnp.where(target > self.line.chip, target - self.line.chip, self.line.chip - target)
            turn = True if fed is None else self.line.fed(target) == fed

            @pl.when(jnp.logical_and(distance == self.line.chips - index, turn))
            def _():
                self.step(step)

            return carry

        return one

    def mine(self, step):
        return self.term[step % self.slots, span(self.line.core, self.rows), :]

    def pass_on(self, step):
        line, target = self.line, self.line.target(step)
        onward = target > line.chip
        slot = jnp.where(onward, target, jnp.where(target == line.chip - 1, line.chips, target))
        device = jnp.where(onward, line.me + 2, line.me - 2)
        return remote(self.total.at[step % 2], self.lines.at[slot], self.line_send.at[step % 2], self.line_recv.at[slot], {"tp": device})

    def add(self, slot):
        remote(self.total.at[0], self.lines.at[slot], self.line_send.at[0], self.line_recv.at[slot], {"tp": self.line.partner}).wait_recv()
        self.out[...] += self.lines[slot].astype(jnp.float32)

    def free(self, step):
        @pl.when(step >= self.slots)
        def _():
            self.share(step - self.slots).wait_send()

    def step(self, step):
        line, target = self.line, self.line.target(step)
        self.share(step).wait_recv()
        self.out[...] = self.mine(step).astype(jnp.float32) + self.shares[step].astype(jnp.float32)

        @pl.when(jnp.logical_and(target >= line.chip, line.has_left))
        def _():
            self.add(target)

        @pl.when(jnp.logical_and(target <= line.chip, line.has_right))
        def _():
            self.add(jnp.where(target == line.chip, line.chips, target))

        @pl.when(step < line.chips - 1)
        def _():
            @pl.when(step >= 2)
            def _():
                self.pass_on(step - 2).wait_send()

            self.total[step % 2] = self.out[...].astype(low)
            self.pass_on(step).start()

    def finish(self):
        chips = self.line.chips
        for step in range(max(0, chips - 3), chips - 1):
            self.pass_on(step).wait_send()
        for step in range(max(0, chips - self.slots), chips):
            self.share(step).wait_send()


NORM_ROWS = 64


def normed(value, gain):
    return value * lax.rsqrt(jnp.mean(value * value, axis=-1, keepdims=True) + norm_eps) * gain


def norm_back(value, gain, grad):
    scale = lax.rsqrt(jnp.mean(value * value, axis=-1, keepdims=True) + norm_eps)
    unit = value * scale
    scaled = grad * gain
    return scale * (scaled - unit * jnp.mean(scaled * unit, axis=-1, keepdims=True)), jnp.sum(grad * unit, axis=0, keepdims=True)


def by_rows(rows, work, stores=None):
    def step(index, carry):
        work(span(index, NORM_ROWS))
        if stores:
            stores.start(index)
        return carry

    lax.fori_loop(0, rows // NORM_ROWS, step, 0)


class Grid:
    def __init__(self, shards):
        self.shards, self.across = shards, shards // 2
        self.me = lax.axis_index("fsdp")
        self.row, self.column = self.me // self.across, self.me % self.across
        self.others = [(self.me + ahead) % shards for ahead in range(1, shards)]
        self.mates = [self.row * self.across + (self.column + ahead) % self.across for ahead in range(1, self.across)]
        self.twin = (1 - self.row) * self.across + self.column
        self.near = self.mates + [self.twin]

    def is_near(self, shard):
        return jnp.logical_or(shard // self.across == self.row, shard % self.across == self.column)


class NearShards:
    scratch = staticmethod(lambda shards: [DMA((shards // 2,)), DMA((shards // 2,))])

    def __init__(self, grid, own, whole, at, send, receive):
        place = at(whole, grid.me, None)
        self.copies = [remote(own, place, send.at[i], receive.at[i], {"fsdp": peer}) for i, peer in enumerate(grid.near)]

    def start(self):
        for copy in self.copies:
            copy.start()

    def arrive(self):
        for copy in self.copies:
            copy.wait_recv()

    def finish(self):
        for copy in self.copies:
            copy.wait_send()


class FarShards:
    scratch = staticmethod(lambda shards: [DMA((2, shards // 2 - 1)), DMA((2, shards // 2 - 1))])

    def __init__(self, grid, near, whole, at, send, receive):
        self.copies = []
        for i, mate in enumerate(grid.mates):
            self.copies.append(remote(at(near, mate, 0), at(whole, mate, 0), send.at[0, i], receive.at[0, i], {"fsdp": grid.twin}))
            self.copies.append(remote(at(near, grid.twin, 1), at(whole, grid.twin, 1), send.at[1, i], receive.at[1, i], {"fsdp": mate}))

    def start(self):
        for copy in self.copies:
            copy.start()

    def finish(self):
        for copy in self.copies:
            copy.wait_recv()
            copy.wait_send()


class NearSums:
    @staticmethod
    def scratch(shards, rows, columns):
        across = shards // 2
        return [
            pltpu.VMEM((2, across - 1, rows // 2, columns), low),
            pltpu.VMEM((across, rows // 2, columns), low),
            DMA((2, across - 1)), DMA((2, across - 1)), DMA((across, 2)), DMA((across, 2)), DMA((across,)),
        ]

    def __init__(self, grid, part, out, at, relay, base, relay_send, relay_recv, near_send, near_recv, load_sem):
        self.relay, self.base = relay, base
        last = grid.across - 1
        half = base.shape[1]

        def near(source, slot, which, peer):
            target = out.at[slot, pl.ds(which * half, half)]
            return remote(source, target, near_send.at[slot, which], near_recv.at[slot, which], {"fsdp": peer})

        self.by_twin, self.by_mate, self.plain, self.joined, self.loads = [], [], [], [], []
        for i, mate in enumerate(grid.mates):
            far = (1 - grid.row) * grid.across + mate % grid.across
            self.by_twin.append(remote(at(part, far, 0), relay.at[0, i], relay_send.at[0, i], relay_recv.at[0, i], {"fsdp": grid.twin}))
            self.by_mate.append(remote(at(part, far, 1), relay.at[1, i], relay_send.at[1, i], relay_recv.at[1, i], {"fsdp": mate}))
            self.plain.append(near(at(part, mate, 1), i, 1, mate))
            self.joined.append(near(relay.at[0, i], i, 0, mate))
            self.loads.append(pltpu.make_async_copy(at(part, mate, 0), base.at[i], load_sem.at[i]))
        self.plain.append(near(at(part, grid.twin, 0), last, 0, grid.twin))
        self.joined.append(near(relay.at[1, 0], last, 1, grid.twin))
        self.loads.append(pltpu.make_async_copy(at(part, grid.twin, 1), base.at[last], load_sem.at[last]))

    def start(self):
        for copy in self.by_twin + self.by_mate + self.loads:
            copy.start()

    def start_plain(self):
        for copy in self.plain:
            copy.start()

    def join(self):
        for copy in self.by_twin + self.by_mate:
            copy.wait_recv()
        for copy in self.loads:
            copy.wait()
        last = self.base.shape[0] - 1
        for i in range(last):
            self.relay[0, i] = (self.base[i].astype(jnp.float32) + self.relay[0, i].astype(jnp.float32)).astype(low)
        total = self.base[last].astype(jnp.float32)
        for i in range(last):
            total = total + self.relay[1, i].astype(jnp.float32)
        self.relay[1, 0] = total.astype(low)
        for copy in self.joined:
            copy.start()

    def finish(self):
        for copy in self.by_twin + self.by_mate:
            copy.wait_send()
        for copy in self.plain + self.joined:
            copy.wait_recv()
            copy.wait_send()


def row_shard(depth):
    def at(ref, shard, half):
        if half is None:
            return ref.at[span(shard, depth)]
        return ref.at[span(2 * shard + half, depth // 2)]

    return at


def column_shard(rows, width):
    def at(ref, shard, half):
        if half is None:
            return ref.at[:, span(shard, width)]
        return ref.at[pl.ds(half * (rows // 2), rows // 2), span(shard, width)]

    return at


class HeldScatter(Scatter):
    @staticmethod
    def scratch(chips, rows, depth):
        return [
            pltpu.VMEM((2, rows, depth), low),
            pltpu.VMEM((chips, rows, depth), low),
            pltpu.VMEM((chips + 1, rows, depth), low),
            pltpu.VMEM((2, rows, depth), low),
            DMA((2,)), DMA((chips,)), DMA((2,)), DMA((chips + 1,)), DMA((2,)),
        ]

    def __init__(self, line, out, held, *refs):
        super().__init__(line, out, *refs[:-1])
        self.held, self.load_sem = held, refs[-1]

    def load(self, step):
        source = self.held.at[span(2 * self.line.target(step) + self.line.core, self.rows)]
        return pltpu.make_async_copy(source, self.term.at[step % 2], self.load_sem.at[step % 2])

    def share(self, step):
        source = self.held.at[span(2 * self.line.target(step) + 1 - self.line.core, self.rows)]
        return remote(source, self.shares.at[step], self.share_send.at[step % 2], self.share_recv.at[step], {"tp": self.line.partner})

    def mine(self, step):
        self.load(step).wait()

        @pl.when(step < self.line.chips - 1)
        def _():
            self.load(step + 1).start()

        return self.term[step % 2]


class Loads:
    @staticmethod
    def scratch(*operands):
        return [pltpu.VMEM(a.shape, a.dtype) for a in operands] + [DMA((len(operands),))]

    def __init__(self, sources, refs):
        self.refs = refs[: len(sources)]
        self.copies = [pltpu.make_async_copy(source, ref, refs[-1].at[i]) for i, (source, ref) in enumerate(zip(sources, self.refs))]

    def start(self):
        for copy in self.copies:
            copy.start()

    def wait(self, *which):
        for i in which:
            self.copies[i].wait()


class RowStores:
    @staticmethod
    def scratch(size, count, *results):
        return [pltpu.VMEM(a.shape, a.dtype) for a in results] + [DMA((len(results), count))]

    def __init__(self, size, count, refs, outs, sems):
        self.size, self.count, self.refs, self.outs, self.sems = size, count, refs, outs, sems

    def copies(self, index):
        here = span(index, self.size)
        return [pltpu.make_async_copy(a.at[here], b.at[here], self.sems.at[i, index]) for i, (a, b) in enumerate(zip(self.refs, self.outs))]

    def start(self, index):
        for copy in self.copies(index):
            copy.start()

    def wait(self):
        for index in range(self.count):
            for copy in self.copies(index):
                copy.wait()


def turned(block, sign):
    half = HEAD_DIM // 2
    lane = lax.broadcasted_iota(jnp.int32, block.shape, 1)
    width = block.shape[1]
    up = pltpu.roll(block, width - half, 1)
    down = pltpu.roll(block, half, 1)
    return jnp.where(lane % HEAD_DIM < half, -sign * up, sign * down)


def widened(table, width):
    return table if table.shape[1] == width else jnp.concatenate([table] * (width // table.shape[1]), axis=1)


def only_head(block, head):
    lane = lax.broadcasted_iota(jnp.int32, block.shape, 1)
    return jnp.where(lane // HEAD_DIM == head, block, jnp.zeros_like(block))


def causal(tile):
    key = lax.broadcasted_iota(jnp.int32, tile.shape, 0)
    query = lax.broadcasted_iota(jnp.int32, tile.shape, 1)
    return jnp.where(key <= query, tile, masked_score)


def over_keys(chunk, rows, visit):
    start = chunk * rows
    first = start // SEQ_LEN * SEQ_LEN

    def step(index, carry):
        visit(pl.multiple_of(first + index * rows, rows), False)
        return carry

    lax.fori_loop(0, (start - first) // rows, step, 0)
    visit(pl.multiple_of(start, rows), True)


def project_kernel(
    chips, shards,
    gain, inverse, activations_hbm, w_query, w_key, w_value, w_out, w_down,
    tokens_out, weight_out, full_out, qkv_out, keys_out, values_out, cosine_out, sine_out, down_near,
    weight, out_w, qkv, keys_t, values_t, cosine, sine, tokens, activations,
    load_sem, weight_send, weight_recv, weight_keep, table_sem, store_sem, near_send, near_recv, *gather_sems,
):
    line = Line(chips)
    rows = activations.shape[0]
    depth, width = w_query.shape
    grid = Grid(shards)
    shard, others = grid.me, grid.others
    gather = Gather(line, None, tokens, *gather_sems, parts=2)
    down = NearShards(grid, w_down, down_near, column_shard(*w_down.shape), near_send, near_recv)
    parts = (w_query, w_key, w_value, w_out)

    def place(part):
        if part == 3:
            return out_w.at[:, span(shard, depth)]
        return weight.at[span(shard, depth), pl.ds(part * width, width)]

    def give(ahead, part):
        return remote(parts[part], place(part), weight_send.at[ahead, part], weight_recv.at[ahead, part], {"fsdp": others[ahead]})

    def keep(part):
        return pltpu.make_async_copy(parts[part], place(part), weight_keep.at[part])

    tables = [
        pltpu.make_async_copy(source, out, table_sem.at[i])
        for i, (source, out) in enumerate(((cosine, cosine_out), (sine, sine_out), (weight, weight_out), (out_w, full_out)))
    ]

    def stores(index):
        here = span(index, rows)
        return [
            pltpu.make_async_copy(qkv.at[here], qkv_out.at[here], store_sem.at[0, index]),
            pltpu.make_async_copy(keys_t.at[:, here], keys_out.at[:, here], store_sem.at[1, index]),
            pltpu.make_async_copy(values_t.at[:, here], values_out.at[:, here], store_sem.at[2, index]),
            pltpu.make_async_copy(tokens.at[here], tokens_out.at[here], store_sem.at[3, index]),
        ]

    def norm(index, carry):
        there = span(line.me * (rows // NORM_ROWS) + index, NORM_ROWS)
        tokens[there, :] = normed(activations[span(index, NORM_ROWS), :], gain[...]).astype(low)
        return carry

    load = pltpu.make_async_copy(activations_hbm, activations, load_sem)
    load.start()
    line.hello([{"fsdp": other} for other in others])
    load.wait()
    lax.fori_loop(0, rows // NORM_ROWS, norm, 0)
    line.ready(others)
    gather.start()
    for part in range(4):
        keep(part).start()
        for ahead in range(shards - 1):
            give(ahead, part).start()
    position = lax.broadcasted_iota(jnp.int32, (inverse.shape[0], SEQ_LEN), 1).astype(jnp.float32)
    angle = position * inverse[...]
    for table, turn in ((cosine, jnp.cos(angle).T), (sine, jnp.sin(angle).T)):
        table[...] = jnp.concatenate([turn] * (LANES // turn.shape[1]), axis=1)
    for copy in tables[:2]:
        copy.start()

    def project(index):
        here = span(index, rows)
        table = span(index % (SEQ_LEN // rows), rows)
        for part in range(3):
            columns = pl.ds(part * width, width)
            block = dot(tokens[here, :], weight[:, columns])
            if part < 2:
                block = block * widened(cosine[table, :], width) + turned(block, 1.0) * widened(sine[table, :], width)
            qkv[here, columns] = block.astype(low)
            if part:
                (keys_t, values_t)[part - 1][:, here] = block.T.astype(low)
        for copy in stores(index):
            copy.start()

    def step(index, carry):
        @pl.when(jnp.logical_and(index >= 1, index < chips))
        def _():
            gather.step(index)

        @pl.when(index == 2)
        def _():
            for part in range(4):
                keep(part).wait()
                for ahead in range(shards - 1):
                    give(ahead, part).wait_recv()
            for copy in tables[2:]:
                copy.start()
            down.start()

        def side(turn, carry):
            distance, which, across = index - 1, turn % 3, turn // 3
            chip = jnp.where(which == 0, line.chip - distance, jnp.where(which == 1, line.chip + distance, line.chip))
            there = jnp.logical_and(chip >= 0, chip < chips)

            @pl.when(jnp.logical_and(there, jnp.logical_and(index >= 2, jnp.logical_or(which < 2, index == 2))))
            def _():
                @pl.when(across == 1)
                def _():
                    gather.arrive_across(chip)

                project(2 * chip + jnp.where(across == 1, 1 - line.core, line.core))

            return carry

        lax.fori_loop(0, 6, side, 0)
        return carry

    lax.fori_loop(0, chips + 1, step, 0)
    gather.finish(False)
    for part in range(4):
        for ahead in range(shards - 1):
            give(ahead, part).wait_send()
    for copy in tables:
        copy.wait()
    for index in range(2 * chips):
        for copy in stores(index):
            copy.wait()
    down.arrive()
    down.finish()


def project(chips, shards, activations, gain, w_query, w_key, w_value, w_out, inverse, w_down):
    rows, depth = activations.shape
    group_rows = 2 * chips * rows
    width = w_query.shape[1]
    shape = jax.ShapeDtypeStruct
    held = [
        shape((depth, 3 * width), low),
        shape((width, depth), low),
        shape((group_rows, 3 * width), low),
        shape((width, group_rows), low),
        shape((width, group_rows), low),
        shape((SEQ_LEN, LANES), jnp.float32),
        shape((SEQ_LEN, LANES), jnp.float32),
    ]
    return pl.pallas_call(
        lambda *refs: project_kernel(chips, shards, *refs),
        in_specs=[VMEM] * 2 + [ANYWHERE] * 6,
        out_specs=[ANYWHERE] * 9,
        out_shape=[shape((group_rows, depth), low)] + held + [shape((w_down.shape[0], depth), low)],
        scratch_shapes=[pltpu.VMEM(a.shape, a.dtype) for a in held] + [
            pltpu.VMEM((group_rows, depth), low),
            pltpu.VMEM((rows, depth), jnp.float32),
            DMA, DMA((shards - 1, 4)), DMA((shards - 1, 4)), DMA((4,)), DMA((4,)), DMA((4, 2 * chips)),
        ] + NearShards.scratch(shards) + Gather.scratch(chips, 2),
        compiler_params=pltpu.CompilerParams(collective_id=1, has_side_effects=True, vmem_limit_bytes=63 << 20),
        cost_estimate=pl.CostEstimate(flops=6 * group_rows * depth * width, bytes_accessed=4 * group_rows * depth, transcendentals=0),
        name="project",
    )(gain, inverse, activations, w_query, w_key, w_value, w_out, w_down)


def attend_chunk(chunk, rows, qkv, values_t, heads_ref, acc, out, top_ref, sum_ref):
    width = acc.shape[0]
    heads = width // HEAD_DIM
    scaled = qkv[span(chunk, rows), pl.ds(0, width)] * low(HEAD_DIM**-0.5)
    for head in range(heads):
        heads_ref[head] = only_head(scaled, head)
    acc[...] = jnp.zeros_like(acc)
    top_ref[...] = jnp.full_like(top_ref, masked_score)
    sum_ref[...] = jnp.zeros_like(sum_ref)

    def visit(offset, diagonal):
        key_block = qkv[pl.ds(offset, rows), pl.ds(width, width)]
        for head in range(heads):
            feature = pl.ds(head * HEAD_DIM, HEAD_DIM)
            one = pl.ds(head, 1)
            scores = dot(key_block, heads_ref[head], NT)
            if diagonal:
                scores = causal(scores)
            old = top_ref[one, :]
            top = jnp.maximum(old, jnp.max(scores, axis=0, keepdims=True))
            shrink = jnp.exp(old - top)
            weights = jnp.exp(scores - top)
            top_ref[one, :] = top
            sum_ref[one, :] = sum_ref[one, :] * shrink + jnp.sum(weights, axis=0, keepdims=True)
            acc[feature, :] = acc[feature, :] * shrink + dot(values_t[feature, pl.ds(offset, rows)], weights.astype(low))

    over_keys(chunk, rows, visit)
    for head in range(heads):
        feature = pl.ds(head * HEAD_DIM, HEAD_DIM)
        acc[feature, :] = acc[feature, :] / sum_ref[pl.ds(head, 1), :]
    out[...] = acc[...].T.astype(low)


def attend_kernel(
    chips, shards,
    gain, *refs,
):
    sources, (w_gate, w_up, down_near) = refs[:5], refs[5:8]
    hidden_out, tokens_out, mixed_out, totals, grads_out, gate_all, up_all, down_far = refs[8:16]
    hidden, tokens, rows_sem, mixed, mixed_sem = refs[-5:]
    refs = refs[:-5]
    loads = Loads(sources, refs[16:22])
    cotangent, qkv, values_t, w_out, activations = loads.refs
    heads_ref, acc, out, top_ref, sum_ref, grads = refs[22:28]
    loads.start()
    line = Line(chips)
    grid = Grid(shards)
    rows_of = row_shard(w_gate.shape[0])
    line.hello([{"fsdp": peer} for peer in grid.near])
    down = FarShards(grid, down_near, down_far, column_shard(down_near.shape[0], down_near.shape[1] // shards), *refs[28:30])
    gate_near, gate_far = NearShards(grid, w_gate, gate_all, rows_of, *refs[30:32]), FarShards(grid, gate_all, gate_all, rows_of, *refs[32:34])
    up_near, up_far = NearShards(grid, w_up, up_all, rows_of, *refs[34:36]), FarShards(grid, up_all, up_all, rows_of, *refs[36:38])
    sems = refs[38:]
    rows, depth = hidden.shape
    pair = 2 * rows
    states = RowStores(NORM_ROWS, rows // NORM_ROWS, (hidden, tokens), (hidden_out, tokens_out), rows_sem)
    blends = RowStores(pair, chips, (mixed,), (mixed_out,), mixed_sem)
    scatter = Scatter(line, hidden, *sems[:8])
    loads.wait(0)
    grads[...] = cotangent[...].astype(low)
    gather = Gather(line, grads, grads_out, *sems[8:])
    line.ready(grid.near)
    gather.start()
    gate_near.start()
    down.start()
    loads.wait(1, 2, 3, 4)

    def term(index):
        chunk = line.target(index)
        attend_chunk(chunk, pair, qkv, values_t, heads_ref, acc, out, top_ref, sum_ref)
        mixed[span(chunk, pair), :] = out[...]
        blends.start(chunk)
        totals[:, span(chunk, pair)] = top_ref[...] + jnp.log(sum_ref[...])
        scatter.free(index)

        def tile(place, carry):
            columns = span(place, 512)
            scatter.term[index % scatter.slots, :, columns] = dot(out[...], w_out[:, columns]).astype(low)
            return carry

        lax.fori_loop(0, depth // 512, tile, 0)
        scatter.share(index).start()

    def step(index, carry):
        def phase(which, carry):
            @pl.when(jnp.logical_and(which == 1, index < chips))
            def _():
                term(index)

            lax.fori_loop(0, jnp.where(which == 1, 0, chips), scatter.due(index, which == 2), 0)
            return carry

        lax.fori_loop(0, 3, phase, 0)

        @pl.when(jnp.logical_and(index >= 1, index < chips))
        def _():
            gather.step(index)

        @pl.when(index == 1)
        def _():
            up_near.start()

        @pl.when(index == min(2, chips))
        def _():
            gate_near.arrive()
            gate_far.start()

        @pl.when(index == min(3, chips))
        def _():
            up_near.arrive()
            up_far.start()

        return carry

    lax.fori_loop(0, chips + 1, step, 0)

    def norm(here):
        state = activations[here, :] + hidden[here, :]
        hidden[here, :] = state
        tokens[here, :] = normed(state, gain[...]).astype(low)

    by_rows(rows, norm, states)
    scatter.finish()
    gather.finish(True)
    blends.wait()
    states.wait()
    for near in (gate_near, up_near):
        near.finish()
    for far in (down, gate_far, up_far):
        far.finish()


def attend(chips, shards, qkv, values_t, w_out, activations, cotangent, gain, w_gate, w_up, down_near):
    rows, depth = activations.shape
    pair = 2 * rows
    group_rows = chips * pair
    width = w_out.shape[0]
    heads = width // HEAD_DIM
    shape = jax.ShapeDtypeStruct
    stored = [shape((rows, depth), jnp.float32), shape((rows, depth), low), shape((group_rows, width), low)]
    return pl.pallas_call(
        lambda *refs: attend_kernel(chips, shards, *refs),
        in_specs=[VMEM] + [ANYWHERE] * 8,
        out_specs=[ANYWHERE] * 3 + [VMEM] + [ANYWHERE] * 4,
        out_shape=stored + [
            shape((heads, group_rows), jnp.float32),
            shape((group_rows, depth), low),
            shape((depth, w_gate.shape[1]), low),
            shape((depth, w_gate.shape[1]), low),
            shape(down_near.shape, low),
        ],
        scratch_shapes=Loads.scratch(cotangent, qkv, values_t, w_out, activations) + [
            pltpu.VMEM((heads, pair, width), low),
            pltpu.VMEM((width, pair), jnp.float32),
            pltpu.VMEM((pair, width), low),
            pltpu.VMEM((heads, pair), jnp.float32),
            pltpu.VMEM((heads, pair), jnp.float32),
            pltpu.VMEM((rows, depth), low),
        ] + FarShards.scratch(shards) + (NearShards.scratch(shards) + FarShards.scratch(shards)) * 2 + Scatter.scratch(chips, rows, depth) + Gather.scratch(chips)
        + RowStores.scratch(NORM_ROWS, rows // NORM_ROWS, *stored[:2]) + RowStores.scratch(pair, chips, stored[2]),
        compiler_params=pltpu.CompilerParams(collective_id=2, has_side_effects=True, vmem_limit_bytes=63 << 20),
        cost_estimate=pl.CostEstimate(flops=2 * group_rows * (SEQ_LEN + depth) * width, bytes_accessed=4 * group_rows * depth, transcendentals=group_rows * SEQ_LEN * heads // 2),
        name="attend",
    )(gain, cotangent, qkv, values_t, w_out, activations, w_gate, w_up, down_near)


def back_chunk(chunk, rows, grad, qkv, keys_t, mixed, totals, dkey, dvalue, heads_ref, grads_ref, acc, inner_ref):
    width = acc.shape[0]
    heads = width // HEAD_DIM
    here = span(chunk, rows)
    scaled = qkv[here, pl.ds(0, width)] * low(HEAD_DIM**-0.5)
    product = grad.astype(jnp.float32) * mixed[here, :].astype(jnp.float32)
    shape = (inner_ref.shape[0], width)
    pick = (lax.broadcasted_iota(jnp.int32, shape, 1) // HEAD_DIM == lax.broadcasted_iota(jnp.int32, shape, 0)).astype(jnp.float32)
    inner_ref[...] = lax.dot_general(pick, product, NT, precision=lax.Precision.HIGHEST, preferred_element_type=jnp.float32)
    for head in range(heads):
        heads_ref[head] = only_head(scaled, head)
        grads_ref[head] = only_head(grad, head)
    acc[...] = jnp.zeros_like(acc)

    def visit(offset, diagonal):
        keys = pl.ds(offset, rows)
        key_block = qkv[keys, pl.ds(width, width)]
        value_block = qkv[keys, pl.ds(2 * width, width)]
        key_sum, value_sum = dkey[keys, :], dvalue[keys, :]
        for head in range(heads):
            feature = pl.ds(head * HEAD_DIM, HEAD_DIM)
            scores = dot(key_block, heads_ref[head], NT)
            if diagonal:
                scores = causal(scores)
            probs = jnp.exp(scores - totals[pl.ds(head, 1), here])
            dprobs = dot(value_block, grads_ref[head], NT)
            dscores = (probs * (dprobs - inner_ref[pl.ds(head, 1), :])).astype(low)
            value_sum = value_sum + dot(probs.astype(low), grads_ref[head])
            key_sum = key_sum + dot(dscores, heads_ref[head])
            acc[feature, :] = acc[feature, :] + dot(keys_t[feature, keys], dscores)
        dkey[keys, :] = key_sum
        dvalue[keys, :] = value_sum

    over_keys(chunk, rows, visit)


def back_kernel(
    chips, shards,
    branch, terms, inner, grads, grad_both, *refs,
):
    sources, (down, branch_out, qkv_out, grad_down, grad_out, both_from) = refs[:7], refs[7:13]
    qkv_grad, qkv_sem = refs[-2:]
    refs = refs[:-2]
    loads = Loads(sources, refs[13:21])
    w_out, qkv, keys_t, mixed, totals, cosine, sine = loads.refs
    inner_chunk, grad_chunk, down_sum, down_tile, out_sum, out_stage, out_from, branch_chunk, dkey, dvalue = refs[21:31]
    heads_ref, grads_ref, acc, inner_ref, inner_sem, grad_sem, branch_sem, tile_sem, out_send, out_recv = refs[31:41]
    sums = refs[41:48]
    sems = refs[48:]
    line = Line(chips)
    rows, depth = down.shape
    pair = 2 * rows
    width = w_out.shape[0]
    results = RowStores(pair, chips, (qkv_grad,), (qkv_out,), qkv_sem)
    scatter = HeldScatter(line, down, terms, *sems[:9])
    gather = Gather(line, branch, branch_out, *sems[9:], parts=2)

    def fetch(step):
        return pltpu.make_async_copy(inner.at[span(line.target(step), pair)], inner_chunk, inner_sem)

    def fetch_grad(step):
        return pltpu.make_async_copy(grads.at[span(line.target(step), pair)], grad_chunk, grad_sem)

    grid = Grid(shards)
    shard, others = grid.me, grid.others
    columns_out = depth // shards
    both = NearSums(grid, grad_both, both_from, row_shard(columns_out), *sums)

    def give(turn):
        return remote(out_stage.at[turn], out_from.at[turn], out_send.at[turn], out_recv.at[turn], {"fsdp": others[turn]})

    def keep_tile(place):
        return pltpu.make_async_copy(down_tile, grad_down.at[span(place, 256)], tile_sem)

    line.hello([{"fsdp": other} for other in others])
    loads.start()
    fetch(0).start()
    fetch_grad(0).start()
    scatter.load(0).start()
    line.ready(others)
    gather.start()
    both.start()
    out_sum[...] = jnp.zeros_like(out_sum)
    dkey[...] = jnp.zeros_like(dkey)
    dvalue[...] = jnp.zeros_like(dvalue)

    def unrotated(block, chunk):
        table = span(chunk % (SEQ_LEN // pair), pair)
        return (block * widened(cosine[table, :], width) + turned(block * widened(sine[table, :], width), -1.0)).astype(low)

    def attention(chunk):
        gather.arrive_across(chunk)
        copy = pltpu.make_async_copy(branch_out.at[span(chunk, pair)], branch_chunk, branch_sem)
        copy.start()
        copy.wait()
        out_sum[...] += dot(mixed[span(chunk, pair), :], branch_chunk[...], TN)
        grad = dot(branch_chunk[...], w_out[...], NT).astype(low)
        back_chunk(chunk, pair, grad, qkv, keys_t, mixed, totals, dkey, dvalue, heads_ref, grads_ref, acc, inner_ref)
        qkv_grad[span(chunk, pair), pl.ds(0, width)] = unrotated(acc[...].T * HEAD_DIM**-0.5, chunk)

    def close():
        def part(chunk, carry):
            here = span(chunk, pair)
            qkv_grad[here, pl.ds(width, width)] = unrotated(dkey[here, :], chunk)
            qkv_grad[here, pl.ds(2 * width, width)] = dvalue[here, :].astype(low)
            results.start(chunk)
            return carry

        lax.fori_loop(0, chips, part, 0)

    def step(index, carry):
        @pl.when(index == 0)
        def _():
            loads.wait(*range(7))
            gather.keep().wait()

        @pl.when(index < chips)
        def _():
            scatter.free(index)
            scatter.share(index).start()

        @pl.when(index == chips)
        def _():
            for turn in range(shards - 1):
                out_stage[turn] = out_sum[:, span(others[turn], columns_out)].astype(low)
                give(turn).start()
            close()

        lax.fori_loop(0, chips, scatter.due(index, None), 0)

        @pl.when(jnp.logical_and(index >= 1, index < chips))
        def _():
            gather.step(index)

        @pl.when(index == 1)
        def _():
            both.start_plain()

        @pl.when(index == 2)
        def _():
            both.join()

        @pl.when(index < chips)
        def _():
            attention(line.target(chips - 1 - index))

        def weights(turn, carry):
            fetch(turn).wait()
            fetch_grad(turn).wait()

            def tile(place, carry):
                here = span(place, 256)
                part = dot(inner_chunk[:, here], grad_chunk[...], TN)

                @pl.when(turn == 0)
                def _():
                    down_sum[here, :] = part

                @pl.when(turn > 0)
                def _():
                    down_sum[here, :] += part

                @pl.when(turn == chips - 1)
                def _():
                    @pl.when(place > 0)
                    def _():
                        keep_tile(place - 1).wait()

                    down_tile[...] = down_sum[here, :].astype(low)
                    keep_tile(place).start()

                return carry

            lax.fori_loop(0, down_sum.shape[0] // 256, tile, 0)

            @pl.when(turn < chips - 1)
            def _():
                fetch(turn + 1).start()
                fetch_grad(turn + 1).start()

            return carry

        lax.fori_loop(jnp.where(index == 0, 0, index + 1), jnp.minimum(index + 2, chips), weights, 0)
        return carry

    lax.fori_loop(0, chips + 1, step, 0)
    total = out_sum[:, span(shard, columns_out)]
    for turn in range(shards - 1):
        give(turn).wait_recv()
        total = total + out_from[turn].astype(jnp.float32)
    grad_out[...] = total
    for turn in range(shards - 1):
        give(turn).wait_send()
    keep_tile(down_sum.shape[0] // 256 - 1).wait()
    both.finish()
    results.wait()
    scatter.finish()
    gather.finish(False)


def back(chips, shards, branch, terms, inner, grads, grad_both, w_out, qkv, keys_t, mixed, totals, cosine, sine):
    rows, depth = branch.shape
    pair = 2 * rows
    group_rows = chips * pair
    width = w_out.shape[0]
    hidden = inner.shape[1]
    heads = width // HEAD_DIM
    shape = jax.ShapeDtypeStruct
    held = (w_out, qkv, keys_t, mixed, totals, cosine, sine)
    return pl.pallas_call(
        lambda *refs: back_kernel(chips, shards, *refs),
        in_specs=[VMEM] + [ANYWHERE] * 11,
        out_specs=[VMEM, ANYWHERE, ANYWHERE, ANYWHERE, VMEM, ANYWHERE],
        out_shape=[
            shape((rows, depth), jnp.float32),
            shape((group_rows, depth), low),
            shape((group_rows, 3 * width), low),
            shape((hidden, depth), low),
            shape((width, depth // shards), jnp.float32),
            shape((shards // 2, depth // shards, grad_both.shape[1]), low),
        ],
        scratch_shapes=Loads.scratch(*held) + [
            pltpu.VMEM((pair, hidden), low),
            pltpu.VMEM((pair, depth), low),
            pltpu.VMEM((hidden, depth), jnp.float32),
            pltpu.VMEM((256, depth), low),
            pltpu.VMEM((width, depth), jnp.float32),
            pltpu.VMEM((shards - 1, width, depth // shards), low),
            pltpu.VMEM((shards - 1, width, depth // shards), low),
            pltpu.VMEM((pair, depth), low),
            pltpu.VMEM((group_rows, width), jnp.float32),
            pltpu.VMEM((group_rows, width), jnp.float32),
            pltpu.VMEM((heads, pair, width), low),
            pltpu.VMEM((heads, pair, width), low),
            pltpu.VMEM((width, pair), jnp.float32),
            pltpu.VMEM((8, pair), jnp.float32),
            DMA, DMA, DMA, DMA, DMA((shards - 1,)), DMA((shards - 1,)),
        ] + NearSums.scratch(shards, depth // shards, grad_both.shape[1]) + HeldScatter.scratch(chips, rows, depth) + Gather.scratch(chips, 2)
        + RowStores.scratch(pair, chips, shape((group_rows, 3 * width), low)),
        compiler_params=pltpu.CompilerParams(collective_id=4, has_side_effects=True, vmem_limit_bytes=67043328),
        cost_estimate=pl.CostEstimate(flops=1 << 20, bytes_accessed=1 << 20, transcendentals=0),
        name="back",
    )(branch, terms, inner, grads, grad_both, *held)


def spread_kernel(
    chips, shards,
    gain, gain_part, qkv_hbm, weight_hbm, activations_hbm, attn_tokens, grad_down,
    input_out, qkv_out, gain_sum, down_from,
    input_part, rows_sem, grad_qkv, sum_sem, qkv_grad, weight, activations, held_sem,
    attn_cols, qkv_stage, qkv_from, gains, gains_tp, gains_fsdp,
    attn_sem, qkv_send, qkv_recv, tp_send, tp_recv, fsdp_send, fsdp_recv, *sems,
):
    line = Line(chips)
    size = 2 * chips
    rows, depth = input_part.shape
    pair = 2 * rows
    grid = Grid(shards)
    shard = grid.me
    columns = depth // shards
    loads = Loads((qkv_hbm, weight_hbm, activations_hbm), (qkv_grad, weight, activations, held_sem))
    down = NearSums(grid, grad_down, down_from, column_shard(grad_down.shape[0], columns), *sems[:7])
    scatter = Scatter(line, input_part, *sems[7:])

    def peer(turn):
        return (shard + 1 + turn) % shards

    def fetch(turn):
        return pltpu.make_async_copy(attn_tokens.at[:, span(peer(turn), columns)], attn_cols.at[turn % 2], attn_sem.at[turn % 2])

    def give(turn):
        return remote(qkv_stage.at[turn], qkv_from.at[turn], qkv_send.at[turn], qkv_recv.at[turn], {"fsdp": peer(turn)})

    def tell_tp(ahead):
        return remote(gains, gains_tp.at[line.me], tp_send.at[ahead - 1], tp_recv.at[line.me], {"tp": (line.me + ahead) % size})

    def tell_fsdp(ahead):
        return remote(gains, gains_fsdp.at[shard], fsdp_send.at[ahead - 1], fsdp_recv.at[shard], {"fsdp": (shard + ahead) % shards})

    for ahead in range(1, size):
        hello({"tp": (line.me + ahead) % size})
    for ahead in range(1, shards):
        hello({"fsdp": (shard + ahead) % shards})
    loads.start()
    fetch(0).start()
    loads.wait(0, 1)
    pl.semaphore_wait(pltpu.get_barrier_semaphore(), size - 1 + shards - 1)
    down.start()
    down.start_plain()

    def weights(turn, carry):
        @pl.when(turn < shards - 1)
        def _():
            fetch(turn + 1).start()

        fetch(turn).wait()
        part = dot(attn_cols[turn % 2], qkv_grad[...], TN)

        @pl.when(turn < shards - 1)
        def _():
            qkv_stage[turn] = part.astype(low)
            give(turn).start()

        @pl.when(turn == shards - 1)
        def _():
            grad_qkv[...] = part

        return carry

    def term(index):
        scatter.free(index)
        here = span(line.target(index), pair)

        def tile(place, carry):
            there = span(place, 512)
            scatter.term[index % scatter.slots, :, there] = dot(qkv_grad[here, :], weight[there, :], NT).astype(low)
            return carry

        lax.fori_loop(0, depth // 512, tile, 0)
        scatter.share(index).start()

    def step(index, carry):
        def phase(which, carry):
            @pl.when(jnp.logical_and(which == 1, index < chips))
            def _():
                term(index)

            @pl.when(jnp.logical_and(which == 2, index < 2))
            def _():
                lax.fori_loop(index, jnp.where(index == 0, 1, shards), weights, 0)

            @pl.when(jnp.logical_and(which == 2, index == 2))
            def _():
                down.join()

            outer = jnp.logical_or(which == 0, which == 3)
            lax.fori_loop(0, jnp.where(outer, chips, 0), scatter.due(index, which == 3), 0)
            return carry

        lax.fori_loop(0, 4, phase, 0)
        return carry

    lax.fori_loop(0, chips + 1, step, 0)
    gains[0:1, :] = jnp.zeros((1, depth), jnp.float32)
    gains[1:2, :] = gain_part[...]

    def norm(here):
        part, grad = norm_back(activations[here, :], gain[...], input_part[here, :])
        input_part[here, :] = part
        gains[0:1, :] += grad

    loads.wait(2)
    results = RowStores(NORM_ROWS, rows // NORM_ROWS, (input_part,), (input_out,), rows_sem)
    by_rows(rows, norm, results)

    gains_tp[line.me] = gains[...]
    for ahead in range(1, size):
        tell_tp(ahead).start()
    for turn in range(shards - 1):
        give(turn).wait_recv()
        grad_qkv[...] += qkv_from[turn].astype(jnp.float32)
    summed = RowStores(columns, 1, (grad_qkv,), (qkv_out,), sum_sem)
    summed.start(0)
    for ahead in range(1, size):
        source = (line.me + ahead) % size
        remote(gains, gains_tp.at[source], tp_send.at[0], tp_recv.at[source], {"tp": source}).wait_recv()
    total = gains_tp[0]
    for source in range(1, size):
        total = total + gains_tp[source]
    for ahead in range(1, size):
        tell_tp(ahead).wait_send()
    gains[...] = total
    gains_fsdp[shard] = total
    for ahead in range(1, shards):
        tell_fsdp(ahead).start()
    for ahead in range(1, shards):
        source = (shard + ahead) % shards
        remote(gains, gains_fsdp.at[source], fsdp_send.at[0], fsdp_recv.at[source], {"fsdp": source}).wait_recv()
    total = gains_fsdp[0]
    for source in range(1, shards):
        total = total + gains_fsdp[source]
    gain_sum[...] = total
    for ahead in range(1, shards):
        tell_fsdp(ahead).wait_send()
    for turn in range(shards - 1):
        give(turn).wait_send()
    down.finish()
    results.wait()
    summed.wait()
    scatter.finish()


def spread(chips, shards, qkv_grad, weight, activations, gain, gain_part, attn_tokens, grad_down):
    group_rows = qkv_grad.shape[0]
    rows, depth = activations.shape
    width = qkv_grad.shape[1] // 3
    columns = depth // shards
    size = 2 * chips
    shape = jax.ShapeDtypeStruct
    stored = [shape((rows, depth), jnp.float32), shape((columns, 3 * width), jnp.float32)]
    return pl.pallas_call(
        lambda *refs: spread_kernel(chips, shards, *refs),
        in_specs=[VMEM] * 2 + [ANYWHERE] * 5,
        out_specs=[ANYWHERE] * 2 + [VMEM, ANYWHERE],
        out_shape=stored + [
            shape((2, depth), jnp.float32),
            shape((shards // 2, grad_down.shape[0], columns), low),
        ],
        scratch_shapes=RowStores.scratch(NORM_ROWS, rows // NORM_ROWS, stored[0]) + RowStores.scratch(columns, 1, stored[1]) + Loads.scratch(qkv_grad, weight, activations) + [
            pltpu.VMEM((2, group_rows, columns), low),
            pltpu.VMEM((shards - 1, columns, 3 * width), low),
            pltpu.VMEM((shards - 1, columns, 3 * width), low),
            pltpu.VMEM((2, depth), jnp.float32),
            pltpu.VMEM((size, 2, depth), jnp.float32),
            pltpu.VMEM((shards, 2, depth), jnp.float32),
            DMA((2,)), DMA((shards - 1,)), DMA((shards - 1,)),
            DMA((size - 1,)), DMA((size,)), DMA((shards - 1,)), DMA((shards,)),
        ] + NearSums.scratch(shards, grad_down.shape[0], columns) + Scatter.scratch(chips, rows, depth),
        compiler_params=pltpu.CompilerParams(collective_id=5, has_side_effects=True, vmem_limit_bytes=63 << 20),
        cost_estimate=pl.CostEstimate(flops=1 << 20, bytes_accessed=1 << 20, transcendentals=0),
        name="spread",
    )(gain, gain_part, qkv_grad, weight, activations, attn_tokens, grad_down)


def chip_at(place, chips):
    return jnp.where(2 * place < chips, 2 * place, 2 * (chips - 1 - place) + 1)


def place_of(chip, chips):
    return jnp.where(chip % 2 == 0, chip // 2, chips - 1 - chip // 2)


def feed_kernel(
    chips, shards,
    gain, hidden_hbm, cotangent_hbm, tokens, grads_hbm, w_gate, w_up, w_down, gate_all, up_all, down_near, down_far,
    hidden_grad_out, branch_out, gain_part, inner_out, grad_both, down_out,
    hidden_grad, branch, rows_sem, hidden_state, cotangent, state_sem, down_tile, down_sem, tokens_all, gate_w, up_w, down_w, grads, inner, gate_grad, up_grad, term, from_core, from_ring, total, tile_gate, tile_up,
    load_sem, own_sem, grad_sem, store_sem, tile_sem,
    ring_send, ring_recv, core_send, core_recv, share_send, share_recv, total_send, total_recv,
):
    rows, depth = hidden_grad.shape
    pair = 2 * rows
    width = gate_w.shape[1]
    me = lax.axis_index("tp")
    chip, core = me // 2, me % 2
    place = place_of(chip, chips)
    following = {"tp": 2 * chip_at((place + 1) % chips, chips) + core}
    before = {"tp": 2 * chip_at((place + chips - 1) % chips, chips) + core}
    partner = {"tp": 2 * chip + 1 - core}

    grid = Grid(shards)
    part = w_gate.shape[0]

    def load(array, source, shard, tile, whole):
        cut = span(tile, 256)
        if array == 2:
            place = lambda ref: ref.at[cut, span(shard, part)]
            own = lambda ref: ref.at[cut]
        else:
            place = lambda ref: ref.at[span(shard, part), cut]
            own = lambda ref: ref.at[:, cut]
        target = place((gate_w, up_w, down_w)[array])
        return pltpu.make_async_copy(place(source) if whole else own(source), target, load_sem.at[array, shard, tile])

    def load_weights(tile, carry):
        for shard in range(shards):
            own, near = grid.me == shard, grid.is_near(shard)

            @pl.when(own)
            def _():
                for array, source in enumerate((w_gate, w_up, w_down)):
                    load(array, source, shard, tile, False).start()

            @pl.when(jnp.logical_not(own))
            def _():
                for array, source in enumerate((gate_all, up_all)):
                    load(array, source, shard, tile, True).start()

            @pl.when(jnp.logical_and(near, jnp.logical_not(own)))
            def _():
                load(2, down_near, shard, tile, True).start()

            @pl.when(jnp.logical_not(near))
            def _():
                load(2, down_far, shard, tile, True).start()

        return carry

    own = pltpu.make_async_copy(tokens, tokens_all.at[span(me, rows)], own_sem)
    states = Loads((hidden_hbm, cotangent_hbm), (hidden_state, cotangent, state_sem))

    def source(slot):
        return chip_at((place + chips - slot) % chips, chips)

    def fetch(slot):
        return pltpu.make_async_copy(grads_hbm.at[span(source(slot), pair)], grads.at[slot % 2], grad_sem.at[slot % 2])

    def block(slot):
        return tokens_all.at[span(2 * source(slot) + core, rows)]

    def to_ring(slot):
        return remote(block(slot), block(slot), ring_send.at[slot], ring_recv.at[slot], following)

    def to_core(slot):
        return remote(block(slot), block(slot), core_send.at[slot], core_recv.at[slot], partner)

    def store(slot):
        return pltpu.make_async_copy(inner.at[slot], inner_out.at[span(source(slot), pair)], store_sem.at[slot])

    def keep_down(slot, tile):
        there = down_out.at[span(source(slot), pair), span(tile, 256)]
        return pltpu.make_async_copy(down_tile.at[tile % 2], there, down_sem.at[tile % 2])

    def down_term(slot, carry):
        def tile(index, carry):
            @pl.when(index > 1)
            def _():
                keep_down(slot, index - 2).wait()

            down_tile[index % 2] = dot(inner[slot], down_w[:, span(index, 256)]).astype(low)
            keep_down(slot, index).start()
            return carry

        lax.fori_loop(0, depth // 256, tile, 0)
        for index in range(depth // 256 - 2, depth // 256):
            keep_down(slot, index).wait()
        return carry

    def share(slot):
        place = jnp.where(slot == 0, 0, 1 + slot % 2)
        return remote(term.at[span(1 - core, rows)], from_core.at[place], share_send, share_recv.at[place], partner)

    def pass_on(slot):
        return remote(total.at[slot % 2], from_ring.at[slot - 1], total_send.at[slot % 2], total_recv.at[slot - 1], following)

    for device in (following, before, partner):
        hello(device)
    own.start()
    fetch(0).start()
    lax.fori_loop(0, width // 256, load_weights, 0)
    own.wait()
    pl.semaphore_wait(pltpu.get_barrier_semaphore(), 3)

    def step(slot, carry):
        here = slot % 2
        wide_rows = span(source(slot), pair)
        mine = span(core, rows)

        @pl.when(slot > 0)
        def _():
            to_ring(slot - 1).wait_recv()

        @pl.when(slot < chips - 1)
        def _():
            to_ring(slot).start()
            fetch(slot + 1).start()

        to_core(slot).start()

        @pl.when(slot == 1)
        def _():
            states.start()

        to_core(slot).wait_recv()
        fetch(slot).wait()

        def narrow(tile, carry):
            columns = span(tile, 256)

            @pl.when(slot == 0)
            def _():
                for shard in range(shards):
                    for array, source in enumerate((gate_all, up_all, down_near)):
                        load(array, source, shard, tile, True).wait()

            token = tokens_all[wide_rows, :]
            gate = dot(token, gate_w[:, columns])
            up = dot(token, up_w[:, columns])
            grad = dot(grads[here], down_w[columns, :], NT)
            squash = jax.nn.sigmoid(gate)
            act = gate * squash
            inner[slot, :, columns] = (act * up).astype(low)
            up_grad[wide_rows, columns] = (grad * act).astype(low)
            gate_grad[wide_rows, columns] = (grad * up * squash * (1.0 + gate * (1.0 - squash))).astype(low)
            return carry

        lax.fori_loop(0, width // 256, narrow, 0, unroll=2)
        store(slot).start()

        @pl.when(slot > 0)
        def _():
            share(slot - 1).wait_send()

        def wide(tile, carry):
            columns = span(tile, 256)
            part = dot(gate_grad[wide_rows, :], gate_w[columns, :], NT) + dot(up_grad[wide_rows, :], up_w[columns, :], NT)
            term[:, columns] = part.astype(low)
            return carry

        lax.fori_loop(0, depth // 256, wide, 0)
        share(slot).start()

        @pl.when(slot == 0)
        def _():
            hidden_grad[...] = term[mine, :].astype(jnp.float32)

        middle = jnp.logical_and(slot >= 2, slot < chips - 1)
        lax.fori_loop(jnp.where(slot == 2, 0, slot), jnp.where(middle, slot + 1, 0), down_term, 0)

        @pl.when(slot > 0)
        def _():
            share(slot).wait_recv()

            @pl.when(slot > 2)
            def _():
                pass_on(slot - 2).wait_send()

            @pl.when(slot == 1)
            def _():
                total[here] = (term[mine, :].astype(jnp.float32) + from_core[1 + here].astype(jnp.float32)).astype(low)

            @pl.when(slot > 1)
            def _():
                pass_on(slot - 1).wait_recv()
                total[here] = (term[mine, :].astype(jnp.float32) + from_core[1 + here].astype(jnp.float32) + from_ring[slot - 2].astype(jnp.float32)).astype(low)

            pass_on(slot).start()

        return carry

    lax.fori_loop(0, chips, step, 0)

    def tiles(index):
        there = span(index, 256)
        return (
            pltpu.make_async_copy(tile_gate.at[index % 2], grad_both.at[there, pl.ds(0, width)], tile_sem.at[0, index % 2]),
            pltpu.make_async_copy(tile_up.at[index % 2], grad_both.at[there, pl.ds(width, width)], tile_sem.at[1, index % 2]),
        )

    def weights(index, carry):
        @pl.when(index > 1)
        def _():
            for copy in tiles(index - 2):
                copy.wait()

        token = tokens_all[:, span(index, 256)]
        tile_gate[index % 2] = dot(token, gate_grad[...], TN).astype(low)
        tile_up[index % 2] = dot(token, up_grad[...], TN).astype(low)
        for copy in tiles(index):
            copy.start()
        return carry

    lax.fori_loop(0 if chips < 4 else chips - 1, chips, down_term, 0)
    lax.fori_loop(0, depth // 256, weights, 0)
    states.wait(0, 1)
    share(0).wait_recv()
    pass_on(chips - 1).wait_recv()
    gain_part[...] = jnp.zeros_like(gain_part)

    def norm(here):
        grad = hidden_grad[here, :] + from_core[0, here, :].astype(jnp.float32) + from_ring[chips - 2, here, :].astype(jnp.float32)
        part, gain_grad = norm_back(hidden_state[here, :], gain[...], grad)
        full = cotangent[here, :] + part
        hidden_grad[here, :] = full
        branch[here, :] = full.astype(low)
        gain_part[...] += gain_grad

    results = RowStores(NORM_ROWS, rows // NORM_ROWS, (hidden_grad, branch), (hidden_grad_out, branch_out), rows_sem)
    by_rows(rows, norm, results)
    share(chips - 1).wait_send()
    for slot in range(chips):
        to_core(slot).wait_send()
        if slot < chips - 1:
            to_ring(slot).wait_send()
        if slot >= max(1, chips - 2):
            pass_on(slot).wait_send()
        store(slot).wait()
    for index in range(depth // 256 - 2, depth // 256):
        for copy in tiles(index):
            copy.wait()
    results.wait()


def feed(chips, shards, hidden_state, cotangent, gain, tokens, grads, w_gate, w_up, w_down, gate_all, up_all, down_near, down_far):
    rows, depth = tokens.shape
    pair = 2 * rows
    group_rows = chips * pair
    width = w_down.shape[0]
    shape = jax.ShapeDtypeStruct
    stored = [shape((rows, depth), jnp.float32), shape((rows, depth), low)]
    return pl.pallas_call(
        lambda *refs: feed_kernel(chips, shards, *refs),
        in_specs=[VMEM] + [ANYWHERE] * 11,
        out_specs=[ANYWHERE] * 2 + [VMEM] + [ANYWHERE] * 3,
        out_shape=stored + [
            shape((1, depth), jnp.float32),
            shape((group_rows, width), low),
            shape((depth, 2 * width), low),
            shape((group_rows, depth), low),
        ],
        scratch_shapes=RowStores.scratch(NORM_ROWS, rows // NORM_ROWS, *stored) + Loads.scratch(hidden_state, cotangent) + [
            pltpu.VMEM((2, pair, 256), low),
            DMA((2,)),
            pltpu.VMEM((group_rows, depth), low),
            pltpu.VMEM((depth, width), low),
            pltpu.VMEM((depth, width), low),
            pltpu.VMEM((width, depth), low),
            pltpu.VMEM((2, pair, depth), low),
            pltpu.VMEM((chips, pair, width), low),
            pltpu.VMEM((group_rows, width), low),
            pltpu.VMEM((group_rows, width), low),
            pltpu.VMEM((pair, depth), low),
            pltpu.VMEM((3, rows, depth), low),
            pltpu.VMEM((chips - 1, rows, depth), low),
            pltpu.VMEM((2, rows, depth), low),
            pltpu.VMEM((2, 256, width), low),
            pltpu.VMEM((2, 256, width), low),
            DMA((3, shards, width // 256)), DMA, DMA((2,)), DMA((chips,)), DMA((2, 2)),
            DMA((chips,)), DMA((chips,)), DMA((chips,)), DMA((chips,)),
            DMA, DMA((3,)), DMA((2,)), DMA((chips - 1,)),
        ],
        compiler_params=pltpu.CompilerParams(collective_id=3, has_side_effects=True, vmem_limit_bytes=67043328),
        cost_estimate=pl.CostEstimate(flops=16 * group_rows * depth * width, bytes_accessed=10 * group_rows * depth, transcendentals=group_rows * width),
        name="feed",
    )(gain, hidden_state, cotangent, tokens, grads, w_gate, w_up, w_down, gate_all, up_all, down_near, down_far)


def finish_kernel(
    shard_ref, hidden, down, hidden_grad, input_part, both, both_from, grad_down, down_from, grad_qkv, grad_out, gains,
    output, input_grad, query, key, value, out, gate, up, down_out, gain_attn, gain_mlp,
):
    gain_attn[...] = gains[0:1, :]
    gain_mlp[...] = gains[1:2, :]
    output[...] = hidden[...] + down[...]
    input_grad[...] = hidden_grad[...] + input_part[...]
    width = query.shape[1]
    for part, ref in enumerate((query, key, value)):
        ref[...] = grad_qkv[:, pl.ds(part * width, width)]
    out[...] = grad_out[...]
    wide = gate.shape[1]
    for side, ref in enumerate((gate, up)):
        columns = pl.ds(side * wide, wide)
        total = both[:, columns].astype(jnp.float32)
        for turn in range(both_from.shape[0]):
            total = total + both_from[turn, :, columns].astype(jnp.float32)
        ref[...] = total
    total = grad_down[...].astype(jnp.float32)
    for turn in range(down_from.shape[0]):
        total = total + down_from[turn].astype(jnp.float32)
    down_out[...] = total


def finish(shard, hidden, down, hidden_grad, input_part, both, both_from, grad_down, down_from, grad_qkv, grad_out, gains):
    steps = 4
    shape = jax.ShapeDtypeStruct
    columns = down_from.shape[2]
    results = [shape(hidden.shape, jnp.float32)] * 2
    results += [shape((columns, grad_qkv.shape[1] // 3), jnp.float32)] * 3 + [shape(grad_out.shape, jnp.float32)]
    results += [shape((columns, both.shape[1] // 2), jnp.float32)] * 2 + [shape((grad_down.shape[0], columns), jnp.float32)]
    spec = lambda a: pl.BlockSpec((a.shape[0] // steps, a.shape[1]), lambda i, s: (i, 0))
    spec3 = lambda a: pl.BlockSpec((a.shape[0], a.shape[1] // steps, a.shape[2]), lambda i, s: (0, i, 0))
    return pl.pallas_call(
        finish_kernel,
        grid_spec=pltpu.PrefetchScalarGridSpec(
            num_scalar_prefetch=1,
            grid=(steps,),
            in_specs=[
                spec(hidden), spec(down), spec(hidden_grad), spec(input_part),
                pl.BlockSpec((columns // steps, both.shape[1]), lambda i, s: (s[0] * steps + i, 0)),
                spec3(both_from),
                pl.BlockSpec((grad_down.shape[0] // steps, columns), lambda i, s: (i, s[0])),
                spec3(down_from), spec(grad_qkv), spec(grad_out),
                pl.BlockSpec(gains.shape, lambda i, s: (0, 0)),
            ],
            out_specs=[spec(a) for a in results] + [pl.BlockSpec((1, gains.shape[1]), lambda i, s: (0, 0))] * 2,
        ),
        out_shape=results + [shape((1, gains.shape[1]), jnp.float32)] * 2,
        name="finish",
    )(shard.reshape(1), hidden, down, hidden_grad, input_part, both, both_from, grad_down, down_from, grad_qkv, grad_out, gains)


def rope_frequencies():
    column = np.arange(HEAD_DIM // 2)
    return jnp.asarray((rope_base ** (-2.0 * column / HEAD_DIM)).astype(np.float32)[:, None])


def make_body(mesh):
    chips, shards = mesh.shape["tp"] // 2, mesh.shape["fsdp"]

    def body(activations, gain_attn, w_query, w_key, w_value, w_out, gain_mlp, w_gate, w_up, w_down, cotangent):
        gain_attn, gain_mlp = gain_attn[None, :], gain_mlp[None, :]
        seen_attn, w_qkv, full_out, qkv, keys_t, values_t, cosine, sine, down_near = project(
            chips, shards, activations, gain_attn, w_query, w_key, w_value, w_out, rope_frequencies(), w_down
        )
        hidden_state, normed_mlp, mixed, totals, seen_grad, gate_all, up_all, down_far = attend(
            chips, shards, qkv, values_t, full_out, activations, cotangent, gain_mlp, w_gate, w_up, down_near
        )
        hidden_grad, branch_grad, gain_part, inner, grad_both, terms = feed(
            chips, shards, hidden_state, cotangent, gain_mlp, normed_mlp, seen_grad,
            w_gate, w_up, w_down, gate_all, up_all, down_near, down_far,
        )
        down, _, qkv_grad, grad_down, grad_out, both_from = back(
            chips, shards, branch_grad, terms, inner, seen_grad, grad_both, full_out, qkv, keys_t, mixed, totals, cosine, sine
        )
        input_part, grad_qkv, gain_sums, down_from = spread(
            chips, shards, qkv_grad, w_qkv, activations, gain_attn, gain_part, seen_attn, grad_down
        )
        output, input_grad, grad_query, grad_key, grad_value, grad_out, grad_gate, grad_up, grad_down, gain_attn, gain_mlp = finish(
            lax.axis_index("fsdp"), hidden_state, down, hidden_grad, input_part,
            grad_both, both_from, grad_down, down_from, grad_qkv, grad_out, gain_sums,
        )
        return (
            output, input_grad, gain_attn[0], grad_query, grad_key, grad_value, grad_out, gain_mlp[0],
            grad_gate, grad_up, grad_down,
        )

    return body


def solution(mesh):
    tokens = P(("fsdp", "tp"), None)
    column = P("fsdp", "tp")
    row = P("tp", "fsdp")
    in_specs = (tokens, P(), column, column, column, row, P(), column, column, row, tokens)
    out_specs = (tokens, tokens, P(), column, column, column, row, P(), column, column, row)
    return jax.shard_map(make_body(mesh), mesh=mesh, in_specs=in_specs, out_specs=out_specs, check_vma=False)
```
